32 devices in a mesh: row: 8 (over z, x), col: 4 (over y, core).
Axes of the slice: x: 2, y: 2, z: 4, core: 2. Of those that a mesh axis runs over, the one named last changes fastest.
Arguments:
- latents: bfloat16 [1408, 24576], P('col', 'row'), may hold values from -6 to 6
- skip_input: bfloat16 [1408, 24576], P('col', 'row'), may hold values from -6 to 6
- condition: bfloat16 [24, 1408], P('row', 'col'), may hold values from -6 to 6
- text_states: bfloat16 [24, 333, 1024], P('row', None, 'col'), may hold values from -6 to 6
- text_lengths: int32 [24], P('row'), may hold values from 42 to 333
- positions: int32 [2, 24576], P(None, 'row'), may hold values from 0 to 31
- out_grad: float32 [1408, 24576], P('col', 'row'), may hold values from -6 to 6
- skip_weight: bfloat16 [2, 1408, 1408], P(None, 'row', 'col'), may hold values from -0.109375 to 0.109375
- modulation: bfloat16 [1408, 2, 1408], P('row', None, 'col'), may hold values from -0.15625 to 0.15625
- self_inputs: bfloat16 [1408, 3, 1408], P('row', None, 'col'), may hold values from -0.15625 to 0.15625
- self_output: bfloat16 [1408, 1408], P('col', 'row'), may hold values from -1.75 to 1.75
- cross_query: bfloat16 [1408, 1408], P('row', 'col'), may hold values from -0.15625 to 0.15625
- cross_keyvalue: bfloat16 [1024, 2, 1408], P('row', None, 'col'), may hold values from -0.1875 to 0.1875
- cross_output: bfloat16 [1408, 1408], P('col', 'row'), may hold values from -1 to 1
- expand_weight: bfloat16 [1408, 6144], P('row', 'col'), may hold values from -0.15625 to 0.15625
- reduce_weight: bfloat16 [6144, 1408], P('col', 'row'), may hold values from -0.078125 to 0.078125
- skip_gain: float32 [1408], P('col'), may hold values from 0.5 to 1.5
- skip_bias: float32 [1408], P('col'), may hold values from -3 to 3
- cross_gain: float32 [1408], P('col'), may hold values from 0.5 to 1.5
- cross_bias: float32 [1408], P('col'), may hold values from -3 to 3
- hidden_gain: float32 [1408], P('col'), may hold values from 0.5 to 1.5
- hidden_bias: float32 [1408], P('col'), may hold values from -3 to 3
- query_gain: float32 [88], replicated, may hold values from 0.5 to 1.5
- key_gain: float32 [88], replicated, may hold values from 0.5 to 1.5
- cross_query_gain: float32 [88], replicated, may hold values from 0.5 to 1.5
- text_key_gain: float32 [88], replicated, may hold values from 0.5 to 1.5
Outputs:
- output: float32 [1408, 24576], P('col', 'row')
- grad_latents: float32 [1408, 24576], P('col', 'row')
- grad_skip: float32 [1408, 24576], P('col', 'row')
- grad_skip_weight: float32 [2, 1408, 1408], P(None, 'row', 'col')
- grad_modulation: float32 [1408, 2, 1408], P('row', None, 'col')
- grad_self_inputs: float32 [1408, 3, 1408], P('row', None, 'col')
- grad_self_output: float32 [1408, 1408], P('col', 'row')
- grad_cross_query: float32 [1408, 1408], P('row', 'col')
- grad_cross_keyvalue: float32 [1024, 2, 1408], P('row', None, 'col')
- grad_cross_output: float32 [1408, 1408], P('col', 'row')
- grad_expand: float32 [1408, 6144], P('row', 'col')
- grad_reduce: float32 [6144, 1408], P('col', 'row')
- grad_skip_gain: float32 [1408], P('col')
- grad_skip_bias: float32 [1408], P('col')
- grad_cross_gain: float32 [1408], P('col')
- grad_cross_bias: float32 [1408], P('col')
- grad_hidden_gain: float32 [1408], P('col')
- grad_hidden_bias: float32 [1408], P('col')
- grad_query_gain: float32 [88], replicated
- grad_key_gain: float32 [88], replicated
- grad_cross_query_gain: float32 [88], replicated
- grad_text_key_gain: float32 [88], replicated
The draws below stay inside these ranges and needn't reach their ends.
All inputs are finite; a program needn't handle non-finite values.
Results may differ from the reference program's by a relative error of at most 0.025.
Values may be sent and summed in bfloat16 or wider, within the bound.
A program may use at most 512 MiB of HBM per device.

```python
import math
import jax
import jax.numpy as jnp
from jax import lax

D = 1408
H = 16
HD = 88
FF = 6144
TD = 1024
TT = 333
L = 1024
SEQS = 24
TOKENS = 24576


def place_ends(drawn, rng, smallest, high):
    extent = drawn.shape
    place = [jax.random.randint(jax.random.fold_in(rng, axis), (), 0, extent[axis]) for axis in range(len(extent))]
    drawn = drawn.at[tuple(place)].set(smallest)
    longest = extent.index(max(extent))
    place[longest] = (place[longest] + 1) % extent[longest]
    return drawn.at[tuple(place)].set(high)


def block_levels(own_key, dims, shards, smallest, top_value):
    gain, own = 1.0, jax.random.fold_in(own_key, 6)
    for position, parts in shards:
        draws = jnp.exp(jax.random.uniform(jax.random.fold_in(own, position), (parts,), jnp.float32, smallest / len(shards), top_value / len(shards)))
        gain = gain * jnp.repeat(draws, dims[position] // parts).reshape([-1 if axis == position else 1 for axis in range(len(dims))])
    return gain


def bell_draw(key, extent, spread, limit, cuts=(), kind=jnp.bfloat16):
    gain = block_levels(key, extent, cuts, -0.22, 0.18) if cuts else 1.0
    drawn = jax.random.normal(key, extent, jnp.float32) * spread * gain
    return jnp.minimum(jnp.maximum(drawn, -limit), limit).astype(kind)


def setup_inputs(seed: int = 0) -> dict:
    key_list = jax.random.split(jax.random.key(seed), 27)
    latents = bell_draw(key_list[0], (D, TOKENS), 1.0, 6.0, ((0, 4), (1, 8)))
    skip_input = bell_draw(key_list[1], (D, TOKENS), 1.0, 6.0, ((0, 4), (1, 8)))
    condition = bell_draw(key_list[2], (SEQS, D), 1.0, 6.0, ((0, 8), (1, 4)))
    text_states = bell_draw(key_list[3], (SEQS, TT, TD), 1.0, 6.0, ((0, 8), (2, 4)))
    text_lengths = place_ends(jax.random.randint(key_list[4], (SEQS,), TT // 8 + 1, TT + 1), jax.random.fold_in(key_list[4], 1), TT // 8 + 1, TT).astype(jnp.int32)
    positions = place_ends(jax.random.randint(key_list[5], (2, TOKENS), 0, 32), jax.random.fold_in(key_list[5], 1), 0, 31).astype(jnp.int32)
    out_grad = bell_draw(key_list[6], (D, TOKENS), 1.0, 6.0, ((0, 4), (1, 8)), jnp.float32)
    skip_weight = bell_draw(key_list[7], (2, D, D), (2 * D) ** -0.5, 0.109375, ((1, 8), (2, 4)))
    modulation = bell_draw(key_list[8], (D, 2, D), D ** -0.5, 0.15625, ((0, 8), (2, 4)))
    self_inputs = bell_draw(key_list[9], (D, 3, D), D ** -0.5, 0.15625, ((0, 8), (2, 4)))
    self_output = bell_draw(key_list[10], (D, D), (D * 8 // L) ** -0.5, 1.75, ((0, 4), (1, 8)))
    cross_query = bell_draw(key_list[11], (D, D), D ** -0.5, 0.15625, ((0, 8), (1, 4)))
    cross_keyvalue = bell_draw(key_list[12], (TD, 2, D), TD ** -0.5, 0.1875, ((0, 8), (2, 4)))
    cross_output = bell_draw(key_list[13], (D, D), (D * 8 // TT) ** -0.5, 1.0, ((0, 4), (1, 8)))
    expand_weight = bell_draw(key_list[14], (D, FF), D ** -0.5, 0.15625, ((0, 8), (1, 4)))
    reduce_weight = bell_draw(key_list[15], (FF, D), FF ** -0.5, 0.078125, ((0, 4), (1, 8)))
    skip_gain = jnp.clip(1.0 + 0.1 * jax.random.normal(key_list[16], (D,), jnp.float32), 0.5, 1.5)
    skip_bias = bell_draw(key_list[17], (D,), 0.5, 3.0, ((0, 4),), jnp.float32)
    cross_gain = jnp.clip(1.0 + 0.1 * jax.random.normal(key_list[18], (D,), jnp.float32), 0.5, 1.5)
    cross_bias = bell_draw(key_list[19], (D,), 0.5, 3.0, ((0, 4),), jnp.float32)
    hidden_gain = jnp.clip(1.0 + 0.1 * jax.random.normal(key_list[20], (D,), jnp.float32), 0.5, 1.5)
    hidden_bias = bell_draw(key_list[21], (D,), 0.5, 3.0, ((0, 4),), jnp.float32)
    query_gain = jnp.clip(1.0 + 0.1 * jax.random.normal(key_list[22], (HD,), jnp.float32), 0.5, 1.5)
    key_gain = jnp.clip(1.0 + 0.1 * jax.random.normal(key_list[23], (HD,), jnp.float32), 0.5, 1.5)
    cross_query_gain = jnp.clip(1.0 + 0.1 * jax.random.normal(key_list[24], (HD,), jnp.float32), 0.5, 1.5)
    text_key_gain = jnp.clip(1.0 + 0.1 * jax.random.normal(key_list[25], (HD,), jnp.float32), 0.5, 1.5)
    return dict(latents=latents, skip_input=skip_input, condition=condition, text_states=text_states, text_lengths=text_lengths, positions=positions, out_grad=out_grad, skip_weight=skip_weight, modulation=modulation, self_inputs=self_inputs, self_output=self_output, cross_query=cross_query, cross_keyvalue=cross_keyvalue, cross_output=cross_output, expand_weight=expand_weight, reduce_weight=reduce_weight, skip_gain=skip_gain, skip_bias=skip_bias, cross_gain=cross_gain, cross_bias=cross_bias, hidden_gain=hidden_gain, hidden_bias=hidden_bias, query_gain=query_gain, key_gain=key_gain, cross_query_gain=cross_query_gain, text_key_gain=text_key_gain)


@jax.custom_vjp
def low(v):
    return lax.optimization_barrier(v.astype(jnp.bfloat16)).astype(jnp.float32)

@jax.custom_vjp
def low_back(v):
    return v

def low_keep(v):
    return (low(v), None)

def low_pass(kept, grad):
    return (grad,)

def back_keep(v):
    return (v, None)

def back_low(kept, grad):
    return (low(grad),)
low.defvjp(low_keep, low_pass)
low_back.defvjp(back_keep, back_low)
EPSILON = 1e-06
HIGHEST = lax.Precision.HIGHEST

def matmul(left, right):
    return jnp.dot(left, right, precision=HIGHEST)

def layer_norm(values):
    average = lax.optimization_barrier(jnp.mean(values, -1, keepdims=True))
    centred = values - average
    variance = lax.optimization_barrier(jnp.mean(centred * centred, -1, keepdims=True))
    return centred * lax.rsqrt(variance + EPSILON)

def rope_tables(places, head_dim):
    quarter = head_dim // 4
    freqs = jnp.exp(jnp.arange(quarter, dtype=jnp.float32) * (-4.0 * math.log(10000.0) / head_dim))
    angle_rows = places[0].astype(jnp.float32)[:, None] * freqs[None, :]
    angle_cols = places[1].astype(jnp.float32)[:, None] * freqs[None, :]
    cosine = jnp.concatenate([jnp.cos(angle_rows), jnp.cos(angle_rows), jnp.cos(angle_cols), jnp.cos(angle_cols)], 1)
    sine = jnp.concatenate([jnp.sin(angle_rows), jnp.sin(angle_rows), jnp.sin(angle_cols), jnp.sin(angle_cols)], 1)
    return (cosine, sine)

def rotate(values):
    quarter = values.shape[-1] // 4
    part_one = values[..., :quarter]
    part_two = values[..., quarter:2 * quarter]
    part_three = values[..., 2 * quarter:3 * quarter]
    part_four = values[..., 3 * quarter:]
    return jnp.concatenate([-part_two, part_one, -part_four, part_three], -1)

def apply_rope(values, cosine, sine):
    return values * cosine + rotate(values) * sine

def attend(query_in, key_in, value_in, valid):
    product = low_back(jnp.einsum('qhd,khd->hqk', query_in, key_in, precision=HIGHEST))
    scores = product * HD ** (-0.5)
    scores = jnp.where(valid[None, None, :], scores, -1000000000.0)
    weights = low(jax.nn.softmax(scores, -1))
    mixed = jnp.einsum('hqk,khd->qhd', weights, value_in, precision=HIGHEST)
    return low(low_back(mixed))

def one_sequence(params, latent, skipped, cond, text, length, places):
    skip_weight, modulation, self_inputs, self_output, cross_query, cross_keyvalue, cross_output, expand_weight, reduce_weight, skip_gain, skip_bias, cross_gain, cross_bias, hidden_gain, hidden_bias, query_gain, key_gain, cross_query_gain, text_key_gain = params
    joined = low_back(matmul(latent, skip_weight[0]) + matmul(skipped, skip_weight[1]))
    stream = layer_norm(joined) * skip_gain + skip_bias
    embed = low(jax.nn.silu(cond))
    modul = low_back(matmul(embed, modulation.reshape(D, 2 * D))).reshape(2, D)
    normed = low(layer_norm(stream) * (1.0 + modul[1]) + modul[0])
    triple = low_back(matmul(normed, self_inputs.reshape(D, 3 * D))).reshape(L, 3, H, HD)
    cosine, sine = rope_tables(places, HD)
    cosine = cosine[:, None, :]
    sine = sine[:, None, :]
    query_one = low(apply_rope(layer_norm(triple[:, 0]) * query_gain, cosine, sine))
    key_one = low(apply_rope(layer_norm(triple[:, 1]) * key_gain, cosine, sine))
    value_one = low(triple[:, 2])
    every = jnp.arange(L) < L
    mixed = attend(query_one, key_one, value_one, every).reshape(L, D)
    stream = stream + low_back(matmul(mixed, self_output))
    normed = low(layer_norm(stream) * cross_gain + cross_bias)
    raw_query = low_back(matmul(normed, cross_query)).reshape(L, H, HD)
    pair = low_back(matmul(text, cross_keyvalue.reshape(TD, 2 * D))).reshape(TT, 2, H, HD)
    query_two = low(layer_norm(raw_query) * cross_query_gain)
    key_two = low(layer_norm(pair[:, 0]) * text_key_gain)
    value_two = low(pair[:, 1])
    valid = jnp.arange(TT) < length
    mixed = attend(query_two, key_two, value_two, valid).reshape(L, D)
    stream = stream + low_back(matmul(mixed, cross_output))
    normed = low(layer_norm(stream) * hidden_gain + hidden_bias)
    inner = low_back(matmul(normed, expand_weight))
    activated = low(jax.nn.gelu(inner, approximate=True))
    return stream + low_back(matmul(activated, reduce_weight))

def reference(latents, skip_input, condition, text_states, text_lengths, positions, out_grad, skip_weight, modulation, self_inputs, self_output, cross_query, cross_keyvalue, cross_output, expand_weight, reduce_weight, skip_gain, skip_bias, cross_gain, cross_bias, hidden_gain, hidden_bias, query_gain, key_gain, cross_query_gain, text_key_gain):
    params = tuple((item.astype(jnp.float32) for item in (skip_weight, modulation, self_inputs, self_output, cross_query, cross_keyvalue, cross_output, expand_weight, reduce_weight, skip_gain, skip_bias, cross_gain, cross_bias, hidden_gain, hidden_bias, query_gain, key_gain, cross_query_gain, text_key_gain)))
    latent_all = latents.astype(jnp.float32).T.reshape(SEQS, L, D)
    skip_all = skip_input.astype(jnp.float32).T.reshape(SEQS, L, D)
    cond_all = condition.astype(jnp.float32)
    text_all = text_states.astype(jnp.float32)
    place_all = positions.reshape(2, SEQS, L).transpose(1, 0, 2)

    def forward(weights, latent_in, skip_in):

        def per_item(item):
            return jax.checkpoint(one_sequence)(weights, *item)
        return lax.map(per_item, (latent_in, skip_in, cond_all, text_all, text_lengths, place_all))
    result, pull = jax.vjp(forward, params, latent_all, skip_all)
    grads, grad_latent, grad_skipped = pull(out_grad.T.reshape(SEQS, L, D))
    return (result.reshape(TOKENS, D).T, grad_latent.reshape(TOKENS, D).T, grad_skipped.reshape(TOKENS, D).T, grads[0], grads[1], grads[2], grads[3], grads[4], grads[5], grads[6], grads[7], grads[8], grads[9], grads[10], grads[11], grads[12], grads[13], grads[14], grads[15], grads[16], grads[17], grads[18])
```

```python
from functools import partial
import math

import jax
import jax.numpy as jnp
from jax import lax
from jax.experimental import pallas as pl
from jax.experimental.pallas import tpu as pltpu
from jax.sharding import PartitionSpec as P

L = 1024
EPSILON = 1e-06
BF = jnp.bfloat16
F32 = jnp.float32
KEYPAD = 128
DEVICES = ("col", "row")


def einsum(spec, left, right):
    return jnp.einsum(spec, left, right, preferred_element_type=F32)


def dot(left, right, dims):
    return lax.dot_general(left, right, (dims, ((), ())), preferred_element_type=F32)


def block_of(length):
    return 256 if length % 256 == 0 else length


def attend_kernel(masked, scale, length_ref, q_ref, k_ref, v_ref, o_ref, lse_ref):
    queries = q_ref.shape[2]
    keys = k_ref.shape[2]
    step = block_of(queries)
    key = k_ref[0]
    value = v_ref[0]
    for first in range(0, queries, step):
        query = q_ref[0, :, first : first + step]
        scores = dot(key, query, ((0,), (0,))) * scale
        if masked:
            place = lax.broadcasted_iota(jnp.int32, (keys, step), 0)
            scores = jnp.where(place < length_ref[0], scores, -1e9)
        peak = jnp.max(scores, 0, keepdims=True)
        expo = jnp.exp(scores - peak)
        total = jnp.sum(expo, 0, keepdims=True)
        probs = (expo * (1.0 / total)).astype(BF)
        o_ref[0, :, first : first + step] = dot(value, probs, ((1,), (0,))).astype(BF)
        lse_ref[0, :, first : first + step] = peak + jnp.log(total)


def attend_back_kernel(
    masked, scale, length_ref, q_ref, k_ref, v_ref, g_ref, lse_ref, dq_ref, dk_ref, dv_ref
):
    queries = q_ref.shape[2]
    keys = k_ref.shape[2]
    step = block_of(queries)
    key = k_ref[0]
    value = v_ref[0]
    grad_key = None
    grad_value = None
    for first in range(0, queries, step):
        query = q_ref[0, :, first : first + step]
        grad = g_ref[0, :, first : first + step]
        scores = dot(key, query, ((0,), (0,))) * scale
        if masked:
            place = lax.broadcasted_iota(jnp.int32, (keys, step), 0)
            scores = jnp.where(place < length_ref[0], scores, -1e9)
        probs = jnp.exp(scores - lse_ref[0, :, first : first + step])
        part_value = dot(grad, probs.astype(BF), ((1,), (1,)))
        grad_probs = dot(value, grad, ((0,), (0,)))
        crossed = probs * grad_probs
        delta = jnp.sum(crossed, 0, keepdims=True)
        product = ((crossed - probs * delta) * scale).astype(BF)
        dq_ref[0, :, first : first + step] = dot(key, product, ((1,), (0,))).astype(dq_ref.dtype)
        part_key = dot(query, product, ((1,), (1,)))
        grad_key = part_key if grad_key is None else grad_key + part_key
        grad_value = part_value if grad_value is None else grad_value + part_value
    dk_ref[0] = grad_key.astype(dk_ref.dtype)
    dv_ref[0] = grad_value.astype(dv_ref.dtype)


def costs(heads, queries, keys, dim, products, moved):
    return pl.CostEstimate(
        flops=2 * products * heads * queries * keys * dim,
        transcendentals=heads * queries * keys,
        bytes_accessed=moved,
    )


def attend(length, query, key, value, masked):
    heads, dim, queries = query.shape
    keys = key.shape[2]
    wide = pl.BlockSpec((1, dim, queries), lambda h: (h, 0, 0))
    narrow = pl.BlockSpec((1, dim, keys), lambda h: (h, 0, 0))
    line = pl.BlockSpec((1, 1, queries), lambda h: (h, 0, 0))
    return pl.pallas_call(
        partial(attend_kernel, masked, dim ** (-0.5)),
        grid=(heads,),
        in_specs=[pl.BlockSpec(memory_space=pltpu.SMEM), wide, narrow, narrow],
        out_specs=[wide, line],
        out_shape=[
            jax.ShapeDtypeStruct((heads, dim, queries), BF),
            jax.ShapeDtypeStruct((heads, 1, queries), F32),
        ],
        cost_estimate=costs(heads, queries, keys, dim, 2, 4 * heads * dim * (queries + keys)),
    )(length, query, key, value)


def attend_back(length, query, key, value, grad, logsum, masked, kind):
    heads, dim, queries = query.shape
    keys = key.shape[2]
    wide = pl.BlockSpec((1, dim, queries), lambda h: (h, 0, 0))
    narrow = pl.BlockSpec((1, dim, keys), lambda h: (h, 0, 0))
    line = pl.BlockSpec((1, 1, queries), lambda h: (h, 0, 0))
    return pl.pallas_call(
        partial(attend_back_kernel, masked, dim ** (-0.5)),
        grid=(heads,),
        in_specs=[pl.BlockSpec(memory_space=pltpu.SMEM), wide, narrow, narrow, wide, line],
        out_specs=[wide, narrow, narrow],
        out_shape=[
            jax.ShapeDtypeStruct((heads, dim, queries), kind),
            jax.ShapeDtypeStruct((heads, dim, keys), kind),
            jax.ShapeDtypeStruct((heads, dim, keys), kind),
        ],
        cost_estimate=costs(heads, queries, keys, dim, 5, 7 * heads * dim * (queries + keys)),
    )(length, query, key, value, grad, logsum)


def normalize(values):
    average = jnp.mean(values, 0, keepdims=True)
    centred = values - average
    inverse = lax.rsqrt(jnp.mean(centred * centred, 0, keepdims=True) + EPSILON)
    return centred * inverse, inverse


def norm_back(grad, normal, inverse):
    average = jnp.mean(grad, 0, keepdims=True)
    crossed = jnp.mean(grad * normal, 0, keepdims=True)
    return inverse * (grad - average - normal * crossed)


def head_norm(values, gain):
    average = jnp.mean(values, 1, keepdims=True)
    centred = values - average
    variance = jnp.mean(centred * centred, 1, keepdims=True)
    return centred * lax.rsqrt(variance + EPSILON) * gain[None, :, None]


def rope_tables(places, head_dim):
    quarter = head_dim // 4
    freqs = jnp.exp(jnp.arange(quarter, dtype=F32) * (-4.0 * math.log(10000.0) / head_dim))
    rows = freqs[:, None] * places[0].astype(F32)[None, :]
    cols = freqs[:, None] * places[1].astype(F32)[None, :]
    angles = jnp.concatenate([rows, rows, cols, cols], 0)
    return jnp.cos(angles), jnp.sin(angles)


def rotate(values):
    quarter = values.shape[1] // 4
    one, two, three, four = (values[:, i * quarter : (i + 1) * quarter] for i in range(4))
    return jnp.concatenate([-two, one, -four, three], 1)


class Piece:
    def __init__(self, start, count, group, sequence):
        self.start = start
        self.count = count
        self.group = group
        self.sequence = sequence


def pieces_of(cols, sequences):
    mine = lax.axis_index("col")
    if cols == 4 and sequences == 3:
        return [
            Piece(0, L // 2, 2, mine // 2),
            Piece(2 * L, L // 4, 4, jnp.int32(2)),
        ]
    return [Piece(s * L, L // cols, cols, jnp.int32(s)) for s in range(sequences)]


def groups_of(size, cols):
    return [list(range(i, i + size)) for i in range(0, cols, size)]


def exchange(values, size, cols):
    if size == cols:
        return lax.all_to_all(values, "col", 0, 0, tiled=True)
    return lax.all_to_all(
        values, "col", 0, 0, tiled=True, axis_index_groups=groups_of(size, cols)
    )


def to_tokens(values, pieces, cols):
    width = values.shape[0]
    parts = []
    for piece in pieces:
        region = values[:, piece.start : piece.start + cols * piece.count]
        parts.append(region.reshape(width, cols, piece.count).transpose(1, 0, 2))
    stacked = jnp.concatenate(parts, 2)
    return exchange(stacked, cols, cols).reshape(cols * width, -1)


def to_features(values, pieces, cols):
    width = values.shape[0] // cols
    got = exchange(values.reshape(cols, width, -1), cols, cols)
    parts = []
    at = 0
    for piece in pieces:
        part = got[:, :, at : at + piece.count]
        parts.append(part.transpose(1, 0, 2).reshape(width, cols * piece.count))
        at += piece.count
    return jnp.concatenate(parts, 1)


def to_heads(values, piece, cols):
    many, heads, dim, count = values.shape
    size = piece.group
    split = values.reshape(many, size, heads // size, dim, count).transpose(1, 0, 2, 3, 4)
    got = exchange(split, size, cols)
    return got.transpose(1, 2, 3, 0, 4).reshape(many, heads // size, dim, size * count)


def from_heads(values, piece, cols):
    many, heads, dim, total = values.shape
    size = piece.group
    split = values.reshape(many, heads, dim, size, total // size).transpose(3, 0, 1, 2, 4)
    got = exchange(split, size, cols)
    return got.transpose(1, 0, 2, 3, 4).reshape(many, size * heads, dim, total // size)


def gather_weights(blocks):
    cols = lax.axis_size("col")
    most = max(block.shape[0] for block in blocks)
    padded = [jnp.pad(b, ((0, most - b.shape[0]), (0, 0))) for b in blocks]
    whole = lax.all_gather(jnp.stack(padded, 0), DEVICES, axis=1, tiled=True)
    result = []
    for index, block in enumerate(blocks):
        part = whole[index].reshape(cols, -1, most, block.shape[1])[:, :, : block.shape[0]]
        result.append(part.reshape(cols, -1, block.shape[1]))
    return result


def pick(values, axis, index):
    return lax.dynamic_index_in_dim(values, index, axis, False)


def add(left, right):
    return (left.astype(F32) + right.astype(F32)).astype(BF)


def swap(values, axis, bit):
    size = lax.axis_size(axis)
    return lax.ppermute(values, axis, [(i, i ^ bit) for i in range(size)])


def halves(blocks):
    core = lax.axis_index("col") % 2
    split = blocks.reshape(blocks.shape[0] // 2, 2, *blocks.shape[1:])
    return pick(split, 1, core), pick(split, 1, 1 - core)


def scatter_grad(keep, send, across):
    cols = lax.axis_size("col")
    rows = lax.axis_size("row")
    if (rows, cols) != (8, 4):
        core = lax.axis_index("col") % 2
        pair = jnp.stack([keep, send], 1)
        pair = jnp.where(core == 0, pair, pair[:, ::-1])
        flat = pair.reshape(-1, keep.shape[2])
        return lax.psum_scatter(flat, DEVICES, scatter_dimension=0, tiled=True).astype(F32)
    up = lax.axis_index("col") // 2
    side = lax.axis_index("row") % 2
    level = lax.axis_index("row") // 2
    shape = (2, 4, 2, keep.shape[1] // 8, keep.shape[2])
    got = swap(send, "col", 1).reshape(shape)
    keep = keep.reshape(shape)

    def stage(kept, got, axis, index, name, bit):
        away = add(pick(kept, axis, 1 - index), pick(got, axis, 1 - index))
        here = add(pick(kept, axis, index), pick(got, axis, index))
        return here, swap(away, name, bit)

    if across:
        keep, got = stage(keep, got, 2, side, "row", 1)
        keep, got = stage(keep, got, 0, up, "col", 2)
    else:
        keep, got = stage(keep, got, 0, up, "col", 2)
        keep, got = stage(keep, got, 1, side, "row", 1)
    total = add(keep, got)
    result = pick(total, 0, level).astype(F32)
    for other in (1, 2, 3):
        result = result + swap(pick(total, 0, level ^ other), "row", 2 * other).astype(F32)
    return result


def weight_grad(spec, across, fixed, blocks):
    mine, others = halves(blocks)
    send = einsum(spec, fixed, others).astype(BF)
    keep = einsum(spec, fixed, mine).astype(BF)
    return scatter_grad(keep, send, across)


def shards(
    latents,
    skip_input,
    condition,
    text_states,
    text_lengths,
    positions,
    out_grad,
    skip_weight,
    modulation,
    self_inputs,
    self_output,
    cross_query,
    cross_keyvalue,
    cross_output,
    expand_weight,
    reduce_weight,
    skip_gain,
    skip_bias,
    cross_gain,
    cross_bias,
    hidden_gain,
    hidden_bias,
    query_gain,
    key_gain,
    cross_query_gain,
    text_key_gain,
):
    cols = lax.axis_size("col")
    rows = lax.axis_size("row")
    mine = lax.axis_index("col")
    my_row = lax.axis_index("row")
    width, row_tokens = latents.shape
    depth = width * cols
    dim = query_gain.shape[0]
    heads = depth // dim
    sequences = row_tokens // L
    tokens = row_tokens // cols
    texts = text_states.shape[1]
    keys = -(-texts // KEYPAD) * KEYPAD
    pieces = pieces_of(cols, sequences)
    starts = [sum(p.count for p in pieces[:i]) for i in range(len(pieces))]

    def cut(values, index):
        return values[..., starts[index] : starts[index] + pieces[index].count]

    first = gather_weights(
        [skip_weight[0], skip_weight[1], self_inputs[:, 0], self_inputs[:, 1], self_inputs[:, 2]]
    )
    w_skip, w_self = first[:2], first[2:]
    w_attn, w_query, w_cross, *w_text = gather_weights(
        [self_output.T, cross_query, cross_output.T, cross_keyvalue[:, 0], cross_keyvalue[:, 1]]
    )
    w_expand, w_reduce = gather_weights([expand_weight, reduce_weight.T])

    gains = jnp.stack(
        [skip_gain, skip_bias, cross_gain, cross_bias, hidden_gain, hidden_bias], 0
    )
    gains = lax.all_gather(gains, "col", axis=1, tiled=True)[:, :, None]
    gain_skip, bias_skip, gain_cross, bias_cross, gain_hidden, bias_hidden = gains

    latent = to_tokens(latents, pieces, cols)
    skipped = to_tokens(skip_input, pieces, cols)
    grad_out = to_tokens(out_grad.astype(BF), pieces, cols)
    text = lax.all_gather(
        jnp.pad(text_states, ((0, 0), (0, keys - texts), (0, 0))), "col", axis=2, tiled=True
    )
    places = jnp.concatenate(
        [
            lax.dynamic_slice_in_dim(positions, p.start + mine * p.count, p.count, 1)
            for p in pieces
        ],
        1,
    )

    embed = lax.all_gather(jax.nn.silu(condition.astype(F32)).astype(BF), "row", axis=0, tiled=True)
    embed_all = lax.all_gather(embed, "col", axis=1, tiled=True)
    block_rows = depth // rows
    embed_rows = lax.dynamic_slice_in_dim(embed_all, my_row * block_rows, block_rows, 1)
    modul_part = einsum("sd,dke->ske", embed_rows, modulation)
    modul = lax.psum(modul_part, "row")
    modul = lax.dynamic_slice_in_dim(modul, my_row * sequences, sequences, 0)
    modul = lax.all_gather(modul, "col", axis=2, tiled=True)
    token_index = lax.broadcasted_iota(jnp.int32, (1, tokens), 1)
    chosen = jnp.stack([lax.dynamic_index_in_dim(modul, p.sequence, 0, False) for p in pieces], 0)
    chosen = lax.optimization_barrier(chosen.reshape(-1, depth)).T

    def per_token(which):
        result = chosen[:, which : which + 1]
        for index in range(1, len(pieces)):
            column = chosen[:, 2 * index + which : 2 * index + which + 1]
            result = jnp.where(token_index >= starts[index], column, result)
        return jnp.broadcast_to(result, (depth, tokens))

    shifting = per_token(0)
    scaling = 1.0 + per_token(1)

    def project(weight, values):
        return einsum("ckn,kt->cnt", weight, values).reshape(-1, values.shape[1])

    def output_project(weight, values):
        return einsum("cnk,ckt->nt", weight, values.reshape(cols, -1, values.shape[1]))

    joined = project(w_skip[0], latent) + project(w_skip[1], skipped)
    skip_normal, skip_inverse = normalize(joined)
    stream = skip_normal * gain_skip + bias_skip
    normal_one, inverse_one = normalize(stream)
    normed_one = (normal_one * scaling + shifting).astype(BF)
    raw = [project(w, normed_one).reshape(heads, dim, tokens) for w in w_self]
    cosine, sine = rope_tables(places, dim)

    def self_piece(value, gain):
        normal = head_norm(value, gain)
        return normal * cosine[None] + rotate(normal) * sine[None]

    rot_query, query_pull = jax.vjp(self_piece, raw[0], query_gain)
    rot_key, key_pull = jax.vjp(self_piece, raw[1], key_gain)
    triple = jnp.stack([rot_query.astype(BF), rot_key.astype(BF), raw[2].astype(BF)], 0)
    none = jnp.zeros((1,), jnp.int32)
    saved_self = []
    mixed_parts = []
    for index, piece in enumerate(pieces):
        whole = to_heads(cut(triple, index), piece, cols)
        mixed, logsum = attend(none, whole[0], whole[1], whole[2], False)
        saved_self.append((whole, logsum))
        mixed_parts.append(from_heads(mixed[None], piece, cols)[0])
    mixed_one = jnp.concatenate(mixed_parts, 2).reshape(depth, tokens)
    stream = stream + output_project(w_attn, mixed_one)
    normal_two, inverse_two = normalize(stream)
    normed_two = (normal_two * gain_cross + bias_cross).astype(BF)
    raw_cross = project(w_query, normed_two).reshape(heads, dim, tokens)
    norm_query, cross_pull = jax.vjp(head_norm, raw_cross, cross_query_gain)
    query_two = norm_query.astype(BF)
    my_text = jnp.concatenate(
        [lax.dynamic_index_in_dim(text, p.sequence, 0, False) for p in pieces], 0
    )
    raw_text = einsum("ckn,tk->cnt", w_text[0], my_text).reshape(heads, dim, -1)
    norm_key, text_pull = jax.vjp(head_norm, raw_text, text_key_gain)
    key_two = norm_key.astype(BF)
    value_two = einsum("ckn,tk->cnt", w_text[1], my_text).reshape(heads, dim, -1).astype(BF)
    saved_cross = []
    mixed_parts = []
    for index, piece in enumerate(pieces):
        length = lax.dynamic_index_in_dim(text_lengths, piece.sequence, 0, True)
        here = slice(index * keys, (index + 1) * keys)
        inputs = (length, cut(query_two, index), key_two[:, :, here], value_two[:, :, here])
        mixed, logsum = attend(*inputs, True)
        saved_cross.append((inputs, logsum))
        mixed_parts.append(mixed)
    mixed_two = jnp.concatenate(mixed_parts, 2).reshape(depth, tokens)
    stream = stream + output_project(w_cross, mixed_two)
    normal_three, inverse_three = normalize(stream)
    normed_three = (normal_three * gain_hidden + bias_hidden).astype(BF)
    inner = einsum("ckn,kt->cnt", w_expand, normed_three)
    activated, gelu_pull = jax.vjp(partial(jax.nn.gelu, approximate=True), inner)
    act = activated.astype(BF)
    output = stream + einsum("cnk,ckt->nt", w_reduce, act)
    result = to_features(output.astype(BF), pieces, cols).astype(F32)

    g_reduce = weight_grad("nt,ckt->cnk", True, grad_out, act)
    g_act = einsum("cnk,nt->ckt", w_reduce, grad_out)
    g_inner = gelu_pull(g_act)[0].astype(BF)
    g_expand = weight_grad("kt,cnt->ckn", False, normed_three, g_inner)
    g_normed = einsum("ckn,cnt->kt", w_expand, g_inner)
    g_hidden_gain = jnp.sum(g_normed * normal_three, 1)
    g_hidden_bias = jnp.sum(g_normed, 1)
    g_stream = grad_out.astype(F32) + norm_back(g_normed * gain_hidden, normal_three, inverse_three)

    g_low = g_stream.astype(BF)
    by_block = lambda values: values.reshape(cols, width, -1)
    g_cross_out = weight_grad("nt,ckt->cnk", True, g_low, by_block(mixed_two))
    g_mixed = einsum("cnk,nt->ckt", w_cross, g_low).astype(BF).reshape(heads, dim, tokens)
    g_queries = []
    g_keys = []
    g_values = []
    for index, piece in enumerate(pieces):
        inputs, logsum = saved_cross[index]
        g_q, g_k, g_v = attend_back(*inputs, cut(g_mixed, index), logsum, True, F32)
        g_queries.append(g_q)
        g_keys.append(g_k)
        g_values.append(g_v)
    g_raw_cross, g_cq_gain = cross_pull(jnp.concatenate(g_queries, 2))
    g_raw_text, g_tk_gain = text_pull(jnp.concatenate(g_keys, 2))
    g_craw = g_raw_cross.astype(BF).reshape(depth, tokens)
    g_pair = [
        by_block(g_raw_text.astype(BF).reshape(depth, -1)),
        by_block(jnp.concatenate(g_values, 2).astype(BF).reshape(depth, -1)),
    ]
    g_text = [weight_grad("tk,cnt->ckn", a, my_text, g) for a, g in zip((True, False), g_pair)]
    g_query_weight = weight_grad("kt,cnt->ckn", False, normed_two, by_block(g_craw))
    g_normed = einsum("ckn,cnt->kt", w_query, by_block(g_craw))
    g_cross_gain = jnp.sum(g_normed * normal_two, 1)
    g_cross_bias = jnp.sum(g_normed, 1)
    g_stream = g_stream + norm_back(g_normed * gain_cross, normal_two, inverse_two)

    g_low = g_stream.astype(BF)
    g_self_out = weight_grad("nt,ckt->cnk", True, g_low, by_block(mixed_one))
    g_mixed = einsum("cnk,nt->ckt", w_attn, g_low).astype(BF).reshape(heads, dim, tokens)
    g_parts = []
    for index, piece in enumerate(pieces):
        whole, logsum = saved_self[index]
        grad = to_heads(cut(g_mixed, index)[None], piece, cols)[0]
        parts = attend_back(none, whole[0], whole[1], whole[2], grad, logsum, False, BF)
        g_parts.append(from_heads(jnp.stack(parts, 0), piece, cols))
    g_heads = jnp.concatenate(g_parts, 3)
    g_raw_q, g_q_gain = query_pull(g_heads[0].astype(F32))
    g_raw_k, g_k_gain = key_pull(g_heads[1].astype(F32))
    g_triple = [
        by_block(g.reshape(depth, tokens))
        for g in (g_raw_q.astype(BF), g_raw_k.astype(BF), g_heads[2])
    ]
    g_self_in = [
        weight_grad("kt,cnt->ckn", a, normed_one, g)
        for a, g in zip((True, False, False), g_triple)
    ]
    g_normed = sum(einsum("ckn,cnt->kt", w, g) for w, g in zip(w_self, g_triple))
    crossed = g_normed * normal_one
    sums = jnp.stack(
        [
            jnp.stack([jnp.sum(cut(g_normed, i), 1), jnp.sum(cut(crossed, i), 1)], 0)
            for i in range(len(pieces))
        ],
        0,
    )
    which = jnp.stack(
        [jnp.where(jnp.arange(sequences) == p.sequence, 1.0, 0.0) for p in pieces], 0
    )
    g_modul = jnp.sum(which[:, :, None, None] * sums[:, None], 0)
    g_modul = lax.psum_scatter(g_modul, "col", scatter_dimension=2, tiled=True).astype(BF)
    g_modul = lax.all_gather(g_modul, "row", axis=0, tiled=True)
    g_modulation = einsum("sd,ske->dke", embed_rows, g_modul)
    g_stream = g_stream + norm_back(g_normed * scaling, normal_one, inverse_one)

    g_skip_gain = jnp.sum(g_stream * skip_normal, 1)
    g_skip_bias = jnp.sum(g_stream, 1)
    g_joined = norm_back(g_stream * gain_skip, skip_normal, skip_inverse).astype(BF)
    g_blocks = by_block(g_joined)
    g_skip_weight = [
        weight_grad("kt,cnt->ckn", a, v, g_blocks)
        for a, v in ((True, latent), (False, skipped))
    ]
    g_latent = einsum("ckn,cnt->kt", w_skip[0], g_blocks)
    g_skipped = einsum("ckn,cnt->kt", w_skip[1], g_blocks)
    g_latents = to_features(g_latent.astype(BF), pieces, cols).astype(F32)
    g_skip = to_features(g_skipped.astype(BF), pieces, cols).astype(F32)

    g_gains = jnp.stack(
        [g_skip_gain, g_skip_bias, g_cross_gain, g_cross_bias, g_hidden_gain, g_hidden_bias], 0
    )
    g_gains = lax.psum(g_gains, ("row", "col"))
    g_gains = lax.dynamic_slice_in_dim(g_gains, mine * width, width, 1)
    g_head = lax.psum(jnp.stack([g_q_gain, g_k_gain, g_cq_gain, g_tk_gain], 0), ("row", "col"))
    return (
        result,
        g_latents,
        g_skip,
        jnp.stack(g_skip_weight, 0),
        g_modulation,
        jnp.stack(g_self_in, 1),
        g_self_out.T,
        g_query_weight,
        jnp.stack(g_text, 1),
        g_cross_out.T,
        g_expand,
        g_reduce.T,
        *[g_gains[i] for i in range(6)],
        *[g_head[i] for i in range(4)],
    )


def solution(mesh):
    return jax.shard_map(
        shards,
        mesh=mesh,
        in_specs=(
            P("col", "row"),
            P("col", "row"),
            P("row", "col"),
            P("row", None, "col"),
            P("row"),
            P(None, "row"),
            P("col", "row"),
            P(None, "row", "col"),
            P("row", None, "col"),
            P("row", None, "col"),
            P("col", "row"),
            P("row", "col"),
            P("row", None, "col"),
            P("col", "row"),
            P("row", "col"),
            P("col", "row"),
            P("col"),
            P("col"),
            P("col"),
            P("col"),
            P("col"),
            P("col"),
            P(),
            P(),
            P(),
            P(),
        ),
        out_specs=(
            P("col", "row"),
            P("col", "row"),
            P("col", "row"),
            P(None, "row", "col"),
            P("row", None, "col"),
            P("row", None, "col"),
            P("col", "row"),
            P("row", "col"),
            P("row", None, "col"),
            P("col", "row"),
            P("row", "col"),
            P("col", "row"),
            P("col"),
            P("col"),
            P("col"),
            P("col"),
            P("col"),
            P("col"),
            P(),
            P(),
            P(),
            P(),
        ),
        check_vma=False,
    )
```

```python
from functools import partial
import math

import jax
import jax.numpy as jnp
from jax import lax
from jax.experimental import pallas as pl
from jax.experimental.pallas import tpu as pltpu
from jax.sharding import PartitionSpec as P

L = 1024
EPSILON = 1e-06
BF = jnp.bfloat16
F32 = jnp.float32
KEYPAD = 128
DEVICES = ("col", "row")
LOG2E = math.log2(math.e)
VMEM = 60 << 20


def einsum(spec, left, right):
    return jnp.einsum(spec, left, right, preferred_element_type=F32)


def dot(left, right, dims):
    return lax.dot_general(left, right, (dims, ((), ())), preferred_element_type=F32)


def params():
    return pltpu.CompilerParams(vmem_limit_bytes=VMEM)


def step_of(count):
    return 256 if count % 256 == 0 else count


def wide(ref, head):
    parts = [ref[s, 0, head] for s in range(ref.shape[0])]
    return parts[0] if len(parts) == 1 else jnp.concatenate(parts, 1)


def valid_keys(length_ref, keys, step):
    return lax.broadcasted_iota(jnp.int32, (keys, step), 0) < length_ref[0]


def attend_kernel(masked, length_ref, q_ref, k_ref, v_ref, o_ref, l_ref):
    groups, _, heads, dim, count = q_ref.shape
    step = step_of(count)
    factor = dim ** (-0.5) * LOG2E
    for head in range(heads):
        key = wide(k_ref, head).T
        value = wide(v_ref, head)
        keys = key.shape[0]
        value = jnp.concatenate([value, jnp.ones((8, keys), BF)], 0)
        for place in range(0, groups * count, step):
            group, first = divmod(place, count)
            query = q_ref[group, 0, head, :, first : first + step]
            expo = jnp.exp2(dot(key, query, ((1,), (0,))) * factor)
            if masked:
                expo = jnp.where(valid_keys(length_ref, keys, step), expo, 0.0)
            both = dot(value, expo.astype(BF), ((1,), (0,)))
            total = both[dim : dim + 1]
            o_ref[group, head, :, first : first + step] = (both[:dim] * (1.0 / total)).astype(BF)
            l_ref[head, :, place : place + step] = jnp.log2(total)


def attend_back_kernel(
    masked, length_ref, q_ref, k_ref, v_ref, m_ref, g_ref, l_ref, *outs
):
    groups, _, heads, dim, count = q_ref.shape
    step = step_of(count)
    scale = dim ** (-0.5)
    for head in range(heads):
        key = wide(k_ref, head)
        keys = key.shape[1]
        turned = key.T
        value = jnp.concatenate([wide(v_ref, head), jnp.ones((8, keys), BF)], 0).T
        g_key = g_value = None
        for place in range(0, groups * count, step):
            group, first = divmod(place, count)
            here = slice(first, first + step)
            query = q_ref[group, 0, head, :, here]
            grad = g_ref[group, head, :, here]
            delta = -jnp.sum(
                grad.astype(F32) * m_ref[group, head, :, here].astype(F32), 0, keepdims=True
            )
            high = delta.astype(BF)
            rest = (delta - high.astype(F32)).astype(BF)
            more = jnp.concatenate([grad, high, rest, jnp.zeros((6, step), BF)], 0)
            probs = jnp.exp2(
                dot(turned, query, ((1,), (0,))) * (scale * LOG2E)
                - l_ref[head, :, place : place + step]
            )
            if masked:
                probs = jnp.where(valid_keys(length_ref, keys, step), probs, 0.0)
            product = (probs * dot(value, more, ((1,), (0,)))).astype(BF)
            g_query = dot(key, product, ((1,), (0,))) * scale
            part_value = dot(grad, probs.astype(BF), ((1,), (1,)))
            part_key = dot(query, product, ((1,), (1,)))
            g_value = part_value if g_value is None else g_value + part_value
            g_key = part_key if g_key is None else g_key + part_key
            outs[0][group, 0, head, :, here] = g_query.astype(outs[0].dtype)
        g_key = g_key * scale
        if len(outs) == 1:
            for group in range(groups):
                here = slice(group * count, (group + 1) * count)
                outs[0][group, 1, head] = g_key[:, here].astype(BF)
                outs[0][group, 2, head] = g_value[:, here].astype(BF)
        else:
            outs[1][0, 0, head] = g_key
            outs[2][0, 0, head] = g_value


def costs(heads, queries, keys, dim, products):
    return pl.CostEstimate(
        flops=2 * products * heads * queries * keys * 256,
        transcendentals=heads * queries * keys,
        bytes_accessed=2 * products * heads * dim * (queries + keys),
    )


def head_block(shape, count, kind=0):
    groups, _, _, dim, tokens = shape
    return pl.BlockSpec((groups, 1, count, dim, tokens), lambda h: (0, kind, h, 0, 0))


def mix_block(shape, count):
    groups, _, _, dim, tokens = shape
    return pl.BlockSpec((groups, count, dim, tokens), lambda h: (0, h, 0, 0))


def attend(length, query, key, value, kinds, masked, most):
    groups, _, heads, dim, count = query.shape
    many = math.gcd(heads, most)
    total = groups * count
    keys = key.shape[0] * key.shape[4]
    return pl.pallas_call(
        partial(attend_kernel, masked),
        grid=(heads // many,),
        in_specs=[pl.BlockSpec(memory_space=pltpu.SMEM)]
        + [head_block(a.shape, many, kind) for a, kind in zip((query, key, value), kinds)],
        out_specs=[
            mix_block(query.shape, many),
            pl.BlockSpec((many, 1, total), lambda h: (h, 0, 0)),
        ],
        out_shape=[
            jax.ShapeDtypeStruct((groups, heads, dim, count), BF),
            jax.ShapeDtypeStruct((heads, 1, total), F32),
        ],
        cost_estimate=costs(heads, total, keys, dim, 2),
        compiler_params=params(),
        name="attend",
    )(length, query, key, value)


def attend_back(length, query, key, value, kinds, mixed, grad, logs, masked, most, stacked):
    groups, _, heads, dim, count = query.shape
    many = math.gcd(heads, most)
    total = groups * count
    keys = key.shape[0] * key.shape[4]
    if stacked:
        out_specs = pl.BlockSpec((groups, 3, many, dim, count), lambda h: (0, 0, h, 0, 0))
        out_shape = jax.ShapeDtypeStruct((groups, 3, heads, dim, count), BF)
    else:
        out_specs = [head_block(a.shape, many) for a in (query, key, value)]
        out_shape = [jax.ShapeDtypeStruct(a.shape, F32) for a in (query, key, value)]
    return pl.pallas_call(
        partial(attend_back_kernel, masked),
        grid=(heads // many,),
        in_specs=[pl.BlockSpec(memory_space=pltpu.SMEM)]
        + [head_block(a.shape, many, kind) for a, kind in zip((query, key, value), kinds)]
        + [mix_block(query.shape, many)] * 2
        + [pl.BlockSpec((many, 1, total), lambda h: (h, 0, 0))],
        out_specs=out_specs,
        out_shape=out_shape,
        cost_estimate=costs(heads, total, keys, dim, 5),
        compiler_params=params(),
        name="attend_back",
    )(length, query, key, value, mixed, grad, logs)


def work(rows, depth, tokens, moved):
    return pl.CostEstimate(flops=2 * rows * depth * tokens, transcendentals=0, bytes_accessed=moved)


def full(shape):
    return pl.BlockSpec(shape, lambda *_: (0,) * len(shape))


def project(weight, kinds, values, dtypes, joined=False):
    _, cols, depth, width = weight.shape
    tokens = values[0].shape[1]
    outs = 1 if joined else len(kinds)

    def kernel(*refs):
        blocks = refs[: len(kinds)]
        given = refs[len(kinds) : -outs]
        total = None
        for index, block in enumerate(blocks):
            part = dot(block[0, 0], given[index % len(given)][...], ((0,), (0,)))
            if not joined:
                refs[index - outs][...] = part.astype(dtypes[index])
            total = part if total is None else total + part
        if joined:
            refs[-1][...] = total.astype(dtypes[0])

    return pl.pallas_call(
        kernel,
        grid=(cols,),
        in_specs=[
            pl.BlockSpec((1, 1, depth, width), partial(lambda k, c: (k, c, 0, 0), kind))
            for kind in kinds
        ]
        + [full(v.shape) for v in values],
        out_specs=[pl.BlockSpec((width, tokens), lambda c: (c, 0))] * outs,
        out_shape=[jax.ShapeDtypeStruct((cols * width, tokens), dtypes[i]) for i in range(outs)],
        cost_estimate=work(len(kinds) * cols * width, depth, tokens, 8 * depth * tokens),
        compiler_params=params(),
        name="project",
    )(*([weight] * len(kinds)), *values)


def rebuild(weight, kinds, values, dtype):
    _, cols, depth, width = weight.shape
    tokens = values[0].shape[1]
    tile = depth // 4

    def kernel(*refs):
        total = None
        for block, given in zip(refs[: len(kinds)], refs[len(kinds) : -1]):
            for col in range(cols):
                part = dot(block[0, col], given[col * width : (col + 1) * width, :], ((1,), (0,)))
                total = part if total is None else total + part
        refs[-1][...] = total.astype(dtype)

    return pl.pallas_call(
        kernel,
        grid=(4,),
        in_specs=[
            pl.BlockSpec((1, cols, tile, width), partial(lambda k, j: (k, 0, j, 0), kind))
            for kind in kinds
        ]
        + [full(v.shape) for v in values],
        out_specs=pl.BlockSpec((tile, tokens), lambda j: (j, 0)),
        out_shape=jax.ShapeDtypeStruct((depth, tokens), dtype),
        cost_estimate=work(depth, len(kinds) * cols * width, tokens, 8 * depth * tokens),
        compiler_params=params(),
        name="rebuild",
    )(*([weight] * len(kinds)), *values)


def outer(core, left, rights, flip):
    rows, tokens = left.shape
    cols = lax.axis_size("col")
    width = rights[0].shape[0] // cols

    def kernel(core_ref, left_ref, *refs):
        for index in range(len(rights)):
            part = dot(left_ref[...], refs[index][...], ((1,), (1,)))
            refs[-1][index, 0] = part.astype(BF)

    return pl.pallas_call(
        kernel,
        grid_spec=pltpu.PrefetchScalarGridSpec(
            num_scalar_prefetch=1,
            grid=(cols // 2,),
            in_specs=[pl.BlockSpec((rows, tokens), lambda y, core: (0, 0))]
            + [
                pl.BlockSpec((width, tokens), lambda y, core: (2 * y + (core[0] ^ flip), 0))
                for _ in rights
            ],
            out_specs=pl.BlockSpec(
                (len(rights), 1, rows, width), lambda y, core: (0, y, 0, 0)
            ),
        ),
        out_shape=jax.ShapeDtypeStruct((len(rights), cols // 2, rows, width), BF),
        cost_estimate=work(
            rows, tokens, len(rights) * cols // 2 * width, 3 * rows * cols * width * len(rights)
        ),
        compiler_params=params(),
        name="outer",
    )(core, left, *rights)


def expand(blocks, values):
    many = len(blocks)
    depth, hidden = blocks[0].shape
    tokens = values.shape[1]
    tile = 384 if hidden % 384 == 0 else hidden
    slope = 0.79788456
    cubic = 0.044715

    def kernel(*refs):
        values_ref, act_ref, slope_ref = refs[many:]
        for index in range(many):
            inner = dot(refs[index][...], values_ref[...], ((0,), (0,)))
            square = inner * inner
            bent = jnp.tanh(inner * (slope + slope * cubic * square))
            half = 0.5 + 0.5 * bent
            act_ref[index] = (inner * half).astype(BF)
            rise = slope + 3.0 * slope * cubic * square
            slope_ref[index] = (half + 0.5 * inner * (1.0 - bent * bent) * rise).astype(BF)

    return pl.pallas_call(
        kernel,
        grid=(hidden // tile,),
        in_specs=[pl.BlockSpec((depth, tile), lambda j: (0, j))] * many + [full(values.shape)],
        out_specs=[pl.BlockSpec((many, tile, tokens), lambda j: (0, j, 0))] * 2,
        out_shape=[jax.ShapeDtypeStruct((many, hidden, tokens), BF)] * 2,
        cost_estimate=work(many * hidden, depth, tokens, 3 * many * hidden * depth),
        compiler_params=params(),
        name="expand",
    )(*blocks, values)


def expand_back(blocks, values, slopes):
    many = len(blocks)
    depth, hidden = blocks[0].shape
    tokens = values.shape[1]
    tile = 384 if hidden % 384 == 0 else hidden

    def kernel(*refs):
        values_ref, slope_ref, out_ref = refs[many:]
        for index in range(many):
            part = dot(refs[index][...], values_ref[...], ((0,), (0,)))
            out_ref[index] = (part * slope_ref[index].astype(F32)).astype(BF)

    return pl.pallas_call(
        kernel,
        grid=(hidden // tile,),
        in_specs=[pl.BlockSpec((depth, tile), lambda j: (0, j))] * many
        + [full(values.shape), pl.BlockSpec((many, tile, tokens), lambda j: (0, j, 0))],
        out_specs=pl.BlockSpec((many, tile, tokens), lambda j: (0, j, 0)),
        out_shape=jax.ShapeDtypeStruct((many, hidden, tokens), BF),
        cost_estimate=work(many * hidden, depth, tokens, 3 * many * hidden * depth),
        compiler_params=params(),
        name="expand_back",
    )(*blocks, values, slopes)


def contract(blocks, values, added, dtype):
    many = len(blocks)
    depth, hidden = blocks[0].shape
    tokens = values.shape[2]
    tile = depth // 4
    extra = [] if added is None else [added]

    def kernel(*refs):
        values_ref = refs[many]
        total = refs[many + 1][...] if extra else None
        for index in range(many):
            part = dot(refs[index][...], values_ref[index], ((1,), (0,)))
            total = part if total is None else total + part
        refs[-1][...] = total.astype(dtype)

    line = pl.BlockSpec((tile, tokens), lambda j: (j, 0))
    return pl.pallas_call(
        kernel,
        grid=(4,),
        in_specs=[pl.BlockSpec((tile, hidden), lambda j: (j, 0))] * many
        + [full(values.shape)]
        + [line] * len(extra),
        out_specs=line,
        out_shape=jax.ShapeDtypeStruct((depth, tokens), dtype),
        cost_estimate=work(depth, many * hidden, tokens, 3 * many * hidden * depth),
        compiler_params=params(),
        name="contract",
    )(*blocks, values, *extra)


def hidden_outer(base, grad_out, act, normed, grad_inner):
    many, hidden, tokens = act.shape
    depth = grad_out.shape[0]
    parts = 2 if hidden % 256 == 0 else 1
    tile = hidden // parts

    def kernel(base_ref, out_ref, act_ref, normed_ref, inner_ref, grad_ref):
        kind = pl.program_id(0)

        @pl.when(kind == 0)
        def _():
            grad_ref[0, 0] = dot(normed_ref[...], inner_ref[0], ((1,), (1,))).astype(BF)

        @pl.when(kind == 1)
        def _():
            grad_ref[0, 0] = dot(out_ref[...], act_ref[0], ((1,), (1,))).astype(BF)

    return pl.pallas_call(
        kernel,
        grid_spec=pltpu.PrefetchScalarGridSpec(
            num_scalar_prefetch=1,
            grid=(2, many, parts),
            in_specs=[
                pl.BlockSpec((depth, tokens), lambda s, p, j, b: (0, 0)),
                pl.BlockSpec((1, tile, tokens), lambda s, p, j, b: (s * p, s * j, 0)),
                pl.BlockSpec((depth, tokens), lambda s, p, j, b: (0, 0)),
                pl.BlockSpec(
                    (1, tile, tokens),
                    lambda s, p, j, b: (p + s * (many - 1 - p), j + s * (parts - 1 - j), 0),
                ),
            ],
            out_specs=pl.BlockSpec((1, 1, depth, tile), lambda s, p, j, b: (s, p ^ b[0], 0, j)),
        ),
        out_shape=jax.ShapeDtypeStruct((2, many, depth, hidden), BF),
        cost_estimate=work(2 * depth, tokens, many * hidden, 5 * many * depth * hidden),
        compiler_params=params(),
        name="hidden_outer",
    )(base, grad_out, act, normed, grad_inner)


def assemble(place, own, got):
    _, rows, width = own.shape

    def kernel(place_ref, own_ref, got_ref, out_ref):
        @pl.when(pl.program_id(1) == place_ref[1])
        def _():
            out_ref[0, 0] = own_ref[0]

        @pl.when(pl.program_id(1) != place_ref[1])
        def _():
            out_ref[0, 0] = got_ref[0]

    spec = pl.BlockSpec((1, rows, width), lambda z, x, place: (z ^ place[0], 0, 0))
    return pl.pallas_call(
        kernel,
        grid_spec=pltpu.PrefetchScalarGridSpec(
            num_scalar_prefetch=1,
            grid=(4, 2),
            in_specs=[spec, spec],
            out_specs=pl.BlockSpec((1, 1, rows, width), lambda z, x, place: (z, x, 0, 0)),
        ),
        out_shape=jax.ShapeDtypeStruct((4, 2, rows, width), BF),
        cost_estimate=work(1, 1, 1, 48 * rows * width),
        name="assemble",
    )(place, own, got).reshape(8 * rows, width)


def normalize(values):
    average = jnp.mean(values, 0, keepdims=True)
    centred = values - average
    inverse = lax.rsqrt(jnp.mean(centred * centred, 0, keepdims=True) + EPSILON)
    return centred * inverse, inverse


def norm_back(grad, normal, inverse):
    average = jnp.mean(grad, 0, keepdims=True)
    crossed = jnp.mean(grad * normal, 0, keepdims=True)
    return inverse * (grad - average - normal * crossed)


def head_norm(values, gain):
    average = jnp.mean(values, 1, keepdims=True)
    centred = values - average
    variance = jnp.mean(centred * centred, 1, keepdims=True)
    return centred * lax.rsqrt(variance + EPSILON) * gain[None, :, None]


def rope_tables(places, head_dim):
    quarter = head_dim // 4
    freqs = jnp.exp(jnp.arange(quarter, dtype=F32) * (-4.0 * math.log(10000.0) / head_dim))
    rows = freqs[:, None] * places[0].astype(F32)[None, :]
    cols = freqs[:, None] * places[1].astype(F32)[None, :]
    angles = jnp.concatenate([rows, rows, cols, cols], 0)
    return jnp.cos(angles), jnp.sin(angles)


def rotate(values):
    quarter = values.shape[1] // 4
    one, two, three, four = (values[:, i * quarter : (i + 1) * quarter] for i in range(4))
    return jnp.concatenate([-two, one, -four, three], 1)


class Piece:
    def __init__(self, start, count, group, sequence):
        self.start = start
        self.count = count
        self.group = group
        self.sequence = sequence


def pieces_of(cols, sequences):
    mine = lax.axis_index("col")
    if cols == 4 and sequences == 3:
        return [
            Piece(0, L // 2, 2, mine // 2),
            Piece(2 * L, L // 4, 4, jnp.int32(2)),
        ]
    return [Piece(s * L, L // cols, cols, jnp.int32(s)) for s in range(sequences)]


def groups_of(size, cols):
    return [list(range(i, i + size)) for i in range(0, cols, size)]


def exchange(values, size, cols):
    if size == cols:
        return lax.all_to_all(values, "col", 0, 0, tiled=True)
    return lax.all_to_all(
        values, "col", 0, 0, tiled=True, axis_index_groups=groups_of(size, cols)
    )


def to_tokens(values, pieces, cols):
    width = values.shape[0]
    parts = []
    for piece in pieces:
        region = values[:, piece.start : piece.start + cols * piece.count]
        parts.append(region.reshape(width, cols, piece.count).transpose(1, 0, 2))
    stacked = jnp.concatenate(parts, 2)
    return exchange(stacked, cols, cols).reshape(cols * width, -1)


def to_features(values, pieces, cols):
    width = values.shape[0] // cols
    got = exchange(values.reshape(cols, width, -1), cols, cols)
    parts = []
    at = 0
    for piece in pieces:
        part = got[:, :, at : at + piece.count]
        parts.append(part.transpose(1, 0, 2).reshape(width, cols * piece.count))
        at += piece.count
    return jnp.concatenate(parts, 1)


def shared(values, axis):
    size = lax.axis_size(axis)
    return lax.all_to_all(
        jnp.broadcast_to(values[None], (size, *values.shape)), axis, 0, 0, tiled=True
    )


def swap(values, axis, bit):
    size = lax.axis_size(axis)
    return lax.ppermute(values, axis, [(i, i ^ bit) for i in range(size)])


def custom_mesh():
    return (lax.axis_size("row"), lax.axis_size("col")) == (8, 4)


def gather_weights(blocks):
    cols = lax.axis_size("col")
    most = max(block.shape[0] for block in blocks)
    padded = [jnp.pad(b, ((0, most - b.shape[0]), (0, 0))) for b in blocks]
    whole = lax.all_gather(jnp.stack(padded, 0), DEVICES, axis=1, tiled=True)
    return whole.reshape(len(blocks), cols, -1, blocks[0].shape[1])


def gather_blocks(block, across, place):
    if not custom_mesh():
        cols = lax.axis_size("col")
        whole = lax.all_gather(block, DEVICES, axis=0, tiled=True).reshape(cols, -1, block.shape[1])
        return [whole[i] for i in range(cols)]
    stack = jnp.stack([block] + [swap(block, "row", 2 * level) for level in (1, 2, 3)], 0)
    if across:
        mine = assemble(place, stack, swap(stack, "row", 1))
        other = swap(mine, "col", 2)
    else:
        up = swap(stack, "col", 2)
        mine = assemble(place, stack, swap(stack, "row", 1))
        other = assemble(place, up, swap(up, "row", 1))
    return [mine, swap(mine, "col", 1), other, swap(other, "col", 1)]


def pick(values, axis, index):
    return lax.dynamic_index_in_dim(values, index, axis, False)


def add(left, right):
    return (left.astype(F32) + right.astype(F32)).astype(BF)


class Reduction:
    def __init__(self, core, left, rights, across):
        self.across = across
        self.many = len(rights)
        self.stage = 0
        if not custom_mesh():
            cols = lax.axis_size("col")
            whole = jnp.stack(
                [einsum("kt,cnt->ckn", left, r.reshape(cols, -1, r.shape[1])) for r in rights], 0
            )
            flat = whole.reshape(self.many, -1, whole.shape[3]).astype(BF)
            self.state = [lax.psum_scatter(flat, DEVICES, scatter_dimension=1, tiled=True)]
            return
        shape = (self.many, 2, 4, 2, left.shape[0] // 8, rights[0].shape[0] // 4)
        send = outer(core, left, rights, 1)
        got = swap(send, "col", 1)
        keep = outer(core, left, rights, 0)
        self.state = [keep.reshape(shape), got.reshape(shape)]

    def half(self, side):
        kept, got = self.state
        axis = (3 if kept.ndim == 6 else 2) if side else 1
        name, bit = ("row", 1) if side else ("col", 2)
        index = lax.axis_index("row") % 2 if side else lax.axis_index("col") // 2
        away = add(pick(kept, axis, 1 - index), pick(got, axis, 1 - index))
        here = add(pick(kept, axis, index), pick(got, axis, index))
        self.state = [here, swap(away, name, bit)]

    def advance(self):
        if not custom_mesh() or self.stage == 4:
            return
        self.stage += 1
        if self.stage <= 2:
            self.half(self.across == (self.stage == 1))
        elif self.stage == 3:
            level = lax.axis_index("row") // 2
            total = add(*self.state)
            self.state = [pick(total, 1, level)] + [
                swap(pick(total, 1, level ^ other), "row", 2 * other) for other in (1, 2, 3)
            ]
        else:
            total = self.state[0].astype(F32)
            for other in self.state[1:]:
                total = total + other.astype(F32)
            self.state = [total]

    def result(self):
        while custom_mesh() and self.stage < 4:
            self.advance()
        return self.state[0].astype(F32)


def tick(values, running):
    active = [r for r in running if r.stage < 4]
    if active and custom_mesh():
        values, states = lax.optimization_barrier((values, [r.state for r in active]))
        for reduction, state in zip(active, states):
            reduction.state = state
            reduction.advance()
    return values


def shards(
    latents,
    skip_input,
    condition,
    text_states,
    text_lengths,
    positions,
    out_grad,
    skip_weight,
    modulation,
    self_inputs,
    self_output,
    cross_query,
    cross_keyvalue,
    cross_output,
    expand_weight,
    reduce_weight,
    skip_gain,
    skip_bias,
    cross_gain,
    cross_bias,
    hidden_gain,
    hidden_bias,
    query_gain,
    key_gain,
    cross_query_gain,
    text_key_gain,
):
    cols = lax.axis_size("col")
    rows = lax.axis_size("row")
    mine = lax.axis_index("col")
    my_row = lax.axis_index("row")
    width, row_tokens = latents.shape
    depth = width * cols
    dim = query_gain.shape[0]
    heads = depth // dim
    sequences = row_tokens // L
    tokens = row_tokens // cols
    texts = text_states.shape[1]
    keys = -(-texts // KEYPAD) * KEYPAD
    pieces = pieces_of(cols, sequences)
    starts = [sum(p.count for p in pieces[:i]) for i in range(len(pieces))]
    core = (mine % 2).astype(jnp.int32)[None]
    place = jnp.stack([my_row // 2, my_row % 2]).astype(jnp.int32)
    base = (mine if custom_mesh() else jnp.zeros_like(mine)).astype(jnp.int32)[None]

    def cut(values, index):
        return values[..., starts[index] : starts[index] + pieces[index].count]

    weights_one = gather_weights(
        [skip_weight[0], skip_weight[1], self_inputs[:, 0], self_inputs[:, 1], self_inputs[:, 2]]
    )
    weights_two = gather_weights(
        [self_output.T, cross_query, cross_output.T, cross_keyvalue[:, 0], cross_keyvalue[:, 1]]
    )
    w_expand = gather_blocks(expand_weight, True, place)
    w_reduce = gather_blocks(reduce_weight.T, False, place)

    latent = to_tokens(latents, pieces, cols)
    skipped = to_tokens(skip_input, pieces, cols)
    grad_out = to_tokens(out_grad.astype(BF), pieces, cols)
    places = jnp.concatenate(
        [
            lax.dynamic_slice_in_dim(positions, p.start + mine * p.count, p.count, 1)
            for p in pieces
        ],
        1,
    )

    embed = jax.nn.silu(condition.astype(F32)).astype(BF)
    embed = shared(embed, "row").reshape(-1, width)
    embed = shared(embed, "col").transpose(1, 0, 2).reshape(-1, depth)
    block_rows = depth // rows
    embed_rows = lax.dynamic_slice_in_dim(embed, my_row * block_rows, block_rows, 1)
    modul = einsum("sd,dke->ske", embed_rows, modulation).reshape(rows, sequences, 2, width)
    modul = jnp.sum(lax.all_to_all(modul, "row", 0, 0, tiled=True), 0)
    gains = jnp.stack(
        [skip_gain, skip_bias, cross_gain, cross_bias, hidden_gain, hidden_bias], 0
    )
    table = jnp.concatenate([gains, modul.reshape(-1, width)], 0)
    table = shared(table, "col").transpose(1, 0, 2).reshape(-1, depth)
    modul = table[6:].reshape(sequences, 2, depth)
    chosen = [lax.dynamic_index_in_dim(modul, p.sequence, 0, False) for p in pieces]
    columns = lax.optimization_barrier(jnp.concatenate([table[:6], *chosen], 0)).T
    gain_skip, bias_skip, gain_cross, bias_cross, gain_hidden, bias_hidden = (
        columns[:, i : i + 1] for i in range(6)
    )
    token_index = lax.broadcasted_iota(jnp.int32, (1, tokens), 1)

    def per_token(which):
        result = columns[:, 6 + which : 7 + which]
        for index in range(1, len(pieces)):
            column = columns[:, 6 + 2 * index + which : 7 + 2 * index + which]
            result = jnp.where(token_index >= starts[index], column, result)
        return jnp.broadcast_to(result, (depth, tokens))

    shifting = per_token(0)
    scaling = 1.0 + per_token(1)

    joined = project(weights_one, [0, 1], [latent, skipped], [F32], True)[0]
    skip_normal, skip_inverse = normalize(joined)
    stream = skip_normal * gain_skip + bias_skip
    normal_one, inverse_one = normalize(stream)
    normed_one = (normal_one * scaling + shifting).astype(BF)
    raw = project(weights_one, [2, 3, 4], [normed_one], [F32, F32, BF])
    raw = [r.reshape(heads, dim, tokens) for r in raw]
    cosine, sine = rope_tables(places, dim)

    def self_piece(value, gain):
        normal = head_norm(value, gain)
        return normal * cosine[None] + rotate(normal) * sine[None]

    rot_query, query_pull = jax.vjp(self_piece, raw[0], query_gain)
    rot_key, key_pull = jax.vjp(self_piece, raw[1], key_gain)
    triple = [rot_query.astype(BF), rot_key.astype(BF), raw[2]]

    text = shared(jnp.pad(text_states, ((0, 0), (0, keys - texts), (0, 0))), "col")
    text = jnp.concatenate(
        [lax.dynamic_index_in_dim(text, p.sequence, 1, False) for p in pieces], 1
    )
    text = text.transpose(0, 2, 1).reshape(-1, len(pieces) * keys)
    text_rows = text.shape[0] // rows
    text_wide = jnp.pad(
        text.reshape(rows, text_rows, -1), ((0, 0), (0, block_rows - text_rows), (0, 0))
    ).reshape(depth, -1)

    def to_heads(parts, index):
        size = pieces[index].group
        split = [cut(p, index).reshape(size, heads // size, dim, -1) for p in parts]
        return exchange(jnp.stack(split, 1), size, cols)

    none = jnp.zeros((1,), jnp.int32)
    saved_self = []
    mixed_parts = []
    for index, piece in enumerate(pieces):
        whole = to_heads(triple, index)
        mixed, logs = attend(none, whole, whole, whole, (0, 1, 2), False, 2)
        saved_self.append((whole, mixed, logs))
        mixed_parts.append(exchange(mixed, piece.group, cols).reshape(depth, -1))
    mixed_one = jnp.concatenate(mixed_parts, 1)
    stream = stream + rebuild(weights_two, [0], [mixed_one], F32)
    normal_two, inverse_two = normalize(stream)
    normed_two = (normal_two * gain_cross + bias_cross).astype(BF)
    raw_cross = project(weights_two, [1], [normed_two], [F32])[0].reshape(heads, dim, tokens)
    norm_query, cross_pull = jax.vjp(head_norm, raw_cross, cross_query_gain)
    raw_text, value_two = project(weights_two, [3, 4], [text_wide], [F32, BF])
    norm_key, text_pull = jax.vjp(head_norm, raw_text.reshape(heads, dim, -1), text_key_gain)
    query_two = norm_query.astype(BF)
    key_two = norm_key.astype(BF)
    value_two = value_two.reshape(heads, dim, -1)
    saved_cross = []
    mixed_parts = []
    for index, piece in enumerate(pieces):
        length = lax.dynamic_index_in_dim(text_lengths, piece.sequence, 0, True)
        here = slice(index * keys, (index + 1) * keys)
        inputs = [cut(query_two, index), key_two[:, :, here], value_two[:, :, here]]
        inputs = [length] + [a[None, None] for a in inputs] + [(0, 0, 0)]
        mixed, logs = attend(*inputs, True, 4)
        saved_cross.append((inputs, mixed, logs))
        mixed_parts.append(mixed.reshape(depth, -1))
    mixed_two = jnp.concatenate(mixed_parts, 1)
    stream = stream + rebuild(weights_two, [2], [mixed_two], F32)
    normal_three, inverse_three = normalize(stream)
    normed_three = (normal_three * gain_hidden + bias_hidden).astype(BF)
    act, slopes = expand(w_expand, normed_three)
    output = contract(w_reduce, act, stream, BF)
    result = to_features(output, pieces, cols).astype(F32)

    g_inner = expand_back(w_reduce, grad_out, slopes)
    g_normed = contract(w_expand, g_inner, None, F32)
    g_hidden = hidden_outer(base, grad_out, act, normed_three, g_inner)
    g_hidden = lax.psum_scatter(
        g_hidden.reshape(2, -1, g_hidden.shape[3]), DEVICES, scatter_dimension=1, tiled=True
    ).astype(F32)
    g_hidden_gain = jnp.sum(g_normed * normal_three, 1)
    g_hidden_bias = jnp.sum(g_normed, 1)
    g_stream = grad_out.astype(F32) + norm_back(g_normed * gain_hidden, normal_three, inverse_three)

    running = []
    g_low = g_stream.astype(BF)
    g_mixed = project(weights_two, [2], [g_low], [BF])[0].reshape(heads, dim, tokens)
    r_cross = Reduction(core, g_low, [mixed_two], True)
    running.append(r_cross)
    g_queries = []
    g_keys = []
    g_values = []
    for index, piece in enumerate(pieces):
        inputs, mixed, logs = saved_cross[index]
        grads = attend_back(*inputs, mixed, cut(g_mixed, index)[None], logs, True, 4, False)
        g_queries.append(grads[0][0, 0])
        g_keys.append(grads[1][0, 0])
        g_values.append(grads[2][0, 0])
    g_queries, g_keys, g_values = tick((g_queries, g_keys, g_values), running)
    g_raw_cross, g_cq_gain = cross_pull(jnp.concatenate(g_queries, 2))
    g_raw_text, g_tk_gain = text_pull(jnp.concatenate(g_keys, 2))
    g_craw = g_raw_cross.astype(BF).reshape(depth, tokens)
    g_pair = [
        g_raw_text.astype(BF).reshape(depth, -1),
        jnp.concatenate(g_values, 2).astype(BF).reshape(depth, -1),
    ]
    g_normed = rebuild(weights_two, [1], [g_craw], F32)
    r_query = Reduction(core, normed_two, [g_craw], False)
    r_text = Reduction(core, text, g_pair, True)
    g_normed = tick(g_normed, running)
    running += [r_query, r_text]
    g_cross_gain = jnp.sum(g_normed * normal_two, 1)
    g_cross_bias = jnp.sum(g_normed, 1)
    g_stream = g_stream + norm_back(g_normed * gain_cross, normal_two, inverse_two)

    g_low = g_stream.astype(BF)
    g_mixed = project(weights_two, [0], [g_low], [BF])[0].reshape(heads, dim, tokens)
    g_mixed = tick(g_mixed, running)
    r_attn = Reduction(core, g_low, [mixed_one], False)
    g_parts = []
    for index, piece in enumerate(pieces):
        whole, mixed, logs = saved_self[index]
        grad = exchange(
            cut(g_mixed, index).reshape(piece.group, -1, dim, piece.count), piece.group, cols
        )
        part = attend_back(
            none, whole, whole, whole, (0, 1, 2), mixed, grad, logs, False, 2, True
        )
        part = tick(part, running)
        if index == 0:
            running.append(r_attn)
        g_parts.append(exchange(part, piece.group, cols))
    g_heads = [
        jnp.concatenate([p[:, i].reshape(heads, dim, -1) for p in g_parts], 2) for i in range(3)
    ]
    g_raw_q, g_q_gain = query_pull(g_heads[0].astype(F32))
    g_raw_k, g_k_gain = key_pull(g_heads[1].astype(F32))
    g_triple = [
        g.reshape(depth, tokens) for g in (g_raw_q.astype(BF), g_raw_k.astype(BF), g_heads[2])
    ]
    g_triple = tick(g_triple, running)
    g_normed = rebuild(weights_one, [2, 3, 4], g_triple, F32)
    g_normed = tick(g_normed, running)
    r_self = [
        Reduction(core, normed_one, g_triple[:2], True),
        Reduction(core, normed_one, g_triple[2:], False),
    ]
    crossed = g_normed * normal_one
    sums = jnp.stack(
        [
            jnp.stack([jnp.sum(cut(g_normed, i), 1), jnp.sum(cut(crossed, i), 1)], 0)
            for i in range(len(pieces))
        ],
        0,
    )
    which = jnp.stack(
        [jnp.where(jnp.arange(sequences) == p.sequence, 1.0, 0.0) for p in pieces], 0
    )
    g_modul = jnp.sum(which[:, :, None, None] * sums[:, None], 0)
    g_modul = g_modul.reshape(sequences, 2, cols, width).transpose(2, 0, 1, 3)
    g_modul = jnp.sum(lax.all_to_all(g_modul, "col", 0, 0, tiled=True), 0).astype(BF)
    g_modul = shared(g_modul, "row").reshape(-1, 2, width)
    g_modulation = einsum("sd,ske->dke", embed_rows, g_modul)
    g_stream = g_stream + norm_back(g_normed * scaling, normal_one, inverse_one)

    g_skip_gain = jnp.sum(g_stream * skip_normal, 1)
    g_skip_bias = jnp.sum(g_stream, 1)
    g_joined = norm_back(g_stream * gain_skip, skip_normal, skip_inverse).astype(BF)
    g_joined = tick(g_joined, running)
    r_skip = [
        Reduction(core, latent, [g_joined], True),
        Reduction(core, skipped, [g_joined], False),
    ]
    running += r_self
    g_latent = rebuild(weights_one, [0], [g_joined], BF)
    g_skipped = rebuild(weights_one, [1], [g_joined], BF)
    g_latent, g_skipped = tick((g_latent, g_skipped), running)
    g_latents = to_features(g_latent, pieces, cols).astype(F32)
    g_skip = to_features(g_skipped, pieces, cols).astype(F32)

    g_gains = jnp.stack(
        [g_skip_gain, g_skip_bias, g_cross_gain, g_cross_bias, g_hidden_gain, g_hidden_bias], 0
    )
    g_gains = g_gains.reshape(6, cols, width).transpose(1, 0, 2)
    g_head = jnp.stack([g_q_gain, g_k_gain, g_cq_gain, g_tk_gain], 0).reshape(1, -1, width)
    packed = jnp.concatenate([g_gains, jnp.broadcast_to(g_head, (cols, *g_head.shape[1:]))], 1)
    packed = jnp.sum(lax.all_to_all(packed, "col", 0, 0, tiled=True), 0)
    packed = jnp.sum(shared(packed, "row"), 0)
    g_gains = packed[:6]
    g_head = packed[6:].reshape(4, dim)
    return (
        result,
        g_latents,
        g_skip,
        jnp.concatenate([r.result() for r in r_skip], 0),
        g_modulation,
        jnp.concatenate([r.result() for r in r_self], 0).transpose(1, 0, 2),
        r_attn.result()[0].T,
        r_query.result()[0],
        r_text.result().transpose(1, 0, 2),
        r_cross.result()[0].T,
        g_hidden[0],
        g_hidden[1].T,
        *[g_gains[i] for i in range(6)],
        *[g_head[i] for i in range(4)],
    )


def solution(mesh):
    return jax.shard_map(
        shards,
        mesh=mesh,
        in_specs=(
            P("col", "row"),
            P("col", "row"),
            P("row", "col"),
            P("row", None, "col"),
            P("row"),
            P(None, "row"),
            P("col", "row"),
            P(None, "row", "col"),
            P("row", None, "col"),
            P("row", None, "col"),
            P("col", "row"),
            P("row", "col"),
            P("row", None, "col"),
            P("col", "row"),
            P("row", "col"),
            P("col", "row"),
            P("col"),
            P("col"),
            P("col"),
            P("col"),
            P("col"),
            P("col"),
            P(),
            P(),
            P(),
            P(),
        ),
        out_specs=(
            P("col", "row"),
            P("col", "row"),
            P("col", "row"),
            P(None, "row", "col"),
            P("row", None, "col"),
            P("row", None, "col"),
            P("col", "row"),
            P("row", "col"),
            P("row", None, "col"),
            P("col", "row"),
            P("row", "col"),
            P("col", "row"),
            P("col"),
            P("col"),
            P("col"),
            P("col"),
            P("col"),
            P("col"),
            P(),
            P(),
            P(),
            P(),
        ),
        check_vma=False,
    )
```

```python
from functools import partial
import math

import jax
import jax.numpy as jnp
from jax import lax
from jax.experimental import pallas as pl
from jax.experimental.pallas import tpu as pltpu
from jax.sharding import PartitionSpec as P

L = 1024
EPSILON = 1e-06
BF = jnp.bfloat16
F32 = jnp.float32
KEYPAD = 128
DEVICES = ("col", "row")
LOG2E = math.log2(math.e)
VMEM = 60 << 20


def einsum(spec, left, right):
    return jnp.einsum(spec, left, right, preferred_element_type=F32)


def dot(left, right, dims):
    return lax.dot_general(left, right, (dims, ((), ())), preferred_element_type=F32)


def params():
    return pltpu.CompilerParams(vmem_limit_bytes=VMEM)


def step_of(count):
    return 256 if count % 256 == 0 else count


def wide(ref, head):
    parts = [ref[s, 0, head] for s in range(ref.shape[0])]
    return parts[0] if len(parts) == 1 else jnp.concatenate(parts, 1)


def valid_keys(length_ref, keys, step):
    return lax.broadcasted_iota(jnp.int32, (keys, step), 0) < length_ref[0]


def attend_kernel(masked, length_ref, q_ref, k_ref, v_ref, o_ref, r_ref, l_ref):
    groups, _, heads, dim, count = q_ref.shape
    step = step_of(count)
    factor = dim ** (-0.5) * LOG2E
    for head in range(heads):
        key = wide(k_ref, head).T
        value = wide(v_ref, head)
        keys = key.shape[0]
        value = jnp.concatenate([value, jnp.ones((8, keys), BF)], 0)
        for place in range(0, groups * count, step):
            group, first = divmod(place, count)
            query = q_ref[group, 0, head, :, first : first + step]
            expo = jnp.exp2(dot(key, query, ((1,), (0,))) * factor)
            if masked:
                expo = jnp.where(valid_keys(length_ref, keys, step), expo, 0.0)
            both = dot(value, expo.astype(BF), ((1,), (0,)))
            total = both[dim : dim + 1]
            mixed = both[:dim] * (1.0 / total)
            high = mixed.astype(BF)
            o_ref[group, head, :, first : first + step] = high
            r_ref[group, head, :, first : first + step] = (mixed - high.astype(F32)).astype(BF)
            l_ref[head, :, place : place + step] = jnp.log2(total)


def attend_back_kernel(
    masked, length_ref, q_ref, k_ref, v_ref, m_ref, r_ref, g_ref, l_ref, *outs
):
    groups, _, heads, dim, count = q_ref.shape
    step = step_of(count)
    scale = dim ** (-0.5)
    for head in range(heads):
        key = wide(k_ref, head)
        keys = key.shape[1]
        turned = key.T
        value = jnp.concatenate([wide(v_ref, head), jnp.ones((8, keys), BF)], 0).T
        g_key = g_value = None
        for place in range(0, groups * count, step):
            group, first = divmod(place, count)
            here = slice(first, first + step)
            query = q_ref[group, 0, head, :, here]
            grad = g_ref[group, head, :, here]
            mixed = m_ref[group, head, :, here].astype(F32)
            mixed = mixed + r_ref[group, head, :, here].astype(F32)
            delta = -jnp.sum(grad.astype(F32) * mixed, 0, keepdims=True)
            high = delta.astype(BF)
            rest = (delta - high.astype(F32)).astype(BF)
            more = jnp.concatenate([grad, high, rest, jnp.zeros((6, step), BF)], 0)
            probs = jnp.exp2(
                dot(turned, query, ((1,), (0,))) * (scale * LOG2E)
                - l_ref[head, :, place : place + step]
            )
            if masked:
                probs = jnp.where(valid_keys(length_ref, keys, step), probs, 0.0)
            product = (probs * dot(value, more, ((1,), (0,)))).astype(BF)
            g_query = dot(key, product, ((1,), (0,))) * scale
            part_value = dot(grad, probs.astype(BF), ((1,), (1,)))
            part_key = dot(query, product, ((1,), (1,)))
            g_value = part_value if g_value is None else g_value + part_value
            g_key = part_key if g_key is None else g_key + part_key
            outs[0][group, 0, head, :, here] = g_query.astype(outs[0].dtype)
        g_key = g_key * scale
        if len(outs) == 1:
            for group in range(groups):
                here = slice(group * count, (group + 1) * count)
                outs[0][group, 1, head] = g_key[:, here].astype(BF)
                outs[0][group, 2, head] = g_value[:, here].astype(BF)
        else:
            outs[1][0, 0, head] = g_key
            outs[2][0, 0, head] = g_value


def costs(heads, queries, keys, dim, products):
    return pl.CostEstimate(
        flops=2 * products * heads * queries * keys * 256,
        transcendentals=heads * queries * keys,
        bytes_accessed=2 * products * heads * dim * (queries + keys),
    )


def head_block(shape, count, kind=0):
    groups, _, _, dim, tokens = shape
    return pl.BlockSpec((groups, 1, count, dim, tokens), lambda h: (0, kind, h, 0, 0))


def mix_block(shape, count):
    groups, _, _, dim, tokens = shape
    return pl.BlockSpec((groups, count, dim, tokens), lambda h: (0, h, 0, 0))


def attend(length, query, key, value, kinds, masked, most):
    groups, _, heads, dim, count = query.shape
    many = math.gcd(heads, most)
    total = groups * count
    keys = key.shape[0] * key.shape[4]
    return pl.pallas_call(
        partial(attend_kernel, masked),
        grid=(heads // many,),
        in_specs=[pl.BlockSpec(memory_space=pltpu.SMEM)]
        + [head_block(a.shape, many, kind) for a, kind in zip((query, key, value), kinds)],
        out_specs=[
            mix_block(query.shape, many),
            mix_block(query.shape, many),
            pl.BlockSpec((many, 1, total), lambda h: (h, 0, 0)),
        ],
        out_shape=[
            jax.ShapeDtypeStruct((groups, heads, dim, count), BF),
            jax.ShapeDtypeStruct((groups, heads, dim, count), BF),
            jax.ShapeDtypeStruct((heads, 1, total), F32),
        ],
        cost_estimate=costs(heads, total, keys, dim, 2),
        compiler_params=params(),
        name="attend",
    )(length, query, key, value)


def attend_back(length, query, key, value, kinds, kept, grad, masked, most, stacked):
    mixed, rest, logs = kept
    groups, _, heads, dim, count = query.shape
    many = math.gcd(heads, most)
    total = groups * count
    keys = key.shape[0] * key.shape[4]
    if stacked:
        out_specs = pl.BlockSpec((groups, 3, many, dim, count), lambda h: (0, 0, h, 0, 0))
        out_shape = jax.ShapeDtypeStruct((groups, 3, heads, dim, count), BF)
    else:
        out_specs = [head_block(a.shape, many) for a in (query, key, value)]
        out_shape = [jax.ShapeDtypeStruct(a.shape, F32) for a in (query, key, value)]
    return pl.pallas_call(
        partial(attend_back_kernel, masked),
        grid=(heads // many,),
        in_specs=[pl.BlockSpec(memory_space=pltpu.SMEM)]
        + [head_block(a.shape, many, kind) for a, kind in zip((query, key, value), kinds)]
        + [mix_block(query.shape, many)] * 3
        + [pl.BlockSpec((many, 1, total), lambda h: (h, 0, 0))],
        out_specs=out_specs,
        out_shape=out_shape,
        cost_estimate=costs(heads, total, keys, dim, 5),
        compiler_params=params(),
        name="attend_back",
    )(length, query, key, value, mixed, rest, grad, logs)


def work(rows, depth, tokens, moved):
    return pl.CostEstimate(flops=2 * rows * depth * tokens, transcendentals=0, bytes_accessed=moved)


def lanes(width):
    return -(-width // 128) * 128


def full(shape):
    return pl.BlockSpec(shape, lambda *_: (0,) * len(shape))


def project(weight, kinds, values, dtypes, joined=False):
    _, cols, depth, width = weight.shape
    tokens = values[0].shape[1]
    outs = 1 if joined else len(kinds)

    def kernel(*refs):
        blocks = refs[: len(kinds)]
        given = refs[len(kinds) : -outs]
        total = None
        for index, block in enumerate(blocks):
            part = dot(block[0, 0], given[index % len(given)][...], ((0,), (0,)))
            if not joined:
                refs[index - outs][...] = part.astype(dtypes[index])
            total = part if total is None else total + part
        if joined:
            refs[-1][...] = total.astype(dtypes[0])

    return pl.pallas_call(
        kernel,
        grid=(cols,),
        in_specs=[
            pl.BlockSpec((1, 1, depth, width), partial(lambda k, c: (k, c, 0, 0), kind))
            for kind in kinds
        ]
        + [full(v.shape) for v in values],
        out_specs=[pl.BlockSpec((width, tokens), lambda c: (c, 0))] * outs,
        out_shape=[jax.ShapeDtypeStruct((cols * width, tokens), dtypes[i]) for i in range(outs)],
        cost_estimate=work(len(kinds) * cols * width, depth, tokens, 8 * depth * tokens),
        compiler_params=params(),
        name="project",
    )(*([weight] * len(kinds)), *values)


def rebuild(weight, kinds, values, dtype):
    _, cols, depth, width = weight.shape
    tokens = values[0].shape[1]
    tile = depth // 4

    def kernel(*refs):
        total = None
        for block, given in zip(refs[: len(kinds)], refs[len(kinds) : -1]):
            for col in range(cols):
                part = dot(block[0, col], given[col * width : (col + 1) * width, :], ((1,), (0,)))
                total = part if total is None else total + part
        refs[-1][...] = total.astype(dtype)

    return pl.pallas_call(
        kernel,
        grid=(4,),
        in_specs=[
            pl.BlockSpec((1, cols, tile, width), partial(lambda k, j: (k, 0, j, 0), kind))
            for kind in kinds
        ]
        + [full(v.shape) for v in values],
        out_specs=pl.BlockSpec((tile, tokens), lambda j: (j, 0)),
        out_shape=jax.ShapeDtypeStruct((depth, tokens), dtype),
        cost_estimate=work(depth, len(kinds) * cols * width, tokens, 8 * depth * tokens),
        compiler_params=params(),
        name="rebuild",
    )(*([weight] * len(kinds)), *values)


def project_blocks(base, blocks, width, values):
    many = len(blocks)
    depth, broad = blocks[0].shape
    tokens = values.shape[1]
    tile = depth // 4

    def kernel(base_ref, *refs):
        values_ref, out_ref = refs[many:]

        @pl.when(pl.program_id(0) == 0)
        def _():
            out_ref[...] = jnp.zeros_like(out_ref)

        for index in range(many):
            here = pl.ds(pl.multiple_of((index ^ base_ref[0]) * width, width), width)
            out_ref[here, :] += dot(refs[index][...], values_ref[...], ((0,), (0,)))[:width]

    return pl.pallas_call(
        kernel,
        grid_spec=pltpu.PrefetchScalarGridSpec(
            num_scalar_prefetch=1,
            grid=(4,),
            in_specs=[pl.BlockSpec((tile, broad), lambda j, b: (j, 0))] * many
            + [pl.BlockSpec((tile, tokens), lambda j, b: (j, 0))],
            out_specs=pl.BlockSpec((many * width, tokens), lambda j, b: (0, 0)),
        ),
        out_shape=jax.ShapeDtypeStruct((many * width, tokens), F32),
        cost_estimate=work(many * width, depth, tokens, 4 * depth * tokens),
        compiler_params=params(),
        name="project_blocks",
    )(base, *blocks, values)


def rebuild_blocks(base, blocks, width, values):
    many = len(blocks)
    depth, broad = blocks[0].shape
    tokens = values.shape[1]
    tile = depth // 4

    def kernel(base_ref, *refs):
        values_ref, out_ref = refs[many:]
        total = None
        for index in range(many):
            here = pl.ds(pl.multiple_of((index ^ base_ref[0]) * width, width), width)
            part = dot(refs[index][:, :width], values_ref[here, :], ((1,), (0,)))
            total = part if total is None else total + part
        out_ref[...] = total.astype(BF)

    return pl.pallas_call(
        kernel,
        grid_spec=pltpu.PrefetchScalarGridSpec(
            num_scalar_prefetch=1,
            grid=(4,),
            in_specs=[pl.BlockSpec((tile, broad), lambda j, b: (j, 0))] * many
            + [pl.BlockSpec(values.shape, lambda j, b: (0, 0))],
            out_specs=pl.BlockSpec((tile, tokens), lambda j, b: (j, 0)),
        ),
        out_shape=jax.ShapeDtypeStruct((depth, tokens), BF),
        cost_estimate=work(many * width, depth, tokens, 4 * depth * tokens),
        compiler_params=params(),
        name="rebuild_blocks",
    )(base, *blocks, values)


def outer(core, left, rights, flip):
    rows, tokens = left.shape
    cols = lax.axis_size("col")
    width = rights[0].shape[0] // cols
    broad = lanes(width)

    def kernel(core_ref, left_ref, *refs):
        for index in range(len(rights)):
            right = refs[index][...]
            if broad > width:
                right = jnp.concatenate([right, jnp.zeros((broad - width, tokens), BF)], 0)
            part = dot(left_ref[...], right, ((1,), (1,)))
            refs[-1][index, 0] = part.astype(BF)

    return pl.pallas_call(
        kernel,
        grid_spec=pltpu.PrefetchScalarGridSpec(
            num_scalar_prefetch=1,
            grid=(cols // 2,),
            in_specs=[pl.BlockSpec((rows, tokens), lambda y, core: (0, 0))]
            + [
                pl.BlockSpec((width, tokens), lambda y, core: (2 * y + (core[0] ^ flip), 0))
                for _ in rights
            ],
            out_specs=pl.BlockSpec(
                (len(rights), 1, rows, broad), lambda y, core: (0, y, 0, 0)
            ),
        ),
        out_shape=jax.ShapeDtypeStruct((len(rights), cols // 2, rows, broad), BF),
        cost_estimate=work(
            rows, tokens, len(rights) * cols // 2 * width, 3 * rows * cols * width * len(rights)
        ),
        compiler_params=params(),
        name="outer",
    )(core, left, *rights)


def expand(blocks, values):
    many = len(blocks)
    depth, hidden = blocks[0].shape
    tokens = values.shape[1]
    tile = 384 if hidden % 384 == 0 else hidden
    slope = 0.79788456
    cubic = 0.044715

    def kernel(*refs):
        values_ref, act_ref, slope_ref = refs[many:]
        for index in range(many):
            inner = dot(refs[index][...], values_ref[...], ((0,), (0,)))
            square = inner * inner
            bent = jnp.tanh(inner * (slope + slope * cubic * square))
            half = 0.5 + 0.5 * bent
            act_ref[index] = (inner * half).astype(BF)
            rise = slope + 3.0 * slope * cubic * square
            slope_ref[index] = (half + 0.5 * inner * (1.0 - bent * bent) * rise).astype(BF)

    return pl.pallas_call(
        kernel,
        grid=(hidden // tile,),
        in_specs=[pl.BlockSpec((depth, tile), lambda j: (0, j))] * many + [full(values.shape)],
        out_specs=[pl.BlockSpec((many, tile, tokens), lambda j: (0, j, 0))] * 2,
        out_shape=[jax.ShapeDtypeStruct((many, hidden, tokens), BF)] * 2,
        cost_estimate=work(many * hidden, depth, tokens, 3 * many * hidden * depth),
        compiler_params=params(),
        name="expand",
    )(*blocks, values)


def expand_back(blocks, values, slopes):
    many = len(blocks)
    depth, hidden = blocks[0].shape
    tokens = values.shape[1]
    tile = 384 if hidden % 384 == 0 else hidden

    def kernel(*refs):
        values_ref, slope_ref, out_ref = refs[many:]
        for index in range(many):
            part = dot(refs[index][...], values_ref[...], ((0,), (0,)))
            out_ref[index] = (part * slope_ref[index].astype(F32)).astype(BF)

    return pl.pallas_call(
        kernel,
        grid=(hidden // tile,),
        in_specs=[pl.BlockSpec((depth, tile), lambda j: (0, j))] * many
        + [full(values.shape), pl.BlockSpec((many, tile, tokens), lambda j: (0, j, 0))],
        out_specs=pl.BlockSpec((many, tile, tokens), lambda j: (0, j, 0)),
        out_shape=jax.ShapeDtypeStruct((many, hidden, tokens), BF),
        cost_estimate=work(many * hidden, depth, tokens, 3 * many * hidden * depth),
        compiler_params=params(),
        name="expand_back",
    )(*blocks, values, slopes)


def contract(blocks, values, added, dtype):
    many = len(blocks)
    depth, hidden = blocks[0].shape
    tokens = values.shape[2]
    tile = depth // 4
    extra = [] if added is None else [added]

    def kernel(*refs):
        values_ref = refs[many]
        total = refs[many + 1][...] if extra else None
        for index in range(many):
            part = dot(refs[index][...], values_ref[index], ((1,), (0,)))
            total = part if total is None else total + part
        refs[-1][...] = total.astype(dtype)

    line = pl.BlockSpec((tile, tokens), lambda j: (j, 0))
    return pl.pallas_call(
        kernel,
        grid=(4,),
        in_specs=[pl.BlockSpec((tile, hidden), lambda j: (j, 0))] * many
        + [full(values.shape)]
        + [line] * len(extra),
        out_specs=line,
        out_shape=jax.ShapeDtypeStruct((depth, tokens), dtype),
        cost_estimate=work(depth, many * hidden, tokens, 3 * many * hidden * depth),
        compiler_params=params(),
        name="contract",
    )(*blocks, values, *extra)


def hidden_outer(base, grad_out, act, normed, grad_inner):
    many, hidden, tokens = act.shape
    depth = grad_out.shape[0]
    parts = 2 if hidden % 256 == 0 else 1
    tile = hidden // parts

    def kernel(base_ref, out_ref, act_ref, normed_ref, inner_ref, grad_ref):
        kind = pl.program_id(0)

        @pl.when(kind == 0)
        def _():
            grad_ref[0, 0] = dot(normed_ref[...], inner_ref[0], ((1,), (1,))).astype(BF)

        @pl.when(kind == 1)
        def _():
            grad_ref[0, 0] = dot(out_ref[...], act_ref[0], ((1,), (1,))).astype(BF)

    return pl.pallas_call(
        kernel,
        grid_spec=pltpu.PrefetchScalarGridSpec(
            num_scalar_prefetch=1,
            grid=(2, many, parts),
            in_specs=[
                pl.BlockSpec((depth, tokens), lambda s, p, j, b: (0, 0)),
                pl.BlockSpec((1, tile, tokens), lambda s, p, j, b: (s * p, s * j, 0)),
                pl.BlockSpec((depth, tokens), lambda s, p, j, b: (0, 0)),
                pl.BlockSpec(
                    (1, tile, tokens),
                    lambda s, p, j, b: (p + s * (many - 1 - p), j + s * (parts - 1 - j), 0),
                ),
            ],
            out_specs=pl.BlockSpec((1, 1, depth, tile), lambda s, p, j, b: (s, p ^ b[0], 0, j)),
        ),
        out_shape=jax.ShapeDtypeStruct((2, many, depth, hidden), BF),
        cost_estimate=work(2 * depth, tokens, many * hidden, 5 * many * depth * hidden),
        compiler_params=params(),
        name="hidden_outer",
    )(base, grad_out, act, normed, grad_inner)


def assemble(place, own, got):
    _, rows, width = own.shape

    def kernel(place_ref, own_ref, got_ref, out_ref):
        @pl.when(pl.program_id(1) == place_ref[1])
        def _():
            out_ref[0, 0] = own_ref[0]

        @pl.when(pl.program_id(1) != place_ref[1])
        def _():
            out_ref[0, 0] = got_ref[0]

    spec = pl.BlockSpec((1, rows, width), lambda z, x, place: (z ^ place[0], 0, 0))
    return pl.pallas_call(
        kernel,
        grid_spec=pltpu.PrefetchScalarGridSpec(
            num_scalar_prefetch=1,
            grid=(4, 2),
            in_specs=[spec, spec],
            out_specs=pl.BlockSpec((1, 1, rows, width), lambda z, x, place: (z, x, 0, 0)),
        ),
        out_shape=jax.ShapeDtypeStruct((4, 2, rows, width), BF),
        cost_estimate=work(1, 1, 1, 48 * rows * width),
        name="assemble",
    )(place, own, got).reshape(8 * rows, width)


def normalize(values):
    average = jnp.mean(values, 0, keepdims=True)
    centred = values - average
    inverse = lax.rsqrt(jnp.mean(centred * centred, 0, keepdims=True) + EPSILON)
    return centred * inverse, inverse


def norm_back(grad, normal, inverse):
    average = jnp.mean(grad, 0, keepdims=True)
    crossed = jnp.mean(grad * normal, 0, keepdims=True)
    return inverse * (grad - average - normal * crossed)


def head_norm(values, gain):
    average = jnp.mean(values, 1, keepdims=True)
    centred = values - average
    variance = jnp.mean(centred * centred, 1, keepdims=True)
    return centred * lax.rsqrt(variance + EPSILON) * gain[None, :, None]


def rope_tables(places, head_dim):
    quarter = head_dim // 4
    freqs = jnp.exp(jnp.arange(quarter, dtype=F32) * (-4.0 * math.log(10000.0) / head_dim))
    rows = freqs[:, None] * places[0].astype(F32)[None, :]
    cols = freqs[:, None] * places[1].astype(F32)[None, :]
    angles = jnp.concatenate([rows, rows, cols, cols], 0)
    return jnp.cos(angles), jnp.sin(angles)


def rotate(values):
    quarter = values.shape[1] // 4
    one, two, three, four = (values[:, i * quarter : (i + 1) * quarter] for i in range(4))
    return jnp.concatenate([-two, one, -four, three], 1)


class Piece:
    def __init__(self, start, count, group, sequence):
        self.start = start
        self.count = count
        self.group = group
        self.sequence = sequence


def pieces_of(cols, sequences):
    mine = lax.axis_index("col")
    if cols == 4 and sequences == 3:
        return [
            Piece(0, L // 2, 2, mine // 2),
            Piece(2 * L, L // 4, 4, jnp.int32(2)),
        ]
    return [Piece(s * L, L // cols, cols, jnp.int32(s)) for s in range(sequences)]


def groups_of(size, cols):
    return [list(range(i, i + size)) for i in range(0, cols, size)]


def exchange(values, size, cols):
    if size == cols:
        return lax.all_to_all(values, "col", 0, 0, tiled=True)
    return lax.all_to_all(
        values, "col", 0, 0, tiled=True, axis_index_groups=groups_of(size, cols)
    )


def to_tokens(values, pieces, cols):
    width = values.shape[0]
    parts = []
    for piece in pieces:
        region = values[:, piece.start : piece.start + cols * piece.count]
        parts.append(region.reshape(width, cols, piece.count).transpose(1, 0, 2))
    stacked = jnp.concatenate(parts, 2)
    return exchange(stacked, cols, cols).reshape(cols * width, -1)


def to_features(values, pieces, cols):
    width = values.shape[0] // cols
    got = exchange(values.reshape(cols, width, -1), cols, cols)
    parts = []
    at = 0
    for piece in pieces:
        part = got[:, :, at : at + piece.count]
        parts.append(part.transpose(1, 0, 2).reshape(width, cols * piece.count))
        at += piece.count
    return jnp.concatenate(parts, 1)


def shared(values, axis):
    size = lax.axis_size(axis)
    return lax.all_to_all(
        jnp.broadcast_to(values[None], (size, *values.shape)), axis, 0, 0, tiled=True
    )


def swap(values, axis, bit):
    size = lax.axis_size(axis)
    return lax.ppermute(values, axis, [(i, i ^ bit) for i in range(size)])


def custom_mesh():
    return (lax.axis_size("row"), lax.axis_size("col")) == (8, 4)


def gather_weights(blocks):
    cols = lax.axis_size("col")
    most = max(block.shape[0] for block in blocks)
    padded = [jnp.pad(b, ((0, most - b.shape[0]), (0, 0))) for b in blocks]
    whole = lax.all_gather(jnp.stack(padded, 0), DEVICES, axis=1, tiled=True)
    return whole.reshape(len(blocks), cols, -1, blocks[0].shape[1])


class Gathering:
    last = 4

    def __init__(self, block, across, place):
        self.across = across
        self.place = place
        self.stage = 0
        self.state = [block]
        if not custom_mesh():
            cols = lax.axis_size("col")
            whole = lax.all_gather(block, DEVICES, axis=0, tiled=True)
            self.state = list(whole.reshape(cols, -1, block.shape[1]))
            self.stage = self.last

    def advance(self):
        state = self.state
        self.stage += 1
        if self.stage == 1:
            self.state = state + [swap(state[0], "row", 2 * level) for level in (1, 2, 3)]
        elif self.stage == 2:
            stack = jnp.stack(state, 0)
            self.state = [stack, swap(stack, "row", 1) if self.across else swap(stack, "col", 2)]
        elif self.stage == 3 and self.across:
            mine = assemble(self.place, *state)
            self.state = [mine, swap(mine, "col", 1), swap(mine, "col", 2)]
        elif self.stage == 3:
            self.state = state + [swap(a, "row", 1) for a in state]
        elif self.across:
            self.state = state + [swap(state[2], "col", 1)]
        else:
            mine = assemble(self.place, state[0], state[2])
            other = assemble(self.place, state[1], state[3])
            self.state = [mine, swap(mine, "col", 1), other, swap(other, "col", 1)]

    def result(self):
        while self.stage < self.last:
            self.advance()
        return self.state


def pick(values, axis, index):
    return lax.dynamic_index_in_dim(values, index, axis, False)


def add(left, right):
    return (left.astype(F32) + right.astype(F32)).astype(BF)


class Reduction:
    last = 4

    def __init__(self, core, left, rights, across):
        self.across = across
        self.many = len(rights)
        self.stage = 0 if custom_mesh() else self.last
        if not custom_mesh():
            cols = lax.axis_size("col")
            whole = jnp.stack(
                [einsum("kt,cnt->ckn", left, r.reshape(cols, -1, r.shape[1])) for r in rights], 0
            )
            flat = whole.reshape(self.many, -1, whole.shape[3]).astype(BF)
            self.state = [lax.psum_scatter(flat, DEVICES, scatter_dimension=1, tiled=True)]
            return
        self.width = rights[0].shape[0] // 4
        shape = (self.many, 2, 4, 2, left.shape[0] // 8, lanes(self.width))
        send = outer(core, left, rights, 1)
        got = swap(send, "col", 1)
        keep = outer(core, left, rights, 0)
        self.state = [keep.reshape(shape), got.reshape(shape)]

    def half(self, side):
        kept, got = self.state
        axis = (3 if kept.ndim == 6 else 2) if side else 1
        name, bit = ("row", 1) if side else ("col", 2)
        index = lax.axis_index("row") % 2 if side else lax.axis_index("col") // 2
        away = add(pick(kept, axis, 1 - index), pick(got, axis, 1 - index))
        here = add(pick(kept, axis, index), pick(got, axis, index))
        self.state = [here, swap(away, name, bit)]

    def advance(self):
        self.stage += 1
        if self.stage <= 2:
            self.half(self.across == (self.stage == 1))
        elif self.stage == 3:
            level = lax.axis_index("row") // 2
            total = add(*self.state)
            self.state = [pick(total, 1, level)] + [
                swap(pick(total, 1, level ^ other), "row", 2 * other) for other in (1, 2, 3)
            ]
        else:
            total = self.state[0].astype(F32)
            for other in self.state[1:]:
                total = total + other.astype(F32)
            self.state = [total[..., : self.width]]

    def result(self):
        while self.stage < self.last:
            self.advance()
        return self.state[0].astype(F32)


def tick(values, running):
    active = [r for r in running if r.stage < r.last]
    if active:
        values, states = lax.optimization_barrier((values, [r.state for r in active]))
        for beside, state in zip(active, states):
            beside.state = state
            beside.advance()
    return values


def after(values, done):
    return lax.optimization_barrier((values, done))[0]


def shards(
    latents,
    skip_input,
    condition,
    text_states,
    text_lengths,
    positions,
    out_grad,
    skip_weight,
    modulation,
    self_inputs,
    self_output,
    cross_query,
    cross_keyvalue,
    cross_output,
    expand_weight,
    reduce_weight,
    skip_gain,
    skip_bias,
    cross_gain,
    cross_bias,
    hidden_gain,
    hidden_bias,
    query_gain,
    key_gain,
    cross_query_gain,
    text_key_gain,
):
    cols = lax.axis_size("col")
    rows = lax.axis_size("row")
    mine = lax.axis_index("col")
    my_row = lax.axis_index("row")
    width, row_tokens = latents.shape
    depth = width * cols
    dim = query_gain.shape[0]
    heads = depth // dim
    sequences = row_tokens // L
    tokens = row_tokens // cols
    texts = text_states.shape[1]
    keys = -(-texts // KEYPAD) * KEYPAD
    pieces = pieces_of(cols, sequences)
    starts = [sum(p.count for p in pieces[:i]) for i in range(len(pieces))]
    core = (mine % 2).astype(jnp.int32)[None]
    place = jnp.stack([my_row // 2, my_row % 2]).astype(jnp.int32)
    base = (mine if custom_mesh() else jnp.zeros_like(mine)).astype(jnp.int32)[None]

    def cut(values, index):
        return values[..., starts[index] : starts[index] + pieces[index].count]

    block_rows = depth // rows
    split = (width // block_rows, block_rows, row_tokens)
    both = jnp.stack([latents.reshape(split), skip_input.reshape(split)], 1)
    both = to_tokens(both.reshape(2 * width, row_tokens), pieces, cols)

    weights_one = gather_weights([self_inputs[:, i] for i in range(3)])
    skip_block = jnp.concatenate([skip_weight[0], skip_weight[1]], 0)
    skip_block = jnp.pad(skip_block, ((0, 0), (0, lanes(width) - width)))
    w_skip = Gathering(skip_block, True, place).result()
    expanding = Gathering(expand_weight, True, place)
    reducing = Gathering(reduce_weight.T, False, place)
    gathers = [expanding, reducing]

    places = jnp.concatenate(
        [
            lax.dynamic_slice_in_dim(positions, p.start + mine * p.count, p.count, 1)
            for p in pieces
        ],
        1,
    )

    embed = jax.nn.silu(condition.astype(F32)).astype(BF)
    embed = shared(embed, "row").reshape(-1, width)
    embed = shared(embed, "col").transpose(1, 0, 2).reshape(-1, depth)
    embed_rows = lax.dynamic_slice_in_dim(embed, my_row * block_rows, block_rows, 1)
    modul = einsum("sd,dke->ske", embed_rows, modulation).reshape(rows, sequences, 2, width)
    modul = jnp.sum(lax.all_to_all(modul, "row", 0, 0, tiled=True), 0)
    gains = jnp.stack(
        [skip_gain, skip_bias, cross_gain, cross_bias, hidden_gain, hidden_bias], 0
    )
    table = jnp.concatenate([gains, modul.reshape(-1, width)], 0)
    table = shared(table, "col").transpose(1, 0, 2).reshape(-1, depth)
    modul = table[6:].reshape(sequences, 2, depth)
    chosen = [lax.dynamic_index_in_dim(modul, p.sequence, 0, False) for p in pieces]
    columns = lax.optimization_barrier(jnp.concatenate([table[:6], *chosen], 0)).T
    gain_skip, bias_skip, gain_cross, bias_cross, gain_hidden, bias_hidden = (
        columns[:, i : i + 1] for i in range(6)
    )
    token_index = lax.broadcasted_iota(jnp.int32, (1, tokens), 1)

    def per_token(which):
        result = columns[:, 6 + which : 7 + which]
        for index in range(1, len(pieces)):
            column = columns[:, 6 + 2 * index + which : 7 + 2 * index + which]
            result = jnp.where(token_index >= starts[index], column, result)
        return jnp.broadcast_to(result, (depth, tokens))

    shifting = per_token(0)
    scaling = 1.0 + per_token(1)

    joined = project_blocks(base, w_skip, width, both)
    joined = tick(joined, gathers)
    weights_two = gather_weights(
        [self_output.T, cross_query, cross_output.T, cross_keyvalue[:, 0], cross_keyvalue[:, 1]]
    )
    skip_normal, skip_inverse = normalize(joined)
    stream = skip_normal * gain_skip + bias_skip
    normal_one, inverse_one = normalize(stream)
    normed_one = (normal_one * scaling + shifting).astype(BF)
    raw = project(weights_one, [0, 1, 2], [normed_one], [F32, F32, BF])
    raw = tick(raw, gathers)
    raw = [r.reshape(heads, dim, tokens) for r in raw]
    cosine, sine = rope_tables(places, dim)

    def self_piece(value, gain):
        normal = head_norm(value, gain)
        return normal * cosine[None] + rotate(normal) * sine[None]

    rot_query, query_pull = jax.vjp(self_piece, raw[0], query_gain)
    rot_key, key_pull = jax.vjp(self_piece, raw[1], key_gain)
    triple = [rot_query.astype(BF), rot_key.astype(BF), raw[2]]

    text = shared(jnp.pad(after(text_states, joined), ((0, 0), (0, keys - texts), (0, 0))), "col")
    text = jnp.concatenate(
        [lax.dynamic_index_in_dim(text, p.sequence, 1, False) for p in pieces], 1
    )
    text = text.transpose(0, 2, 1).reshape(-1, len(pieces) * keys)
    text_rows = text.shape[0] // rows
    text_wide = jnp.pad(
        text.reshape(rows, text_rows, -1), ((0, 0), (0, block_rows - text_rows), (0, 0))
    ).reshape(depth, -1)

    def to_heads(parts, index):
        size = pieces[index].group
        split = [cut(p, index).reshape(size, heads // size, dim, -1) for p in parts]
        return exchange(jnp.stack(split, 1), size, cols)

    none = jnp.zeros((1,), jnp.int32)
    saved_self = []
    mixed_parts = []
    for index, piece in enumerate(pieces):
        whole = to_heads(triple, index)
        kept = attend(none, whole, whole, whole, (0, 1, 2), False, 2)
        saved_self.append((whole, kept))
        mixed = tick(kept[0], gathers)
        mixed_parts.append(exchange(mixed, piece.group, cols).reshape(depth, -1))
    mixed_one = jnp.concatenate(mixed_parts, 1)
    stream = stream + rebuild(weights_two, [0], [mixed_one], F32)
    normal_two, inverse_two = normalize(stream)
    normed_two = (normal_two * gain_cross + bias_cross).astype(BF)
    raw_cross = project(weights_two, [1], [normed_two], [F32])[0].reshape(heads, dim, tokens)
    norm_query, cross_pull = jax.vjp(head_norm, raw_cross, cross_query_gain)
    raw_text, value_two = project(weights_two, [3, 4], [text_wide], [F32, BF])
    norm_key, text_pull = jax.vjp(head_norm, raw_text.reshape(heads, dim, -1), text_key_gain)
    query_two = norm_query.astype(BF)
    key_two = norm_key.astype(BF)
    value_two = value_two.reshape(heads, dim, -1)
    saved_cross = []
    mixed_parts = []
    for index, piece in enumerate(pieces):
        length = lax.dynamic_index_in_dim(text_lengths, piece.sequence, 0, True)
        here = slice(index * keys, (index + 1) * keys)
        inputs = [cut(query_two, index), key_two[:, :, here], value_two[:, :, here]]
        inputs = [length] + [a[None, None] for a in inputs] + [(0, 0, 0)]
        kept = attend(*inputs, True, 4)
        saved_cross.append((inputs, kept))
        mixed_parts.append(kept[0].reshape(depth, -1))
    mixed_two = jnp.concatenate(mixed_parts, 1)
    stream = stream + rebuild(weights_two, [2], [mixed_two], F32)
    normal_three, inverse_three = normalize(stream)
    normed_three = (normal_three * gain_hidden + bias_hidden).astype(BF)
    w_expand = expanding.result()
    w_reduce = reducing.result()
    grad_out = to_tokens(after(out_grad, joined).astype(BF), pieces, cols)
    act, slopes = expand(w_expand, normed_three)
    output = contract(w_reduce, act, stream, BF)
    result = to_features(output, pieces, cols).astype(F32)

    g_inner = expand_back(w_reduce, grad_out, slopes)
    g_normed = contract(w_expand, g_inner, None, F32)
    g_hidden = hidden_outer(base, grad_out, act, normed_three, g_inner)
    g_hidden = lax.psum_scatter(
        g_hidden.reshape(2, -1, g_hidden.shape[3]), DEVICES, scatter_dimension=1, tiled=True
    ).astype(F32)
    g_hidden_gain = jnp.sum(g_normed * normal_three, 1)
    g_hidden_bias = jnp.sum(g_normed, 1)
    g_stream = grad_out.astype(F32) + norm_back(g_normed * gain_hidden, normal_three, inverse_three)

    running = []
    g_low = g_stream.astype(BF)
    g_mixed = project(weights_two, [2], [g_low], [BF])[0].reshape(heads, dim, tokens)
    r_cross = Reduction(core, g_low, [mixed_two], True)
    running.append(r_cross)
    g_queries = []
    g_keys = []
    g_values = []
    for index, piece in enumerate(pieces):
        inputs, kept = saved_cross[index]
        grads = attend_back(*inputs, kept, cut(g_mixed, index)[None], True, 4, False)
        g_queries.append(grads[0][0, 0])
        g_keys.append(grads[1][0, 0])
        g_values.append(grads[2][0, 0])
    g_queries, g_keys, g_values = tick((g_queries, g_keys, g_values), running)
    g_raw_cross, g_cq_gain = cross_pull(jnp.concatenate(g_queries, 2))
    g_raw_text, g_tk_gain = text_pull(jnp.concatenate(g_keys, 2))
    g_craw = g_raw_cross.astype(BF).reshape(depth, tokens)
    g_pair = [
        g_raw_text.astype(BF).reshape(depth, -1),
        jnp.concatenate(g_values, 2).astype(BF).reshape(depth, -1),
    ]
    g_normed = rebuild(weights_two, [1], [g_craw], F32)
    r_query = Reduction(core, normed_two, [g_craw], False)
    r_text = Reduction(core, text, g_pair, True)
    g_normed = tick(g_normed, running)
    running += [r_query, r_text]
    g_cross_gain = jnp.sum(g_normed * normal_two, 1)
    g_cross_bias = jnp.sum(g_normed, 1)
    g_stream = g_stream + norm_back(g_normed * gain_cross, normal_two, inverse_two)

    g_low = g_stream.astype(BF)
    g_mixed = project(weights_two, [0], [g_low], [BF])[0].reshape(heads, dim, tokens)
    g_mixed = tick(g_mixed, running)
    r_attn = Reduction(core, g_low, [mixed_one], False)
    g_parts = []
    for index, piece in enumerate(pieces):
        whole, kept = saved_self[index]
        grad = exchange(
            cut(g_mixed, index).reshape(piece.group, -1, dim, piece.count), piece.group, cols
        )
        part = attend_back(
            none, whole, whole, whole, (0, 1, 2), kept, grad, False, 2, True
        )
        part = tick(part, running)
        if index == 0:
            running.append(r_attn)
        g_parts.append(exchange(part, piece.group, cols))
    g_heads = [
        jnp.concatenate([p[:, i].reshape(heads, dim, -1) for p in g_parts], 2) for i in range(3)
    ]
    g_raw_q, g_q_gain = query_pull(g_heads[0].astype(F32))
    g_raw_k, g_k_gain = key_pull(g_heads[1].astype(F32))
    g_triple = [
        g.reshape(depth, tokens) for g in (g_raw_q.astype(BF), g_raw_k.astype(BF), g_heads[2])
    ]
    g_triple = tick(g_triple, running)
    r_self = [
        Reduction(core, normed_one, g_triple[:2], True),
        Reduction(core, normed_one, g_triple[2:], False),
    ]
    g_normed = rebuild(weights_one, [0, 1, 2], g_triple, F32)
    g_normed = tick(g_normed, running)
    running += r_self
    crossed = g_normed * normal_one
    sums = jnp.stack(
        [
            jnp.stack([jnp.sum(cut(g_normed, i), 1), jnp.sum(cut(crossed, i), 1)], 0)
            for i in range(len(pieces))
        ],
        0,
    )
    which = jnp.stack(
        [jnp.where(jnp.arange(sequences) == p.sequence, 1.0, 0.0) for p in pieces], 0
    )
    g_modul = jnp.sum(which[:, :, None, None] * sums[:, None], 0)
    g_modul = g_modul.reshape(sequences, 2, cols, width).transpose(2, 0, 1, 3)
    g_modul = jnp.sum(lax.all_to_all(g_modul, "col", 0, 0, tiled=True), 0).astype(BF)
    g_modul = shared(g_modul, "row").reshape(-1, 2, width)
    g_modulation = einsum("sd,ske->dke", embed_rows, g_modul)
    g_stream = g_stream + norm_back(g_normed * scaling, normal_one, inverse_one)

    g_skip_gain = jnp.sum(g_stream * skip_normal, 1)
    g_skip_bias = jnp.sum(g_stream, 1)
    g_joined = norm_back(g_stream * gain_skip, skip_normal, skip_inverse).astype(BF)
    g_joined = tick(g_joined, running)
    r_skip = Reduction(core, both, [g_joined], True)
    g_both = rebuild_blocks(base, w_skip, width, g_joined)
    g_both = to_features(g_both, pieces, cols).reshape(split[0], 2, block_rows, row_tokens)
    g_latents, g_skip = (g_both[:, i].reshape(width, row_tokens).astype(F32) for i in range(2))

    g_gains = jnp.stack(
        [g_skip_gain, g_skip_bias, g_cross_gain, g_cross_bias, g_hidden_gain, g_hidden_bias], 0
    )
    g_gains = g_gains.reshape(6, cols, width).transpose(1, 0, 2)
    g_head = jnp.stack([g_q_gain, g_k_gain, g_cq_gain, g_tk_gain], 0).reshape(1, -1, width)
    packed = jnp.concatenate([g_gains, jnp.broadcast_to(g_head, (cols, *g_head.shape[1:]))], 1)
    packed = jnp.sum(lax.all_to_all(packed, "col", 0, 0, tiled=True), 0)
    packed = jnp.sum(shared(packed, "row"), 0)
    g_gains = packed[:6]
    g_head = packed[6:].reshape(4, dim)
    return (
        result,
        g_latents,
        g_skip,
        r_skip.result().reshape(2, block_rows, width),
        g_modulation,
        jnp.concatenate([r.result() for r in r_self], 0).transpose(1, 0, 2),
        r_attn.result()[0].T,
        r_query.result()[0],
        r_text.result().transpose(1, 0, 2),
        r_cross.result()[0].T,
        g_hidden[0],
        g_hidden[1].T,
        *[g_gains[i] for i in range(6)],
        *[g_head[i] for i in range(4)],
    )


def solution(mesh):
    return jax.shard_map(
        shards,
        mesh=mesh,
        in_specs=(
            P("col", "row"),
            P("col", "row"),
            P("row", "col"),
            P("row", None, "col"),
            P("row"),
            P(None, "row"),
            P("col", "row"),
            P(None, "row", "col"),
            P("row", None, "col"),
            P("row", None, "col"),
            P("col", "row"),
            P("row", "col"),
            P("row", None, "col"),
            P("col", "row"),
            P("row", "col"),
            P("col", "row"),
            P("col"),
            P("col"),
            P("col"),
            P("col"),
            P("col"),
            P("col"),
            P(),
            P(),
            P(),
            P(),
        ),
        out_specs=(
            P("col", "row"),
            P("col", "row"),
            P("col", "row"),
            P(None, "row", "col"),
            P("row", None, "col"),
            P("row", None, "col"),
            P("col", "row"),
            P("row", "col"),
            P("row", None, "col"),
            P("col", "row"),
            P("row", "col"),
            P("col", "row"),
            P("col"),
            P("col"),
            P("col"),
            P("col"),
            P("col"),
            P("col"),
            P(),
            P(),
            P(),
            P(),
        ),
        check_vma=False,
    )
```

```python
from functools import partial
import math

import jax
import jax.numpy as jnp
from jax import lax
from jax.experimental import pallas as pl
from jax.experimental.pallas import tpu as pltpu
from jax.sharding import PartitionSpec as P

L = 1024
EPSILON = 1e-06
BF = jnp.bfloat16
F32 = jnp.float32
KEYPAD = 128
DEVICES = ("col", "row")
LOG2E = math.log2(math.e)
VMEM = 60 << 20


def einsum(spec, left, right):
    return jnp.einsum(spec, left, right, preferred_element_type=F32)


def dot(left, right, dims):
    return lax.dot_general(left, right, (dims, ((), ())), preferred_element_type=F32)


def params():
    return pltpu.CompilerParams(vmem_limit_bytes=VMEM)


def step_of(count):
    return 256 if count % 256 == 0 else count


def wide(ref, head):
    parts = [ref[s, 0, head] for s in range(ref.shape[0])]
    return parts[0] if len(parts) == 1 else jnp.concatenate(parts, 1)


def valid_keys(length_ref, keys, step):
    return lax.broadcasted_iota(jnp.int32, (keys, step), 0) < length_ref[0]


def attend_kernel(masked, length_ref, q_ref, k_ref, v_ref, o_ref, r_ref, l_ref):
    groups, _, heads, dim, count = q_ref.shape
    step = step_of(count)
    factor = dim ** (-0.5) * LOG2E
    for head in range(heads):
        key = wide(k_ref, head).T
        value = wide(v_ref, head)
        keys = key.shape[0]
        value = jnp.concatenate([value, jnp.ones((8, keys), BF)], 0)
        for place in range(0, groups * count, step):
            group, first = divmod(place, count)
            query = q_ref[group, 0, head, :, first : first + step]
            expo = jnp.exp2(dot(key, query, ((1,), (0,))) * factor)
            if masked:
                expo = jnp.where(valid_keys(length_ref, keys, step), expo, 0.0)
            both = dot(value, expo.astype(BF), ((1,), (0,)))
            total = both[dim : dim + 1]
            mixed = both[:dim] * (1.0 / total)
            high = mixed.astype(BF)
            o_ref[group, head, :, first : first + step] = high
            r_ref[group, head, :, first : first + step] = (mixed - high.astype(F32)).astype(BF)
            l_ref[head, :, place : place + step] = jnp.log2(total)


def attend_back_kernel(
    masked, length_ref, q_ref, k_ref, v_ref, m_ref, r_ref, g_ref, l_ref, *outs
):
    groups, _, heads, dim, count = q_ref.shape
    step = step_of(count)
    scale = dim ** (-0.5)
    for head in range(heads):
        key = wide(k_ref, head)
        keys = key.shape[1]
        turned = key.T
        value = jnp.concatenate([wide(v_ref, head), jnp.ones((8, keys), BF)], 0).T
        g_key = g_value = None
        for place in range(0, groups * count, step):
            group, first = divmod(place, count)
            here = slice(first, first + step)
            query = q_ref[group, 0, head, :, here]
            grad = g_ref[group, head, :, here]
            mixed = m_ref[group, head, :, here].astype(F32)
            mixed = mixed + r_ref[group, head, :, here].astype(F32)
            delta = -jnp.sum(grad.astype(F32) * mixed, 0, keepdims=True)
            high = delta.astype(BF)
            rest = (delta - high.astype(F32)).astype(BF)
            more = jnp.concatenate([grad, high, rest, jnp.zeros((6, step), BF)], 0)
            probs = jnp.exp2(
                dot(turned, query, ((1,), (0,))) * (scale * LOG2E)
                - l_ref[head, :, place : place + step]
            )
            if masked:
                probs = jnp.where(valid_keys(length_ref, keys, step), probs, 0.0)
            product = (probs * dot(value, more, ((1,), (0,)))).astype(BF)
            g_query = dot(key, product, ((1,), (0,))) * scale
            part_value = dot(grad, probs.astype(BF), ((1,), (1,)))
            part_key = dot(query, product, ((1,), (1,)))
            g_value = part_value if g_value is None else g_value + part_value
            g_key = part_key if g_key is None else g_key + part_key
            outs[0][group, 0, head, :, here] = g_query.astype(outs[0].dtype)
        g_key = g_key * scale
        if len(outs) == 1:
            for group in range(groups):
                here = slice(group * count, (group + 1) * count)
                outs[0][group, 1, head] = g_key[:, here].astype(BF)
                outs[0][group, 2, head] = g_value[:, here].astype(BF)
        else:
            outs[1][0, 0, head] = g_key
            outs[2][0, 0, head] = g_value


def costs(heads, queries, keys, dim, products):
    return pl.CostEstimate(
        flops=2 * products * heads * queries * keys * 256,
        transcendentals=heads * queries * keys,
        bytes_accessed=2 * products * heads * dim * (queries + keys),
    )


def head_block(shape, count, kind=0):
    groups, _, _, dim, tokens = shape
    return pl.BlockSpec((groups, 1, count, dim, tokens), lambda h: (0, kind, h, 0, 0))


def mix_block(shape, count):
    groups, _, _, dim, tokens = shape
    return pl.BlockSpec((groups, count, dim, tokens), lambda h: (0, h, 0, 0))


def attend(length, query, key, value, kinds, masked, most):
    groups, _, heads, dim, count = query.shape
    many = math.gcd(heads, most)
    total = groups * count
    keys = key.shape[0] * key.shape[4]
    return pl.pallas_call(
        partial(attend_kernel, masked),
        grid=(heads // many,),
        in_specs=[pl.BlockSpec(memory_space=pltpu.SMEM)]
        + [head_block(a.shape, many, kind) for a, kind in zip((query, key, value), kinds)],
        out_specs=[
            mix_block(query.shape, many),
            mix_block(query.shape, many),
            pl.BlockSpec((many, 1, total), lambda h: (h, 0, 0)),
        ],
        out_shape=[
            jax.ShapeDtypeStruct((groups, heads, dim, count), BF),
            jax.ShapeDtypeStruct((groups, heads, dim, count), BF),
            jax.ShapeDtypeStruct((heads, 1, total), F32),
        ],
        cost_estimate=costs(heads, total, keys, dim, 2),
        compiler_params=params(),
        name="attend",
    )(length, query, key, value)


def attend_back(length, query, key, value, kinds, kept, grad, masked, most, stacked):
    mixed, rest, logs = kept
    groups, _, heads, dim, count = query.shape
    many = math.gcd(heads, most)
    total = groups * count
    keys = key.shape[0] * key.shape[4]
    if stacked:
        out_specs = pl.BlockSpec((groups, 3, many, dim, count), lambda h: (0, 0, h, 0, 0))
        out_shape = jax.ShapeDtypeStruct((groups, 3, heads, dim, count), BF)
    else:
        out_specs = [head_block(a.shape, many) for a in (query, key, value)]
        out_shape = [jax.ShapeDtypeStruct(a.shape, F32) for a in (query, key, value)]
    return pl.pallas_call(
        partial(attend_back_kernel, masked),
        grid=(heads // many,),
        in_specs=[pl.BlockSpec(memory_space=pltpu.SMEM)]
        + [head_block(a.shape, many, kind) for a, kind in zip((query, key, value), kinds)]
        + [mix_block(query.shape, many)] * 3
        + [pl.BlockSpec((many, 1, total), lambda h: (h, 0, 0))],
        out_specs=out_specs,
        out_shape=out_shape,
        cost_estimate=costs(heads, total, keys, dim, 5),
        compiler_params=params(),
        name="attend_back",
    )(length, query, key, value, mixed, rest, grad, logs)


def work(rows, depth, tokens, moved):
    return pl.CostEstimate(
        flops=2 * rows * depth * tokens,
        transcendentals=0,
        bytes_accessed=moved,
    )


def lanes(width):
    return -(-width // 128) * 128


def full(shape):
    return pl.BlockSpec(shape, lambda *_: (0,) * len(shape))


def project(weight, kinds, values, dtypes, joined=False):
    _, cols, depth, width = weight.shape
    tokens = values[0].shape[1]
    outs = 1 if joined else len(kinds)

    def kernel(*refs):
        blocks = refs[: len(kinds)]
        given = refs[len(kinds) : -outs]
        total = None
        for index, block in enumerate(blocks):
            part = dot(block[0, 0], given[index % len(given)][...], ((0,), (0,)))
            if not joined:
                refs[index - outs][...] = part.astype(dtypes[index])
            total = part if total is None else total + part
        if joined:
            refs[-1][...] = total.astype(dtypes[0])

    return pl.pallas_call(
        kernel,
        grid=(cols,),
        in_specs=[
            pl.BlockSpec((1, 1, depth, width), partial(lambda k, c: (k, c, 0, 0), kind))
            for kind in kinds
        ]
        + [full(v.shape) for v in values],
        out_specs=[pl.BlockSpec((width, tokens), lambda c: (c, 0))] * outs,
        out_shape=[jax.ShapeDtypeStruct((cols * width, tokens), dtypes[i]) for i in range(outs)],
        cost_estimate=work(len(kinds) * cols * width, depth, tokens, 8 * depth * tokens),
        compiler_params=params(),
        name="project",
    )(*([weight] * len(kinds)), *values)


def rebuild(weight, kinds, values, dtype):
    _, cols, depth, width = weight.shape
    tokens = values[0].shape[1]
    tile = depth // 4

    def kernel(*refs):
        total = None
        for block, given in zip(refs[: len(kinds)], refs[len(kinds) : -1]):
            for col in range(cols):
                part = dot(block[0, col], given[col * width : (col + 1) * width, :], ((1,), (0,)))
                total = part if total is None else total + part
        refs[-1][...] = total.astype(dtype)

    return pl.pallas_call(
        kernel,
        grid=(4,),
        in_specs=[
            pl.BlockSpec((1, cols, tile, width), partial(lambda k, j: (k, 0, j, 0), kind))
            for kind in kinds
        ]
        + [full(v.shape) for v in values],
        out_specs=pl.BlockSpec((tile, tokens), lambda j: (j, 0)),
        out_shape=jax.ShapeDtypeStruct((depth, tokens), dtype),
        cost_estimate=work(depth, len(kinds) * cols * width, tokens, 8 * depth * tokens),
        compiler_params=params(),
        name="rebuild",
    )(*([weight] * len(kinds)), *values)


def project_blocks(base, blocks, width, values):
    many = len(blocks)
    depth, broad = blocks[0].shape
    tokens = values.shape[1]
    tile = depth // 4

    def kernel(base_ref, *refs):
        values_ref, out_ref = refs[many:]

        @pl.when(pl.program_id(0) == 0)
        def _():
            out_ref[...] = jnp.zeros_like(out_ref)

        for index in range(many):
            here = pl.ds(pl.multiple_of((index ^ base_ref[0]) * width, width), width)
            out_ref[here, :] += dot(refs[index][...], values_ref[...], ((0,), (0,)))[:width]

    return pl.pallas_call(
        kernel,
        grid_spec=pltpu.PrefetchScalarGridSpec(
            num_scalar_prefetch=1,
            grid=(4,),
            in_specs=[pl.BlockSpec((tile, broad), lambda j, b: (j, 0))] * many
            + [pl.BlockSpec((tile, tokens), lambda j, b: (j, 0))],
            out_specs=pl.BlockSpec((many * width, tokens), lambda j, b: (0, 0)),
        ),
        out_shape=jax.ShapeDtypeStruct((many * width, tokens), F32),
        cost_estimate=work(many * width, depth, tokens, 4 * depth * tokens),
        compiler_params=params(),
        name="project_blocks",
    )(base, *blocks, values)


def rebuild_blocks(base, blocks, width, values):
    many = len(blocks)
    depth, broad = blocks[0].shape
    tokens = values.shape[1]
    tile = depth // 4

    def kernel(base_ref, *refs):
        values_ref, out_ref = refs[many:]
        total = None
        for index in range(many):
            here = pl.ds(pl.multiple_of((index ^ base_ref[0]) * width, width), width)
            part = dot(refs[index][:, :width], values_ref[here, :], ((1,), (0,)))
            total = part if total is None else total + part
        out_ref[...] = total.astype(BF)

    return pl.pallas_call(
        kernel,
        grid_spec=pltpu.PrefetchScalarGridSpec(
            num_scalar_prefetch=1,
            grid=(4,),
            in_specs=[pl.BlockSpec((tile, broad), lambda j, b: (j, 0))] * many
            + [pl.BlockSpec(values.shape, lambda j, b: (0, 0))],
            out_specs=pl.BlockSpec((tile, tokens), lambda j, b: (j, 0)),
        ),
        out_shape=jax.ShapeDtypeStruct((depth, tokens), BF),
        cost_estimate=work(many * width, depth, tokens, 4 * depth * tokens),
        compiler_params=params(),
        name="rebuild_blocks",
    )(base, *blocks, values)


def outer(core, left, rights, flip):
    rows, tokens = left.shape
    cols = lax.axis_size("col")
    width = rights[0].shape[0] // cols
    broad = lanes(width)

    def kernel(core_ref, left_ref, *refs):
        for index in range(len(rights)):
            right = refs[index][...]
            if broad > width:
                right = jnp.concatenate([right, jnp.zeros((broad - width, tokens), BF)], 0)
            part = dot(left_ref[...], right, ((1,), (1,)))
            refs[-1][index, 0] = part.astype(BF)

    return pl.pallas_call(
        kernel,
        grid_spec=pltpu.PrefetchScalarGridSpec(
            num_scalar_prefetch=1,
            grid=(cols // 2,),
            in_specs=[pl.BlockSpec((rows, tokens), lambda y, core: (0, 0))]
            + [
                pl.BlockSpec((width, tokens), lambda y, core: (2 * y + (core[0] ^ flip), 0))
                for _ in rights
            ],
            out_specs=pl.BlockSpec(
                (len(rights), 1, rows, broad), lambda y, core: (0, y, 0, 0)
            ),
        ),
        out_shape=jax.ShapeDtypeStruct((len(rights), cols // 2, rows, broad), BF),
        cost_estimate=work(
            rows, tokens, len(rights) * cols // 2 * width, 3 * rows * cols * width * len(rights)
        ),
        compiler_params=params(),
        name="outer",
    )(core, left, *rights)


def expand(weight, kind, values):
    _, many, depth, hidden = weight.shape
    tokens = values.shape[1]
    tile = 384 if hidden % 384 == 0 else hidden
    slope = 0.79788456
    cubic = 0.044715

    def kernel(weight_ref, values_ref, act_ref, slope_ref):
        for index in range(many):
            inner = dot(weight_ref[0, index], values_ref[...], ((0,), (0,)))
            square = inner * inner
            bent = jnp.tanh(inner * (slope + slope * cubic * square))
            half = 0.5 + 0.5 * bent
            act_ref[index] = (inner * half).astype(BF)
            rise = slope + 3.0 * slope * cubic * square
            slope_ref[index] = (half + 0.5 * inner * (1.0 - bent * bent) * rise).astype(BF)

    return pl.pallas_call(
        kernel,
        grid=(hidden // tile,),
        in_specs=[
            pl.BlockSpec((1, many, depth, tile), lambda j: (kind, 0, 0, j)),
            full(values.shape),
        ],
        out_specs=[pl.BlockSpec((many, tile, tokens), lambda j: (0, j, 0))] * 2,
        out_shape=[jax.ShapeDtypeStruct((many, hidden, tokens), BF)] * 2,
        cost_estimate=work(many * hidden, depth, tokens, 3 * many * hidden * depth),
        compiler_params=params(),
        name="expand",
    )(weight, values)


def expand_back(weight, kind, values, slopes):
    _, many, depth, hidden = weight.shape
    tokens = values.shape[1]
    tile = 384 if hidden % 384 == 0 else hidden

    def kernel(weight_ref, values_ref, slope_ref, out_ref):
        for index in range(many):
            part = dot(weight_ref[0, index], values_ref[...], ((0,), (0,)))
            out_ref[index] = (part * slope_ref[index].astype(F32)).astype(BF)

    return pl.pallas_call(
        kernel,
        grid=(hidden // tile,),
        in_specs=[
            pl.BlockSpec((1, many, depth, tile), lambda j: (kind, 0, 0, j)),
            full(values.shape),
            pl.BlockSpec((many, tile, tokens), lambda j: (0, j, 0)),
        ],
        out_specs=pl.BlockSpec((many, tile, tokens), lambda j: (0, j, 0)),
        out_shape=jax.ShapeDtypeStruct((many, hidden, tokens), BF),
        cost_estimate=work(many * hidden, depth, tokens, 3 * many * hidden * depth),
        compiler_params=params(),
        name="expand_back",
    )(weight, values, slopes)


def contract(weight, kind, values, added, dtype):
    _, many, depth, hidden = weight.shape
    tokens = values.shape[2]
    tile = depth // 4
    extra = [] if added is None else [added]

    def kernel(weight_ref, values_ref, *refs):
        total = refs[0][...] if extra else None
        for index in range(many):
            part = dot(weight_ref[0, index], values_ref[index], ((1,), (0,)))
            total = part if total is None else total + part
        refs[-1][...] = total.astype(dtype)

    line = pl.BlockSpec((tile, tokens), lambda j: (j, 0))
    return pl.pallas_call(
        kernel,
        grid=(4,),
        in_specs=[
            pl.BlockSpec((1, many, tile, hidden), lambda j: (kind, 0, j, 0)),
            full(values.shape),
        ]
        + [line] * len(extra),
        out_specs=line,
        out_shape=jax.ShapeDtypeStruct((depth, tokens), dtype),
        cost_estimate=work(depth, many * hidden, tokens, 3 * many * hidden * depth),
        compiler_params=params(),
        name="contract",
    )(weight, values, *extra)


def hidden_outer(grad_out, act, normed, grad_inner):
    many, hidden, tokens = act.shape
    depth = grad_out.shape[0]
    parts = 2 if hidden % 256 == 0 else 1
    tile = hidden // parts

    def kernel(out_ref, act_ref, normed_ref, inner_ref, grad_ref):
        kind = pl.program_id(0)

        @pl.when(kind == 0)
        def _():
            grad_ref[0, 0] = dot(normed_ref[...], inner_ref[0], ((1,), (1,))).astype(BF)

        @pl.when(kind == 1)
        def _():
            grad_ref[0, 0] = dot(out_ref[...], act_ref[0], ((1,), (1,))).astype(BF)

    return pl.pallas_call(
        kernel,
        grid=(2, many, parts),
        in_specs=[
            pl.BlockSpec((depth, tokens), lambda s, p, j: (0, 0)),
            pl.BlockSpec((1, tile, tokens), lambda s, p, j: (s * p, s * j, 0)),
            pl.BlockSpec((depth, tokens), lambda s, p, j: (0, 0)),
            pl.BlockSpec(
                (1, tile, tokens),
                lambda s, p, j: (p + s * (many - 1 - p), j + s * (parts - 1 - j), 0),
            ),
        ],
        out_specs=pl.BlockSpec((1, 1, depth, tile), lambda s, p, j: (s, p, 0, j)),
        out_shape=jax.ShapeDtypeStruct((2, many, depth, hidden), BF),
        cost_estimate=work(2 * depth, tokens, many * hidden, 5 * many * depth * hidden),
        compiler_params=params(),
        name="hidden_outer",
    )(grad_out, act, normed, grad_inner)


def assemble(place, own, got, middle=None):
    rows, width = own.shape[-2:]

    def kernel(place_ref, own_ref, got_ref, out_ref):
        @pl.when(pl.program_id(0) == place_ref[1])
        def _():
            out_ref[0, 0] = own_ref[...].reshape(rows, width)

        @pl.when(pl.program_id(0) != place_ref[1])
        def _():
            out_ref[0, 0] = got_ref[...].reshape(rows, width)

    def spec(ours):
        def index(x, z, place):
            phase = place[1] if ours else 1 - place[1]
            inside = (x == phase).astype(jnp.int32)
            level = (inside * z + (1 - inside) * 3 * (1 - phase)) ^ place[0]
            return (level, 0, 0) if middle is None else (level, middle, 0, 0)

        shape = (1, rows, width) if middle is None else (1, 1, rows, width)
        return pl.BlockSpec(shape, index)

    return pl.pallas_call(
        kernel,
        grid_spec=pltpu.PrefetchScalarGridSpec(
            num_scalar_prefetch=1,
            grid=(2, 4),
            in_specs=[spec(True), spec(False)],
            out_specs=pl.BlockSpec((1, 1, rows, width), lambda x, z, place: (z, x, 0, 0)),
        ),
        out_shape=jax.ShapeDtypeStruct((4, 2, rows, width), BF),
        cost_estimate=work(1, 1, 1, 32 * rows * width),
        name="assemble",
    )(place, own, got).reshape(8 * rows, width)


def normalize(values):
    average = jnp.mean(values, 0, keepdims=True)
    centred = values - average
    inverse = lax.rsqrt(jnp.mean(centred * centred, 0, keepdims=True) + EPSILON)
    return centred * inverse, inverse


def norm_back(grad, normal, inverse):
    average = jnp.mean(grad, 0, keepdims=True)
    crossed = jnp.mean(grad * normal, 0, keepdims=True)
    return inverse * (grad - average - normal * crossed)


def head_norm(values, gain):
    average = jnp.mean(values, 1, keepdims=True)
    centred = values - average
    variance = jnp.mean(centred * centred, 1, keepdims=True)
    return centred * lax.rsqrt(variance + EPSILON) * gain[None, :, None]


def rope_tables(places, head_dim):
    quarter = head_dim // 4
    freqs = jnp.exp(jnp.arange(quarter, dtype=F32) * (-4.0 * math.log(10000.0) / head_dim))
    rows = freqs[:, None] * places[0].astype(F32)[None, :]
    cols = freqs[:, None] * places[1].astype(F32)[None, :]
    angles = jnp.concatenate([rows, rows, cols, cols], 0)
    return jnp.cos(angles), jnp.sin(angles)


def rotate(values):
    quarter = values.shape[1] // 4
    one, two, three, four = (values[:, i * quarter : (i + 1) * quarter] for i in range(4))
    return jnp.concatenate([-two, one, -four, three], 1)


class Piece:
    def __init__(self, start, count, group, sequence):
        self.start = start
        self.count = count
        self.group = group
        self.sequence = sequence


def pieces_of(cols, sequences):
    mine = lax.axis_index("col")
    if cols == 4 and sequences == 3:
        return [
            Piece(0, L // 2, 2, mine // 2),
            Piece(2 * L, L // 4, 4, jnp.int32(2)),
        ]
    return [Piece(s * L, L // cols, cols, jnp.int32(s)) for s in range(sequences)]


def groups_of(size, cols):
    return [list(range(i, i + size)) for i in range(0, cols, size)]


def exchange(values, size, cols):
    if size == cols:
        return lax.all_to_all(values, "col", 0, 0, tiled=True)
    return lax.all_to_all(
        values, "col", 0, 0, tiled=True, axis_index_groups=groups_of(size, cols)
    )


def to_tokens(values, pieces, cols):
    parts = [
        jnp.concatenate(
            [values[:, p.start + j * p.count : p.start + (j + 1) * p.count] for p in pieces], 1
        )
        for j in range(cols)
    ]
    got = exchange(jnp.stack(parts, 0), cols, cols)
    return got.reshape(-1, got.shape[2])


def to_features(values, pieces, cols):
    got = exchange(values.reshape(cols, -1, values.shape[1]), cols, cols)
    parts = []
    at = 0
    for piece in pieces:
        parts += [got[j, :, at : at + piece.count] for j in range(cols)]
        at += piece.count
    return jnp.concatenate(parts, 1)


def shared(values, axis):
    size = lax.axis_size(axis)
    return lax.all_to_all(
        jnp.broadcast_to(values[None], (size, *values.shape)), axis, 0, 0, tiled=True
    )


def swap(values, axis, bit):
    size = lax.axis_size(axis)
    return lax.ppermute(values, axis, [(i, i ^ bit) for i in range(size)])


def custom_mesh():
    return (lax.axis_size("row"), lax.axis_size("col")) == (8, 4)


def gather_weights(blocks):
    cols = lax.axis_size("col")
    most = max(block.shape[0] for block in blocks)
    padded = [jnp.pad(b, ((0, most - b.shape[0]), (0, 0))) for b in blocks]
    whole = lax.all_gather(jnp.stack(padded, 0), DEVICES, axis=1, tiled=True)
    return whole.reshape(len(blocks), cols, -1, blocks[0].shape[1])


class Gathering:
    last = 4

    def __init__(self, block, up, place):
        self.up = up
        self.place = place
        self.stage = 0
        self.state = [block]
        if not custom_mesh():
            cols = lax.axis_size("col")
            whole = lax.all_gather(block, DEVICES, axis=0, tiled=True)
            self.state = list(whole.reshape(cols, -1, block.shape[1]))
            self.stage = self.last

    def levels(self, block):
        return [block] + [swap(block, "row", 2 * level) for level in (1, 2, 3)]

    def advance(self):
        state = self.state
        self.stage += 1
        if self.stage == 1:
            self.state = [state[0], swap(state[0], "col", 2)] if self.up else self.levels(state[0])
        elif self.stage == 2:
            stack = jnp.stack(state, 0)
            self.state = self.levels(stack) if self.up else [stack, swap(stack, "col", 2)]
        elif self.stage == 3 and self.up:
            stack = jnp.stack(state, 0)
            self.state = [stack, swap(stack, "row", 1)]
        elif self.stage == 3:
            self.state = state + [swap(a, "row", 1) for a in state]
        else:
            if self.up:
                mine, other = (assemble(self.place, *state, k) for k in (0, 1))
            else:
                mine = assemble(self.place, state[0], state[2])
                other = assemble(self.place, state[1], state[3])
            self.state = [mine, swap(mine, "col", 1), other, swap(other, "col", 1)]

    def result(self):
        while self.stage < self.last:
            self.advance()
        return self.state


def pick(values, axis, index):
    return lax.dynamic_index_in_dim(values, index, axis, False)


def add(left, right):
    return (left.astype(F32) + right.astype(F32)).astype(BF)


class Reduction:
    last = 4

    def __init__(self, core, left, rights, across):
        self.across = across
        self.many = len(rights)
        self.stage = 0 if custom_mesh() else self.last
        if not custom_mesh():
            cols = lax.axis_size("col")
            whole = jnp.stack(
                [einsum("kt,cnt->ckn", left, r.reshape(cols, -1, r.shape[1])) for r in rights], 0
            )
            flat = whole.reshape(self.many, -1, whole.shape[3]).astype(BF)
            self.state = [lax.psum_scatter(flat, DEVICES, scatter_dimension=1, tiled=True)]
            return
        self.width = rights[0].shape[0] // 4
        shape = (self.many, 2, 4, 2, left.shape[0] // 8, lanes(self.width))
        send = outer(core, left, rights, 1)
        got = swap(send, "col", 1)
        keep = outer(core, left, rights, 0)
        self.state = [keep.reshape(shape), got.reshape(shape)]

    def half(self, side):
        kept, got = self.state
        axis = (3 if kept.ndim == 6 else 2) if side else 1
        name, bit = ("row", 1) if side else ("col", 2)
        index = lax.axis_index("row") % 2 if side else lax.axis_index("col") // 2
        away = add(pick(kept, axis, 1 - index), pick(got, axis, 1 - index))
        here = add(pick(kept, axis, index), pick(got, axis, index))
        self.state = [here, swap(away, name, bit)]

    def advance(self):
        self.stage += 1
        if self.stage <= 2:
            self.half(self.across == (self.stage == 1))
        elif self.stage == 3:
            level = lax.axis_index("row") // 2
            total = add(*self.state)
            self.state = [pick(total, 1, level)] + [
                swap(pick(total, 1, level ^ other), "row", 2 * other) for other in (1, 2, 3)
            ]
        else:
            total = self.state[0].astype(F32)
            for other in self.state[1:]:
                total = total + other.astype(F32)
            self.state = [total[..., : self.width]]

    def result(self):
        while self.stage < self.last:
            self.advance()
        return self.state[0].astype(F32)


def tick(values, running):
    active = [r for r in running if r.stage < r.last]
    if active:
        values, states = lax.optimization_barrier((values, [r.state for r in active]))
        for beside, state in zip(active, states):
            beside.state = state
            beside.advance()
    return values


def after(values, done):
    return lax.optimization_barrier((values, done))[0]


def shards(
    latents,
    skip_input,
    condition,
    text_states,
    text_lengths,
    positions,
    out_grad,
    skip_weight,
    modulation,
    self_inputs,
    self_output,
    cross_query,
    cross_keyvalue,
    cross_output,
    expand_weight,
    reduce_weight,
    skip_gain,
    skip_bias,
    cross_gain,
    cross_bias,
    hidden_gain,
    hidden_bias,
    query_gain,
    key_gain,
    cross_query_gain,
    text_key_gain,
):
    cols = lax.axis_size("col")
    rows = lax.axis_size("row")
    mine = lax.axis_index("col")
    my_row = lax.axis_index("row")
    width, row_tokens = latents.shape
    depth = width * cols
    dim = query_gain.shape[0]
    heads = depth // dim
    sequences = row_tokens // L
    tokens = row_tokens // cols
    texts = text_states.shape[1]
    keys = -(-texts // KEYPAD) * KEYPAD
    pieces = pieces_of(cols, sequences)
    starts = [sum(p.count for p in pieces[:i]) for i in range(len(pieces))]
    core = (mine % 2).astype(jnp.int32)[None]
    place = jnp.stack([my_row // 2, my_row % 2]).astype(jnp.int32)
    base = (mine if custom_mesh() else jnp.zeros_like(mine)).astype(jnp.int32)[None]

    def cut(values, index):
        return values[..., starts[index] : starts[index] + pieces[index].count]

    block_rows = depth // rows
    split = (width // block_rows, block_rows, row_tokens)
    both = jnp.stack([latents.reshape(split), skip_input.reshape(split)], 1)
    both = to_tokens(both.reshape(2 * width, row_tokens), pieces, cols)

    weights_one = gather_weights([*(self_inputs[:, i] for i in range(3)), self_output.T])
    weights_two = gather_weights(
        [cross_query, cross_output.T, cross_keyvalue[:, 0], cross_keyvalue[:, 1]]
    )
    skip_block = jnp.concatenate([skip_weight[0], skip_weight[1]], 0)
    skip_block = jnp.pad(skip_block, ((0, 0), (0, lanes(width) - width)))
    w_skip = Gathering(skip_block, False, place).result()
    weights_hidden = gather_weights([expand_weight, reduce_weight.T])

    places = jnp.concatenate(
        [
            lax.dynamic_slice_in_dim(positions, p.start + mine * p.count, p.count, 1)
            for p in pieces
        ],
        1,
    )

    embed = jax.nn.silu(after(condition, both).astype(F32)).astype(BF)
    embed = shared(embed, "row").reshape(-1, width)
    embed = shared(embed, "col").transpose(1, 0, 2).reshape(-1, depth)
    embed_rows = lax.dynamic_slice_in_dim(embed, my_row * block_rows, block_rows, 1)
    modul = einsum("sd,dke->ske", embed_rows, modulation).reshape(rows, sequences, 2, width)
    modul = jnp.sum(lax.all_to_all(modul, "row", 0, 0, tiled=True), 0)
    gains = jnp.stack(
        [skip_gain, skip_bias, cross_gain, cross_bias, hidden_gain, hidden_bias], 0
    )
    table = jnp.concatenate([gains, modul.reshape(-1, width)], 0)
    table = shared(table, "col").transpose(1, 0, 2).reshape(-1, depth)
    modul = table[6:].reshape(sequences, 2, depth)
    chosen = [lax.dynamic_index_in_dim(modul, p.sequence, 0, False) for p in pieces]
    columns = lax.optimization_barrier(jnp.concatenate([table[:6], *chosen], 0)).T
    gain_skip, bias_skip, gain_cross, bias_cross, gain_hidden, bias_hidden = (
        columns[:, i : i + 1] for i in range(6)
    )
    token_index = lax.broadcasted_iota(jnp.int32, (1, tokens), 1)

    def per_token(which):
        result = columns[:, 6 + which : 7 + which]
        for index in range(1, len(pieces)):
            column = columns[:, 6 + 2 * index + which : 7 + 2 * index + which]
            result = jnp.where(token_index >= starts[index], column, result)
        return jnp.broadcast_to(result, (depth, tokens))

    shifting = per_token(0)
    scaling = 1.0 + per_token(1)

    joined = project_blocks(base, w_skip, width, both)
    skip_normal, skip_inverse = normalize(joined)
    stream = skip_normal * gain_skip + bias_skip
    normal_one, inverse_one = normalize(stream)
    normed_one = (normal_one * scaling + shifting).astype(BF)
    raw = project(weights_one, [0, 1, 2], [normed_one], [F32, F32, BF])
    raw = [r.reshape(heads, dim, tokens) for r in raw]
    cosine, sine = rope_tables(places, dim)

    def self_piece(value, gain):
        normal = head_norm(value, gain)
        return normal * cosine[None] + rotate(normal) * sine[None]

    rot_query, query_pull = jax.vjp(self_piece, raw[0], query_gain)
    rot_key, key_pull = jax.vjp(self_piece, raw[1], key_gain)
    triple = [rot_query.astype(BF), rot_key.astype(BF), raw[2]]

    text = shared(jnp.pad(after(text_states, raw), ((0, 0), (0, keys - texts), (0, 0))), "col")

    def to_heads(parts, index):
        size = pieces[index].group
        split = [cut(p, index).reshape(size, heads // size, dim, -1) for p in parts]
        return exchange(jnp.stack(split, 1), size, cols)

    none = jnp.zeros((1,), jnp.int32)
    saved_self = []
    mixed_parts = []
    for index, piece in enumerate(pieces):
        whole = to_heads(triple, index)
        kept = attend(none, whole, whole, whole, (0, 1, 2), False, 2)
        saved_self.append((whole, kept))
        mixed_parts.append(exchange(kept[0], piece.group, cols).reshape(depth, -1))
    mixed_one = jnp.concatenate(mixed_parts, 1)
    mixed_one, text = lax.optimization_barrier((mixed_one, text))
    stream = stream + rebuild(weights_one, [3], [mixed_one], F32)
    normal_two, inverse_two = normalize(stream)
    normed_two = (normal_two * gain_cross + bias_cross).astype(BF)
    raw_cross = project(weights_two, [0], [normed_two], [F32])[0].reshape(heads, dim, tokens)
    norm_query, cross_pull = jax.vjp(head_norm, raw_cross, cross_query_gain)
    text = jnp.concatenate(
        [lax.dynamic_index_in_dim(text, p.sequence, 1, False) for p in pieces], 1
    )
    text = text.transpose(0, 2, 1).reshape(-1, len(pieces) * keys)
    text_rows = text.shape[0] // rows
    text_wide = jnp.pad(
        text.reshape(rows, text_rows, -1), ((0, 0), (0, block_rows - text_rows), (0, 0))
    ).reshape(depth, -1)
    raw_text, value_two = project(weights_two, [2, 3], [text_wide], [F32, BF])
    norm_key, text_pull = jax.vjp(head_norm, raw_text.reshape(heads, dim, -1), text_key_gain)
    query_two = norm_query.astype(BF)
    key_two = norm_key.astype(BF)
    value_two = value_two.reshape(heads, dim, -1)
    saved_cross = []
    mixed_parts = []
    for index, piece in enumerate(pieces):
        length = lax.dynamic_index_in_dim(text_lengths, piece.sequence, 0, True)
        here = slice(index * keys, (index + 1) * keys)
        inputs = [cut(query_two, index), key_two[:, :, here], value_two[:, :, here]]
        inputs = [length] + [a[None, None] for a in inputs] + [(0, 0, 0)]
        kept = attend(*inputs, True, 4)
        saved_cross.append((inputs, kept))
        mixed_parts.append(kept[0].reshape(depth, -1))
    mixed_two = jnp.concatenate(mixed_parts, 1)
    stream = stream + rebuild(weights_two, [1], [mixed_two], F32)
    normal_three, inverse_three = normalize(stream)
    normed_three = (normal_three * gain_hidden + bias_hidden).astype(BF)
    grad_out = to_tokens(after(out_grad, joined).astype(BF), pieces, cols)
    act, slopes = expand(weights_hidden, 0, normed_three)
    output = contract(weights_hidden, 1, act, stream, BF)
    result = to_features(output, pieces, cols).astype(F32)

    g_inner = expand_back(weights_hidden, 1, grad_out, slopes)
    g_normed = contract(weights_hidden, 0, g_inner, None, F32)
    g_hidden = hidden_outer(grad_out, act, normed_three, g_inner)
    g_hidden = lax.psum_scatter(
        g_hidden.reshape(2, -1, g_hidden.shape[3]), DEVICES, scatter_dimension=1, tiled=True
    ).astype(F32)
    g_hidden_gain = jnp.sum(g_normed * normal_three, 1)
    g_hidden_bias = jnp.sum(g_normed, 1)
    g_stream = grad_out.astype(F32) + norm_back(g_normed * gain_hidden, normal_three, inverse_three)

    running = []
    g_low = g_stream.astype(BF)
    g_mixed = project(weights_two, [1], [g_low], [BF])[0].reshape(heads, dim, tokens)
    r_cross = Reduction(core, g_low, [mixed_two], True)
    running.append(r_cross)
    g_queries = []
    g_keys = []
    g_values = []
    for index, piece in enumerate(pieces):
        inputs, kept = saved_cross[index]
        grads = attend_back(*inputs, kept, cut(g_mixed, index)[None], True, 4, False)
        g_queries.append(grads[0][0, 0])
        g_keys.append(grads[1][0, 0])
        g_values.append(grads[2][0, 0])
    g_queries, g_keys, g_values = tick((g_queries, g_keys, g_values), running)
    g_raw_cross, g_cq_gain = cross_pull(jnp.concatenate(g_queries, 2))
    g_raw_text, g_tk_gain = text_pull(jnp.concatenate(g_keys, 2))
    g_craw = g_raw_cross.astype(BF).reshape(depth, tokens)
    g_pair = [
        g_raw_text.astype(BF).reshape(depth, -1),
        jnp.concatenate(g_values, 2).astype(BF).reshape(depth, -1),
    ]
    g_normed = rebuild(weights_two, [0], [g_craw], F32)
    r_query = Reduction(core, normed_two, [g_craw], False)
    r_text = Reduction(core, text, g_pair, True)
    g_normed = tick(g_normed, running)
    running += [r_query, r_text]
    g_cross_gain = jnp.sum(g_normed * normal_two, 1)
    g_cross_bias = jnp.sum(g_normed, 1)
    g_stream = g_stream + norm_back(g_normed * gain_cross, normal_two, inverse_two)

    g_low = g_stream.astype(BF)
    g_mixed = project(weights_one, [3], [g_low], [BF])[0].reshape(heads, dim, tokens)
    g_mixed = tick(g_mixed, running)
    r_attn = Reduction(core, g_low, [mixed_one], False)
    g_parts = []
    for index, piece in enumerate(pieces):
        whole, kept = saved_self[index]
        grad = exchange(
            cut(g_mixed, index).reshape(piece.group, -1, dim, piece.count), piece.group, cols
        )
        part = attend_back(
            none, whole, whole, whole, (0, 1, 2), kept, grad, False, 2, True
        )
        part = tick(part, running)
        if index == 0:
            running.append(r_attn)
        g_parts.append(exchange(part, piece.group, cols))
    g_heads = [
        jnp.concatenate([p[:, i].reshape(heads, dim, -1) for p in g_parts], 2) for i in range(3)
    ]
    g_raw_q, g_q_gain = query_pull(g_heads[0].astype(F32))
    g_raw_k, g_k_gain = key_pull(g_heads[1].astype(F32))
    g_triple = [
        g.reshape(depth, tokens) for g in (g_raw_q.astype(BF), g_raw_k.astype(BF), g_heads[2])
    ]
    g_triple = tick(g_triple, running)
    r_self = [
        Reduction(core, normed_one, g_triple[:2], True),
        Reduction(core, normed_one, g_triple[2:], False),
    ]
    g_normed = rebuild(weights_one, [0, 1, 2], g_triple, F32)
    running += r_self
    g_normed = tick(g_normed, running)
    crossed = g_normed * normal_one
    sums = jnp.stack(
        [
            jnp.stack([jnp.sum(cut(g_normed, i), 1), jnp.sum(cut(crossed, i), 1)], 0)
            for i in range(len(pieces))
        ],
        0,
    )
    which = jnp.stack(
        [jnp.where(jnp.arange(sequences) == p.sequence, 1.0, 0.0) for p in pieces], 0
    )
    g_modul = jnp.sum(which[:, :, None, None] * sums[:, None], 0)
    g_modul = g_modul.reshape(sequences, 2, cols, width).transpose(2, 0, 1, 3)
    g_modul = jnp.sum(lax.all_to_all(g_modul, "col", 0, 0, tiled=True), 0).astype(BF)
    g_modul = shared(g_modul, "row").reshape(-1, 2, width)
    g_modulation = einsum("sd,ske->dke", embed_rows, g_modul)
    g_stream = g_stream + norm_back(g_normed * scaling, normal_one, inverse_one)

    g_skip_gain = jnp.sum(g_stream * skip_normal, 1)
    g_skip_bias = jnp.sum(g_stream, 1)
    g_joined = norm_back(g_stream * gain_skip, skip_normal, skip_inverse).astype(BF)
    g_joined = tick(g_joined, running)
    r_skip = Reduction(core, both, [g_joined], True)
    g_both = rebuild_blocks(base, w_skip, width, g_joined)
    g_both = tick(g_both, [r_skip])
    g_inputs = to_features(g_both, pieces, cols).reshape(split[0], 2, block_rows, row_tokens)
    g_latents, g_skip = (g_inputs[:, i].reshape(width, row_tokens).astype(F32) for i in range(2))

    g_gains = jnp.stack(
        [g_skip_gain, g_skip_bias, g_cross_gain, g_cross_bias, g_hidden_gain, g_hidden_bias], 0
    )
    g_gains = g_gains.reshape(6, cols, width).transpose(1, 0, 2)
    g_head = jnp.stack([g_q_gain, g_k_gain, g_cq_gain, g_tk_gain], 0).reshape(1, -1, width)
    g_gains = after(g_gains, g_both)
    packed = jnp.concatenate([g_gains, jnp.broadcast_to(g_head, (cols, *g_head.shape[1:]))], 1)
    packed = jnp.sum(lax.all_to_all(packed, "col", 0, 0, tiled=True), 0)
    packed = jnp.sum(shared(packed, "row"), 0)
    g_gains = packed[:6]
    g_head = packed[6:].reshape(4, dim)
    return (
        result,
        g_latents,
        g_skip,
        r_skip.result().reshape(2, block_rows, width),
        g_modulation,
        jnp.concatenate([r.result() for r in r_self], 0).transpose(1, 0, 2),
        r_attn.result()[0].T,
        r_query.result()[0],
        r_text.result().transpose(1, 0, 2),
        r_cross.result()[0].T,
        g_hidden[0],
        g_hidden[1].T,
        *[g_gains[i] for i in range(6)],
        *[g_head[i] for i in range(4)],
    )


def solution(mesh):
    return jax.shard_map(
        shards,
        mesh=mesh,
        in_specs=(
            P("col", "row"),
            P("col", "row"),
            P("row", "col"),
            P("row", None, "col"),
            P("row"),
            P(None, "row"),
            P("col", "row"),
            P(None, "row", "col"),
            P("row", None, "col"),
            P("row", None, "col"),
            P("col", "row"),
            P("row", "col"),
            P("row", None, "col"),
            P("col", "row"),
            P("row", "col"),
            P("col", "row"),
            P("col"),
            P("col"),
            P("col"),
            P("col"),
            P("col"),
            P("col"),
            P(),
            P(),
            P(),
            P(),
        ),
        out_specs=(
            P("col", "row"),
            P("col", "row"),
            P("col", "row"),
            P(None, "row", "col"),
            P("row", None, "col"),
            P("row", None, "col"),
            P("col", "row"),
            P("row", "col"),
            P("row", None, "col"),
            P("col", "row"),
            P("row", "col"),
            P("col", "row"),
            P("col"),
            P("col"),
            P("col"),
            P("col"),
            P("col"),
            P("col"),
            P(),
            P(),
            P(),
            P(),
        ),
        check_vma=False,
    )
```

```python
from functools import partial
import math

import jax
import jax.numpy as jnp
from jax import lax
from jax.experimental import pallas as pl
from jax.experimental.pallas import tpu as pltpu
from jax.sharding import PartitionSpec as P

L = 1024
EPSILON = 1e-06
BF = jnp.bfloat16
F32 = jnp.float32
KEYPAD = 128
DEVICES = ("col", "row")
LOG2E = math.log2(math.e)
VMEM = 60 << 20


def einsum(spec, left, right):
    return jnp.einsum(spec, left, right, preferred_element_type=F32)


def dot(left, right, dims):
    return lax.dot_general(left, right, (dims, ((), ())), preferred_element_type=F32)


def params():
    return pltpu.CompilerParams(vmem_limit_bytes=VMEM)


def step_of(count):
    return 256 if count % 256 == 0 else count


def wide(ref, head):
    parts = [ref[s, 0, head] for s in range(ref.shape[0])]
    return parts[0] if len(parts) == 1 else jnp.concatenate(parts, 1)


def valid_keys(length_ref, keys, step):
    return lax.broadcasted_iota(jnp.int32, (keys, step), 0) < length_ref[0]


def attend_kernel(masked, length_ref, q_ref, k_ref, v_ref, o_ref, r_ref, l_ref):
    groups, _, heads, dim, count = q_ref.shape
    step = step_of(count)
    factor = dim ** (-0.5) * LOG2E
    for head in range(heads):
        key = wide(k_ref, head).T
        value = wide(v_ref, head)
        keys = key.shape[0]
        value = jnp.concatenate([value, jnp.ones((8, keys), BF)], 0)
        for place in range(0, groups * count, step):
            group, first = divmod(place, count)
            query = q_ref[group, 0, head, :, first : first + step]
            expo = jnp.exp2(dot(key, query, ((1,), (0,))) * factor)
            if masked:
                expo = jnp.where(valid_keys(length_ref, keys, step), expo, 0.0)
            both = dot(value, expo.astype(BF), ((1,), (0,)))
            total = both[dim : dim + 1]
            mixed = both[:dim] * (1.0 / total)
            high = mixed.astype(BF)
            o_ref[group, head, :, first : first + step] = high
            r_ref[group, head, :, first : first + step] = (mixed - high.astype(F32)).astype(BF)
            l_ref[head, :, place : place + step] = jnp.log2(total)


def attend_back_kernel(
    masked, length_ref, q_ref, k_ref, v_ref, m_ref, r_ref, g_ref, l_ref, *outs
):
    groups, _, heads, dim, count = q_ref.shape
    step = step_of(count)
    scale = dim ** (-0.5)
    for head in range(heads):
        key = wide(k_ref, head)
        keys = key.shape[1]
        turned = key.T
        value = jnp.concatenate([wide(v_ref, head), jnp.ones((8, keys), BF)], 0).T
        g_key = g_value = None
        for place in range(0, groups * count, step):
            group, first = divmod(place, count)
            here = slice(first, first + step)
            query = q_ref[group, 0, head, :, here]
            grad = g_ref[group, head, :, here]
            mixed = m_ref[group, head, :, here].astype(F32)
            mixed = mixed + r_ref[group, head, :, here].astype(F32)
            delta = -jnp.sum(grad.astype(F32) * mixed, 0, keepdims=True)
            high = delta.astype(BF)
            rest = (delta - high.astype(F32)).astype(BF)
            more = jnp.concatenate([grad, high, rest, jnp.zeros((6, step), BF)], 0)
            probs = jnp.exp2(
                dot(turned, query, ((1,), (0,))) * (scale * LOG2E)
                - l_ref[head, :, place : place + step]
            )
            if masked:
                probs = jnp.where(valid_keys(length_ref, keys, step), probs, 0.0)
            product = (probs * dot(value, more, ((1,), (0,)))).astype(BF)
            g_query = dot(key, product, ((1,), (0,))) * scale
            part_value = dot(grad, probs.astype(BF), ((1,), (1,)))
            part_key = dot(query, product, ((1,), (1,)))
            g_value = part_value if g_value is None else g_value + part_value
            g_key = part_key if g_key is None else g_key + part_key
            outs[0][group, 0, head, :, here] = g_query.astype(outs[0].dtype)
        g_key = g_key * scale
        if len(outs) == 1:
            for group in range(groups):
                here = slice(group * count, (group + 1) * count)
                outs[0][group, 1, head] = g_key[:, here].astype(BF)
                outs[0][group, 2, head] = g_value[:, here].astype(BF)
        else:
            outs[1][0, 0, head] = g_key
            outs[2][0, 0, head] = g_value


def costs(heads, queries, keys, dim, products):
    return pl.CostEstimate(
        flops=2 * products * heads * queries * keys * 256,
        transcendentals=heads * queries * keys,
        bytes_accessed=2 * products * heads * dim * (queries + keys),
    )


def head_block(shape, count, kind=0):
    groups, _, _, dim, tokens = shape
    return pl.BlockSpec((groups, 1, count, dim, tokens), lambda h: (0, kind, h, 0, 0))


def mix_block(shape, count):
    groups, _, _, dim, tokens = shape
    return pl.BlockSpec((groups, count, dim, tokens), lambda h: (0, h, 0, 0))


def attend(length, query, key, value, kinds, masked, most):
    groups, _, heads, dim, count = query.shape
    many = math.gcd(heads, most)
    total = groups * count
    keys = key.shape[0] * key.shape[4]
    return pl.pallas_call(
        partial(attend_kernel, masked),
        grid=(heads // many,),
        in_specs=[pl.BlockSpec(memory_space=pltpu.SMEM)]
        + [head_block(a.shape, many, kind) for a, kind in zip((query, key, value), kinds)],
        out_specs=[
            mix_block(query.shape, many),
            mix_block(query.shape, many),
            pl.BlockSpec((many, 1, total), lambda h: (h, 0, 0)),
        ],
        out_shape=[
            jax.ShapeDtypeStruct((groups, heads, dim, count), BF),
            jax.ShapeDtypeStruct((groups, heads, dim, count), BF),
            jax.ShapeDtypeStruct((heads, 1, total), F32),
        ],
        cost_estimate=costs(heads, total, keys, dim, 2),
        compiler_params=params(),
        name="attend",
    )(length, query, key, value)


def attend_back(length, query, key, value, kinds, kept, grad, masked, most, stacked):
    mixed, rest, logs = kept
    groups, _, heads, dim, count = query.shape
    many = math.gcd(heads, most)
    total = groups * count
    keys = key.shape[0] * key.shape[4]
    if stacked:
        out_specs = pl.BlockSpec((groups, 3, many, dim, count), lambda h: (0, 0, h, 0, 0))
        out_shape = jax.ShapeDtypeStruct((groups, 3, heads, dim, count), BF)
    else:
        out_specs = [head_block(a.shape, many) for a in (query, key, value)]
        out_shape = [jax.ShapeDtypeStruct(a.shape, F32) for a in (query, key, value)]
    return pl.pallas_call(
        partial(attend_back_kernel, masked),
        grid=(heads // many,),
        in_specs=[pl.BlockSpec(memory_space=pltpu.SMEM)]
        + [head_block(a.shape, many, kind) for a, kind in zip((query, key, value), kinds)]
        + [mix_block(query.shape, many)] * 3
        + [pl.BlockSpec((many, 1, total), lambda h: (h, 0, 0))],
        out_specs=out_specs,
        out_shape=out_shape,
        cost_estimate=costs(heads, total, keys, dim, 5),
        compiler_params=params(),
        name="attend_back",
    )(length, query, key, value, mixed, rest, grad, logs)


def work(rows, depth, tokens, moved):
    return pl.CostEstimate(
        flops=2 * rows * depth * tokens,
        transcendentals=0,
        bytes_accessed=moved,
    )


def lanes(width):
    return -(-width // 128) * 128


def full(shape):
    return pl.BlockSpec(shape, lambda *_: (0,) * len(shape))


def project(weight, kinds, values, dtypes, joined=False):
    _, cols, depth, width = weight.shape
    tokens = values[0].shape[1]
    outs = 1 if joined else len(kinds)

    def kernel(*refs):
        blocks = refs[: len(kinds)]
        given = refs[len(kinds) : -outs]
        total = None
        for index, block in enumerate(blocks):
            part = dot(block[0, 0], given[index % len(given)][...], ((0,), (0,)))
            if not joined:
                refs[index - outs][...] = part.astype(dtypes[index])
            total = part if total is None else total + part
        if joined:
            refs[-1][...] = total.astype(dtypes[0])

    return pl.pallas_call(
        kernel,
        grid=(cols,),
        in_specs=[
            pl.BlockSpec((1, 1, depth, width), partial(lambda k, c: (k, c, 0, 0), kind))
            for kind in kinds
        ]
        + [full(v.shape) for v in values],
        out_specs=[pl.BlockSpec((width, tokens), lambda c: (c, 0))] * outs,
        out_shape=[jax.ShapeDtypeStruct((cols * width, tokens), dtypes[i]) for i in range(outs)],
        cost_estimate=work(len(kinds) * cols * width, depth, tokens, 8 * depth * tokens),
        compiler_params=params(),
        name="project",
    )(*([weight] * len(kinds)), *values)


def rebuild(weight, kinds, values, dtype):
    _, cols, depth, width = weight.shape
    tokens = values[0].shape[1]
    tile = depth // 4

    def kernel(*refs):
        total = None
        for block, given in zip(refs[: len(kinds)], refs[len(kinds) : -1]):
            for col in range(cols):
                part = dot(block[0, col], given[col * width : (col + 1) * width, :], ((1,), (0,)))
                total = part if total is None else total + part
        refs[-1][...] = total.astype(dtype)

    return pl.pallas_call(
        kernel,
        grid=(4,),
        in_specs=[
            pl.BlockSpec((1, cols, tile, width), partial(lambda k, j: (k, 0, j, 0), kind))
            for kind in kinds
        ]
        + [full(v.shape) for v in values],
        out_specs=pl.BlockSpec((tile, tokens), lambda j: (j, 0)),
        out_shape=jax.ShapeDtypeStruct((depth, tokens), dtype),
        cost_estimate=work(depth, len(kinds) * cols * width, tokens, 8 * depth * tokens),
        compiler_params=params(),
        name="rebuild",
    )(*([weight] * len(kinds)), *values)


def project_blocks(base, blocks, width, values):
    many = len(blocks)
    depth, broad = blocks[0].shape
    tokens = values.shape[1]
    tile = depth // 4

    def kernel(base_ref, *refs):
        values_ref, out_ref = refs[many:]

        @pl.when(pl.program_id(0) == 0)
        def _():
            out_ref[...] = jnp.zeros_like(out_ref)

        for index in range(many):
            here = pl.ds(pl.multiple_of((index ^ base_ref[0]) * width, width), width)
            out_ref[here, :] += dot(refs[index][...], values_ref[...], ((0,), (0,)))[:width]

    return pl.pallas_call(
        kernel,
        grid_spec=pltpu.PrefetchScalarGridSpec(
            num_scalar_prefetch=1,
            grid=(4,),
            in_specs=[pl.BlockSpec((tile, broad), lambda j, b: (j, 0))] * many
            + [pl.BlockSpec((tile, tokens), lambda j, b: (j, 0))],
            out_specs=pl.BlockSpec((many * width, tokens), lambda j, b: (0, 0)),
        ),
        out_shape=jax.ShapeDtypeStruct((many * width, tokens), F32),
        cost_estimate=work(many * width, depth, tokens, 4 * depth * tokens),
        compiler_params=params(),
        name="project_blocks",
    )(base, *blocks, values)


def rebuild_blocks(base, blocks, width, values):
    many = len(blocks)
    depth, broad = blocks[0].shape
    tokens = values.shape[1]
    tile = depth // 4

    def kernel(base_ref, *refs):
        values_ref, out_ref = refs[many:]
        total = None
        for index in range(many):
            here = pl.ds(pl.multiple_of((index ^ base_ref[0]) * width, width), width)
            part = dot(refs[index][:, :width], values_ref[here, :], ((1,), (0,)))
            total = part if total is None else total + part
        out_ref[...] = total.astype(BF)

    return pl.pallas_call(
        kernel,
        grid_spec=pltpu.PrefetchScalarGridSpec(
            num_scalar_prefetch=1,
            grid=(4,),
            in_specs=[pl.BlockSpec((tile, broad), lambda j, b: (j, 0))] * many
            + [pl.BlockSpec(values.shape, lambda j, b: (0, 0))],
            out_specs=pl.BlockSpec((tile, tokens), lambda j, b: (j, 0)),
        ),
        out_shape=jax.ShapeDtypeStruct((depth, tokens), BF),
        cost_estimate=work(many * width, depth, tokens, 4 * depth * tokens),
        compiler_params=params(),
        name="rebuild_blocks",
    )(base, *blocks, values)


def outer(place, pairs, across, got=None):
    cols = lax.axis_size("col")
    lefts = []
    for left, _ in pairs:
        if not any(left is other for other in lefts):
            lefts.append(left)
    which = [next(i for i, l in enumerate(lefts) if l is left) for left, _ in pairs]
    rights = [right for _, right in pairs]
    many = len(pairs)
    rows, tokens = lefts[0].shape
    width = rights[0].shape[0] // cols
    broad = lanes(width)
    tile = rows // 4
    chunk = tile // 2
    flip = 1 if got is None else 0

    def kernel(place_ref, *refs):
        left_refs = refs[: len(lefts)]
        right_refs = refs[len(lefts) : len(lefts) + many]
        rest = refs[len(lefts) + many :]
        for index in range(many):
            right = right_refs[index][...]
            if broad > width:
                right = jnp.concatenate([right, jnp.zeros((broad - width, tokens), BF)], 0)
            part = dot(left_refs[which[index]][...], right, ((1,), (1,)))
            if got is None:
                rest[0][index, 0] = part.astype(BF)
            elif not across:
                part = (part + rest[0][index, 0].astype(F32)).astype(BF)

                @pl.when(pl.program_id(0) == place_ref[2])
                def _():
                    rest[1][index, 0] = part.reshape(2, chunk, broad)

                @pl.when(pl.program_id(0) != place_ref[2])
                def _():
                    rest[2][index, 0] = part.reshape(2, chunk, broad)
            else:
                part = part + rest[0][index, 0].astype(F32)
                first, second = part[:chunk].astype(BF), part[chunk:].astype(BF)
                lower = place_ref[1] == 0
                rest[1][index, 0, 0] = jnp.where(lower, first, second)
                rest[2][index, 0, 0] = jnp.where(lower, second, first)

    whole = pl.BlockSpec((many, 1, tile, broad), lambda y, z, place: (0, y, z, 0))
    piece = pl.BlockSpec((many, 1, 1, chunk, broad), lambda y, z, place: (0, y, z, 0, 0))

    def phase(ours):
        def index(y, z, place):
            phase = place[2] if ours else 1 - place[2]
            inside = (y == phase).astype(jnp.int32)
            return (0, inside * z + (1 - inside) * 3 * (1 - phase), 0, 0, 0)

        return pl.BlockSpec((many, 1, 2, chunk, broad), index)

    if got is None:
        given, out_specs = [], whole
        out_shape = jax.ShapeDtypeStruct((many, cols // 2, rows, broad), BF)
    else:
        given, out_specs = [got], [piece, piece] if across else [phase(True), phase(False)]
        shape = (many, cols // 2, 4, chunk, broad) if across else (many, 4, 2, chunk, broad)
        out_shape = [jax.ShapeDtypeStruct(shape, BF)] * 2
    return pl.pallas_call(
        kernel,
        grid_spec=pltpu.PrefetchScalarGridSpec(
            num_scalar_prefetch=1,
            grid=(cols // 2, 4),
            in_specs=[pl.BlockSpec((tile, tokens), lambda y, z, place: (z, 0)) for _ in lefts]
            + [
                pl.BlockSpec(
                    (width, tokens), lambda y, z, place: (2 * y + (place[0] ^ flip), 0)
                )
                for _ in rights
            ]
            + [whole] * len(given),
            out_specs=out_specs,
        ),
        out_shape=out_shape,
        cost_estimate=work(
            rows, tokens, many * cols // 2 * broad, 2 * rows * cols * broad * many
        ),
        compiler_params=params(),
        name="outer",
    )(place, *lefts, *rights, *given)


def expand(weight, kind, values):
    _, many, depth, hidden = weight.shape
    tokens = values.shape[1]
    tile = 384 if hidden % 384 == 0 else hidden
    slope = 0.79788456
    cubic = 0.044715

    def kernel(weight_ref, values_ref, act_ref, slope_ref):
        for index in range(many):
            inner = dot(weight_ref[0, index], values_ref[...], ((0,), (0,)))
            square = inner * inner
            bent = jnp.tanh(inner * (slope + slope * cubic * square))
            half = 0.5 + 0.5 * bent
            act_ref[index] = (inner * half).astype(BF)
            rise = slope + 3.0 * slope * cubic * square
            slope_ref[index] = (half + 0.5 * inner * (1.0 - bent * bent) * rise).astype(BF)

    return pl.pallas_call(
        kernel,
        grid=(hidden // tile,),
        in_specs=[
            pl.BlockSpec((1, many, depth, tile), lambda j: (kind, 0, 0, j)),
            full(values.shape),
        ],
        out_specs=[pl.BlockSpec((many, tile, tokens), lambda j: (0, j, 0))] * 2,
        out_shape=[jax.ShapeDtypeStruct((many, hidden, tokens), BF)] * 2,
        cost_estimate=work(many * hidden, depth, tokens, 3 * many * hidden * depth),
        compiler_params=params(),
        name="expand",
    )(weight, values)


def expand_back(weight, kind, values, slopes):
    _, many, depth, hidden = weight.shape
    tokens = values.shape[1]
    tile = 384 if hidden % 384 == 0 else hidden

    def kernel(weight_ref, values_ref, slope_ref, out_ref):
        for index in range(many):
            part = dot(weight_ref[0, index], values_ref[...], ((0,), (0,)))
            out_ref[index] = (part * slope_ref[index].astype(F32)).astype(BF)

    return pl.pallas_call(
        kernel,
        grid=(hidden // tile,),
        in_specs=[
            pl.BlockSpec((1, many, depth, tile), lambda j: (kind, 0, 0, j)),
            full(values.shape),
            pl.BlockSpec((many, tile, tokens), lambda j: (0, j, 0)),
        ],
        out_specs=pl.BlockSpec((many, tile, tokens), lambda j: (0, j, 0)),
        out_shape=jax.ShapeDtypeStruct((many, hidden, tokens), BF),
        cost_estimate=work(many * hidden, depth, tokens, 3 * many * hidden * depth),
        compiler_params=params(),
        name="expand_back",
    )(weight, values, slopes)


def contract(weight, kind, values, added, dtype):
    _, many, depth, hidden = weight.shape
    tokens = values.shape[2]
    tile = depth // 4
    extra = [] if added is None else [added]

    def kernel(weight_ref, values_ref, *refs):
        total = refs[0][...] if extra else None
        for index in range(many):
            part = dot(weight_ref[0, index], values_ref[index], ((1,), (0,)))
            total = part if total is None else total + part
        refs[-1][...] = total.astype(dtype)

    line = pl.BlockSpec((tile, tokens), lambda j: (j, 0))
    return pl.pallas_call(
        kernel,
        grid=(4,),
        in_specs=[
            pl.BlockSpec((1, many, tile, hidden), lambda j: (kind, 0, j, 0)),
            full(values.shape),
        ]
        + [line] * len(extra),
        out_specs=line,
        out_shape=jax.ShapeDtypeStruct((depth, tokens), dtype),
        cost_estimate=work(depth, many * hidden, tokens, 3 * many * hidden * depth),
        compiler_params=params(),
        name="contract",
    )(weight, values, *extra)


def hidden_outer(grad_out, act, normed, grad_inner):
    many, hidden, tokens = act.shape
    depth = grad_out.shape[0]
    parts = 2 if hidden % 256 == 0 else 1
    tile = hidden // parts

    def kernel(out_ref, act_ref, normed_ref, inner_ref, grad_ref):
        kind = pl.program_id(0)

        @pl.when(kind == 0)
        def _():
            grad_ref[0, 0] = dot(normed_ref[...], inner_ref[0], ((1,), (1,))).astype(BF)

        @pl.when(kind == 1)
        def _():
            grad_ref[0, 0] = dot(out_ref[...], act_ref[0], ((1,), (1,))).astype(BF)

    return pl.pallas_call(
        kernel,
        grid=(2, many, parts),
        in_specs=[
            pl.BlockSpec((depth, tokens), lambda s, p, j: (0, 0)),
            pl.BlockSpec((1, tile, tokens), lambda s, p, j: (s * p, s * j, 0)),
            pl.BlockSpec((depth, tokens), lambda s, p, j: (0, 0)),
            pl.BlockSpec(
                (1, tile, tokens),
                lambda s, p, j: (p + s * (many - 1 - p), j + s * (parts - 1 - j), 0),
            ),
        ],
        out_specs=pl.BlockSpec((1, 1, depth, tile), lambda s, p, j: (s, p, 0, j)),
        out_shape=jax.ShapeDtypeStruct((2, many, depth, hidden), BF),
        cost_estimate=work(2 * depth, tokens, many * hidden, 5 * many * depth * hidden),
        compiler_params=params(),
        name="hidden_outer",
    )(grad_out, act, normed, grad_inner)


def assemble(place, own, got, middle=None):
    rows, width = own.shape[-2:]

    def kernel(place_ref, own_ref, got_ref, out_ref):
        @pl.when(pl.program_id(0) == place_ref[1])
        def _():
            out_ref[0, 0] = own_ref[...].reshape(rows, width)

        @pl.when(pl.program_id(0) != place_ref[1])
        def _():
            out_ref[0, 0] = got_ref[...].reshape(rows, width)

    def spec(ours):
        def index(x, z, place):
            phase = place[1] if ours else 1 - place[1]
            inside = (x == phase).astype(jnp.int32)
            level = (inside * z + (1 - inside) * 3 * (1 - phase)) ^ place[0]
            return (level, 0, 0) if middle is None else (level, middle, 0, 0)

        shape = (1, rows, width) if middle is None else (1, 1, rows, width)
        return pl.BlockSpec(shape, index)

    return pl.pallas_call(
        kernel,
        grid_spec=pltpu.PrefetchScalarGridSpec(
            num_scalar_prefetch=1,
            grid=(2, 4),
            in_specs=[spec(True), spec(False)],
            out_specs=pl.BlockSpec((1, 1, rows, width), lambda x, z, place: (z, x, 0, 0)),
        ),
        out_shape=jax.ShapeDtypeStruct((4, 2, rows, width), BF),
        cost_estimate=work(1, 1, 1, 32 * rows * width),
        name="assemble",
    )(place, own, got).reshape(8 * rows, width)


def normalize(values):
    average = jnp.mean(values, 0, keepdims=True)
    centred = values - average
    inverse = lax.rsqrt(jnp.mean(centred * centred, 0, keepdims=True) + EPSILON)
    return centred * inverse, inverse


def norm_back(grad, normal, inverse):
    average = jnp.mean(grad, 0, keepdims=True)
    crossed = jnp.mean(grad * normal, 0, keepdims=True)
    return inverse * (grad - average - normal * crossed)


def head_norm(values, gain):
    average = jnp.mean(values, 1, keepdims=True)
    centred = values - average
    variance = jnp.mean(centred * centred, 1, keepdims=True)
    return centred * lax.rsqrt(variance + EPSILON) * gain[None, :, None]


def rope_tables(places, head_dim):
    quarter = head_dim // 4
    freqs = jnp.exp(jnp.arange(quarter, dtype=F32) * (-4.0 * math.log(10000.0) / head_dim))
    rows = freqs[:, None] * places[0].astype(F32)[None, :]
    cols = freqs[:, None] * places[1].astype(F32)[None, :]
    angles = jnp.concatenate([rows, rows, cols, cols], 0)
    return jnp.cos(angles), jnp.sin(angles)


def rotate(values):
    quarter = values.shape[1] // 4
    one, two, three, four = (values[:, i * quarter : (i + 1) * quarter] for i in range(4))
    return jnp.concatenate([-two, one, -four, three], 1)


class Piece:
    def __init__(self, start, count, group, sequence):
        self.start = start
        self.count = count
        self.group = group
        self.sequence = sequence


def pieces_of(cols, sequences):
    mine = lax.axis_index("col")
    if cols == 4 and sequences == 3:
        return [
            Piece(0, L // 2, 2, mine // 2),
            Piece(2 * L, L // 4, 4, jnp.int32(2)),
        ]
    return [Piece(s * L, L // cols, cols, jnp.int32(s)) for s in range(sequences)]


def groups_of(size, cols):
    return [list(range(i, i + size)) for i in range(0, cols, size)]


def exchange(values, size, cols):
    if size == cols:
        return lax.all_to_all(values, "col", 0, 0, tiled=True)
    return lax.all_to_all(
        values, "col", 0, 0, tiled=True, axis_index_groups=groups_of(size, cols)
    )


def cut_size(pieces):
    return math.gcd(*(p.count for p in pieces), *(p.start for p in pieces))


def locate(pieces, unit, block):
    device = inside = None
    at = 0
    for piece in pieces:
        each = piece.count // unit
        rest = block - piece.start // unit
        there = (rest // each, at + rest % each)
        if device is None:
            device, inside = there
        else:
            later = (rest >= 0).astype(jnp.int32)
            device = later * there[0] + (1 - later) * device
            inside = later * there[1] + (1 - later) * inside
        at += each
    return device, inside


def to_tokens(arrays, pieces, cols, rows):
    width, tokens = arrays[0].shape
    kinds = len(arrays)
    unit = cut_size(pieces)
    total = sum(p.count for p in pieces)
    if unit % 128:
        values = jnp.stack([a.reshape(-1, rows, tokens) for a in arrays], 1).astype(BF)
        values = values.reshape(kinds * width, tokens)
        parts = [
            jnp.concatenate(
                [values[:, p.start + j * p.count : p.start + (j + 1) * p.count] for p in pieces], 1
            )
            for j in range(cols)
        ]
        dealt = jnp.stack(parts, 0)
    else:

        def kernel(*refs):
            for kind in range(kinds):
                for at in range(0, width, rows):
                    to = at * kinds + kind * rows
                    refs[-1][0, to : to + rows] = refs[kind][at : at + rows].astype(BF)

        def index(block):
            device, inside = locate(pieces, unit, block)
            return (device, 0, inside)

        dealt = pl.pallas_call(
            kernel,
            grid=(tokens // unit,),
            in_specs=[pl.BlockSpec((width, unit), lambda b: (0, b))] * kinds,
            out_specs=pl.BlockSpec((1, kinds * width, unit), index),
            out_shape=jax.ShapeDtypeStruct((cols, kinds * width, total), BF),
            cost_estimate=pl.CostEstimate(
                flops=0, transcendentals=0, bytes_accessed=4 * kinds * width * tokens
            ),
            name="deal",
        )(*arrays)
    got = exchange(dealt, cols, cols)
    return got.reshape(-1, total)


def to_features(values, pieces, cols, kinds, rows):
    got = exchange(values.reshape(cols, -1, values.shape[1]), cols, cols)
    unit = cut_size(pieces)
    width = got.shape[1] // kinds
    tokens = cols * got.shape[2]
    if unit % 128:
        parts = []
        at = 0
        for piece in pieces:
            parts += [got[j, :, at : at + piece.count] for j in range(cols)]
            at += piece.count
        whole = jnp.concatenate(parts, 1).astype(F32).reshape(-1, kinds, rows, tokens)
        return [whole[:, kind].reshape(width, tokens) for kind in range(kinds)]

    def kernel(got_ref, *refs):
        for kind in range(kinds):
            for at in range(0, width, rows):
                start = at * kinds + kind * rows
                refs[kind][at : at + rows] = got_ref[0, start : start + rows].astype(F32)

    def index(block):
        device, inside = locate(pieces, unit, block)
        return (device, 0, inside)

    return pl.pallas_call(
        kernel,
        grid=(tokens // unit,),
        in_specs=[pl.BlockSpec((1, kinds * width, unit), index)],
        out_specs=[pl.BlockSpec((width, unit), lambda b: (0, b))] * kinds,
        out_shape=[jax.ShapeDtypeStruct((width, tokens), F32)] * kinds,
        cost_estimate=pl.CostEstimate(
            flops=0, transcendentals=0, bytes_accessed=6 * kinds * width * tokens
        ),
        name="undeal",
    )(got)


def shared(values, axis):
    size = lax.axis_size(axis)
    return lax.all_to_all(
        jnp.broadcast_to(values[None], (size, *values.shape)), axis, 0, 0, tiled=True
    )


def swap(values, axis, bit):
    size = lax.axis_size(axis)
    return lax.ppermute(values, axis, [(i, i ^ bit) for i in range(size)])


def custom_mesh():
    return (lax.axis_size("row"), lax.axis_size("col")) == (8, 4)


def gather_weights(blocks):
    cols = lax.axis_size("col")
    most = max(block.shape[0] for block in blocks)
    padded = [jnp.pad(b, ((0, most - b.shape[0]), (0, 0))) for b in blocks]
    whole = lax.all_gather(jnp.stack(padded, 0), DEVICES, axis=1, tiled=True)
    return whole.reshape(len(blocks), cols, -1, blocks[0].shape[1])


class Gathering:
    last = 4

    def __init__(self, block, up, place):
        self.up = up
        self.place = place
        self.stage = 0
        self.state = [block]
        if not custom_mesh():
            cols = lax.axis_size("col")
            whole = lax.all_gather(block, DEVICES, axis=0, tiled=True)
            self.state = list(whole.reshape(cols, -1, block.shape[1]))
            self.stage = self.last

    def levels(self, block):
        return [block] + [swap(block, "row", 2 * level) for level in (1, 2, 3)]

    def advance(self):
        state = self.state
        self.stage += 1
        if self.stage == 1:
            self.state = [state[0], swap(state[0], "col", 2)] if self.up else self.levels(state[0])
        elif self.stage == 2:
            stack = jnp.stack(state, 0)
            self.state = self.levels(stack) if self.up else [stack, swap(stack, "col", 2)]
        elif self.stage == 3 and self.up:
            stack = jnp.stack(state, 0)
            self.state = [stack, swap(stack, "row", 1)]
        elif self.stage == 3:
            self.state = state + [swap(a, "row", 1) for a in state]
        else:
            if self.up:
                mine, other = (assemble(self.place, *state, k) for k in (0, 1))
            else:
                mine = assemble(self.place, state[0], state[2])
                other = assemble(self.place, state[1], state[3])
            self.state = [mine, swap(mine, "col", 1), other, swap(other, "col", 1)]

    def result(self):
        while self.stage < self.last:
            self.advance()
        return self.state


def pick(values, axis, index):
    return lax.dynamic_index_in_dim(values, index, axis, False)


def add(left, right):
    return (left.astype(F32) + right.astype(F32)).astype(BF)


class Reduction:
    last = 4

    def __init__(self, place, pairs, across):
        self.place = place
        self.across = across
        self.pairs = pairs
        self.width = pairs[0][1].shape[0] // lax.axis_size("col")
        self.stage = 0
        if custom_mesh():
            self.state = [swap(outer(place, pairs, across), "col", 1)]
            return
        self.stage = self.last
        cols = lax.axis_size("col")
        whole = jnp.stack(
            [einsum("kt,cnt->ckn", a, b.reshape(cols, -1, b.shape[1])) for a, b in pairs], 0
        )
        flat = whole.reshape(len(pairs), -1, whole.shape[3]).astype(BF)
        self.state = [lax.psum_scatter(flat, DEVICES, scatter_dimension=1, tiled=True)]

    def advance(self):
        state = self.state
        self.stage += 1
        if self.stage == 1:
            here, away = outer(self.place, self.pairs, self.across, state[0])
            self.state = [here, swap(away, "row", 1) if self.across else swap(away, "col", 2)]
        elif self.stage == 2:
            axis, index = (1, self.place[2]) if self.across else (2, self.place[1])
            away = add(*(pick(a, axis, 1 - index) for a in state))
            here = add(*(pick(a, axis, index) for a in state))
            self.state = [here, swap(away, "col", 2) if self.across else swap(away, "row", 1)]
        elif self.stage == 3:
            level = lax.axis_index("row") // 2
            total = add(*state)
            self.state = [pick(total, 1, level)] + [
                swap(pick(total, 1, level ^ other), "row", 2 * other) for other in (1, 2, 3)
            ]
        else:
            total = state[0].astype(F32)
            for other in state[1:]:
                total = total + other.astype(F32)
            self.state = [total[..., : self.width]]

    def result(self):
        while self.stage < self.last:
            self.advance()
        return self.state[0].astype(F32)


def tick(values, running):
    active = [r for r in running if r.stage < r.last]
    if active:
        values, states = lax.optimization_barrier((values, [r.state for r in active]))
        for beside, state in zip(active, states):
            beside.state = state
            beside.advance()
    return values


def after(values, done):
    return lax.optimization_barrier((values, done))[0]


def shards(
    latents,
    skip_input,
    condition,
    text_states,
    text_lengths,
    positions,
    out_grad,
    skip_weight,
    modulation,
    self_inputs,
    self_output,
    cross_query,
    cross_keyvalue,
    cross_output,
    expand_weight,
    reduce_weight,
    skip_gain,
    skip_bias,
    cross_gain,
    cross_bias,
    hidden_gain,
    hidden_bias,
    query_gain,
    key_gain,
    cross_query_gain,
    text_key_gain,
):
    cols = lax.axis_size("col")
    rows = lax.axis_size("row")
    mine = lax.axis_index("col")
    my_row = lax.axis_index("row")
    width, row_tokens = latents.shape
    depth = width * cols
    dim = query_gain.shape[0]
    heads = depth // dim
    sequences = row_tokens // L
    tokens = row_tokens // cols
    texts = text_states.shape[1]
    keys = -(-texts // KEYPAD) * KEYPAD
    pieces = pieces_of(cols, sequences)
    starts = [sum(p.count for p in pieces[:i]) for i in range(len(pieces))]
    place = jnp.stack([my_row // 2, my_row % 2]).astype(jnp.int32)
    corner = jnp.stack([mine % 2, my_row % 2, mine // 2]).astype(jnp.int32)
    base = (mine if custom_mesh() else jnp.zeros_like(mine)).astype(jnp.int32)[None]

    def cut(values, index):
        return values[..., starts[index] : starts[index] + pieces[index].count]

    block_rows = depth // rows
    both = to_tokens([latents, skip_input], pieces, cols, block_rows)

    weights_one = gather_weights([*(self_inputs[:, i] for i in range(3)), self_output.T])
    weights_two = gather_weights(
        [cross_query, cross_output.T, cross_keyvalue[:, 0], cross_keyvalue[:, 1]]
    )
    skip_block = jnp.concatenate([skip_weight[0], skip_weight[1]], 0)
    skip_block = jnp.pad(skip_block, ((0, 0), (0, lanes(width) - width)))
    w_skip = Gathering(skip_block, True, place).result()
    weights_hidden = gather_weights([expand_weight, reduce_weight.T])

    places = jnp.concatenate(
        [
            lax.dynamic_slice_in_dim(positions, p.start + mine * p.count, p.count, 1)
            for p in pieces
        ],
        1,
    )

    embed = jax.nn.silu(after(condition, both).astype(F32)).astype(BF)
    embed = shared(embed, "row").reshape(-1, width)
    embed = shared(embed, "col").transpose(1, 0, 2).reshape(-1, depth)
    embed_rows = lax.dynamic_slice_in_dim(embed, my_row * block_rows, block_rows, 1)
    modul = einsum("sd,dke->ske", embed_rows, modulation).reshape(rows, sequences, 2, width)
    modul = jnp.sum(lax.all_to_all(modul, "row", 0, 0, tiled=True), 0)
    gains = jnp.stack(
        [skip_gain, skip_bias, cross_gain, cross_bias, hidden_gain, hidden_bias], 0
    )
    table = jnp.concatenate([gains, modul.reshape(-1, width)], 0)
    table = shared(table, "col").transpose(1, 0, 2).reshape(-1, depth)
    modul = table[6:].reshape(sequences, 2, depth)
    chosen = [lax.dynamic_index_in_dim(modul, p.sequence, 0, False) for p in pieces]
    columns = lax.optimization_barrier(jnp.concatenate([table[:6], *chosen], 0)).T
    gain_skip, bias_skip, gain_cross, bias_cross, gain_hidden, bias_hidden = (
        columns[:, i : i + 1] for i in range(6)
    )
    token_index = lax.broadcasted_iota(jnp.int32, (1, tokens), 1)

    def per_token(which):
        result = columns[:, 6 + which : 7 + which]
        for index in range(1, len(pieces)):
            column = columns[:, 6 + 2 * index + which : 7 + 2 * index + which]
            result = jnp.where(token_index >= starts[index], column, result)
        return jnp.broadcast_to(result, (depth, tokens))

    shifting = per_token(0)
    scaling = 1.0 + per_token(1)

    text = shared(jnp.pad(after(text_states, both), ((0, 0), (0, keys - texts), (0, 0))), "col")
    joined = project_blocks(base, w_skip, width, both)
    joined, text = lax.optimization_barrier((joined, text))
    skip_normal, skip_inverse = normalize(joined)
    stream = skip_normal * gain_skip + bias_skip
    normal_one, inverse_one = normalize(stream)
    normed_one = (normal_one * scaling + shifting).astype(BF)
    raw = project(weights_one, [0, 1, 2], [normed_one], [F32, F32, BF])
    raw = [r.reshape(heads, dim, tokens) for r in raw]
    cosine, sine = rope_tables(places, dim)

    def self_piece(value, gain):
        normal = head_norm(value, gain)
        return normal * cosine[None] + rotate(normal) * sine[None]

    rot_query, query_pull = jax.vjp(self_piece, raw[0], query_gain)
    rot_key, key_pull = jax.vjp(self_piece, raw[1], key_gain)
    triple = [rot_query.astype(BF), rot_key.astype(BF), raw[2]]

    def to_heads(parts, index):
        size = pieces[index].group
        split = [cut(p, index).reshape(size, heads // size, dim, -1) for p in parts]
        return exchange(jnp.stack(split, 1), size, cols)

    none = jnp.zeros((1,), jnp.int32)
    saved_self = []
    mixed_parts = []
    for index, piece in enumerate(pieces):
        whole = to_heads(triple, index)
        kept = attend(none, whole, whole, whole, (0, 1, 2), False, 2)
        saved_self.append((whole, kept))
        mixed_parts.append(exchange(kept[0], piece.group, cols).reshape(depth, -1))
    mixed_one = jnp.concatenate(mixed_parts, 1)
    text = after(text, mixed_one)
    stream = stream + rebuild(weights_one, [3], [mixed_one], F32)
    normal_two, inverse_two = normalize(stream)
    normed_two = (normal_two * gain_cross + bias_cross).astype(BF)
    raw_cross = project(weights_two, [0], [normed_two], [F32])[0].reshape(heads, dim, tokens)
    norm_query, cross_pull = jax.vjp(head_norm, raw_cross, cross_query_gain)
    text = jnp.concatenate(
        [lax.dynamic_index_in_dim(text, p.sequence, 1, False) for p in pieces], 1
    )
    text = text.transpose(0, 2, 1).reshape(-1, len(pieces) * keys)
    text_rows = text.shape[0] // rows
    text_wide = jnp.pad(
        text.reshape(rows, text_rows, -1), ((0, 0), (0, block_rows - text_rows), (0, 0))
    ).reshape(depth, -1)
    raw_text, value_two = project(weights_two, [2, 3], [text_wide], [F32, BF])
    norm_key, text_pull = jax.vjp(head_norm, raw_text.reshape(heads, dim, -1), text_key_gain)
    query_two = norm_query.astype(BF)
    key_two = norm_key.astype(BF)
    value_two = value_two.reshape(heads, dim, -1)
    saved_cross = []
    mixed_parts = []
    for index, piece in enumerate(pieces):
        length = lax.dynamic_index_in_dim(text_lengths, piece.sequence, 0, True)
        here = slice(index * keys, (index + 1) * keys)
        inputs = [cut(query_two, index), key_two[:, :, here], value_two[:, :, here]]
        inputs = [length] + [a[None, None] for a in inputs] + [(0, 0, 0)]
        kept = attend(*inputs, True, 4)
        saved_cross.append((inputs, kept))
        mixed_parts.append(kept[0].reshape(depth, -1))
    mixed_two = jnp.concatenate(mixed_parts, 1)
    stream = stream + rebuild(weights_two, [1], [mixed_two], F32)
    normal_three, inverse_three = normalize(stream)
    normed_three = (normal_three * gain_hidden + bias_hidden).astype(BF)
    grad_out = to_tokens([after(out_grad, joined)], pieces, cols, width)
    act, slopes = expand(weights_hidden, 0, normed_three)

    g_inner = expand_back(weights_hidden, 1, grad_out, slopes)
    g_normed = contract(weights_hidden, 0, g_inner, None, F32)
    g_hidden = hidden_outer(grad_out, act, normed_three, g_inner)
    g_hidden = lax.psum_scatter(
        g_hidden.reshape(2, -1, g_hidden.shape[3]), DEVICES, scatter_dimension=1, tiled=True
    ).astype(F32)
    g_hidden_gain = jnp.sum(g_normed * normal_three, 1)
    g_hidden_bias = jnp.sum(g_normed, 1)
    g_stream = grad_out.astype(F32) + norm_back(g_normed * gain_hidden, normal_three, inverse_three)

    g_low = g_stream.astype(BF)
    g_mixed = project(weights_two, [1], [g_low], [BF])[0].reshape(heads, dim, tokens)
    r_cross = Reduction(corner, [(g_low, mixed_two)], True)
    running = [r_cross]
    g_queries = []
    g_keys = []
    g_values = []
    for index, piece in enumerate(pieces):
        inputs, kept = saved_cross[index]
        grads = attend_back(*inputs, kept, cut(g_mixed, index)[None], True, 4, False)
        g_queries.append(grads[0][0, 0])
        g_keys.append(grads[1][0, 0])
        g_values.append(grads[2][0, 0])
    g_queries, g_keys, g_values = tick((g_queries, g_keys, g_values), running)
    g_raw_cross, g_cq_gain = cross_pull(jnp.concatenate(g_queries, 2))
    g_raw_text, g_tk_gain = text_pull(jnp.concatenate(g_keys, 2))
    g_craw = g_raw_cross.astype(BF).reshape(depth, tokens)
    g_pair = [
        g_raw_text.astype(BF).reshape(depth, -1),
        jnp.concatenate(g_values, 2).astype(BF).reshape(depth, -1),
    ]
    g_normed = rebuild(weights_two, [0], [g_craw], F32)
    r_query = Reduction(corner, [(normed_two, g_craw)], False)
    r_text = Reduction(corner, [(text, g) for g in g_pair], True)
    g_normed = tick(g_normed, running)
    running += [r_query, r_text]
    g_cross_gain = jnp.sum(g_normed * normal_two, 1)
    g_cross_bias = jnp.sum(g_normed, 1)
    g_stream = g_stream + norm_back(g_normed * gain_cross, normal_two, inverse_two)

    g_low = g_stream.astype(BF)
    g_mixed = project(weights_one, [3], [g_low], [BF])[0].reshape(heads, dim, tokens)
    g_mixed = tick(g_mixed, running)
    r_attn = Reduction(corner, [(g_low, mixed_one)], False)
    g_parts = []
    for index, piece in enumerate(pieces):
        whole, kept = saved_self[index]
        grad = exchange(
            cut(g_mixed, index).reshape(piece.group, -1, dim, piece.count), piece.group, cols
        )
        part = attend_back(
            none, whole, whole, whole, (0, 1, 2), kept, grad, False, 2, True
        )
        part = tick(part, running)
        if index == 0:
            running.append(r_attn)
        g_parts.append(exchange(part, piece.group, cols))
    g_heads = [
        jnp.concatenate([p[:, i].reshape(heads, dim, -1) for p in g_parts], 2) for i in range(3)
    ]
    g_raw_q, g_q_gain = query_pull(g_heads[0].astype(F32))
    g_raw_k, g_k_gain = key_pull(g_heads[1].astype(F32))
    g_triple = [
        g.reshape(depth, tokens) for g in (g_raw_q.astype(BF), g_raw_k.astype(BF), g_heads[2])
    ]
    g_triple = tick(g_triple, running)
    r_self = [
        Reduction(corner, [(normed_one, g) for g in g_triple[:2]], True),
        Reduction(corner, [(normed_one, g_triple[2])], False),
    ]
    g_normed = rebuild(weights_one, [0, 1, 2], g_triple, F32)
    running += r_self
    g_normed = tick(g_normed, running)
    crossed = g_normed * normal_one
    sums = jnp.stack(
        [
            jnp.stack([jnp.sum(cut(g_normed, i), 1), jnp.sum(cut(crossed, i), 1)], 0)
            for i in range(len(pieces))
        ],
        0,
    )
    which = jnp.stack(
        [jnp.where(jnp.arange(sequences) == p.sequence, 1.0, 0.0) for p in pieces], 0
    )
    g_modul = jnp.sum(which[:, :, None, None] * sums[:, None], 0)
    g_modul = g_modul.reshape(sequences, 2, cols, width).transpose(2, 0, 1, 3)
    g_modul = jnp.sum(lax.all_to_all(g_modul, "col", 0, 0, tiled=True), 0).astype(BF)
    g_stream = g_stream + norm_back(g_normed * scaling, normal_one, inverse_one)

    g_skip_gain = jnp.sum(g_stream * skip_normal, 1)
    g_skip_bias = jnp.sum(g_stream, 1)
    g_joined = norm_back(g_stream * gain_skip, skip_normal, skip_inverse).astype(BF)
    g_joined, g_modul = lax.optimization_barrier((g_joined, g_modul))
    r_skip = Reduction(corner, [(both, g_joined)], True)
    g_both = rebuild_blocks(base, w_skip, width, g_joined)
    late = act
    if custom_mesh():
        g_both, got = lax.optimization_barrier((g_both, r_skip.state[0]))
        here, away = outer(corner, r_skip.pairs, True, got)
        states = [r.state for r in r_self]
        g_both, away, late, states = lax.optimization_barrier((g_both, away, late, states))
        r_skip.stage, r_skip.state = 1, [here, swap(away, "row", 1)]
        for beside, state in zip(r_self, states):
            beside.state = state
            beside.advance()
        late = tick(late, [r_skip])
    g_latents, g_skip = to_features(g_both, pieces, cols, 2, block_rows)
    output = contract(weights_hidden, 1, late, stream, BF)
    result = to_features(output, pieces, cols, 1, width)[0]
    g_modul = shared(after(g_modul, g_skip), "row").reshape(-1, 2, width)
    g_modulation = einsum("sd,ske->dke", embed_rows, g_modul)

    g_gains = jnp.stack(
        [g_skip_gain, g_skip_bias, g_cross_gain, g_cross_bias, g_hidden_gain, g_hidden_bias], 0
    )
    g_gains = g_gains.reshape(6, cols, width).transpose(1, 0, 2)
    g_head = jnp.stack([g_q_gain, g_k_gain, g_cq_gain, g_tk_gain], 0).reshape(1, -1, width)
    g_gains = after(g_gains, g_skip)
    packed = jnp.concatenate([g_gains, jnp.broadcast_to(g_head, (cols, *g_head.shape[1:]))], 1)
    packed = jnp.sum(lax.all_to_all(packed, "col", 0, 0, tiled=True), 0)
    packed = jnp.sum(shared(packed, "row"), 0)
    g_gains = packed[:6]
    g_head = packed[6:].reshape(4, dim)
    return (
        result,
        g_latents,
        g_skip,
        r_skip.result().reshape(2, block_rows, width),
        g_modulation,
        jnp.concatenate([r.result() for r in r_self], 0).transpose(1, 0, 2),
        r_attn.result()[0].T,
        r_query.result()[0],
        r_text.result().transpose(1, 0, 2),
        r_cross.result()[0].T,
        g_hidden[0],
        g_hidden[1].T,
        *[g_gains[i] for i in range(6)],
        *[g_head[i] for i in range(4)],
    )


def solution(mesh):
    return jax.shard_map(
        shards,
        mesh=mesh,
        in_specs=(
            P("col", "row"),
            P("col", "row"),
            P("row", "col"),
            P("row", None, "col"),
            P("row"),
            P(None, "row"),
            P("col", "row"),
            P(None, "row", "col"),
            P("row", None, "col"),
            P("row", None, "col"),
            P("col", "row"),
            P("row", "col"),
            P("row", None, "col"),
            P("col", "row"),
            P("row", "col"),
            P("col", "row"),
            P("col"),
            P("col"),
            P("col"),
            P("col"),
            P("col"),
            P("col"),
            P(),
            P(),
            P(),
            P(),
        ),
        out_specs=(
            P("col", "row"),
            P("col", "row"),
            P("col", "row"),
            P(None, "row", "col"),
            P("row", None, "col"),
            P("row", None, "col"),
            P("col", "row"),
            P("row", "col"),
            P("row", None, "col"),
            P("col", "row"),
            P("row", "col"),
            P("col", "row"),
            P("col"),
            P("col"),
            P("col"),
            P("col"),
            P("col"),
            P("col"),
            P(),
            P(),
            P(),
            P(),
        ),
        check_vma=False,
    )
```

```python
from functools import partial
import math

import jax
import jax.numpy as jnp
from jax import lax
from jax.experimental import pallas as pl
from jax.experimental.pallas import tpu as pltpu
from jax.sharding import PartitionSpec as P

L = 1024
EPSILON = 1e-06
BF = jnp.bfloat16
F32 = jnp.float32
KEYPAD = 128
DEVICES = ("col", "row")
LOG2E = math.log2(math.e)
VMEM = 60 << 20


def einsum(spec, left, right):
    return jnp.einsum(spec, left, right, preferred_element_type=F32)


def dot(left, right, dims):
    return lax.dot_general(left, right, (dims, ((), ())), preferred_element_type=F32)


def params():
    return pltpu.CompilerParams(vmem_limit_bytes=VMEM)


def step_of(count):
    return 256 if count % 256 == 0 else count


def wide(ref, head):
    parts = [ref[s, 0, head] for s in range(ref.shape[0])]
    return parts[0] if len(parts) == 1 else jnp.concatenate(parts, 1)


def valid_keys(length_ref, keys, step):
    return lax.broadcasted_iota(jnp.int32, (keys, step), 0) < length_ref[0]


def attend_kernel(masked, length_ref, q_ref, k_ref, v_ref, o_ref, r_ref, l_ref):
    groups, _, heads, dim, count = q_ref.shape
    step = step_of(count)
    factor = dim ** (-0.5) * LOG2E
    for head in range(heads):
        key = wide(k_ref, head).T
        value = wide(v_ref, head)
        keys = key.shape[0]
        value = jnp.concatenate([value, jnp.ones((8, keys), BF)], 0)
        for place in range(0, groups * count, step):
            group, first = divmod(place, count)
            query = q_ref[group, 0, head, :, first : first + step]
            expo = jnp.exp2(dot(key, query, ((1,), (0,))) * factor)
            if masked:
                expo = jnp.where(valid_keys(length_ref, keys, step), expo, 0.0)
            both = dot(value, expo.astype(BF), ((1,), (0,)))
            total = both[dim : dim + 1]
            mixed = both[:dim] * (1.0 / total)
            high = mixed.astype(BF)
            o_ref[group, head, :, first : first + step] = high
            r_ref[group, head, :, first : first + step] = (mixed - high.astype(F32)).astype(BF)
            l_ref[head, :, place : place + step] = jnp.log2(total)


def attend_back_kernel(
    masked, length_ref, q_ref, k_ref, v_ref, m_ref, r_ref, g_ref, l_ref, *outs
):
    groups, _, heads, dim, count = q_ref.shape
    step = step_of(count)
    scale = dim ** (-0.5)
    for head in range(heads):
        key = wide(k_ref, head)
        keys = key.shape[1]
        turned = key.T
        value = jnp.concatenate([wide(v_ref, head), jnp.ones((8, keys), BF)], 0).T
        g_key = g_value = None
        for place in range(0, groups * count, step):
            group, first = divmod(place, count)
            here = slice(first, first + step)
            query = q_ref[group, 0, head, :, here]
            grad = g_ref[group, head, :, here]
            mixed = m_ref[group, head, :, here].astype(F32)
            mixed = mixed + r_ref[group, head, :, here].astype(F32)
            delta = -jnp.sum(grad.astype(F32) * mixed, 0, keepdims=True)
            high = delta.astype(BF)
            rest = (delta - high.astype(F32)).astype(BF)
            more = jnp.concatenate([grad, high, rest, jnp.zeros((6, step), BF)], 0)
            probs = jnp.exp2(
                dot(turned, query, ((1,), (0,))) * (scale * LOG2E)
                - l_ref[head, :, place : place + step]
            )
            if masked:
                probs = jnp.where(valid_keys(length_ref, keys, step), probs, 0.0)
            product = (probs * dot(value, more, ((1,), (0,)))).astype(BF)
            g_query = dot(key, product, ((1,), (0,))) * scale
            part_value = dot(grad, probs.astype(BF), ((1,), (1,)))
            part_key = dot(query, product, ((1,), (1,)))
            g_value = part_value if g_value is None else g_value + part_value
            g_key = part_key if g_key is None else g_key + part_key
            outs[0][group, 0, head, :, here] = g_query.astype(outs[0].dtype)
        g_key = g_key * scale
        if len(outs) == 1:
            for group in range(groups):
                here = slice(group * count, (group + 1) * count)
                outs[0][group, 1, head] = g_key[:, here].astype(BF)
                outs[0][group, 2, head] = g_value[:, here].astype(BF)
        else:
            outs[1][0, 0, head] = g_key
            outs[2][0, 0, head] = g_value


def costs(heads, queries, keys, dim, products):
    return pl.CostEstimate(
        flops=2 * products * heads * queries * keys * 256,
        transcendentals=heads * queries * keys,
        bytes_accessed=2 * products * heads * dim * (queries + keys),
    )


def head_block(shape, count, kind=0):
    groups, _, _, dim, tokens = shape
    return pl.BlockSpec((groups, 1, count, dim, tokens), lambda h: (0, kind, h, 0, 0))


def mix_block(shape, count):
    groups, _, _, dim, tokens = shape
    return pl.BlockSpec((groups, count, dim, tokens), lambda h: (0, h, 0, 0))


def attend(length, query, key, value, kinds, masked, most):
    groups, _, heads, dim, count = query.shape
    many = math.gcd(heads, most)
    total = groups * count
    keys = key.shape[0] * key.shape[4]
    return pl.pallas_call(
        partial(attend_kernel, masked),
        grid=(heads // many,),
        in_specs=[pl.BlockSpec(memory_space=pltpu.SMEM)]
        + [head_block(a.shape, many, kind) for a, kind in zip((query, key, value), kinds)],
        out_specs=[
            mix_block(query.shape, many),
            mix_block(query.shape, many),
            pl.BlockSpec((many, 1, total), lambda h: (h, 0, 0)),
        ],
        out_shape=[
            jax.ShapeDtypeStruct((groups, heads, dim, count), BF),
            jax.ShapeDtypeStruct((groups, heads, dim, count), BF),
            jax.ShapeDtypeStruct((heads, 1, total), F32),
        ],
        cost_estimate=costs(heads, total, keys, dim, 2),
        compiler_params=params(),
        name="attend",
    )(length, query, key, value)


def attend_back(length, query, key, value, kinds, kept, grad, masked, most, stacked):
    mixed, rest, logs = kept
    groups, _, heads, dim, count = query.shape
    many = math.gcd(heads, most)
    total = groups * count
    keys = key.shape[0] * key.shape[4]
    if stacked:
        out_specs = pl.BlockSpec((groups, 3, many, dim, count), lambda h: (0, 0, h, 0, 0))
        out_shape = jax.ShapeDtypeStruct((groups, 3, heads, dim, count), BF)
    else:
        out_specs = [head_block(a.shape, many) for a in (query, key, value)]
        out_shape = [jax.ShapeDtypeStruct(a.shape, F32) for a in (query, key, value)]
    return pl.pallas_call(
        partial(attend_back_kernel, masked),
        grid=(heads // many,),
        in_specs=[pl.BlockSpec(memory_space=pltpu.SMEM)]
        + [head_block(a.shape, many, kind) for a, kind in zip((query, key, value), kinds)]
        + [mix_block(query.shape, many)] * 3
        + [pl.BlockSpec((many, 1, total), lambda h: (h, 0, 0))],
        out_specs=out_specs,
        out_shape=out_shape,
        cost_estimate=costs(heads, total, keys, dim, 5),
        compiler_params=params(),
        name="attend_back",
    )(length, query, key, value, mixed, rest, grad, logs)


def work(rows, depth, tokens, moved):
    return pl.CostEstimate(
        flops=2 * rows * depth * tokens,
        transcendentals=0,
        bytes_accessed=moved,
    )


def lanes(width):
    return -(-width // 128) * 128


def full(shape):
    return pl.BlockSpec(shape, lambda *_: (0,) * len(shape))


def project(weight, kinds, values, dtypes, joined=False):
    _, cols, depth, width = weight.shape
    tokens = values[0].shape[1]
    outs = 1 if joined else len(kinds)

    def kernel(*refs):
        blocks = refs[: len(kinds)]
        given = refs[len(kinds) : -outs]
        total = None
        for index, block in enumerate(blocks):
            part = dot(block[0, 0], given[index % len(given)][...], ((0,), (0,)))
            if not joined:
                refs[index - outs][...] = part.astype(dtypes[index])
            total = part if total is None else total + part
        if joined:
            refs[-1][...] = total.astype(dtypes[0])

    return pl.pallas_call(
        kernel,
        grid=(cols,),
        in_specs=[
            pl.BlockSpec((1, 1, depth, width), partial(lambda k, c: (k, c, 0, 0), kind))
            for kind in kinds
        ]
        + [full(v.shape) for v in values],
        out_specs=[pl.BlockSpec((width, tokens), lambda c: (c, 0))] * outs,
        out_shape=[jax.ShapeDtypeStruct((cols * width, tokens), dtypes[i]) for i in range(outs)],
        cost_estimate=work(len(kinds) * cols * width, depth, tokens, 8 * depth * tokens),
        compiler_params=params(),
        name="project",
    )(*([weight] * len(kinds)), *values)


def rebuild(weight, kinds, values, dtype):
    _, cols, depth, width = weight.shape
    tokens = values[0].shape[1]
    tile = depth // 4

    def kernel(*refs):
        total = None
        for block, given in zip(refs[: len(kinds)], refs[len(kinds) : -1]):
            for col in range(cols):
                part = dot(block[0, col], given[col * width : (col + 1) * width, :], ((1,), (0,)))
                total = part if total is None else total + part
        refs[-1][...] = total.astype(dtype)

    return pl.pallas_call(
        kernel,
        grid=(4,),
        in_specs=[
            pl.BlockSpec((1, cols, tile, width), partial(lambda k, j: (k, 0, j, 0), kind))
            for kind in kinds
        ]
        + [full(v.shape) for v in values],
        out_specs=pl.BlockSpec((tile, tokens), lambda j: (j, 0)),
        out_shape=jax.ShapeDtypeStruct((depth, tokens), dtype),
        cost_estimate=work(depth, len(kinds) * cols * width, tokens, 8 * depth * tokens),
        compiler_params=params(),
        name="rebuild",
    )(*([weight] * len(kinds)), *values)


def project_blocks(base, blocks, width, values):
    many = len(blocks)
    depth, broad = blocks[0].shape
    tokens = values.shape[1]
    tile = depth // 4

    def kernel(base_ref, *refs):
        values_ref, out_ref = refs[many:]

        @pl.when(pl.program_id(0) == 0)
        def _():
            out_ref[...] = jnp.zeros_like(out_ref)

        for index in range(many):
            here = pl.ds(pl.multiple_of((index ^ base_ref[0]) * width, width), width)
            out_ref[here, :] += dot(refs[index][...], values_ref[...], ((0,), (0,)))[:width]

    return pl.pallas_call(
        kernel,
        grid_spec=pltpu.PrefetchScalarGridSpec(
            num_scalar_prefetch=1,
            grid=(4,),
            in_specs=[pl.BlockSpec((tile, broad), lambda j, b: (j, 0))] * many
            + [pl.BlockSpec((tile, tokens), lambda j, b: (j, 0))],
            out_specs=pl.BlockSpec((many * width, tokens), lambda j, b: (0, 0)),
        ),
        out_shape=jax.ShapeDtypeStruct((many * width, tokens), F32),
        cost_estimate=work(many * width, depth, tokens, 4 * depth * tokens),
        compiler_params=params(),
        name="project_blocks",
    )(base, *blocks, values)


def rebuild_blocks(base, blocks, width, values):
    many = len(blocks)
    depth, broad = blocks[0].shape
    tokens = values.shape[1]
    tile = depth // 4

    def kernel(base_ref, *refs):
        values_ref, out_ref = refs[many:]
        total = None
        for index in range(many):
            here = pl.ds(pl.multiple_of((index ^ base_ref[0]) * width, width), width)
            part = dot(refs[index][:, :width], values_ref[here, :], ((1,), (0,)))
            total = part if total is None else total + part
        out_ref[...] = total.astype(BF)

    return pl.pallas_call(
        kernel,
        grid_spec=pltpu.PrefetchScalarGridSpec(
            num_scalar_prefetch=1,
            grid=(4,),
            in_specs=[pl.BlockSpec((tile, broad), lambda j, b: (j, 0))] * many
            + [pl.BlockSpec(values.shape, lambda j, b: (0, 0))],
            out_specs=pl.BlockSpec((tile, tokens), lambda j, b: (j, 0)),
        ),
        out_shape=jax.ShapeDtypeStruct((depth, tokens), BF),
        cost_estimate=work(many * width, depth, tokens, 4 * depth * tokens),
        compiler_params=params(),
        name="rebuild_blocks",
    )(base, *blocks, values)


def outer(place, pairs, across, got=None):
    cols = lax.axis_size("col")
    lefts = []
    for left, _ in pairs:
        if not any(left is other for other in lefts):
            lefts.append(left)
    which = [next(i for i, l in enumerate(lefts) if l is left) for left, _ in pairs]
    rights = [right for _, right in pairs]
    many = len(pairs)
    rows, tokens = lefts[0].shape
    width = rights[0].shape[0] // cols
    broad = lanes(width)
    chunk = rows // 8
    flip = 1 if got is None else 0

    def kernel(place_ref, *refs):
        left_refs = refs[: len(lefts)]
        right_refs = refs[len(lefts) : len(lefts) + many]
        rest = refs[len(lefts) + many :]
        for index in range(many):
            right = right_refs[index][...]
            if broad > width:
                right = jnp.concatenate([right, jnp.zeros((broad - width, tokens), BF)], 0)
            part = dot(left_refs[which[index]][...], right, ((1,), (1,)))
            if got is None:
                rest[0][index, 0] = part.astype(BF)
            elif not across:
                part = (part + rest[0][index, 0].astype(F32)).astype(BF)

                @pl.when(pl.program_id(0) == place_ref[2])
                def _():
                    rest[1][index] = part.reshape(4, 2, chunk, broad)

                @pl.when(pl.program_id(0) != place_ref[2])
                def _():
                    rest[2][index] = part.reshape(4, 2, chunk, broad)
            else:
                part = (part + rest[0][index, 0].astype(F32)).astype(BF)
                part = part.reshape(4, 2, chunk, broad)

                @pl.when(place_ref[1] == 0)
                def _():
                    rest[1][index, 0] = part[:, 0]
                    rest[2][index, 0] = part[:, 1]

                @pl.when(place_ref[1] != 0)
                def _():
                    rest[1][index, 0] = part[:, 1]
                    rest[2][index, 0] = part[:, 0]

    whole = pl.BlockSpec((many, 1, rows, broad), lambda y, place: (0, y, 0, 0))
    piece = pl.BlockSpec((many, 1, 4, chunk, broad), lambda y, place: (0, y, 0, 0, 0))
    all_rows = pl.BlockSpec((many, 4, 2, chunk, broad), lambda y, place: (0, 0, 0, 0, 0))
    if got is None:
        given, out_specs = [], whole
        out_shape = jax.ShapeDtypeStruct((many, cols // 2, rows, broad), BF)
    else:
        given, out_specs = [got], [piece, piece] if across else [all_rows, all_rows]
        shape = (many, cols // 2, 4, chunk, broad) if across else (many, 4, 2, chunk, broad)
        out_shape = [jax.ShapeDtypeStruct(shape, BF)] * 2
    return pl.pallas_call(
        kernel,
        grid_spec=pltpu.PrefetchScalarGridSpec(
            num_scalar_prefetch=1,
            grid=(cols // 2,),
            in_specs=[pl.BlockSpec((rows, tokens), lambda y, place: (0, 0)) for _ in lefts]
            + [
                pl.BlockSpec((width, tokens), lambda y, place: (2 * y + (place[0] ^ flip), 0))
                for _ in rights
            ]
            + [whole] * len(given),
            out_specs=out_specs,
        ),
        out_shape=out_shape,
        cost_estimate=work(
            rows, tokens, many * cols // 2 * broad, 2 * rows * cols * broad * many
        ),
        compiler_params=params(),
        name="outer",
    )(place, *lefts, *rights, *given)


def expand(weight, kind, values):
    _, many, depth, hidden = weight.shape
    tokens = values.shape[1]
    tile = 384 if hidden % 384 == 0 else hidden
    slope = 0.79788456
    cubic = 0.044715

    def kernel(weight_ref, values_ref, act_ref, slope_ref):
        for index in range(many):
            inner = dot(weight_ref[0, index], values_ref[...], ((0,), (0,)))
            square = inner * inner
            bent = jnp.tanh(inner * (slope + slope * cubic * square))
            half = 0.5 + 0.5 * bent
            act_ref[index] = (inner * half).astype(BF)
            rise = slope + 3.0 * slope * cubic * square
            slope_ref[index] = (half + 0.5 * inner * (1.0 - bent * bent) * rise).astype(BF)

    return pl.pallas_call(
        kernel,
        grid=(hidden // tile,),
        in_specs=[
            pl.BlockSpec((1, many, depth, tile), lambda j: (kind, 0, 0, j)),
            full(values.shape),
        ],
        out_specs=[pl.BlockSpec((many, tile, tokens), lambda j: (0, j, 0))] * 2,
        out_shape=[jax.ShapeDtypeStruct((many, hidden, tokens), BF)] * 2,
        cost_estimate=work(many * hidden, depth, tokens, 3 * many * hidden * depth),
        compiler_params=params(),
        name="expand",
    )(weight, values)


def expand_back(weight, kind, values, slopes):
    _, many, depth, hidden = weight.shape
    tokens = values.shape[1]
    tile = 384 if hidden % 384 == 0 else hidden

    def kernel(weight_ref, values_ref, slope_ref, out_ref):
        for index in range(many):
            part = dot(weight_ref[0, index], values_ref[...], ((0,), (0,)))
            out_ref[index] = (part * slope_ref[index].astype(F32)).astype(BF)

    return pl.pallas_call(
        kernel,
        grid=(hidden // tile,),
        in_specs=[
            pl.BlockSpec((1, many, depth, tile), lambda j: (kind, 0, 0, j)),
            full(values.shape),
            pl.BlockSpec((many, tile, tokens), lambda j: (0, j, 0)),
        ],
        out_specs=pl.BlockSpec((many, tile, tokens), lambda j: (0, j, 0)),
        out_shape=jax.ShapeDtypeStruct((many, hidden, tokens), BF),
        cost_estimate=work(many * hidden, depth, tokens, 3 * many * hidden * depth),
        compiler_params=params(),
        name="expand_back",
    )(weight, values, slopes)


def contract(weight, kind, values, added, dtype):
    _, many, depth, hidden = weight.shape
    tokens = values.shape[2]
    tile = depth // 4
    extra = [] if added is None else [added]

    def kernel(weight_ref, values_ref, *refs):
        total = refs[0][...] if extra else None
        for index in range(many):
            part = dot(weight_ref[0, index], values_ref[index], ((1,), (0,)))
            total = part if total is None else total + part
        refs[-1][...] = total.astype(dtype)

    line = pl.BlockSpec((tile, tokens), lambda j: (j, 0))
    return pl.pallas_call(
        kernel,
        grid=(4,),
        in_specs=[
            pl.BlockSpec((1, many, tile, hidden), lambda j: (kind, 0, j, 0)),
            full(values.shape),
        ]
        + [line] * len(extra),
        out_specs=line,
        out_shape=jax.ShapeDtypeStruct((depth, tokens), dtype),
        cost_estimate=work(depth, many * hidden, tokens, 3 * many * hidden * depth),
        compiler_params=params(),
        name="contract",
    )(weight, values, *extra)


def hidden_outer(grad_out, act, normed, grad_inner):
    many, hidden, tokens = act.shape
    depth = grad_out.shape[0]
    parts = 2 if hidden % 256 == 0 else 1
    tile = hidden // parts

    def kernel(out_ref, act_ref, normed_ref, inner_ref, grad_ref):
        kind = pl.program_id(0)

        @pl.when(kind == 0)
        def _():
            grad_ref[0, 0] = dot(normed_ref[...], inner_ref[0], ((1,), (1,))).astype(BF)

        @pl.when(kind == 1)
        def _():
            grad_ref[0, 0] = dot(out_ref[...], act_ref[0], ((1,), (1,))).astype(BF)

    return pl.pallas_call(
        kernel,
        grid=(2, many, parts),
        in_specs=[
            pl.BlockSpec((depth, tokens), lambda s, p, j: (0, 0)),
            pl.BlockSpec((1, tile, tokens), lambda s, p, j: (s * p, s * j, 0)),
            pl.BlockSpec((depth, tokens), lambda s, p, j: (0, 0)),
            pl.BlockSpec(
                (1, tile, tokens),
                lambda s, p, j: (p + s * (many - 1 - p), j + s * (parts - 1 - j), 0),
            ),
        ],
        out_specs=pl.BlockSpec((1, 1, depth, tile), lambda s, p, j: (s, p, 0, j)),
        out_shape=jax.ShapeDtypeStruct((2, many, depth, hidden), BF),
        cost_estimate=work(2 * depth, tokens, many * hidden, 5 * many * depth * hidden),
        compiler_params=params(),
        name="hidden_outer",
    )(grad_out, act, normed, grad_inner)


def assemble(place, own, got, middle=None):
    rows, width = own.shape[-2:]

    def kernel(place_ref, own_ref, got_ref, out_ref):
        @pl.when(pl.program_id(0) == place_ref[1])
        def _():
            out_ref[0, 0] = own_ref[...].reshape(rows, width)

        @pl.when(pl.program_id(0) != place_ref[1])
        def _():
            out_ref[0, 0] = got_ref[...].reshape(rows, width)

    def spec(ours):
        def index(x, z, place):
            phase = place[1] if ours else 1 - place[1]
            inside = (x == phase).astype(jnp.int32)
            level = (inside * z + (1 - inside) * 3 * (1 - phase)) ^ place[0]
            return (level, 0, 0) if middle is None else (level, middle, 0, 0)

        shape = (1, rows, width) if middle is None else (1, 1, rows, width)
        return pl.BlockSpec(shape, index)

    return pl.pallas_call(
        kernel,
        grid_spec=pltpu.PrefetchScalarGridSpec(
            num_scalar_prefetch=1,
            grid=(2, 4),
            in_specs=[spec(True), spec(False)],
            out_specs=pl.BlockSpec((1, 1, rows, width), lambda x, z, place: (z, x, 0, 0)),
        ),
        out_shape=jax.ShapeDtypeStruct((4, 2, rows, width), BF),
        cost_estimate=work(1, 1, 1, 32 * rows * width),
        name="assemble",
    )(place, own, got).reshape(8 * rows, width)


def normalize(values):
    average = jnp.mean(values, 0, keepdims=True)
    centred = values - average
    inverse = lax.rsqrt(jnp.mean(centred * centred, 0, keepdims=True) + EPSILON)
    return centred * inverse, inverse


def norm_back(grad, normal, inverse):
    average = jnp.mean(grad, 0, keepdims=True)
    crossed = jnp.mean(grad * normal, 0, keepdims=True)
    return inverse * (grad - average - normal * crossed)


def head_norm(values, gain):
    average = jnp.mean(values, 1, keepdims=True)
    centred = values - average
    variance = jnp.mean(centred * centred, 1, keepdims=True)
    return centred * lax.rsqrt(variance + EPSILON) * gain[None, :, None]


def rope_tables(places, head_dim):
    quarter = head_dim // 4
    freqs = jnp.exp(jnp.arange(quarter, dtype=F32) * (-4.0 * math.log(10000.0) / head_dim))
    rows = freqs[:, None] * places[0].astype(F32)[None, :]
    cols = freqs[:, None] * places[1].astype(F32)[None, :]
    angles = jnp.concatenate([rows, rows, cols, cols], 0)
    return jnp.cos(angles), jnp.sin(angles)


def rotate(values):
    quarter = values.shape[1] // 4
    one, two, three, four = (values[:, i * quarter : (i + 1) * quarter] for i in range(4))
    return jnp.concatenate([-two, one, -four, three], 1)


class Piece:
    def __init__(self, start, count, group, sequence):
        self.start = start
        self.count = count
        self.group = group
        self.sequence = sequence


def pieces_of(cols, sequences):
    mine = lax.axis_index("col")
    if cols == 4 and sequences == 3:
        return [
            Piece(0, L // 2, 2, mine // 2),
            Piece(2 * L, L // 4, 4, jnp.int32(2)),
        ]
    return [Piece(s * L, L // cols, cols, jnp.int32(s)) for s in range(sequences)]


def groups_of(size, cols):
    return [list(range(i, i + size)) for i in range(0, cols, size)]


def exchange(values, size, cols):
    if size == cols:
        return lax.all_to_all(values, "col", 0, 0, tiled=True)
    return lax.all_to_all(
        values, "col", 0, 0, tiled=True, axis_index_groups=groups_of(size, cols)
    )


def cut_size(pieces):
    return math.gcd(*(p.count for p in pieces), *(p.start for p in pieces))


def locate(pieces, unit, block):
    device = inside = None
    at = 0
    for piece in pieces:
        each = piece.count // unit
        rest = block - piece.start // unit
        there = (rest // each, at + rest % each)
        if device is None:
            device, inside = there
        else:
            later = (rest >= 0).astype(jnp.int32)
            device = later * there[0] + (1 - later) * device
            inside = later * there[1] + (1 - later) * inside
        at += each
    return device, inside


def to_tokens(arrays, pieces, cols, rows):
    width, tokens = arrays[0].shape
    kinds = len(arrays)
    unit = cut_size(pieces)
    total = sum(p.count for p in pieces)
    if unit % 128:
        values = jnp.stack([a.reshape(-1, rows, tokens) for a in arrays], 1).astype(BF)
        values = values.reshape(kinds * width, tokens)
        parts = [
            jnp.concatenate(
                [values[:, p.start + j * p.count : p.start + (j + 1) * p.count] for p in pieces], 1
            )
            for j in range(cols)
        ]
        dealt = jnp.stack(parts, 0)
    else:

        def kernel(*refs):
            for kind in range(kinds):
                for at in range(0, width, rows):
                    to = at * kinds + kind * rows
                    refs[-1][0, to : to + rows] = refs[kind][at : at + rows].astype(BF)

        def index(block):
            device, inside = locate(pieces, unit, block)
            return (device, 0, inside)

        dealt = pl.pallas_call(
            kernel,
            grid=(tokens // unit,),
            in_specs=[pl.BlockSpec((width, unit), lambda b: (0, b))] * kinds,
            out_specs=pl.BlockSpec((1, kinds * width, unit), index),
            out_shape=jax.ShapeDtypeStruct((cols, kinds * width, total), BF),
            cost_estimate=pl.CostEstimate(
                flops=0, transcendentals=0, bytes_accessed=4 * kinds * width * tokens
            ),
            name="deal",
        )(*arrays)
    got = exchange(dealt, cols, cols)
    return got.reshape(-1, total)


def to_features(values, pieces, cols, kinds, rows):
    got = exchange(values.reshape(cols, -1, values.shape[1]), cols, cols)
    unit = cut_size(pieces)
    width = got.shape[1] // kinds
    tokens = cols * got.shape[2]
    if unit % 128:
        parts = []
        at = 0
        for piece in pieces:
            parts += [got[j, :, at : at + piece.count] for j in range(cols)]
            at += piece.count
        whole = jnp.concatenate(parts, 1).astype(F32).reshape(-1, kinds, rows, tokens)
        return [whole[:, kind].reshape(width, tokens) for kind in range(kinds)]

    def kernel(got_ref, *refs):
        for kind in range(kinds):
            for at in range(0, width, rows):
                start = at * kinds + kind * rows
                refs[kind][at : at + rows] = got_ref[0, start : start + rows].astype(F32)

    def index(block):
        device, inside = locate(pieces, unit, block)
        return (device, 0, inside)

    return pl.pallas_call(
        kernel,
        grid=(tokens // unit,),
        in_specs=[pl.BlockSpec((1, kinds * width, unit), index)],
        out_specs=[pl.BlockSpec((width, unit), lambda b: (0, b))] * kinds,
        out_shape=[jax.ShapeDtypeStruct((width, tokens), F32)] * kinds,
        cost_estimate=pl.CostEstimate(
            flops=0, transcendentals=0, bytes_accessed=6 * kinds * width * tokens
        ),
        name="undeal",
    )(got)


def shared(values, axis):
    size = lax.axis_size(axis)
    return lax.all_to_all(
        jnp.broadcast_to(values[None], (size, *values.shape)), axis, 0, 0, tiled=True
    )


def swap(values, axis, bit):
    size = lax.axis_size(axis)
    return lax.ppermute(values, axis, [(i, i ^ bit) for i in range(size)])


def custom_mesh():
    return (lax.axis_size("row"), lax.axis_size("col")) == (8, 4)


def gather_weights(blocks):
    cols = lax.axis_size("col")
    most = max(block.shape[0] for block in blocks)
    padded = [jnp.pad(b, ((0, most - b.shape[0]), (0, 0))) for b in blocks]
    whole = lax.all_gather(jnp.stack(padded, 0), DEVICES, axis=1, tiled=True)
    return whole.reshape(len(blocks), cols, -1, blocks[0].shape[1])


class Gathering:
    last = 4

    def __init__(self, block, up, place):
        self.up = up
        self.place = place
        self.stage = 0
        self.state = [block]
        if not custom_mesh():
            cols = lax.axis_size("col")
            whole = lax.all_gather(block, DEVICES, axis=0, tiled=True)
            self.state = list(whole.reshape(cols, -1, block.shape[1]))
            self.stage = self.last

    def levels(self, block):
        return [block] + [swap(block, "row", 2 * level) for level in (1, 2, 3)]

    def advance(self):
        state = self.state
        self.stage += 1
        if self.stage == 1:
            self.state = [state[0], swap(state[0], "col", 2)] if self.up else self.levels(state[0])
        elif self.stage == 2:
            stack = jnp.stack(state, 0)
            self.state = self.levels(stack) if self.up else [stack, swap(stack, "col", 2)]
        elif self.stage == 3 and self.up:
            stack = jnp.stack(state, 0)
            self.state = [stack, swap(stack, "row", 1)]
        elif self.stage == 3:
            self.state = state + [swap(a, "row", 1) for a in state]
        else:
            if self.up:
                mine, other = (assemble(self.place, *state, k) for k in (0, 1))
            else:
                mine = assemble(self.place, state[0], state[2])
                other = assemble(self.place, state[1], state[3])
            self.state = [mine, swap(mine, "col", 1), other, swap(other, "col", 1)]

    def result(self):
        while self.stage < self.last:
            self.advance()
        return self.state


def pick(values, axis, index):
    return lax.dynamic_index_in_dim(values, index, axis, False)


def add(left, right):
    return (left.astype(F32) + right.astype(F32)).astype(BF)


class Reduction:
    last = 4

    def __init__(self, place, pairs, across):
        self.place = place
        self.across = across
        self.pairs = pairs
        self.width = pairs[0][1].shape[0] // lax.axis_size("col")
        self.stage = 0
        if custom_mesh():
            self.state = [swap(outer(place, pairs, across), "col", 1)]
            return
        self.stage = self.last
        cols = lax.axis_size("col")
        whole = jnp.stack(
            [einsum("kt,cnt->ckn", a, b.reshape(cols, -1, b.shape[1])) for a, b in pairs], 0
        )
        flat = whole.reshape(len(pairs), -1, whole.shape[3]).astype(BF)
        self.state = [lax.psum_scatter(flat, DEVICES, scatter_dimension=1, tiled=True)]

    def advance(self):
        state = self.state
        self.stage += 1
        if self.stage == 1:
            here, away = outer(self.place, self.pairs, self.across, state[0])
            self.state = [here, swap(away, "row", 1) if self.across else swap(away, "col", 2)]
        elif self.stage == 2:
            axis, index = (1, self.place[2]) if self.across else (2, self.place[1])
            away = add(*(pick(a, axis, 1 - index) for a in state))
            here = add(*(pick(a, axis, index) for a in state))
            self.state = [here, swap(away, "col", 2) if self.across else swap(away, "row", 1)]
        elif self.stage == 3:
            level = lax.axis_index("row") // 2
            total = add(*state)
            self.state = [pick(total, 1, level)] + [
                swap(pick(total, 1, level ^ other), "row", 2 * other) for other in (1, 2, 3)
            ]
        else:
            total = state[0].astype(F32)
            for other in state[1:]:
                total = total + other.astype(F32)
            self.state = [total[..., : self.width]]

    def result(self):
        while self.stage < self.last:
            self.advance()
        return self.state[0].astype(F32)


def tick(values, running):
    active = [r for r in running if r.stage < r.last]
    if active:
        values, states = lax.optimization_barrier((values, [r.state for r in active]))
        for beside, state in zip(active, states):
            beside.state = state
            beside.advance()
    return values


def after(values, done):
    return lax.optimization_barrier((values, done))[0]


def shards(
    latents,
    skip_input,
    condition,
    text_states,
    text_lengths,
    positions,
    out_grad,
    skip_weight,
    modulation,
    self_inputs,
    self_output,
    cross_query,
    cross_keyvalue,
    cross_output,
    expand_weight,
    reduce_weight,
    skip_gain,
    skip_bias,
    cross_gain,
    cross_bias,
    hidden_gain,
    hidden_bias,
    query_gain,
    key_gain,
    cross_query_gain,
    text_key_gain,
):
    cols = lax.axis_size("col")
    rows = lax.axis_size("row")
    mine = lax.axis_index("col")
    my_row = lax.axis_index("row")
    width, row_tokens = latents.shape
    depth = width * cols
    dim = query_gain.shape[0]
    heads = depth // dim
    sequences = row_tokens // L
    tokens = row_tokens // cols
    texts = text_states.shape[1]
    keys = -(-texts // KEYPAD) * KEYPAD
    pieces = pieces_of(cols, sequences)
    starts = [sum(p.count for p in pieces[:i]) for i in range(len(pieces))]
    place = jnp.stack([my_row // 2, my_row % 2]).astype(jnp.int32)
    corner = jnp.stack([mine % 2, my_row % 2, mine // 2]).astype(jnp.int32)
    base = (mine if custom_mesh() else jnp.zeros_like(mine)).astype(jnp.int32)[None]

    def cut(values, index):
        return values[..., starts[index] : starts[index] + pieces[index].count]

    block_rows = depth // rows
    both = to_tokens([latents, skip_input], pieces, cols, block_rows)

    weights = gather_weights(
        [
            *(self_inputs[:, i] for i in range(3)),
            self_output.T,
            cross_query,
            cross_output.T,
            *(cross_keyvalue[:, i] for i in range(2)),
        ]
    )
    skip_block = jnp.concatenate([skip_weight[0], skip_weight[1]], 0)
    skip_block = jnp.pad(skip_block, ((0, 0), (0, lanes(width) - width)))
    w_skip = Gathering(skip_block, False, place).result()
    weights_hidden = gather_weights([expand_weight, reduce_weight.T])

    places = jnp.concatenate(
        [
            lax.dynamic_slice_in_dim(positions, p.start + mine * p.count, p.count, 1)
            for p in pieces
        ],
        1,
    )

    embed = jax.nn.silu(after(condition, both).astype(F32)).astype(BF)
    embed = shared(embed, "row").reshape(-1, width)
    embed = shared(embed, "col").transpose(1, 0, 2).reshape(-1, depth)
    embed_rows = lax.dynamic_slice_in_dim(embed, my_row * block_rows, block_rows, 1)
    modul = einsum("sd,dke->ske", embed_rows, modulation).reshape(rows, sequences, 2, width)
    modul = jnp.sum(lax.all_to_all(modul, "row", 0, 0, tiled=True), 0)
    gains = jnp.stack(
        [skip_gain, skip_bias, cross_gain, cross_bias, hidden_gain, hidden_bias], 0
    )
    table = jnp.concatenate([gains, modul.reshape(-1, width)], 0)
    table = shared(table, "col").transpose(1, 0, 2).reshape(-1, depth)
    modul = table[6:].reshape(sequences, 2, depth)
    chosen = [lax.dynamic_index_in_dim(modul, p.sequence, 0, False) for p in pieces]
    columns = lax.optimization_barrier(jnp.concatenate([table[:6], *chosen], 0)).T
    gain_skip, bias_skip, gain_cross, bias_cross, gain_hidden, bias_hidden = (
        columns[:, i : i + 1] for i in range(6)
    )
    token_index = lax.broadcasted_iota(jnp.int32, (1, tokens), 1)

    def per_token(which):
        result = columns[:, 6 + which : 7 + which]
        for index in range(1, len(pieces)):
            column = columns[:, 6 + 2 * index + which : 7 + 2 * index + which]
            result = jnp.where(token_index >= starts[index], column, result)
        return jnp.broadcast_to(result, (depth, tokens))

    shifting = per_token(0)
    scaling = 1.0 + per_token(1)

    text = shared(jnp.pad(after(text_states, both), ((0, 0), (0, keys - texts), (0, 0))), "col")
    both, text = lax.optimization_barrier((both, text))
    joined = project_blocks(base, w_skip, width, both)
    skip_normal, skip_inverse = normalize(joined)
    stream = skip_normal * gain_skip + bias_skip
    normal_one, inverse_one = normalize(stream)
    normed_one = (normal_one * scaling + shifting).astype(BF)
    raw = project(weights, [0, 1, 2], [normed_one], [F32, F32, BF])
    raw = [r.reshape(heads, dim, tokens) for r in raw]
    cosine, sine = rope_tables(places, dim)

    def self_piece(value, gain):
        normal = head_norm(value, gain)
        return normal * cosine[None] + rotate(normal) * sine[None]

    rot_query, query_pull = jax.vjp(self_piece, raw[0], query_gain)
    rot_key, key_pull = jax.vjp(self_piece, raw[1], key_gain)
    triple = [rot_query.astype(BF), rot_key.astype(BF), raw[2]]

    def to_heads(parts, index):
        size = pieces[index].group
        split = [cut(p, index).reshape(size, heads // size, dim, -1) for p in parts]
        return exchange(jnp.stack(split, 1), size, cols)

    none = jnp.zeros((1,), jnp.int32)
    saved_self = []
    mixed_parts = []
    for index, piece in enumerate(pieces):
        whole = to_heads(triple, index)
        kept = attend(none, whole, whole, whole, (0, 1, 2), False, 2)
        saved_self.append((whole, kept))
        mixed_parts.append(exchange(kept[0], piece.group, cols).reshape(depth, -1))
    mixed_one = jnp.concatenate(mixed_parts, 1)
    text = after(text, mixed_one)
    stream = stream + rebuild(weights, [3], [mixed_one], F32)
    normal_two, inverse_two = normalize(stream)
    normed_two = (normal_two * gain_cross + bias_cross).astype(BF)
    raw_cross = project(weights, [4], [normed_two], [F32])[0].reshape(heads, dim, tokens)
    norm_query, cross_pull = jax.vjp(head_norm, raw_cross, cross_query_gain)
    text = jnp.concatenate(
        [lax.dynamic_index_in_dim(text, p.sequence, 1, False) for p in pieces], 1
    )
    text = text.transpose(0, 2, 1).reshape(-1, len(pieces) * keys)
    text_rows = text.shape[0] // rows
    text_wide = jnp.pad(
        text.reshape(rows, text_rows, -1), ((0, 0), (0, block_rows - text_rows), (0, 0))
    ).reshape(depth, -1)
    raw_text, value_two = project(weights, [6, 7], [text_wide], [F32, BF])
    norm_key, text_pull = jax.vjp(head_norm, raw_text.reshape(heads, dim, -1), text_key_gain)
    query_two = norm_query.astype(BF)
    key_two = norm_key.astype(BF)
    value_two = value_two.reshape(heads, dim, -1)
    saved_cross = []
    mixed_parts = []
    for index, piece in enumerate(pieces):
        length = lax.dynamic_index_in_dim(text_lengths, piece.sequence, 0, True)
        here = slice(index * keys, (index + 1) * keys)
        inputs = [cut(query_two, index), key_two[:, :, here], value_two[:, :, here]]
        inputs = [length] + [a[None, None] for a in inputs] + [(0, 0, 0)]
        kept = attend(*inputs, True, 4)
        saved_cross.append((inputs, kept))
        mixed_parts.append(kept[0].reshape(depth, -1))
    mixed_two = jnp.concatenate(mixed_parts, 1)
    stream = stream + rebuild(weights, [5], [mixed_two], F32)
    normal_three, inverse_three = normalize(stream)
    normed_three = (normal_three * gain_hidden + bias_hidden).astype(BF)
    grad_out = to_tokens([after(out_grad, joined)], pieces, cols, width)
    act, slopes = expand(weights_hidden, 0, normed_three)

    g_inner = expand_back(weights_hidden, 1, grad_out, slopes)
    g_normed = contract(weights_hidden, 0, g_inner, None, F32)
    g_hidden = hidden_outer(grad_out, act, normed_three, g_inner)
    g_hidden = lax.psum_scatter(
        g_hidden.reshape(2, -1, g_hidden.shape[3]), DEVICES, scatter_dimension=1, tiled=True
    ).astype(F32)
    g_hidden_gain = jnp.sum(g_normed * normal_three, 1)
    g_hidden_bias = jnp.sum(g_normed, 1)
    g_stream = grad_out.astype(F32) + norm_back(g_normed * gain_hidden, normal_three, inverse_three)

    g_low = g_stream.astype(BF)
    g_mixed = project(weights, [5], [g_low], [BF])[0].reshape(heads, dim, tokens)
    r_cross = Reduction(corner, [(g_low, mixed_two)], True)
    running = [r_cross]
    g_queries = []
    g_keys = []
    g_values = []
    for index, piece in enumerate(pieces):
        inputs, kept = saved_cross[index]
        grads = attend_back(*inputs, kept, cut(g_mixed, index)[None], True, 4, False)
        g_queries.append(grads[0][0, 0])
        g_keys.append(grads[1][0, 0])
        g_values.append(grads[2][0, 0])
    g_queries, g_keys, g_values = tick((g_queries, g_keys, g_values), running)
    g_raw_cross, g_cq_gain = cross_pull(jnp.concatenate(g_queries, 2))
    g_raw_text, g_tk_gain = text_pull(jnp.concatenate(g_keys, 2))
    g_craw = g_raw_cross.astype(BF).reshape(depth, tokens)
    g_pair = [
        g_raw_text.astype(BF).reshape(depth, -1),
        jnp.concatenate(g_values, 2).astype(BF).reshape(depth, -1),
    ]
    g_normed = rebuild(weights, [4], [g_craw], F32)
    r_query = Reduction(corner, [(normed_two, g_craw)], False)
    r_text = Reduction(corner, [(text, g) for g in g_pair], True)
    g_normed = tick(g_normed, running)
    running += [r_query, r_text]
    g_cross_gain = jnp.sum(g_normed * normal_two, 1)
    g_cross_bias = jnp.sum(g_normed, 1)
    g_stream = g_stream + norm_back(g_normed * gain_cross, normal_two, inverse_two)

    g_low = g_stream.astype(BF)
    g_mixed = project(weights, [3], [g_low], [BF])[0].reshape(heads, dim, tokens)
    g_mixed = tick(g_mixed, running)
    r_attn = Reduction(corner, [(g_low, mixed_one)], False)
    g_parts = []
    for index, piece in enumerate(pieces):
        whole, kept = saved_self[index]
        grad = exchange(
            cut(g_mixed, index).reshape(piece.group, -1, dim, piece.count), piece.group, cols
        )
        part = attend_back(
            none, whole, whole, whole, (0, 1, 2), kept, grad, False, 2, True
        )
        part = tick(part, [r_cross, r_query] if index == 0 else running)
        if index == 0:
            running.append(r_attn)
        g_parts.append(exchange(part, piece.group, cols))
    g_heads = [
        jnp.concatenate([p[:, i].reshape(heads, dim, -1) for p in g_parts], 2) for i in range(3)
    ]
    g_raw_q, g_q_gain = query_pull(g_heads[0].astype(F32))
    g_raw_k, g_k_gain = key_pull(g_heads[1].astype(F32))
    g_triple = [
        g.reshape(depth, tokens) for g in (g_raw_q.astype(BF), g_raw_k.astype(BF), g_heads[2])
    ]
    g_triple = tick(g_triple, running)
    r_self = [
        Reduction(corner, [(normed_one, g) for g in g_triple[:2]], True),
        Reduction(corner, [(normed_one, g_triple[2])], False),
    ]
    g_normed = rebuild(weights, [0, 1, 2], g_triple, F32)
    running += r_self
    g_normed = tick(g_normed, running)
    crossed = g_normed * normal_one
    sums = jnp.stack(
        [
            jnp.stack([jnp.sum(cut(g_normed, i), 1), jnp.sum(cut(crossed, i), 1)], 0)
            for i in range(len(pieces))
        ],
        0,
    )
    which = jnp.stack(
        [jnp.where(jnp.arange(sequences) == p.sequence, 1.0, 0.0) for p in pieces], 0
    )
    g_modul = jnp.sum(which[:, :, None, None] * sums[:, None], 0)
    g_modul = g_modul.reshape(sequences, 2, cols, width).transpose(2, 0, 1, 3)
    g_modul = jnp.sum(lax.all_to_all(g_modul, "col", 0, 0, tiled=True), 0).astype(BF)
    g_stream = g_stream + norm_back(g_normed * scaling, normal_one, inverse_one)

    g_skip_gain = jnp.sum(g_stream * skip_normal, 1)
    g_skip_bias = jnp.sum(g_stream, 1)
    g_joined = norm_back(g_stream * gain_skip, skip_normal, skip_inverse).astype(BF)
    g_joined, g_modul = lax.optimization_barrier((g_joined, g_modul))
    r_skip = Reduction(corner, [(both, g_joined)], True)
    g_both = rebuild_blocks(base, w_skip, width, g_joined)
    if custom_mesh():
        states = [r.state for r in r_self]
        g_both, got, states = lax.optimization_barrier((g_both, r_skip.state[0], states))
        here, away = outer(corner, r_skip.pairs, True, got)
        g_both, away, act, states = lax.optimization_barrier((g_both, away, act, states))
        r_skip.stage, r_skip.state = 1, [here, swap(away, "row", 1)]
        for beside, state in zip(r_self, states):
            beside.state = state
            beside.advance()
        g_latents, g_skip = to_features(g_both, pieces, cols, 2, block_rows)
        output = contract(weights_hidden, 1, act, stream, BF)
        output = tick(output, [r_skip])
        states = [r.state for r in r_self]
        states, here = lax.optimization_barrier((states, r_skip.state[0]))
        r_skip.state[0] = here
        for beside, state in zip(r_self, states):
            beside.state = state
            beside.advance()
    else:
        g_latents, g_skip = to_features(g_both, pieces, cols, 2, block_rows)
        output = contract(weights_hidden, 1, act, stream, BF)
    result = to_features(output, pieces, cols, 1, width)[0]
    g_modul = shared(after(g_modul, result), "row").reshape(-1, 2, width)
    g_modulation = einsum("sd,ske->dke", embed_rows, g_modul)

    g_gains = jnp.stack(
        [g_skip_gain, g_skip_bias, g_cross_gain, g_cross_bias, g_hidden_gain, g_hidden_bias], 0
    )
    g_gains = g_gains.reshape(6, cols, width).transpose(1, 0, 2)
    g_head = jnp.stack([g_q_gain, g_k_gain, g_cq_gain, g_tk_gain], 0).reshape(1, -1, width)
    g_gains = after(g_gains, result)
    packed = jnp.concatenate([g_gains, jnp.broadcast_to(g_head, (cols, *g_head.shape[1:]))], 1)
    packed = jnp.sum(lax.all_to_all(packed, "col", 0, 0, tiled=True), 0)
    packed = jnp.sum(shared(packed, "row"), 0)
    g_gains = packed[:6]
    g_head = packed[6:].reshape(4, dim)
    return (
        result,
        g_latents,
        g_skip,
        r_skip.result().reshape(2, block_rows, width),
        g_modulation,
        jnp.concatenate([r.result() for r in r_self], 0).transpose(1, 0, 2),
        r_attn.result()[0].T,
        r_query.result()[0],
        r_text.result().transpose(1, 0, 2),
        r_cross.result()[0].T,
        g_hidden[0],
        g_hidden[1].T,
        *[g_gains[i] for i in range(6)],
        *[g_head[i] for i in range(4)],
    )


def solution(mesh):
    return jax.shard_map(
        shards,
        mesh=mesh,
        in_specs=(
            P("col", "row"),
            P("col", "row"),
            P("row", "col"),
            P("row", None, "col"),
            P("row"),
            P(None, "row"),
            P("col", "row"),
            P(None, "row", "col"),
            P("row", None, "col"),
            P("row", None, "col"),
            P("col", "row"),
            P("row", "col"),
            P("row", None, "col"),
            P("col", "row"),
            P("row", "col"),
            P("col", "row"),
            P("col"),
            P("col"),
            P("col"),
            P("col"),
            P("col"),
            P("col"),
            P(),
            P(),
            P(),
            P(),
        ),
        out_specs=(
            P("col", "row"),
            P("col", "row"),
            P("col", "row"),
            P(None, "row", "col"),
            P("row", None, "col"),
            P("row", None, "col"),
            P("col", "row"),
            P("row", "col"),
            P("row", None, "col"),
            P("col", "row"),
            P("row", "col"),
            P("col", "row"),
            P("col"),
            P("col"),
            P("col"),
            P("col"),
            P("col"),
            P("col"),
            P(),
            P(),
            P(),
            P(),
        ),
        check_vma=False,
    )
```

```python
from functools import partial
import math

import jax
import jax.numpy as jnp
from jax import lax
from jax.experimental import pallas as pl
from jax.experimental.pallas import tpu as pltpu
from jax.sharding import PartitionSpec as P

L = 1024
EPSILON = 1e-06
BF = jnp.bfloat16
F32 = jnp.float32
KEYPAD = 128
DEVICES = ("col", "row")
LOG2E = math.log2(math.e)
VMEM = 60 << 20


def einsum(spec, left, right):
    return jnp.einsum(spec, left, right, preferred_element_type=F32)


def dot(left, right, dims):
    return lax.dot_general(left, right, (dims, ((), ())), preferred_element_type=F32)


def params():
    return pltpu.CompilerParams(vmem_limit_bytes=VMEM)


def step_of(count):
    return 256 if count % 256 == 0 else count


def wide(ref, head):
    parts = [ref[s, 0, head] for s in range(ref.shape[0])]
    return parts[0] if len(parts) == 1 else jnp.concatenate(parts, 1)


def valid_keys(length_ref, keys, step):
    return lax.broadcasted_iota(jnp.int32, (keys, step), 0) < length_ref[0]


def attend_kernel(masked, length_ref, q_ref, k_ref, v_ref, o_ref, r_ref, l_ref):
    groups, _, heads, dim, count = q_ref.shape
    step = step_of(count)
    factor = dim ** (-0.5) * LOG2E
    for head in range(heads):
        key = wide(k_ref, head).T
        value = wide(v_ref, head)
        keys = key.shape[0]
        value = jnp.concatenate([value, jnp.ones((8, keys), BF)], 0)
        for place in range(0, groups * count, step):
            group, first = divmod(place, count)
            query = q_ref[group, 0, head, :, first : first + step]
            expo = jnp.exp2(dot(key, query, ((1,), (0,))) * factor)
            if masked:
                expo = jnp.where(valid_keys(length_ref, keys, step), expo, 0.0)
            both = dot(value, expo.astype(BF), ((1,), (0,)))
            total = both[dim : dim + 1]
            mixed = both[:dim] * (1.0 / total)
            high = mixed.astype(BF)
            o_ref[group, head, :, first : first + step] = high
            r_ref[group, head, :, first : first + step] = (mixed - high.astype(F32)).astype(BF)
            l_ref[head, :, place : place + step] = jnp.log2(total)


def attend_back_kernel(
    masked, length_ref, q_ref, k_ref, v_ref, m_ref, r_ref, g_ref, l_ref, *outs
):
    groups, _, heads, dim, count = q_ref.shape
    step = step_of(count)
    scale = dim ** (-0.5)
    for head in range(heads):
        key = wide(k_ref, head)
        keys = key.shape[1]
        turned = key.T
        value = jnp.concatenate([wide(v_ref, head), jnp.ones((8, keys), BF)], 0).T
        g_key = g_value = None
        for place in range(0, groups * count, step):
            group, first = divmod(place, count)
            here = slice(first, first + step)
            query = q_ref[group, 0, head, :, here]
            grad = g_ref[group, head, :, here]
            mixed = m_ref[group, head, :, here].astype(F32)
            mixed = mixed + r_ref[group, head, :, here].astype(F32)
            delta = -jnp.sum(grad.astype(F32) * mixed, 0, keepdims=True)
            high = delta.astype(BF)
            rest = (delta - high.astype(F32)).astype(BF)
            more = jnp.concatenate([grad, high, rest, jnp.zeros((6, step), BF)], 0)
            probs = jnp.exp2(
                dot(turned, query, ((1,), (0,))) * (scale * LOG2E)
                - l_ref[head, :, place : place + step]
            )
            if masked:
                probs = jnp.where(valid_keys(length_ref, keys, step), probs, 0.0)
            product = (probs * dot(value, more, ((1,), (0,)))).astype(BF)
            g_query = dot(key, product, ((1,), (0,))) * scale
            part_value = dot(grad, probs.astype(BF), ((1,), (1,)))
            part_key = dot(query, product, ((1,), (1,)))
            g_value = part_value if g_value is None else g_value + part_value
            g_key = part_key if g_key is None else g_key + part_key
            outs[0][group, 0, head, :, here] = g_query.astype(outs[0].dtype)
        g_key = g_key * scale
        if len(outs) == 1:
            for group in range(groups):
                here = slice(group * count, (group + 1) * count)
                outs[0][group, 1, head] = g_key[:, here].astype(BF)
                outs[0][group, 2, head] = g_value[:, here].astype(BF)
        else:
            outs[1][0, 0, head] = g_key
            outs[2][0, 0, head] = g_value


def costs(heads, queries, keys, dim, products):
    return pl.CostEstimate(
        flops=2 * products * heads * queries * keys * 256,
        transcendentals=heads * queries * keys,
        bytes_accessed=2 * products * heads * dim * (queries + keys),
    )


def head_block(shape, count, kind=0):
    groups, _, _, dim, tokens = shape
    return pl.BlockSpec((groups, 1, count, dim, tokens), lambda h: (0, kind, h, 0, 0))


def mix_block(shape, count):
    groups, _, _, dim, tokens = shape
    return pl.BlockSpec((groups, count, dim, tokens), lambda h: (0, h, 0, 0))


def attend(length, query, key, value, kinds, masked, most):
    groups, _, heads, dim, count = query.shape
    many = math.gcd(heads, most)
    total = groups * count
    keys = key.shape[0] * key.shape[4]
    return pl.pallas_call(
        partial(attend_kernel, masked),
        grid=(heads // many,),
        in_specs=[pl.BlockSpec(memory_space=pltpu.SMEM)]
        + [head_block(a.shape, many, kind) for a, kind in zip((query, key, value), kinds)],
        out_specs=[
            mix_block(query.shape, many),
            mix_block(query.shape, many),
            pl.BlockSpec((many, 1, total), lambda h: (h, 0, 0)),
        ],
        out_shape=[
            jax.ShapeDtypeStruct((groups, heads, dim, count), BF),
            jax.ShapeDtypeStruct((groups, heads, dim, count), BF),
            jax.ShapeDtypeStruct((heads, 1, total), F32),
        ],
        cost_estimate=costs(heads, total, keys, dim, 2),
        compiler_params=params(),
        name="attend",
    )(length, query, key, value)


def attend_back(length, query, key, value, kinds, kept, grad, masked, most, stacked):
    mixed, rest, logs = kept
    groups, _, heads, dim, count = query.shape
    many = math.gcd(heads, most)
    total = groups * count
    keys = key.shape[0] * key.shape[4]
    if stacked:
        out_specs = pl.BlockSpec((groups, 3, many, dim, count), lambda h: (0, 0, h, 0, 0))
        out_shape = jax.ShapeDtypeStruct((groups, 3, heads, dim, count), BF)
    else:
        out_specs = [head_block(a.shape, many) for a in (query, key, value)]
        out_shape = [jax.ShapeDtypeStruct(a.shape, F32) for a in (query, key, value)]
    return pl.pallas_call(
        partial(attend_back_kernel, masked),
        grid=(heads // many,),
        in_specs=[pl.BlockSpec(memory_space=pltpu.SMEM)]
        + [head_block(a.shape, many, kind) for a, kind in zip((query, key, value), kinds)]
        + [mix_block(query.shape, many)] * 3
        + [pl.BlockSpec((many, 1, total), lambda h: (h, 0, 0))],
        out_specs=out_specs,
        out_shape=out_shape,
        cost_estimate=costs(heads, total, keys, dim, 5),
        compiler_params=params(),
        name="attend_back",
    )(length, query, key, value, mixed, rest, grad, logs)


def work(rows, depth, tokens, moved):
    return pl.CostEstimate(
        flops=2 * rows * depth * tokens,
        transcendentals=0,
        bytes_accessed=moved,
    )


def lanes(width):
    return -(-width // 128) * 128


def full(shape):
    return pl.BlockSpec(shape, lambda *_: (0,) * len(shape))


def project(weight, kinds, values, dtypes, joined=False):
    _, cols, depth, width = weight.shape
    tokens = values[0].shape[1]
    outs = 1 if joined else len(kinds)

    def kernel(*refs):
        blocks = refs[: len(kinds)]
        given = refs[len(kinds) : -outs]
        total = None
        for index, block in enumerate(blocks):
            part = dot(block[0, 0], given[index % len(given)][...], ((0,), (0,)))
            if not joined:
                refs[index - outs][...] = part.astype(dtypes[index])
            total = part if total is None else total + part
        if joined:
            refs[-1][...] = total.astype(dtypes[0])

    return pl.pallas_call(
        kernel,
        grid=(cols,),
        in_specs=[
            pl.BlockSpec((1, 1, depth, width), partial(lambda k, c: (k, c, 0, 0), kind))
            for kind in kinds
        ]
        + [full(v.shape) for v in values],
        out_specs=[pl.BlockSpec((width, tokens), lambda c: (c, 0))] * outs,
        out_shape=[jax.ShapeDtypeStruct((cols * width, tokens), dtypes[i]) for i in range(outs)],
        cost_estimate=work(len(kinds) * cols * width, depth, tokens, 8 * depth * tokens),
        compiler_params=params(),
        name="project",
    )(*([weight] * len(kinds)), *values)


def rebuild(weight, kinds, values, dtype):
    _, cols, depth, width = weight.shape
    tokens = values[0].shape[1]
    tile = depth // 4

    def kernel(*refs):
        total = None
        for block, given in zip(refs[: len(kinds)], refs[len(kinds) : -1]):
            for col in range(cols):
                part = dot(block[0, col], given[col * width : (col + 1) * width, :], ((1,), (0,)))
                total = part if total is None else total + part
        refs[-1][...] = total.astype(dtype)

    return pl.pallas_call(
        kernel,
        grid=(4,),
        in_specs=[
            pl.BlockSpec((1, cols, tile, width), partial(lambda k, j: (k, 0, j, 0), kind))
            for kind in kinds
        ]
        + [full(v.shape) for v in values],
        out_specs=pl.BlockSpec((tile, tokens), lambda j: (j, 0)),
        out_shape=jax.ShapeDtypeStruct((depth, tokens), dtype),
        cost_estimate=work(depth, len(kinds) * cols * width, tokens, 8 * depth * tokens),
        compiler_params=params(),
        name="rebuild",
    )(*([weight] * len(kinds)), *values)


def project_blocks(base, blocks, width, values):
    many = len(blocks)
    depth, broad = blocks[0].shape
    tokens = values.shape[1]
    tile = depth // 4

    def kernel(base_ref, *refs):
        values_ref, out_ref = refs[many:]

        @pl.when(pl.program_id(0) == 0)
        def _():
            out_ref[...] = jnp.zeros_like(out_ref)

        for index in range(many):
            here = pl.ds(pl.multiple_of((index ^ base_ref[0]) * width, width), width)
            out_ref[here, :] += dot(refs[index][...], values_ref[...], ((0,), (0,)))[:width]

    return pl.pallas_call(
        kernel,
        grid_spec=pltpu.PrefetchScalarGridSpec(
            num_scalar_prefetch=1,
            grid=(4,),
            in_specs=[pl.BlockSpec((tile, broad), lambda j, b: (j, 0))] * many
            + [pl.BlockSpec((tile, tokens), lambda j, b: (j, 0))],
            out_specs=pl.BlockSpec((many * width, tokens), lambda j, b: (0, 0)),
        ),
        out_shape=jax.ShapeDtypeStruct((many * width, tokens), F32),
        cost_estimate=work(many * width, depth, tokens, 4 * depth * tokens),
        compiler_params=params(),
        name="project_blocks",
    )(base, *blocks, values)


def rebuild_blocks(base, blocks, width, values):
    many = len(blocks)
    depth, broad = blocks[0].shape
    tokens = values.shape[1]
    tile = depth // 4

    def kernel(base_ref, *refs):
        values_ref, out_ref = refs[many:]
        total = None
        for index in range(many):
            here = pl.ds(pl.multiple_of((index ^ base_ref[0]) * width, width), width)
            part = dot(refs[index][:, :width], values_ref[here, :], ((1,), (0,)))
            total = part if total is None else total + part
        out_ref[...] = total.astype(BF)

    return pl.pallas_call(
        kernel,
        grid_spec=pltpu.PrefetchScalarGridSpec(
            num_scalar_prefetch=1,
            grid=(4,),
            in_specs=[pl.BlockSpec((tile, broad), lambda j, b: (j, 0))] * many
            + [pl.BlockSpec(values.shape, lambda j, b: (0, 0))],
            out_specs=pl.BlockSpec((tile, tokens), lambda j, b: (j, 0)),
        ),
        out_shape=jax.ShapeDtypeStruct((depth, tokens), BF),
        cost_estimate=work(many * width, depth, tokens, 4 * depth * tokens),
        compiler_params=params(),
        name="rebuild_blocks",
    )(base, *blocks, values)


def outer(place, pairs, across, got=None):
    cols = lax.axis_size("col")
    lefts = []
    for left, _ in pairs:
        if not any(left is other for other in lefts):
            lefts.append(left)
    which = [next(i for i, l in enumerate(lefts) if l is left) for left, _ in pairs]
    rights = [right for _, right in pairs]
    many = len(pairs)
    rows, tokens = lefts[0].shape
    width = rights[0].shape[0] // cols
    broad = lanes(width)
    chunk = rows // 8
    flip = 1 if got is None else 0

    def kernel(place_ref, *refs):
        left_refs = refs[: len(lefts)]
        right_refs = refs[len(lefts) : len(lefts) + many]
        rest = refs[len(lefts) + many :]
        for index in range(many):
            right = right_refs[index][...]
            if broad > width:
                right = jnp.concatenate([right, jnp.zeros((broad - width, tokens), BF)], 0)
            part = dot(left_refs[which[index]][...], right, ((1,), (1,)))
            if got is None:
                rest[0][index, 0] = part.astype(BF)
            elif not across:
                part = (part + rest[0][index, 0].astype(F32)).astype(BF)

                @pl.when(pl.program_id(0) == place_ref[2])
                def _():
                    rest[1][index] = part.reshape(4, 2, chunk, broad)

                @pl.when(pl.program_id(0) != place_ref[2])
                def _():
                    rest[2][index] = part.reshape(4, 2, chunk, broad)
            else:
                part = (part + rest[0][index, 0].astype(F32)).astype(BF)
                part = part.reshape(4, 2, chunk, broad)

                @pl.when(place_ref[1] == 0)
                def _():
                    rest[1][index, 0] = part[:, 0]
                    rest[2][index, 0] = part[:, 1]

                @pl.when(place_ref[1] != 0)
                def _():
                    rest[1][index, 0] = part[:, 1]
                    rest[2][index, 0] = part[:, 0]

    whole = pl.BlockSpec((many, 1, rows, broad), lambda y, place: (0, y, 0, 0))
    piece = pl.BlockSpec((many, 1, 4, chunk, broad), lambda y, place: (0, y, 0, 0, 0))
    all_rows = pl.BlockSpec((many, 4, 2, chunk, broad), lambda y, place: (0, 0, 0, 0, 0))
    if got is None:
        given, out_specs = [], whole
        out_shape = jax.ShapeDtypeStruct((many, cols // 2, rows, broad), BF)
    else:
        given, out_specs = [got], [piece, piece] if across else [all_rows, all_rows]
        shape = (many, cols // 2, 4, chunk, broad) if across else (many, 4, 2, chunk, broad)
        out_shape = [jax.ShapeDtypeStruct(shape, BF)] * 2
    return pl.pallas_call(
        kernel,
        grid_spec=pltpu.PrefetchScalarGridSpec(
            num_scalar_prefetch=1,
            grid=(cols // 2,),
            in_specs=[pl.BlockSpec((rows, tokens), lambda y, place: (0, 0)) for _ in lefts]
            + [
                pl.BlockSpec((width, tokens), lambda y, place: (2 * y + (place[0] ^ flip), 0))
                for _ in rights
            ]
            + [whole] * len(given),
            out_specs=out_specs,
        ),
        out_shape=out_shape,
        cost_estimate=work(
            rows, tokens, many * cols // 2 * broad, 2 * rows * cols * broad * many
        ),
        compiler_params=params(),
        name="outer",
    )(place, *lefts, *rights, *given)


def outer_all(pairs):
    cols = lax.axis_size("col")
    if not custom_mesh():
        return jnp.stack(
            [einsum("kt,cnt->ckn", a, b.reshape(cols, -1, b.shape[1])).astype(BF) for a, b in pairs]
        )
    lefts = []
    for left, _ in pairs:
        if not any(left is other for other in lefts):
            lefts.append(left)
    which = [next(i for i, l in enumerate(lefts) if l is left) for left, _ in pairs]
    rights = [right for _, right in pairs]
    many = len(pairs)
    rows = lefts[0].shape[0]
    width = rights[0].shape[0] // cols

    def kernel(*refs):
        for index in range(many):
            left = refs[which[index]][...]
            part = dot(left, refs[len(lefts) + index][...], ((1,), (1,)))
            refs[-1][index, 0] = part.astype(BF)

    return pl.pallas_call(
        kernel,
        grid=(cols,),
        in_specs=[full(left.shape) for left in lefts]
        + [pl.BlockSpec((width, right.shape[1]), lambda c: (c, 0)) for right in rights],
        out_specs=pl.BlockSpec((many, 1, rows, width), lambda c: (0, c, 0, 0)),
        out_shape=jax.ShapeDtypeStruct((many, cols, rows, width), BF),
        cost_estimate=work(
            many * rows, lefts[0].shape[1], cols * width, 3 * many * rows * cols * width
        ),
        compiler_params=params(),
        name="outer_all",
    )(*lefts, *rights)


def expand(weight, kind, values):
    _, many, depth, hidden = weight.shape
    tokens = values.shape[1]
    tile = 384 if hidden % 384 == 0 else hidden
    slope = 0.79788456
    cubic = 0.044715

    def kernel(weight_ref, values_ref, act_ref, slope_ref):
        for index in range(many):
            inner = dot(weight_ref[0, index], values_ref[...], ((0,), (0,)))
            square = inner * inner
            bent = jnp.tanh(inner * (slope + slope * cubic * square))
            half = 0.5 + 0.5 * bent
            act_ref[index] = (inner * half).astype(BF)
            rise = slope + 3.0 * slope * cubic * square
            slope_ref[index] = (half + 0.5 * inner * (1.0 - bent * bent) * rise).astype(BF)

    return pl.pallas_call(
        kernel,
        grid=(hidden // tile,),
        in_specs=[
            pl.BlockSpec((1, many, depth, tile), lambda j: (kind, 0, 0, j)),
            full(values.shape),
        ],
        out_specs=[pl.BlockSpec((many, tile, tokens), lambda j: (0, j, 0))] * 2,
        out_shape=[jax.ShapeDtypeStruct((many, hidden, tokens), BF)] * 2,
        cost_estimate=work(many * hidden, depth, tokens, 3 * many * hidden * depth),
        compiler_params=params(),
        name="expand",
    )(weight, values)


def expand_back(weight, kind, values, slopes):
    _, many, depth, hidden = weight.shape
    tokens = values.shape[1]
    tile = 384 if hidden % 384 == 0 else hidden

    def kernel(weight_ref, values_ref, slope_ref, out_ref):
        for index in range(many):
            part = dot(weight_ref[0, index], values_ref[...], ((0,), (0,)))
            out_ref[index] = (part * slope_ref[index].astype(F32)).astype(BF)

    return pl.pallas_call(
        kernel,
        grid=(hidden // tile,),
        in_specs=[
            pl.BlockSpec((1, many, depth, tile), lambda j: (kind, 0, 0, j)),
            full(values.shape),
            pl.BlockSpec((many, tile, tokens), lambda j: (0, j, 0)),
        ],
        out_specs=pl.BlockSpec((many, tile, tokens), lambda j: (0, j, 0)),
        out_shape=jax.ShapeDtypeStruct((many, hidden, tokens), BF),
        cost_estimate=work(many * hidden, depth, tokens, 3 * many * hidden * depth),
        compiler_params=params(),
        name="expand_back",
    )(weight, values, slopes)


def contract(weight, kind, values, added, dtype):
    _, many, depth, hidden = weight.shape
    tokens = values.shape[2]
    tile = depth // 4
    extra = [] if added is None else [added]

    def kernel(weight_ref, values_ref, *refs):
        total = refs[0][...] if extra else None
        for index in range(many):
            part = dot(weight_ref[0, index], values_ref[index], ((1,), (0,)))
            total = part if total is None else total + part
        refs[-1][...] = total.astype(dtype)

    line = pl.BlockSpec((tile, tokens), lambda j: (j, 0))
    return pl.pallas_call(
        kernel,
        grid=(4,),
        in_specs=[
            pl.BlockSpec((1, many, tile, hidden), lambda j: (kind, 0, j, 0)),
            full(values.shape),
        ]
        + [line] * len(extra),
        out_specs=line,
        out_shape=jax.ShapeDtypeStruct((depth, tokens), dtype),
        cost_estimate=work(depth, many * hidden, tokens, 3 * many * hidden * depth),
        compiler_params=params(),
        name="contract",
    )(weight, values, *extra)


def hidden_outer(grad_out, act, normed, grad_inner):
    many, hidden, tokens = act.shape
    depth = grad_out.shape[0]
    parts = 2 if hidden % 256 == 0 else 1
    tile = hidden // parts

    def kernel(out_ref, act_ref, normed_ref, inner_ref, grad_ref):
        kind = pl.program_id(0)

        @pl.when(kind == 0)
        def _():
            grad_ref[0, 0] = dot(normed_ref[...], inner_ref[0], ((1,), (1,))).astype(BF)

        @pl.when(kind == 1)
        def _():
            grad_ref[0, 0] = dot(out_ref[...], act_ref[0], ((1,), (1,))).astype(BF)

    return pl.pallas_call(
        kernel,
        grid=(2, many, parts),
        in_specs=[
            pl.BlockSpec((depth, tokens), lambda s, p, j: (0, 0)),
            pl.BlockSpec((1, tile, tokens), lambda s, p, j: (s * p, s * j, 0)),
            pl.BlockSpec((depth, tokens), lambda s, p, j: (0, 0)),
            pl.BlockSpec(
                (1, tile, tokens),
                lambda s, p, j: (p + s * (many - 1 - p), j + s * (parts - 1 - j), 0),
            ),
        ],
        out_specs=pl.BlockSpec((1, 1, depth, tile), lambda s, p, j: (s, p, 0, j)),
        out_shape=jax.ShapeDtypeStruct((2, many, depth, hidden), BF),
        cost_estimate=work(2 * depth, tokens, many * hidden, 5 * many * depth * hidden),
        compiler_params=params(),
        name="hidden_outer",
    )(grad_out, act, normed, grad_inner)


def assemble(place, own, got, middle=None):
    rows, width = own.shape[-2:]

    def kernel(place_ref, own_ref, got_ref, out_ref):
        @pl.when(pl.program_id(0) == place_ref[1])
        def _():
            out_ref[0, 0] = own_ref[...].reshape(rows, width)

        @pl.when(pl.program_id(0) != place_ref[1])
        def _():
            out_ref[0, 0] = got_ref[...].reshape(rows, width)

    def spec(ours):
        def index(x, z, place):
            phase = place[1] if ours else 1 - place[1]
            inside = (x == phase).astype(jnp.int32)
            level = (inside * z + (1 - inside) * 3 * (1 - phase)) ^ place[0]
            return (level, 0, 0) if middle is None else (level, middle, 0, 0)

        shape = (1, rows, width) if middle is None else (1, 1, rows, width)
        return pl.BlockSpec(shape, index)

    return pl.pallas_call(
        kernel,
        grid_spec=pltpu.PrefetchScalarGridSpec(
            num_scalar_prefetch=1,
            grid=(2, 4),
            in_specs=[spec(True), spec(False)],
            out_specs=pl.BlockSpec((1, 1, rows, width), lambda x, z, place: (z, x, 0, 0)),
        ),
        out_shape=jax.ShapeDtypeStruct((4, 2, rows, width), BF),
        cost_estimate=work(1, 1, 1, 32 * rows * width),
        name="assemble",
    )(place, own, got).reshape(8 * rows, width)


def normalize(values):
    average = jnp.mean(values, 0, keepdims=True)
    centred = values - average
    inverse = lax.rsqrt(jnp.mean(centred * centred, 0, keepdims=True) + EPSILON)
    return centred * inverse, inverse


def norm_back(grad, normal, inverse):
    average = jnp.mean(grad, 0, keepdims=True)
    crossed = jnp.mean(grad * normal, 0, keepdims=True)
    return inverse * (grad - average - normal * crossed)


def head_norm(values, gain):
    average = jnp.mean(values, 1, keepdims=True)
    centred = values - average
    variance = jnp.mean(centred * centred, 1, keepdims=True)
    return centred * lax.rsqrt(variance + EPSILON) * gain[None, :, None]


def rope_tables(places, head_dim):
    quarter = head_dim // 4
    freqs = jnp.exp(jnp.arange(quarter, dtype=F32) * (-4.0 * math.log(10000.0) / head_dim))
    rows = freqs[:, None] * places[0].astype(F32)[None, :]
    cols = freqs[:, None] * places[1].astype(F32)[None, :]
    angles = jnp.concatenate([rows, rows, cols, cols], 0)
    return jnp.cos(angles), jnp.sin(angles)


def rotate(values):
    quarter = values.shape[1] // 4
    one, two, three, four = (values[:, i * quarter : (i + 1) * quarter] for i in range(4))
    return jnp.concatenate([-two, one, -four, three], 1)


class Piece:
    def __init__(self, start, count, group, sequence):
        self.start = start
        self.count = count
        self.group = group
        self.sequence = sequence


def pieces_of(cols, sequences):
    mine = lax.axis_index("col")
    if cols == 4 and sequences == 3:
        return [
            Piece(0, L // 2, 2, mine // 2),
            Piece(2 * L, L // 4, 4, jnp.int32(2)),
        ]
    return [Piece(s * L, L // cols, cols, jnp.int32(s)) for s in range(sequences)]


def groups_of(size, cols):
    return [list(range(i, i + size)) for i in range(0, cols, size)]


def exchange(values, size, cols):
    if size == cols:
        return lax.all_to_all(values, "col", 0, 0, tiled=True)
    return lax.all_to_all(
        values, "col", 0, 0, tiled=True, axis_index_groups=groups_of(size, cols)
    )


def cut_size(pieces):
    return math.gcd(*(p.count for p in pieces), *(p.start for p in pieces))


def locate(pieces, unit, block):
    device = inside = None
    at = 0
    for piece in pieces:
        each = piece.count // unit
        rest = block - piece.start // unit
        there = (rest // each, at + rest % each)
        if device is None:
            device, inside = there
        else:
            later = (rest >= 0).astype(jnp.int32)
            device = later * there[0] + (1 - later) * device
            inside = later * there[1] + (1 - later) * inside
        at += each
    return device, inside


def to_tokens(arrays, pieces, cols, rows):
    width, tokens = arrays[0].shape
    kinds = len(arrays)
    unit = cut_size(pieces)
    total = sum(p.count for p in pieces)
    if unit % 128:
        values = jnp.stack([a.reshape(-1, rows, tokens) for a in arrays], 1).astype(BF)
        values = values.reshape(kinds * width, tokens)
        parts = [
            jnp.concatenate(
                [values[:, p.start + j * p.count : p.start + (j + 1) * p.count] for p in pieces], 1
            )
            for j in range(cols)
        ]
        dealt = jnp.stack(parts, 0)
    else:

        def kernel(*refs):
            for kind in range(kinds):
                for at in range(0, width, rows):
                    to = at * kinds + kind * rows
                    refs[-1][0, to : to + rows] = refs[kind][at : at + rows].astype(BF)

        def index(block):
            device, inside = locate(pieces, unit, block)
            return (device, 0, inside)

        dealt = pl.pallas_call(
            kernel,
            grid=(tokens // unit,),
            in_specs=[pl.BlockSpec((width, unit), lambda b: (0, b))] * kinds,
            out_specs=pl.BlockSpec((1, kinds * width, unit), index),
            out_shape=jax.ShapeDtypeStruct((cols, kinds * width, total), BF),
            cost_estimate=pl.CostEstimate(
                flops=0, transcendentals=0, bytes_accessed=4 * kinds * width * tokens
            ),
            name="deal",
        )(*arrays)
    got = exchange(dealt, cols, cols)
    return got.reshape(-1, total)


def to_features(values, pieces, cols, kinds, rows):
    got = exchange(values.reshape(cols, -1, values.shape[1]), cols, cols)
    unit = cut_size(pieces)
    width = got.shape[1] // kinds
    tokens = cols * got.shape[2]
    if unit % 128:
        parts = []
        at = 0
        for piece in pieces:
            parts += [got[j, :, at : at + piece.count] for j in range(cols)]
            at += piece.count
        whole = jnp.concatenate(parts, 1).astype(F32).reshape(-1, kinds, rows, tokens)
        return [whole[:, kind].reshape(width, tokens) for kind in range(kinds)]

    def kernel(got_ref, *refs):
        for kind in range(kinds):
            for at in range(0, width, rows):
                start = at * kinds + kind * rows
                refs[kind][at : at + rows] = got_ref[0, start : start + rows].astype(F32)

    def index(block):
        device, inside = locate(pieces, unit, block)
        return (device, 0, inside)

    return pl.pallas_call(
        kernel,
        grid=(tokens // unit,),
        in_specs=[pl.BlockSpec((1, kinds * width, unit), index)],
        out_specs=[pl.BlockSpec((width, unit), lambda b: (0, b))] * kinds,
        out_shape=[jax.ShapeDtypeStruct((width, tokens), F32)] * kinds,
        cost_estimate=pl.CostEstimate(
            flops=0, transcendentals=0, bytes_accessed=6 * kinds * width * tokens
        ),
        name="undeal",
    )(got)


def shared(values, axis):
    size = lax.axis_size(axis)
    return lax.all_to_all(
        jnp.broadcast_to(values[None], (size, *values.shape)), axis, 0, 0, tiled=True
    )


def swap(values, axis, bit):
    size = lax.axis_size(axis)
    return lax.ppermute(values, axis, [(i, i ^ bit) for i in range(size)])


def custom_mesh():
    return (lax.axis_size("row"), lax.axis_size("col")) == (8, 4)


def gather_weights(blocks):
    cols = lax.axis_size("col")
    most = max(block.shape[0] for block in blocks)
    padded = [jnp.pad(b, ((0, most - b.shape[0]), (0, 0))) for b in blocks]
    whole = lax.all_gather(jnp.stack(padded, 0), DEVICES, axis=1, tiled=True)
    return whole.reshape(len(blocks), cols, -1, blocks[0].shape[1])


class Gathering:
    last = 4

    def __init__(self, block, up, place):
        self.up = up
        self.place = place
        self.stage = 0
        self.state = [block]
        if not custom_mesh():
            cols = lax.axis_size("col")
            whole = lax.all_gather(block, DEVICES, axis=0, tiled=True)
            self.state = list(whole.reshape(cols, -1, block.shape[1]))
            self.stage = self.last

    def levels(self, block):
        return [block] + [swap(block, "row", 2 * level) for level in (1, 2, 3)]

    def advance(self):
        state = self.state
        self.stage += 1
        if self.stage == 1:
            self.state = [state[0], swap(state[0], "col", 2)] if self.up else self.levels(state[0])
        elif self.stage == 2:
            stack = jnp.stack(state, 0)
            self.state = self.levels(stack) if self.up else [stack, swap(stack, "col", 2)]
        elif self.stage == 3 and self.up:
            stack = jnp.stack(state, 0)
            self.state = [stack, swap(stack, "row", 1)]
        elif self.stage == 3:
            self.state = state + [swap(a, "row", 1) for a in state]
        else:
            if self.up:
                mine, other = (assemble(self.place, *state, k) for k in (0, 1))
            else:
                mine = assemble(self.place, state[0], state[2])
                other = assemble(self.place, state[1], state[3])
            self.state = [mine, swap(mine, "col", 1), other, swap(other, "col", 1)]

    def result(self):
        while self.stage < self.last:
            self.advance()
        return self.state


def pick(values, axis, index):
    return lax.dynamic_index_in_dim(values, index, axis, False)


def add(left, right):
    return (left.astype(F32) + right.astype(F32)).astype(BF)


class Reduction:
    last = 4

    def __init__(self, place, pairs, across):
        self.place = place
        self.across = across
        self.pairs = pairs
        self.width = pairs[0][1].shape[0] // lax.axis_size("col")
        self.stage = 0
        if custom_mesh():
            self.state = [swap(outer(place, pairs, across), "col", 1)]
            return
        self.stage = self.last
        cols = lax.axis_size("col")
        whole = jnp.stack(
            [einsum("kt,cnt->ckn", a, b.reshape(cols, -1, b.shape[1])) for a, b in pairs], 0
        )
        flat = whole.reshape(len(pairs), -1, whole.shape[3]).astype(BF)
        self.state = [lax.psum_scatter(flat, DEVICES, scatter_dimension=1, tiled=True)]

    def advance(self):
        state = self.state
        self.stage += 1
        if self.stage == 1:
            here, away = outer(self.place, self.pairs, self.across, state[0])
            self.state = [here, swap(away, "row", 1) if self.across else swap(away, "col", 2)]
        elif self.stage == 2:
            axis, index = (1, self.place[2]) if self.across else (2, self.place[1])
            away = add(*(pick(a, axis, 1 - index) for a in state))
            here = add(*(pick(a, axis, index) for a in state))
            self.state = [here, swap(away, "col", 2) if self.across else swap(away, "row", 1)]
        elif self.stage == 3:
            level = lax.axis_index("row") // 2
            total = add(*state)
            self.state = [pick(total, 1, level)] + [
                swap(pick(total, 1, level ^ other), "row", 2 * other) for other in (1, 2, 3)
            ]
        else:
            total = state[0].astype(F32)
            for other in state[1:]:
                total = total + other.astype(F32)
            self.state = [total[..., : self.width]]

    def result(self):
        while self.stage < self.last:
            self.advance()
        return self.state[0].astype(F32)


def tick(values, running):
    active = [r for r in running if r.stage < r.last]
    if active:
        values, states = lax.optimization_barrier((values, [r.state for r in active]))
        for beside, state in zip(active, states):
            beside.state = state
            beside.advance()
    return values


def after(values, done):
    return lax.optimization_barrier((values, done))[0]


def shards(
    latents,
    skip_input,
    condition,
    text_states,
    text_lengths,
    positions,
    out_grad,
    skip_weight,
    modulation,
    self_inputs,
    self_output,
    cross_query,
    cross_keyvalue,
    cross_output,
    expand_weight,
    reduce_weight,
    skip_gain,
    skip_bias,
    cross_gain,
    cross_bias,
    hidden_gain,
    hidden_bias,
    query_gain,
    key_gain,
    cross_query_gain,
    text_key_gain,
):
    cols = lax.axis_size("col")
    rows = lax.axis_size("row")
    mine = lax.axis_index("col")
    my_row = lax.axis_index("row")
    width, row_tokens = latents.shape
    depth = width * cols
    dim = query_gain.shape[0]
    heads = depth // dim
    sequences = row_tokens // L
    tokens = row_tokens // cols
    texts = text_states.shape[1]
    keys = -(-texts // KEYPAD) * KEYPAD
    pieces = pieces_of(cols, sequences)
    starts = [sum(p.count for p in pieces[:i]) for i in range(len(pieces))]
    place = jnp.stack([my_row // 2, my_row % 2]).astype(jnp.int32)
    corner = jnp.stack([mine % 2, my_row % 2, mine // 2]).astype(jnp.int32)
    base = (mine if custom_mesh() else jnp.zeros_like(mine)).astype(jnp.int32)[None]

    def cut(values, index):
        return values[..., starts[index] : starts[index] + pieces[index].count]

    block_rows = depth // rows
    both = to_tokens([latents, skip_input], pieces, cols, block_rows)

    weights_one = gather_weights([*(self_inputs[:, i] for i in range(3)), self_output.T])
    weights_two = gather_weights(
        [cross_query, cross_output.T, *(cross_keyvalue[:, i] for i in range(2))]
    )
    skip_block = jnp.concatenate([skip_weight[0], skip_weight[1]], 0)
    skip_block = jnp.pad(skip_block, ((0, 0), (0, lanes(width) - width)))
    w_skip = Gathering(skip_block, False, place).result()
    weights_hidden = gather_weights([expand_weight, reduce_weight.T])

    places = jnp.concatenate(
        [
            lax.dynamic_slice_in_dim(positions, p.start + mine * p.count, p.count, 1)
            for p in pieces
        ],
        1,
    )

    embed = jax.nn.silu(after(condition, both).astype(F32)).astype(BF)
    embed = shared(embed, "row").reshape(-1, width)
    embed = shared(embed, "col").transpose(1, 0, 2).reshape(-1, depth)
    embed_rows = lax.dynamic_slice_in_dim(embed, my_row * block_rows, block_rows, 1)
    modul = einsum("sd,dke->ske", embed_rows, modulation).reshape(rows, sequences, 2, width)
    modul = jnp.sum(lax.all_to_all(modul, "row", 0, 0, tiled=True), 0)
    gains = jnp.stack(
        [skip_gain, skip_bias, cross_gain, cross_bias, hidden_gain, hidden_bias], 0
    )
    table = jnp.concatenate([gains, modul.reshape(-1, width)], 0)
    table = shared(table, "col").transpose(1, 0, 2).reshape(-1, depth)
    modul = table[6:].reshape(sequences, 2, depth)
    chosen = [lax.dynamic_index_in_dim(modul, p.sequence, 0, False) for p in pieces]
    columns = lax.optimization_barrier(jnp.concatenate([table[:6], *chosen], 0)).T
    gain_skip, bias_skip, gain_cross, bias_cross, gain_hidden, bias_hidden = (
        columns[:, i : i + 1] for i in range(6)
    )
    token_index = lax.broadcasted_iota(jnp.int32, (1, tokens), 1)

    def per_token(which):
        result = columns[:, 6 + which : 7 + which]
        for index in range(1, len(pieces)):
            column = columns[:, 6 + 2 * index + which : 7 + 2 * index + which]
            result = jnp.where(token_index >= starts[index], column, result)
        return jnp.broadcast_to(result, (depth, tokens))

    shifting = per_token(0)
    scaling = 1.0 + per_token(1)

    text = shared(jnp.pad(after(text_states, both), ((0, 0), (0, keys - texts), (0, 0))), "col")
    joined = project_blocks(base, w_skip, width, both)
    skip_normal, skip_inverse = normalize(joined)
    stream = skip_normal * gain_skip + bias_skip
    normal_one, inverse_one = normalize(stream)
    normed_one = (normal_one * scaling + shifting).astype(BF)
    raw = project(weights_one, [0, 1, 2], [normed_one], [F32, F32, BF])
    raw, text = lax.optimization_barrier((raw, text))
    raw = [r.reshape(heads, dim, tokens) for r in raw]
    cosine, sine = rope_tables(places, dim)

    def self_piece(value, gain):
        normal = head_norm(value, gain)
        return normal * cosine[None] + rotate(normal) * sine[None]

    rot_query, query_pull = jax.vjp(self_piece, raw[0], query_gain)
    rot_key, key_pull = jax.vjp(self_piece, raw[1], key_gain)
    triple = [rot_query.astype(BF), rot_key.astype(BF), raw[2]]

    def to_heads(parts, index):
        size = pieces[index].group
        split = [cut(p, index).reshape(size, heads // size, dim, -1) for p in parts]
        return exchange(jnp.stack(split, 1), size, cols)

    none = jnp.zeros((1,), jnp.int32)
    saved_self = []
    mixed_parts = []
    for index, piece in enumerate(pieces):
        whole = to_heads(triple, index)
        kept = attend(none, whole, whole, whole, (0, 1, 2), False, 2)
        saved_self.append((whole, kept))
        mixed_parts.append(exchange(kept[0], piece.group, cols).reshape(depth, -1))
    mixed_one = jnp.concatenate(mixed_parts, 1)
    text = after(text, mixed_one)
    stream = stream + rebuild(weights_one, [3], [mixed_one], F32)
    normal_two, inverse_two = normalize(stream)
    normed_two = (normal_two * gain_cross + bias_cross).astype(BF)
    raw_cross = project(weights_two, [0], [normed_two], [F32])[0].reshape(heads, dim, tokens)
    norm_query, cross_pull = jax.vjp(head_norm, raw_cross, cross_query_gain)
    text = jnp.concatenate(
        [lax.dynamic_index_in_dim(text, p.sequence, 1, False) for p in pieces], 1
    )
    text = text.transpose(0, 2, 1).reshape(-1, len(pieces) * keys)
    text_rows = text.shape[0] // rows
    text_wide = jnp.pad(
        text.reshape(rows, text_rows, -1), ((0, 0), (0, block_rows - text_rows), (0, 0))
    ).reshape(depth, -1)
    raw_text, value_two = project(weights_two, [2, 3], [text_wide], [F32, BF])
    norm_key, text_pull = jax.vjp(head_norm, raw_text.reshape(heads, dim, -1), text_key_gain)
    query_two = norm_query.astype(BF)
    key_two = norm_key.astype(BF)
    value_two = value_two.reshape(heads, dim, -1)
    saved_cross = []
    mixed_parts = []
    for index, piece in enumerate(pieces):
        length = lax.dynamic_index_in_dim(text_lengths, piece.sequence, 0, True)
        here = slice(index * keys, (index + 1) * keys)
        inputs = [cut(query_two, index), key_two[:, :, here], value_two[:, :, here]]
        inputs = [length] + [a[None, None] for a in inputs] + [(0, 0, 0)]
        kept = attend(*inputs, True, 4)
        saved_cross.append((inputs, kept))
        mixed_parts.append(kept[0].reshape(depth, -1))
    mixed_two = jnp.concatenate(mixed_parts, 1)
    stream = stream + rebuild(weights_two, [1], [mixed_two], F32)
    normal_three, inverse_three = normalize(stream)
    normed_three = (normal_three * gain_hidden + bias_hidden).astype(BF)
    grad_out = to_tokens([after(out_grad, joined)], pieces, cols, width)
    act, slopes = expand(weights_hidden, 0, normed_three)

    g_inner = expand_back(weights_hidden, 1, grad_out, slopes)
    g_hidden = hidden_outer(grad_out, act, normed_three, g_inner)
    g_inner, g_hidden = lax.optimization_barrier((g_inner, g_hidden))
    g_normed = contract(weights_hidden, 0, g_inner, None, F32)
    g_hidden = lax.psum_scatter(
        g_hidden.reshape(2, -1, g_hidden.shape[3]), DEVICES, scatter_dimension=1, tiled=True
    ).astype(F32)
    g_hidden_gain = jnp.sum(g_normed * normal_three, 1)
    g_hidden_bias = jnp.sum(g_normed, 1)
    g_stream = grad_out.astype(F32) + norm_back(g_normed * gain_hidden, normal_three, inverse_three)

    g_low = g_stream.astype(BF)
    g_mixed = project(weights_two, [1], [g_low], [BF])[0].reshape(heads, dim, tokens)
    pairs = [(g_low, mixed_two)]
    g_queries = []
    g_keys = []
    g_values = []
    for index, piece in enumerate(pieces):
        inputs, kept = saved_cross[index]
        grads = attend_back(*inputs, kept, cut(g_mixed, index)[None], True, 4, False)
        g_queries.append(grads[0][0, 0])
        g_keys.append(grads[1][0, 0])
        g_values.append(grads[2][0, 0])
    g_raw_cross, g_cq_gain = cross_pull(jnp.concatenate(g_queries, 2))
    g_raw_text, g_tk_gain = text_pull(jnp.concatenate(g_keys, 2))
    g_craw = g_raw_cross.astype(BF).reshape(depth, tokens)
    g_pair = [
        g_raw_text.astype(BF).reshape(depth, -1),
        jnp.concatenate(g_values, 2).astype(BF).reshape(depth, -1),
    ]
    g_normed = rebuild(weights_two, [0], [g_craw], F32)
    pairs += [(normed_two, g_craw), *((text_wide, g) for g in g_pair)]
    g_cross_gain = jnp.sum(g_normed * normal_two, 1)
    g_cross_bias = jnp.sum(g_normed, 1)
    g_stream = g_stream + norm_back(g_normed * gain_cross, normal_two, inverse_two)

    g_low = g_stream.astype(BF)
    g_mixed = project(weights_one, [3], [g_low], [BF])[0].reshape(heads, dim, tokens)
    pairs.append((g_low, mixed_one))
    middle = outer_all(pairs)
    middle = lax.psum_scatter(
        middle.reshape(len(pairs), -1, width), DEVICES, scatter_dimension=1, tiled=True
    ).astype(F32)
    g_parts = []
    for index, piece in enumerate(pieces):
        whole, kept = saved_self[index]
        grad = exchange(
            cut(g_mixed, index).reshape(piece.group, -1, dim, piece.count), piece.group, cols
        )
        part = attend_back(
            none, whole, whole, whole, (0, 1, 2), kept, grad, False, 2, True
        )
        g_parts.append(exchange(part, piece.group, cols))
    g_heads = [
        jnp.concatenate([p[:, i].reshape(heads, dim, -1) for p in g_parts], 2) for i in range(3)
    ]
    g_raw_q, g_q_gain = query_pull(g_heads[0].astype(F32))
    g_raw_k, g_k_gain = key_pull(g_heads[1].astype(F32))
    g_triple = [
        g.reshape(depth, tokens) for g in (g_raw_q.astype(BF), g_raw_k.astype(BF), g_heads[2])
    ]
    r_self = [
        Reduction(corner, [(normed_one, g) for g in g_triple[:2]], True),
        Reduction(corner, [(normed_one, g_triple[2])], False),
    ]
    g_normed = rebuild(weights_one, [0, 1, 2], g_triple, F32)
    g_normed = tick(g_normed, r_self)
    g_normed, kept = lax.optimization_barrier((g_normed, [r.state[0] for r in r_self]))
    for beside, part in zip(r_self, kept):
        beside.state[0] = part
    crossed = g_normed * normal_one
    sums = jnp.stack(
        [
            jnp.stack([jnp.sum(cut(g_normed, i), 1), jnp.sum(cut(crossed, i), 1)], 0)
            for i in range(len(pieces))
        ],
        0,
    )
    which = jnp.stack(
        [jnp.where(jnp.arange(sequences) == p.sequence, 1.0, 0.0) for p in pieces], 0
    )
    g_modul = jnp.sum(which[:, :, None, None] * sums[:, None], 0)
    g_modul = g_modul.reshape(sequences, 2, cols, width).transpose(2, 0, 1, 3)
    g_modul = jnp.sum(lax.all_to_all(g_modul, "col", 0, 0, tiled=True), 0).astype(BF)
    g_stream = g_stream + norm_back(g_normed * scaling, normal_one, inverse_one)

    g_skip_gain = jnp.sum(g_stream * skip_normal, 1)
    g_skip_bias = jnp.sum(g_stream, 1)
    g_joined = norm_back(g_stream * gain_skip, skip_normal, skip_inverse).astype(BF)
    g_joined, g_modul = lax.optimization_barrier((g_joined, g_modul))
    r_skip = Reduction(corner, [(both, g_joined)], True)
    g_both = rebuild_blocks(base, w_skip, width, g_joined)
    if custom_mesh():
        states = [r.state for r in r_self]
        g_both, got, states = lax.optimization_barrier((g_both, r_skip.state[0], states))
        here, away = outer(corner, r_skip.pairs, True, got)
        g_both, away, act, states = lax.optimization_barrier((g_both, away, act, states))
        r_skip.stage, r_skip.state = 1, [here, swap(away, "row", 1)]
        for beside, state in zip(r_self, states):
            beside.state = state
            beside.advance()
        g_latents, g_skip = to_features(g_both, pieces, cols, 2, block_rows)
        output = contract(weights_hidden, 1, act, stream, BF)
        output = tick(output, [r_skip])
        states = [r.state for r in r_self]
        states, here = lax.optimization_barrier((states, r_skip.state[0]))
        r_skip.state[0] = here
        for beside, state in zip(r_self, states):
            beside.state = state
            beside.advance()
    else:
        g_latents, g_skip = to_features(g_both, pieces, cols, 2, block_rows)
        output = contract(weights_hidden, 1, act, stream, BF)
    g_modul = shared(after(g_modul, g_skip), "row").reshape(-1, 2, width)
    g_modulation = einsum("sd,ske->dke", embed_rows, g_modul)

    g_gains = jnp.stack(
        [g_skip_gain, g_skip_bias, g_cross_gain, g_cross_bias, g_hidden_gain, g_hidden_bias], 0
    )
    g_gains = g_gains.reshape(6, cols, width).transpose(1, 0, 2)
    g_head = jnp.stack([g_q_gain, g_k_gain, g_cq_gain, g_tk_gain], 0).reshape(1, -1, width)
    g_gains = after(g_gains, g_skip)
    packed = jnp.concatenate([g_gains, jnp.broadcast_to(g_head, (cols, *g_head.shape[1:]))], 1)
    packed = jnp.sum(lax.all_to_all(packed, "col", 0, 0, tiled=True), 0)
    packed = jnp.sum(shared(packed, "row"), 0)
    output, g_hidden, packed, g_modulation = lax.optimization_barrier(
        (output, g_hidden, packed, g_modulation)
    )
    result = to_features(output, pieces, cols, 1, width)[0]
    g_gains = packed[:6]
    g_head = packed[6:].reshape(4, dim)
    return (
        result,
        g_latents,
        g_skip,
        r_skip.result().reshape(2, block_rows, width),
        g_modulation,
        jnp.concatenate([r.result() for r in r_self], 0).transpose(1, 0, 2),
        middle[4].T,
        middle[1],
        middle[2:4, :text_rows].transpose(1, 0, 2),
        middle[0].T,
        g_hidden[0],
        g_hidden[1].T,
        *[g_gains[i] for i in range(6)],
        *[g_head[i] for i in range(4)],
    )


def solution(mesh):
    return jax.shard_map(
        shards,
        mesh=mesh,
        in_specs=(
            P("col", "row"),
            P("col", "row"),
            P("row", "col"),
            P("row", None, "col"),
            P("row"),
            P(None, "row"),
            P("col", "row"),
            P(None, "row", "col"),
            P("row", None, "col"),
            P("row", None, "col"),
            P("col", "row"),
            P("row", "col"),
            P("row", None, "col"),
            P("col", "row"),
            P("row", "col"),
            P("col", "row"),
            P("col"),
            P("col"),
            P("col"),
            P("col"),
            P("col"),
            P("col"),
            P(),
            P(),
            P(),
            P(),
        ),
        out_specs=(
            P("col", "row"),
            P("col", "row"),
            P("col", "row"),
            P(None, "row", "col"),
            P("row", None, "col"),
            P("row", None, "col"),
            P("col", "row"),
            P("row", "col"),
            P("row", None, "col"),
            P("col", "row"),
            P("row", "col"),
            P("col", "row"),
            P("col"),
            P("col"),
            P("col"),
            P("col"),
            P("col"),
            P("col"),
            P(),
            P(),
            P(),
            P(),
        ),
        check_vma=False,
    )
```

```python
from functools import partial
import math

import jax
import jax.numpy as jnp
from jax import lax
from jax.experimental import pallas as pl
from jax.experimental.pallas import tpu as pltpu
from jax.sharding import PartitionSpec as P

L = 1024
EPSILON = 1e-06
BF = jnp.bfloat16
F32 = jnp.float32
KEYPAD = 128
DEVICES = ("col", "row")
LOG2E = math.log2(math.e)
VMEM = 60 << 20


def einsum(spec, left, right):
    return jnp.einsum(spec, left, right, preferred_element_type=F32)


def dot(left, right, dims):
    return lax.dot_general(left, right, (dims, ((), ())), preferred_element_type=F32)


def params():
    return pltpu.CompilerParams(vmem_limit_bytes=VMEM)


def step_of(count):
    return 256 if count % 256 == 0 else count


def wide(ref, head):
    parts = [ref[s, 0, head] for s in range(ref.shape[0])]
    return parts[0] if len(parts) == 1 else jnp.concatenate(parts, 1)


def valid_keys(length_ref, keys, step):
    return lax.broadcasted_iota(jnp.int32, (keys, step), 0) < length_ref[0]


def attend_kernel(masked, length_ref, q_ref, k_ref, v_ref, o_ref, r_ref, l_ref):
    groups, _, heads, dim, count = q_ref.shape
    step = step_of(count)
    factor = dim ** (-0.5) * LOG2E
    for head in range(heads):
        key = wide(k_ref, head).T
        value = wide(v_ref, head)
        keys = key.shape[0]
        value = jnp.concatenate([value, jnp.ones((8, keys), BF)], 0)
        for place in range(0, groups * count, step):
            group, first = divmod(place, count)
            query = q_ref[group, 0, head, :, first : first + step]
            expo = jnp.exp2(dot(key, query, ((1,), (0,))) * factor)
            if masked:
                expo = jnp.where(valid_keys(length_ref, keys, step), expo, 0.0)
            both = dot(value, expo.astype(BF), ((1,), (0,)))
            total = both[dim : dim + 1]
            mixed = both[:dim] * (1.0 / total)
            high = mixed.astype(BF)
            o_ref[group, head, :, first : first + step] = high
            r_ref[group, head, :, first : first + step] = (mixed - high.astype(F32)).astype(BF)
            l_ref[head, :, place : place + step] = jnp.log2(total)


def attend_back_kernel(
    masked, length_ref, q_ref, k_ref, v_ref, m_ref, r_ref, g_ref, l_ref, *outs
):
    groups, _, heads, dim, count = q_ref.shape
    step = step_of(count)
    scale = dim ** (-0.5)
    for head in range(heads):
        key = wide(k_ref, head)
        keys = key.shape[1]
        turned = key.T
        value = jnp.concatenate([wide(v_ref, head), jnp.ones((8, keys), BF)], 0).T
        g_key = g_value = None
        for place in range(0, groups * count, step):
            group, first = divmod(place, count)
            here = slice(first, first + step)
            query = q_ref[group, 0, head, :, here]
            grad = g_ref[group, head, :, here]
            mixed = m_ref[group, head, :, here].astype(F32)
            mixed = mixed + r_ref[group, head, :, here].astype(F32)
            delta = -jnp.sum(grad.astype(F32) * mixed, 0, keepdims=True)
            high = delta.astype(BF)
            rest = (delta - high.astype(F32)).astype(BF)
            more = jnp.concatenate([grad, high, rest, jnp.zeros((6, step), BF)], 0)
            probs = jnp.exp2(
                dot(turned, query, ((1,), (0,))) * (scale * LOG2E)
                - l_ref[head, :, place : place + step]
            )
            if masked:
                probs = jnp.where(valid_keys(length_ref, keys, step), probs, 0.0)
            product = (probs * dot(value, more, ((1,), (0,)))).astype(BF)
            g_query = dot(key, product, ((1,), (0,))) * scale
            part_value = dot(grad, probs.astype(BF), ((1,), (1,)))
            part_key = dot(query, product, ((1,), (1,)))
            g_value = part_value if g_value is None else g_value + part_value
            g_key = part_key if g_key is None else g_key + part_key
            outs[0][group, 0, head, :, here] = g_query.astype(outs[0].dtype)
        g_key = g_key * scale
        if len(outs) == 1:
            for group in range(groups):
                here = slice(group * count, (group + 1) * count)
                outs[0][group, 1, head] = g_key[:, here].astype(BF)
                outs[0][group, 2, head] = g_value[:, here].astype(BF)
        else:
            outs[1][0, 0, head] = g_key
            outs[2][0, 0, head] = g_value


def costs(heads, queries, keys, dim, products):
    return pl.CostEstimate(
        flops=2 * products * heads * queries * keys * 256,
        transcendentals=heads * queries * keys,
        bytes_accessed=2 * products * heads * dim * (queries + keys),
    )


def head_block(shape, count, kind=0):
    groups, _, _, dim, tokens = shape
    return pl.BlockSpec((groups, 1, count, dim, tokens), lambda h: (0, kind, h, 0, 0))


def mix_block(shape, count):
    groups, _, _, dim, tokens = shape
    return pl.BlockSpec((groups, count, dim, tokens), lambda h: (0, h, 0, 0))


def attend(length, query, key, value, kinds, masked, most):
    groups, _, heads, dim, count = query.shape
    many = math.gcd(heads, most)
    total = groups * count
    keys = key.shape[0] * key.shape[4]
    return pl.pallas_call(
        partial(attend_kernel, masked),
        grid=(heads // many,),
        in_specs=[pl.BlockSpec(memory_space=pltpu.SMEM)]
        + [head_block(a.shape, many, kind) for a, kind in zip((query, key, value), kinds)],
        out_specs=[
            mix_block(query.shape, many),
            mix_block(query.shape, many),
            pl.BlockSpec((many, 1, total), lambda h: (h, 0, 0)),
        ],
        out_shape=[
            jax.ShapeDtypeStruct((groups, heads, dim, count), BF),
            jax.ShapeDtypeStruct((groups, heads, dim, count), BF),
            jax.ShapeDtypeStruct((heads, 1, total), F32),
        ],
        cost_estimate=costs(heads, total, keys, dim, 2),
        compiler_params=params(),
        name="attend",
    )(length, query, key, value)


def attend_back(length, query, key, value, kinds, kept, grad, masked, most, stacked):
    mixed, rest, logs = kept
    groups, _, heads, dim, count = query.shape
    many = math.gcd(heads, most)
    total = groups * count
    keys = key.shape[0] * key.shape[4]
    if stacked:
        out_specs = pl.BlockSpec((groups, 3, many, dim, count), lambda h: (0, 0, h, 0, 0))
        out_shape = jax.ShapeDtypeStruct((groups, 3, heads, dim, count), BF)
    else:
        out_specs = [head_block(a.shape, many) for a in (query, key, value)]
        out_shape = [jax.ShapeDtypeStruct(a.shape, F32) for a in (query, key, value)]
    return pl.pallas_call(
        partial(attend_back_kernel, masked),
        grid=(heads // many,),
        in_specs=[pl.BlockSpec(memory_space=pltpu.SMEM)]
        + [head_block(a.shape, many, kind) for a, kind in zip((query, key, value), kinds)]
        + [mix_block(query.shape, many)] * 3
        + [pl.BlockSpec((many, 1, total), lambda h: (h, 0, 0))],
        out_specs=out_specs,
        out_shape=out_shape,
        cost_estimate=costs(heads, total, keys, dim, 5),
        compiler_params=params(),
        name="attend_back",
    )(length, query, key, value, mixed, rest, grad, logs)


def work(rows, depth, tokens, moved):
    return pl.CostEstimate(
        flops=2 * rows * depth * tokens,
        transcendentals=0,
        bytes_accessed=moved,
    )


def lanes(width):
    return -(-width // 128) * 128


def full(shape):
    return pl.BlockSpec(shape, lambda *_: (0,) * len(shape))


def project(weight, kinds, values, dtypes, joined=False):
    _, cols, depth, width = weight.shape
    tokens = values[0].shape[1]
    outs = 1 if joined else len(kinds)

    def kernel(*refs):
        blocks = refs[: len(kinds)]
        given = refs[len(kinds) : -outs]
        total = None
        for index, block in enumerate(blocks):
            part = dot(block[0, 0], given[index % len(given)][...], ((0,), (0,)))
            if not joined:
                refs[index - outs][...] = part.astype(dtypes[index])
            total = part if total is None else total + part
        if joined:
            refs[-1][...] = total.astype(dtypes[0])

    return pl.pallas_call(
        kernel,
        grid=(cols,),
        in_specs=[
            pl.BlockSpec((1, 1, depth, width), partial(lambda k, c: (k, c, 0, 0), kind))
            for kind in kinds
        ]
        + [full(v.shape) for v in values],
        out_specs=[pl.BlockSpec((width, tokens), lambda c: (c, 0))] * outs,
        out_shape=[jax.ShapeDtypeStruct((cols * width, tokens), dtypes[i]) for i in range(outs)],
        cost_estimate=work(len(kinds) * cols * width, depth, tokens, 8 * depth * tokens),
        compiler_params=params(),
        name="project",
    )(*([weight] * len(kinds)), *values)


def rebuild(weight, kinds, values, dtype):
    _, cols, depth, width = weight.shape
    tokens = values[0].shape[1]
    tile = depth // 4

    def kernel(*refs):
        total = None
        for block, given in zip(refs[: len(kinds)], refs[len(kinds) : -1]):
            for col in range(cols):
                part = dot(block[0, col], given[col * width : (col + 1) * width, :], ((1,), (0,)))
                total = part if total is None else total + part
        refs[-1][...] = total.astype(dtype)

    return pl.pallas_call(
        kernel,
        grid=(4,),
        in_specs=[
            pl.BlockSpec((1, cols, tile, width), partial(lambda k, j: (k, 0, j, 0), kind))
            for kind in kinds
        ]
        + [full(v.shape) for v in values],
        out_specs=pl.BlockSpec((tile, tokens), lambda j: (j, 0)),
        out_shape=jax.ShapeDtypeStruct((depth, tokens), dtype),
        cost_estimate=work(depth, len(kinds) * cols * width, tokens, 8 * depth * tokens),
        compiler_params=params(),
        name="rebuild",
    )(*([weight] * len(kinds)), *values)


def project_blocks(base, blocks, width, values):
    many = len(blocks)
    depth, broad = blocks[0].shape
    tokens = values.shape[1]
    tile = depth // 4

    def kernel(base_ref, *refs):
        values_ref, out_ref = refs[many:]

        @pl.when(pl.program_id(0) == 0)
        def _():
            out_ref[...] = jnp.zeros_like(out_ref)

        for index in range(many):
            here = pl.ds(pl.multiple_of((index ^ base_ref[0]) * width, width), width)
            out_ref[here, :] += dot(refs[index][...], values_ref[...], ((0,), (0,)))[:width]

    return pl.pallas_call(
        kernel,
        grid_spec=pltpu.PrefetchScalarGridSpec(
            num_scalar_prefetch=1,
            grid=(4,),
            in_specs=[pl.BlockSpec((tile, broad), lambda j, b: (j, 0))] * many
            + [pl.BlockSpec((tile, tokens), lambda j, b: (j, 0))],
            out_specs=pl.BlockSpec((many * width, tokens), lambda j, b: (0, 0)),
        ),
        out_shape=jax.ShapeDtypeStruct((many * width, tokens), F32),
        cost_estimate=work(many * width, depth, tokens, 4 * depth * tokens),
        compiler_params=params(),
        name="project_blocks",
    )(base, *blocks, values)


def rebuild_blocks(base, blocks, width, values):
    many = len(blocks)
    depth, broad = blocks[0].shape
    tokens = values.shape[1]
    tile = depth // 4

    def kernel(base_ref, *refs):
        values_ref, out_ref = refs[many:]
        total = None
        for index in range(many):
            here = pl.ds(pl.multiple_of((index ^ base_ref[0]) * width, width), width)
            part = dot(refs[index][:, :width], values_ref[here, :], ((1,), (0,)))
            total = part if total is None else total + part
        out_ref[...] = total.astype(BF)

    return pl.pallas_call(
        kernel,
        grid_spec=pltpu.PrefetchScalarGridSpec(
            num_scalar_prefetch=1,
            grid=(4,),
            in_specs=[pl.BlockSpec((tile, broad), lambda j, b: (j, 0))] * many
            + [pl.BlockSpec(values.shape, lambda j, b: (0, 0))],
            out_specs=pl.BlockSpec((tile, tokens), lambda j, b: (j, 0)),
        ),
        out_shape=jax.ShapeDtypeStruct((depth, tokens), BF),
        cost_estimate=work(many * width, depth, tokens, 4 * depth * tokens),
        compiler_params=params(),
        name="rebuild_blocks",
    )(base, *blocks, values)


def outer(place, pairs, across, got=None):
    cols = lax.axis_size("col")
    lefts = []
    for left, _ in pairs:
        if not any(left is other for other in lefts):
            lefts.append(left)
    which = [next(i for i, l in enumerate(lefts) if l is left) for left, _ in pairs]
    rights = [right for _, right in pairs]
    many = len(pairs)
    rows, tokens = lefts[0].shape
    width = rights[0].shape[0] // cols
    broad = lanes(width)
    chunk = rows // 8
    flip = 1 if got is None else 0

    def kernel(place_ref, *refs):
        left_refs = refs[: len(lefts)]
        right_refs = refs[len(lefts) : len(lefts) + many]
        rest = refs[len(lefts) + many :]
        for index in range(many):
            right = right_refs[index][...]
            if broad > width:
                right = jnp.concatenate([right, jnp.zeros((broad - width, tokens), BF)], 0)
            part = dot(left_refs[which[index]][...], right, ((1,), (1,)))
            if got is None:
                rest[0][index, 0] = part.astype(BF)
            elif not across:
                part = (part + rest[0][index, 0].astype(F32)).astype(BF)

                @pl.when(pl.program_id(0) == place_ref[2])
                def _():
                    rest[1][index] = part.reshape(4, 2, chunk, broad)

                @pl.when(pl.program_id(0) != place_ref[2])
                def _():
                    rest[2][index] = part.reshape(4, 2, chunk, broad)
            else:
                part = (part + rest[0][index, 0].astype(F32)).astype(BF)
                part = part.reshape(4, 2, chunk, broad)

                @pl.when(place_ref[1] == 0)
                def _():
                    rest[1][index, 0] = part[:, 0]
                    rest[2][index, 0] = part[:, 1]

                @pl.when(place_ref[1] != 0)
                def _():
                    rest[1][index, 0] = part[:, 1]
                    rest[2][index, 0] = part[:, 0]

    whole = pl.BlockSpec((many, 1, rows, broad), lambda y, place: (0, y, 0, 0))
    piece = pl.BlockSpec((many, 1, 4, chunk, broad), lambda y, place: (0, y, 0, 0, 0))
    all_rows = pl.BlockSpec((many, 4, 2, chunk, broad), lambda y, place: (0, 0, 0, 0, 0))
    if got is None:
        given, out_specs = [], whole
        out_shape = jax.ShapeDtypeStruct((many, cols // 2, rows, broad), BF)
    else:
        given, out_specs = [got], [piece, piece] if across else [all_rows, all_rows]
        shape = (many, cols // 2, 4, chunk, broad) if across else (many, 4, 2, chunk, broad)
        out_shape = [jax.ShapeDtypeStruct(shape, BF)] * 2
    return pl.pallas_call(
        kernel,
        grid_spec=pltpu.PrefetchScalarGridSpec(
            num_scalar_prefetch=1,
            grid=(cols // 2,),
            in_specs=[pl.BlockSpec((rows, tokens), lambda y, place: (0, 0)) for _ in lefts]
            + [
                pl.BlockSpec((width, tokens), lambda y, place: (2 * y + (place[0] ^ flip), 0))
                for _ in rights
            ]
            + [whole] * len(given),
            out_specs=out_specs,
        ),
        out_shape=out_shape,
        cost_estimate=work(
            rows, tokens, many * cols // 2 * broad, 2 * rows * cols * broad * many
        ),
        compiler_params=params(),
        name="outer",
    )(place, *lefts, *rights, *given)


def outer_all(pairs):
    cols = lax.axis_size("col")
    parts = lax.axis_size("row")
    if not custom_mesh():
        blocks = [einsum("kt,cnt->ckn", a, b.reshape(cols, -1, b.shape[1])) for a, b in pairs]
        blocks = [b.reshape(cols, parts, -1, b.shape[2]).astype(BF) for b in blocks]
        return jnp.concatenate(blocks, 2)
    lefts = []
    for left, _ in pairs:
        if not any(left is other for other in lefts):
            lefts.append(left)
    which = [next(i for i, l in enumerate(lefts) if l is left) for left, _ in pairs]
    rights = [right for _, right in pairs]
    sizes = [left.shape[0] // parts for left, _ in pairs]
    width = rights[0].shape[0] // cols

    def kernel(*refs):
        for index, size in enumerate(sizes):
            left = refs[which[index]][...]
            part = dot(left, refs[len(lefts) + index][...], ((1,), (1,))).astype(BF)
            start = sum(sizes[:index])
            refs[-1][0, :, start : start + size] = part.reshape(parts, size, width)

    return pl.pallas_call(
        kernel,
        grid=(cols,),
        in_specs=[full(left.shape) for left in lefts]
        + [pl.BlockSpec((width, right.shape[1]), lambda c: (c, 0)) for right in rights],
        out_specs=pl.BlockSpec((1, parts, sum(sizes), width), lambda c: (c, 0, 0, 0)),
        out_shape=jax.ShapeDtypeStruct((cols, parts, sum(sizes), width), BF),
        cost_estimate=work(
            parts * sum(sizes), lefts[0].shape[1], cols * width, 3 * parts * sum(sizes) * cols * width
        ),
        compiler_params=params(),
        name="outer_all",
    )(*lefts, *rights)


def expand(weight, kind, values):
    _, many, depth, hidden = weight.shape
    tokens = values.shape[1]
    tile = 384 if hidden % 384 == 0 else hidden
    slope = 0.79788456
    cubic = 0.044715

    def kernel(weight_ref, values_ref, act_ref, slope_ref):
        for index in range(many):
            inner = dot(weight_ref[0, index], values_ref[...], ((0,), (0,)))
            square = inner * inner
            bent = jnp.tanh(inner * (slope + slope * cubic * square))
            half = 0.5 + 0.5 * bent
            act_ref[index] = (inner * half).astype(BF)
            rise = slope + 3.0 * slope * cubic * square
            slope_ref[index] = (half + 0.5 * inner * (1.0 - bent * bent) * rise).astype(BF)

    return pl.pallas_call(
        kernel,
        grid=(hidden // tile,),
        in_specs=[
            pl.BlockSpec((1, many, depth, tile), lambda j: (kind, 0, 0, j)),
            full(values.shape),
        ],
        out_specs=[pl.BlockSpec((many, tile, tokens), lambda j: (0, j, 0))] * 2,
        out_shape=[jax.ShapeDtypeStruct((many, hidden, tokens), BF)] * 2,
        cost_estimate=work(many * hidden, depth, tokens, 3 * many * hidden * depth),
        compiler_params=params(),
        name="expand",
    )(weight, values)


def expand_back(weight, kind, values, slopes):
    _, many, depth, hidden = weight.shape
    tokens = values.shape[1]
    tile = 384 if hidden % 384 == 0 else hidden

    def kernel(weight_ref, values_ref, slope_ref, out_ref):
        for index in range(many):
            part = dot(weight_ref[0, index], values_ref[...], ((0,), (0,)))
            out_ref[index] = (part * slope_ref[index].astype(F32)).astype(BF)

    return pl.pallas_call(
        kernel,
        grid=(hidden // tile,),
        in_specs=[
            pl.BlockSpec((1, many, depth, tile), lambda j: (kind, 0, 0, j)),
            full(values.shape),
            pl.BlockSpec((many, tile, tokens), lambda j: (0, j, 0)),
        ],
        out_specs=pl.BlockSpec((many, tile, tokens), lambda j: (0, j, 0)),
        out_shape=jax.ShapeDtypeStruct((many, hidden, tokens), BF),
        cost_estimate=work(many * hidden, depth, tokens, 3 * many * hidden * depth),
        compiler_params=params(),
        name="expand_back",
    )(weight, values, slopes)


def contract(weight, kind, values, added, dtype):
    _, many, depth, hidden = weight.shape
    tokens = values.shape[2]
    tile = depth // 4
    extra = [] if added is None else [added]

    def kernel(weight_ref, values_ref, *refs):
        total = refs[0][...] if extra else None
        for index in range(many):
            part = dot(weight_ref[0, index], values_ref[index], ((1,), (0,)))
            total = part if total is None else total + part
        refs[-1][...] = total.astype(dtype)

    line = pl.BlockSpec((tile, tokens), lambda j: (j, 0))
    return pl.pallas_call(
        kernel,
        grid=(4,),
        in_specs=[
            pl.BlockSpec((1, many, tile, hidden), lambda j: (kind, 0, j, 0)),
            full(values.shape),
        ]
        + [line] * len(extra),
        out_specs=line,
        out_shape=jax.ShapeDtypeStruct((depth, tokens), dtype),
        cost_estimate=work(depth, many * hidden, tokens, 3 * many * hidden * depth),
        compiler_params=params(),
        name="contract",
    )(weight, values, *extra)


def hidden_outer(grad_out, act, normed, grad_inner):
    many, hidden, tokens = act.shape
    depth = grad_out.shape[0]
    parts = 2 if hidden % 256 == 0 else 1
    tile = hidden // parts

    def kernel(out_ref, act_ref, normed_ref, inner_ref, grad_ref):
        kind = pl.program_id(0)

        @pl.when(kind == 0)
        def _():
            grad_ref[0, 0] = dot(normed_ref[...], inner_ref[0], ((1,), (1,))).astype(BF)

        @pl.when(kind == 1)
        def _():
            grad_ref[0, 0] = dot(out_ref[...], act_ref[0], ((1,), (1,))).astype(BF)

    return pl.pallas_call(
        kernel,
        grid=(2, many, parts),
        in_specs=[
            pl.BlockSpec((depth, tokens), lambda s, p, j: (0, 0)),
            pl.BlockSpec((1, tile, tokens), lambda s, p, j: (s * p, s * j, 0)),
            pl.BlockSpec((depth, tokens), lambda s, p, j: (0, 0)),
            pl.BlockSpec(
                (1, tile, tokens),
                lambda s, p, j: (p + s * (many - 1 - p), j + s * (parts - 1 - j), 0),
            ),
        ],
        out_specs=pl.BlockSpec((1, 1, depth, tile), lambda s, p, j: (s, p, 0, j)),
        out_shape=jax.ShapeDtypeStruct((2, many, depth, hidden), BF),
        cost_estimate=work(2 * depth, tokens, many * hidden, 5 * many * depth * hidden),
        compiler_params=params(),
        name="hidden_outer",
    )(grad_out, act, normed, grad_inner)


def assemble(place, own, got, middle=None):
    rows, width = own.shape[-2:]

    def kernel(place_ref, own_ref, got_ref, out_ref):
        @pl.when(pl.program_id(0) == place_ref[1])
        def _():
            out_ref[0, 0] = own_ref[...].reshape(rows, width)

        @pl.when(pl.program_id(0) != place_ref[1])
        def _():
            out_ref[0, 0] = got_ref[...].reshape(rows, width)

    def spec(ours):
        def index(x, z, place):
            phase = place[1] if ours else 1 - place[1]
            inside = (x == phase).astype(jnp.int32)
            level = (inside * z + (1 - inside) * 3 * (1 - phase)) ^ place[0]
            return (level, 0, 0) if middle is None else (level, middle, 0, 0)

        shape = (1, rows, width) if middle is None else (1, 1, rows, width)
        return pl.BlockSpec(shape, index)

    return pl.pallas_call(
        kernel,
        grid_spec=pltpu.PrefetchScalarGridSpec(
            num_scalar_prefetch=1,
            grid=(2, 4),
            in_specs=[spec(True), spec(False)],
            out_specs=pl.BlockSpec((1, 1, rows, width), lambda x, z, place: (z, x, 0, 0)),
        ),
        out_shape=jax.ShapeDtypeStruct((4, 2, rows, width), BF),
        cost_estimate=work(1, 1, 1, 32 * rows * width),
        name="assemble",
    )(place, own, got).reshape(8 * rows, width)


def normalize(values):
    average = jnp.mean(values, 0, keepdims=True)
    centred = values - average
    inverse = lax.rsqrt(jnp.mean(centred * centred, 0, keepdims=True) + EPSILON)
    return centred * inverse, inverse


def norm_back(grad, normal, inverse):
    average = jnp.mean(grad, 0, keepdims=True)
    crossed = jnp.mean(grad * normal, 0, keepdims=True)
    return inverse * (grad - average - normal * crossed)


def head_norm(values, gain):
    average = jnp.mean(values, 1, keepdims=True)
    centred = values - average
    variance = jnp.mean(centred * centred, 1, keepdims=True)
    return centred * lax.rsqrt(variance + EPSILON) * gain[None, :, None]


def rope_tables(places, head_dim):
    quarter = head_dim // 4
    freqs = jnp.exp(jnp.arange(quarter, dtype=F32) * (-4.0 * math.log(10000.0) / head_dim))
    rows = freqs[:, None] * places[0].astype(F32)[None, :]
    cols = freqs[:, None] * places[1].astype(F32)[None, :]
    angles = jnp.concatenate([rows, rows, cols, cols], 0)
    return jnp.cos(angles), jnp.sin(angles)


def rotate(values):
    quarter = values.shape[1] // 4
    one, two, three, four = (values[:, i * quarter : (i + 1) * quarter] for i in range(4))
    return jnp.concatenate([-two, one, -four, three], 1)


class Piece:
    def __init__(self, start, count, group, sequence):
        self.start = start
        self.count = count
        self.group = group
        self.sequence = sequence


def pieces_of(cols, sequences):
    mine = lax.axis_index("col")
    if cols == 4 and sequences == 3:
        return [
            Piece(0, L // 2, 2, mine // 2),
            Piece(2 * L, L // 4, 4, jnp.int32(2)),
        ]
    return [Piece(s * L, L // cols, cols, jnp.int32(s)) for s in range(sequences)]


def groups_of(size, cols):
    return [list(range(i, i + size)) for i in range(0, cols, size)]


def exchange(values, size, cols):
    if size == cols:
        return lax.all_to_all(values, "col", 0, 0, tiled=True)
    return lax.all_to_all(
        values, "col", 0, 0, tiled=True, axis_index_groups=groups_of(size, cols)
    )


def cut_size(pieces):
    return math.gcd(*(p.count for p in pieces), *(p.start for p in pieces))


def locate(pieces, unit, block):
    device = inside = None
    at = 0
    for piece in pieces:
        each = piece.count // unit
        rest = block - piece.start // unit
        there = (rest // each, at + rest % each)
        if device is None:
            device, inside = there
        else:
            later = (rest >= 0).astype(jnp.int32)
            device = later * there[0] + (1 - later) * device
            inside = later * there[1] + (1 - later) * inside
        at += each
    return device, inside


def to_tokens(arrays, pieces, cols, rows):
    width, tokens = arrays[0].shape
    kinds = len(arrays)
    unit = cut_size(pieces)
    total = sum(p.count for p in pieces)
    if unit % 128:
        values = jnp.stack([a.reshape(-1, rows, tokens) for a in arrays], 1).astype(BF)
        values = values.reshape(kinds * width, tokens)
        parts = [
            jnp.concatenate(
                [values[:, p.start + j * p.count : p.start + (j + 1) * p.count] for p in pieces], 1
            )
            for j in range(cols)
        ]
        dealt = jnp.stack(parts, 0)
    else:

        def kernel(*refs):
            for kind in range(kinds):
                for at in range(0, width, rows):
                    to = at * kinds + kind * rows
                    refs[-1][0, to : to + rows] = refs[kind][at : at + rows].astype(BF)

        def index(block):
            device, inside = locate(pieces, unit, block)
            return (device, 0, inside)

        dealt = pl.pallas_call(
            kernel,
            grid=(tokens // unit,),
            in_specs=[pl.BlockSpec((width, unit), lambda b: (0, b))] * kinds,
            out_specs=pl.BlockSpec((1, kinds * width, unit), index),
            out_shape=jax.ShapeDtypeStruct((cols, kinds * width, total), BF),
            cost_estimate=pl.CostEstimate(
                flops=0, transcendentals=0, bytes_accessed=4 * kinds * width * tokens
            ),
            name="deal",
        )(*arrays)
    got = exchange(dealt, cols, cols)
    return got.reshape(-1, total)


def to_features(values, pieces, cols, kinds, rows):
    got = exchange(values.reshape(cols, -1, values.shape[1]), cols, cols)
    unit = cut_size(pieces)
    width = got.shape[1] // kinds
    tokens = cols * got.shape[2]
    if unit % 128:
        parts = []
        at = 0
        for piece in pieces:
            parts += [got[j, :, at : at + piece.count] for j in range(cols)]
            at += piece.count
        whole = jnp.concatenate(parts, 1).astype(F32).reshape(-1, kinds, rows, tokens)
        return [whole[:, kind].reshape(width, tokens) for kind in range(kinds)]

    def kernel(got_ref, *refs):
        for kind in range(kinds):
            for at in range(0, width, rows):
                start = at * kinds + kind * rows
                refs[kind][at : at + rows] = got_ref[0, start : start + rows].astype(F32)

    def index(block):
        device, inside = locate(pieces, unit, block)
        return (device, 0, inside)

    return pl.pallas_call(
        kernel,
        grid=(tokens // unit,),
        in_specs=[pl.BlockSpec((1, kinds * width, unit), index)],
        out_specs=[pl.BlockSpec((width, unit), lambda b: (0, b))] * kinds,
        out_shape=[jax.ShapeDtypeStruct((width, tokens), F32)] * kinds,
        cost_estimate=pl.CostEstimate(
            flops=0, transcendentals=0, bytes_accessed=6 * kinds * width * tokens
        ),
        name="undeal",
    )(got)


def shared(values, axis):
    size = lax.axis_size(axis)
    return lax.all_to_all(
        jnp.broadcast_to(values[None], (size, *values.shape)), axis, 0, 0, tiled=True
    )


def swap(values, axis, bit):
    size = lax.axis_size(axis)
    return lax.ppermute(values, axis, [(i, i ^ bit) for i in range(size)])


def custom_mesh():
    return (lax.axis_size("row"), lax.axis_size("col")) == (8, 4)


def gather_weights(blocks):
    cols = lax.axis_size("col")
    most = max(block.shape[0] for block in blocks)
    padded = [jnp.pad(b, ((0, most - b.shape[0]), (0, 0))) for b in blocks]
    whole = lax.all_gather(jnp.stack(padded, 0), DEVICES, axis=1, tiled=True)
    return whole.reshape(len(blocks), cols, -1, blocks[0].shape[1])


class Gathering:
    last = 4

    def __init__(self, block, up, place):
        self.up = up
        self.place = place
        self.stage = 0
        self.state = [block]
        if not custom_mesh():
            cols = lax.axis_size("col")
            whole = lax.all_gather(block, DEVICES, axis=0, tiled=True)
            self.state = list(whole.reshape(cols, -1, block.shape[1]))
            self.stage = self.last

    def levels(self, block):
        return [block] + [swap(block, "row", 2 * level) for level in (1, 2, 3)]

    def advance(self):
        state = self.state
        self.stage += 1
        if self.stage == 1:
            self.state = [state[0], swap(state[0], "col", 2)] if self.up else self.levels(state[0])
        elif self.stage == 2:
            stack = jnp.stack(state, 0)
            self.state = self.levels(stack) if self.up else [stack, swap(stack, "col", 2)]
        elif self.stage == 3 and self.up:
            stack = jnp.stack(state, 0)
            self.state = [stack, swap(stack, "row", 1)]
        elif self.stage == 3:
            self.state = state + [swap(a, "row", 1) for a in state]
        else:
            if self.up:
                mine, other = (assemble(self.place, *state, k) for k in (0, 1))
            else:
                mine = assemble(self.place, state[0], state[2])
                other = assemble(self.place, state[1], state[3])
            self.state = [mine, swap(mine, "col", 1), other, swap(other, "col", 1)]

    def result(self):
        while self.stage < self.last:
            self.advance()
        return self.state


def pick(values, axis, index):
    return lax.dynamic_index_in_dim(values, index, axis, False)


def add(left, right):
    return (left.astype(F32) + right.astype(F32)).astype(BF)


class Reduction:
    last = 4

    def __init__(self, place, pairs, across):
        self.place = place
        self.across = across
        self.pairs = pairs
        self.width = pairs[0][1].shape[0] // lax.axis_size("col")
        self.stage = 0
        if custom_mesh():
            self.state = [swap(outer(place, pairs, across), "col", 1)]
            return
        self.stage = self.last
        cols = lax.axis_size("col")
        whole = jnp.stack(
            [einsum("kt,cnt->ckn", a, b.reshape(cols, -1, b.shape[1])) for a, b in pairs], 0
        )
        flat = whole.reshape(len(pairs), -1, whole.shape[3]).astype(BF)
        self.state = [lax.psum_scatter(flat, DEVICES, scatter_dimension=1, tiled=True)]

    def advance(self):
        state = self.state
        self.stage += 1
        if self.stage == 1:
            here, away = outer(self.place, self.pairs, self.across, state[0])
            self.state = [here, swap(away, "row", 1) if self.across else swap(away, "col", 2)]
        elif self.stage == 2:
            axis, index = (1, self.place[2]) if self.across else (2, self.place[1])
            away = add(*(pick(a, axis, 1 - index) for a in state))
            here = add(*(pick(a, axis, index) for a in state))
            self.state = [here, swap(away, "col", 2) if self.across else swap(away, "row", 1)]
        elif self.stage == 3:
            level = lax.axis_index("row") // 2
            total = add(*state)
            self.state = [pick(total, 1, level)] + [
                swap(pick(total, 1, level ^ other), "row", 2 * other) for other in (1, 2, 3)
            ]
        else:
            total = state[0].astype(F32)
            for other in state[1:]:
                total = total + other.astype(F32)
            self.state = [total[..., : self.width]]

    def result(self):
        while self.stage < self.last:
            self.advance()
        return self.state[0].astype(F32)


def tick(values, running):
    active = [r for r in running if r.stage < r.last]
    if active:
        values, states = lax.optimization_barrier((values, [r.state for r in active]))
        for beside, state in zip(active, states):
            beside.state = state
            beside.advance()
    return values


def after(values, done):
    return lax.optimization_barrier((values, done))[0]


def shards(
    latents,
    skip_input,
    condition,
    text_states,
    text_lengths,
    positions,
    out_grad,
    skip_weight,
    modulation,
    self_inputs,
    self_output,
    cross_query,
    cross_keyvalue,
    cross_output,
    expand_weight,
    reduce_weight,
    skip_gain,
    skip_bias,
    cross_gain,
    cross_bias,
    hidden_gain,
    hidden_bias,
    query_gain,
    key_gain,
    cross_query_gain,
    text_key_gain,
):
    cols = lax.axis_size("col")
    rows = lax.axis_size("row")
    mine = lax.axis_index("col")
    my_row = lax.axis_index("row")
    width, row_tokens = latents.shape
    depth = width * cols
    dim = query_gain.shape[0]
    heads = depth // dim
    sequences = row_tokens // L
    tokens = row_tokens // cols
    texts = text_states.shape[1]
    keys = -(-texts // KEYPAD) * KEYPAD
    pieces = pieces_of(cols, sequences)
    starts = [sum(p.count for p in pieces[:i]) for i in range(len(pieces))]
    place = jnp.stack([my_row // 2, my_row % 2]).astype(jnp.int32)
    corner = jnp.stack([mine % 2, my_row % 2, mine // 2]).astype(jnp.int32)
    base = (mine if custom_mesh() else jnp.zeros_like(mine)).astype(jnp.int32)[None]

    def cut(values, index):
        return values[..., starts[index] : starts[index] + pieces[index].count]

    block_rows = depth // rows
    both = to_tokens([latents, skip_input], pieces, cols, block_rows)

    weights_one = gather_weights([*(self_inputs[:, i] for i in range(3)), self_output.T])
    weights_two = gather_weights(
        [cross_query, cross_output.T, *(cross_keyvalue[:, i] for i in range(2))]
    )
    skip_block = jnp.concatenate([skip_weight[0], skip_weight[1]], 0)
    skip_block = jnp.pad(skip_block, ((0, 0), (0, lanes(width) - width)))
    w_skip = Gathering(skip_block, False, place).result()
    weights_hidden = gather_weights([expand_weight, reduce_weight.T])

    places = jnp.concatenate(
        [
            lax.dynamic_slice_in_dim(positions, p.start + mine * p.count, p.count, 1)
            for p in pieces
        ],
        1,
    )

    embed = jax.nn.silu(after(condition, both).astype(F32)).astype(BF)
    embed = shared(embed, "row").reshape(-1, width)
    embed = shared(embed, "col").transpose(1, 0, 2).reshape(-1, depth)
    embed_rows = lax.dynamic_slice_in_dim(embed, my_row * block_rows, block_rows, 1)
    modul = einsum("sd,dke->ske", embed_rows, modulation).reshape(rows, sequences, 2, width)
    modul = jnp.sum(lax.all_to_all(modul, "row", 0, 0, tiled=True), 0)
    gains = jnp.stack(
        [skip_gain, skip_bias, cross_gain, cross_bias, hidden_gain, hidden_bias], 0
    )
    table = jnp.concatenate([gains, modul.reshape(-1, width)], 0)
    table = shared(table, "col").transpose(1, 0, 2).reshape(-1, depth)
    modul = table[6:].reshape(sequences, 2, depth)
    chosen = [lax.dynamic_index_in_dim(modul, p.sequence, 0, False) for p in pieces]
    columns = lax.optimization_barrier(jnp.concatenate([table[:6], *chosen], 0)).T
    gain_skip, bias_skip, gain_cross, bias_cross, gain_hidden, bias_hidden = (
        columns[:, i : i + 1] for i in range(6)
    )
    token_index = lax.broadcasted_iota(jnp.int32, (1, tokens), 1)

    def per_token(which):
        result = columns[:, 6 + which : 7 + which]
        for index in range(1, len(pieces)):
            column = columns[:, 6 + 2 * index + which : 7 + 2 * index + which]
            result = jnp.where(token_index >= starts[index], column, result)
        return jnp.broadcast_to(result, (depth, tokens))

    shifting = per_token(0)
    scaling = 1.0 + per_token(1)

    text = shared(jnp.pad(after(text_states, both), ((0, 0), (0, keys - texts), (0, 0))), "col")
    joined = project_blocks(base, w_skip, width, both)
    skip_normal, skip_inverse = normalize(joined)
    stream = skip_normal * gain_skip + bias_skip
    normal_one, inverse_one = normalize(stream)
    normed_one = (normal_one * scaling + shifting).astype(BF)
    raw = project(weights_one, [0, 1, 2], [normed_one], [F32, F32, BF])
    raw, text = lax.optimization_barrier((raw, text))
    raw = [r.reshape(heads, dim, tokens) for r in raw]
    cosine, sine = rope_tables(places, dim)

    def self_piece(value, gain):
        normal = head_norm(value, gain)
        return normal * cosine[None] + rotate(normal) * sine[None]

    rot_query, query_pull = jax.vjp(self_piece, raw[0], query_gain)
    rot_key, key_pull = jax.vjp(self_piece, raw[1], key_gain)
    triple = [rot_query.astype(BF), rot_key.astype(BF), raw[2]]

    def to_heads(parts, index):
        size = pieces[index].group
        split = [cut(p, index).reshape(size, heads // size, dim, -1) for p in parts]
        return exchange(jnp.stack(split, 1), size, cols)

    none = jnp.zeros((1,), jnp.int32)
    saved_self = []
    mixed_parts = []
    for index, piece in enumerate(pieces):
        whole = to_heads(triple, index)
        kept = attend(none, whole, whole, whole, (0, 1, 2), False, 2)
        saved_self.append((whole, kept))
        mixed_parts.append(exchange(kept[0], piece.group, cols).reshape(depth, -1))
    mixed_one = jnp.concatenate(mixed_parts, 1)
    text = after(text, mixed_one)
    stream = stream + rebuild(weights_one, [3], [mixed_one], F32)
    normal_two, inverse_two = normalize(stream)
    normed_two = (normal_two * gain_cross + bias_cross).astype(BF)
    raw_cross = project(weights_two, [0], [normed_two], [F32])[0].reshape(heads, dim, tokens)
    norm_query, cross_pull = jax.vjp(head_norm, raw_cross, cross_query_gain)
    text = jnp.concatenate(
        [lax.dynamic_index_in_dim(text, p.sequence, 1, False) for p in pieces], 1
    )
    text = text.transpose(0, 2, 1).reshape(-1, len(pieces) * keys)
    text_rows = text.shape[0] // rows
    text_wide = jnp.pad(
        text.reshape(rows, text_rows, -1), ((0, 0), (0, block_rows - text_rows), (0, 0))
    ).reshape(depth, -1)
    raw_text, value_two = project(weights_two, [2, 3], [text_wide], [F32, BF])
    norm_key, text_pull = jax.vjp(head_norm, raw_text.reshape(heads, dim, -1), text_key_gain)
    query_two = norm_query.astype(BF)
    key_two = norm_key.astype(BF)
    value_two = value_two.reshape(heads, dim, -1)
    saved_cross = []
    mixed_parts = []
    for index, piece in enumerate(pieces):
        length = lax.dynamic_index_in_dim(text_lengths, piece.sequence, 0, True)
        here = slice(index * keys, (index + 1) * keys)
        inputs = [cut(query_two, index), key_two[:, :, here], value_two[:, :, here]]
        inputs = [length] + [a[None, None] for a in inputs] + [(0, 0, 0)]
        kept = attend(*inputs, True, 4)
        saved_cross.append((inputs, kept))
        mixed_parts.append(kept[0].reshape(depth, -1))
    mixed_two = jnp.concatenate(mixed_parts, 1)
    stream = stream + rebuild(weights_two, [1], [mixed_two], F32)
    normal_three, inverse_three = normalize(stream)
    normed_three = (normal_three * gain_hidden + bias_hidden).astype(BF)
    grad_out = to_tokens([after(out_grad, joined)], pieces, cols, width)
    act, slopes = expand(weights_hidden, 0, normed_three)

    g_inner = expand_back(weights_hidden, 1, grad_out, slopes)
    g_hidden = hidden_outer(grad_out, act, normed_three, g_inner)
    g_inner, g_hidden = lax.optimization_barrier((g_inner, g_hidden))
    g_normed = contract(weights_hidden, 0, g_inner, None, F32)
    g_hidden = lax.psum_scatter(
        g_hidden.reshape(2, -1, g_hidden.shape[3]), DEVICES, scatter_dimension=1, tiled=True
    ).astype(F32)
    g_hidden_gain = jnp.sum(g_normed * normal_three, 1)
    g_hidden_bias = jnp.sum(g_normed, 1)
    g_stream = grad_out.astype(F32) + norm_back(g_normed * gain_hidden, normal_three, inverse_three)

    g_low = g_stream.astype(BF)
    g_mixed = project(weights_two, [1], [g_low], [BF])[0].reshape(heads, dim, tokens)
    pairs = [(g_low, mixed_two)]
    g_queries = []
    g_keys = []
    g_values = []
    for index, piece in enumerate(pieces):
        inputs, kept = saved_cross[index]
        grads = attend_back(*inputs, kept, cut(g_mixed, index)[None], True, 4, False)
        g_queries.append(grads[0][0, 0])
        g_keys.append(grads[1][0, 0])
        g_values.append(grads[2][0, 0])
    g_raw_cross, g_cq_gain = cross_pull(jnp.concatenate(g_queries, 2))
    g_raw_text, g_tk_gain = text_pull(jnp.concatenate(g_keys, 2))
    g_craw = g_raw_cross.astype(BF).reshape(depth, tokens)
    g_pair = [
        g_raw_text.astype(BF).reshape(depth, -1),
        jnp.concatenate(g_values, 2).astype(BF).reshape(depth, -1),
    ]
    g_normed = rebuild(weights_two, [0], [g_craw], F32)
    pairs.append((normed_two, g_craw))
    g_cross_gain = jnp.sum(g_normed * normal_two, 1)
    g_cross_bias = jnp.sum(g_normed, 1)
    g_stream = g_stream + norm_back(g_normed * gain_cross, normal_two, inverse_two)

    g_low = g_stream.astype(BF)
    g_mixed = project(weights_one, [3], [g_low], [BF])[0].reshape(heads, dim, tokens)
    pairs += [(g_low, mixed_one), *((text, g) for g in g_pair)]
    middle = outer_all(pairs)
    middle = lax.psum_scatter(
        middle.reshape(-1, width), DEVICES, scatter_dimension=0, tiled=True
    ).astype(F32)
    ends = [block_rows, 2 * block_rows, 3 * block_rows, 3 * block_rows + text_rows]
    middle = jnp.split(middle, ends, 0)
    g_parts = []
    for index, piece in enumerate(pieces):
        whole, kept = saved_self[index]
        grad = exchange(
            cut(g_mixed, index).reshape(piece.group, -1, dim, piece.count), piece.group, cols
        )
        part = attend_back(
            none, whole, whole, whole, (0, 1, 2), kept, grad, False, 2, True
        )
        g_parts.append(exchange(part, piece.group, cols))
    g_heads = [
        jnp.concatenate([p[:, i].reshape(heads, dim, -1) for p in g_parts], 2) for i in range(3)
    ]
    g_raw_q, g_q_gain = query_pull(g_heads[0].astype(F32))
    g_raw_k, g_k_gain = key_pull(g_heads[1].astype(F32))
    g_triple = [
        g.reshape(depth, tokens) for g in (g_raw_q.astype(BF), g_raw_k.astype(BF), g_heads[2])
    ]
    r_self = [
        Reduction(corner, [(normed_one, g) for g in g_triple[:2]], True),
        Reduction(corner, [(normed_one, g_triple[2])], False),
    ]
    g_normed = rebuild(weights_one, [0, 1, 2], g_triple, F32)
    g_normed = tick(g_normed, r_self)
    g_normed, kept = lax.optimization_barrier((g_normed, [r.state[0] for r in r_self]))
    for beside, part in zip(r_self, kept):
        beside.state[0] = part
    crossed = g_normed * normal_one
    sums = jnp.stack(
        [
            jnp.stack([jnp.sum(cut(g_normed, i), 1), jnp.sum(cut(crossed, i), 1)], 0)
            for i in range(len(pieces))
        ],
        0,
    )
    which = jnp.stack(
        [jnp.where(jnp.arange(sequences) == p.sequence, 1.0, 0.0) for p in pieces], 0
    )
    g_modul = jnp.sum(which[:, :, None, None] * sums[:, None], 0)
    g_modul = g_modul.reshape(sequences, 2, cols, width).transpose(2, 0, 1, 3)
    g_modul = jnp.sum(lax.all_to_all(g_modul, "col", 0, 0, tiled=True), 0).astype(BF)
    g_stream = g_stream + norm_back(g_normed * scaling, normal_one, inverse_one)

    g_skip_gain = jnp.sum(g_stream * skip_normal, 1)
    g_skip_bias = jnp.sum(g_stream, 1)
    g_joined = norm_back(g_stream * gain_skip, skip_normal, skip_inverse).astype(BF)
    g_joined, g_modul = lax.optimization_barrier((g_joined, g_modul))
    r_skip = Reduction(corner, [(both, g_joined)], True)
    g_both = rebuild_blocks(base, w_skip, width, g_joined)

    g_gains = jnp.stack(
        [g_skip_gain, g_skip_bias, g_cross_gain, g_cross_bias, g_hidden_gain, g_hidden_bias], 0
    )
    g_gains = g_gains.reshape(6, cols, width).transpose(1, 0, 2)
    g_head = jnp.stack([g_q_gain, g_k_gain, g_cq_gain, g_tk_gain], 0).reshape(1, -1, width)
    packed = jnp.concatenate([g_gains, jnp.broadcast_to(g_head, (cols, *g_head.shape[1:]))], 1)
    packed = jnp.sum(lax.all_to_all(packed, "col", 0, 0, tiled=True), 0)
    packed = jnp.sum(shared(packed, "row"), 0)
    g_modul = shared(g_modul, "row").reshape(-1, 2, width)

    g_both, packed, g_modul = lax.optimization_barrier((g_both, packed, g_modul))
    if custom_mesh():
        g_both, got = lax.optimization_barrier((g_both, r_skip.state[0]))
        here, away = outer(corner, r_skip.pairs, True, got)
        g_both, away, act = lax.optimization_barrier((g_both, away, act))
        r_skip.stage, r_skip.state = 1, [here, swap(away, "row", 1)]
    g_latents, g_skip = to_features(g_both, pieces, cols, 2, block_rows)
    output = contract(weights_hidden, 1, act, stream, BF)
    output = tick(output, r_self)
    output = tick(output, [r_skip])
    if custom_mesh():
        states = [r.state for r in r_self]
        states, r_skip.state = lax.optimization_barrier((states, r_skip.state))
        r_skip.advance()
        for beside, state in zip(r_self, states):
            beside.state = state
            beside.advance()
    output, g_hidden = lax.optimization_barrier((output, g_hidden))
    result = to_features(after(output, g_skip), pieces, cols, 1, width)[0]
    g_modulation = einsum("sd,ske->dke", embed_rows, g_modul)
    g_gains = packed[:6]
    g_head = packed[6:].reshape(4, dim)
    return (
        result,
        g_latents,
        g_skip,
        r_skip.result().reshape(2, block_rows, width),
        g_modulation,
        jnp.concatenate([r.result() for r in r_self], 0).transpose(1, 0, 2),
        middle[2].T,
        middle[1],
        jnp.stack(middle[3:], 1),
        middle[0].T,
        g_hidden[0],
        g_hidden[1].T,
        *[g_gains[i] for i in range(6)],
        *[g_head[i] for i in range(4)],
    )


def solution(mesh):
    return jax.shard_map(
        shards,
        mesh=mesh,
        in_specs=(
            P("col", "row"),
            P("col", "row"),
            P("row", "col"),
            P("row", None, "col"),
            P("row"),
            P(None, "row"),
            P("col", "row"),
            P(None, "row", "col"),
            P("row", None, "col"),
            P("row", None, "col"),
            P("col", "row"),
            P("row", "col"),
            P("row", None, "col"),
            P("col", "row"),
            P("row", "col"),
            P("col", "row"),
            P("col"),
            P("col"),
            P("col"),
            P("col"),
            P("col"),
            P("col"),
            P(),
            P(),
            P(),
            P(),
        ),
        out_specs=(
            P("col", "row"),
            P("col", "row"),
            P("col", "row"),
            P(None, "row", "col"),
            P("row", None, "col"),
            P("row", None, "col"),
            P("col", "row"),
            P("row", "col"),
            P("row", None, "col"),
            P("col", "row"),
            P("row", "col"),
            P("col", "row"),
            P("col"),
            P("col"),
            P("col"),
            P("col"),
            P("col"),
            P("col"),
            P(),
            P(),
            P(),
            P(),
        ),
        check_vma=False,
    )
```

```python
from functools import partial
import math

import jax
import jax.numpy as jnp
from jax import lax
from jax.experimental import pallas as pl
from jax.experimental.pallas import tpu as pltpu
from jax.sharding import PartitionSpec as P

L = 1024
EPSILON = 1e-06
BF = jnp.bfloat16
F32 = jnp.float32
KEYPAD = 128
DEVICES = ("col", "row")
LOG2E = math.log2(math.e)
VMEM = 60 << 20


def einsum(spec, left, right):
    return jnp.einsum(spec, left, right, preferred_element_type=F32)


def dot(left, right, dims):
    return lax.dot_general(left, right, (dims, ((), ())), preferred_element_type=F32)


def params():
    return pltpu.CompilerParams(vmem_limit_bytes=VMEM)


def step_of(count):
    return 256 if count % 256 == 0 else count


def wide(ref, head):
    parts = [ref[s, 0, head] for s in range(ref.shape[0])]
    return parts[0] if len(parts) == 1 else jnp.concatenate(parts, 1)


def valid_keys(length_ref, keys, step):
    return lax.broadcasted_iota(jnp.int32, (keys, step), 0) < length_ref[0]


def attend_kernel(masked, length_ref, q_ref, k_ref, v_ref, o_ref, r_ref, l_ref):
    groups, _, heads, dim, count = q_ref.shape
    step = step_of(count)
    factor = dim ** (-0.5) * LOG2E
    for head in range(heads):
        key = wide(k_ref, head).T
        value = wide(v_ref, head)
        keys = key.shape[0]
        value = jnp.concatenate([value, jnp.ones((8, keys), BF)], 0)
        for place in range(0, groups * count, step):
            group, first = divmod(place, count)
            query = q_ref[group, 0, head, :, first : first + step]
            expo = jnp.exp2(dot(key, query, ((1,), (0,))) * factor)
            if masked:
                expo = jnp.where(valid_keys(length_ref, keys, step), expo, 0.0)
            both = dot(value, expo.astype(BF), ((1,), (0,)))
            total = both[dim : dim + 1]
            mixed = both[:dim] * (1.0 / total)
            high = mixed.astype(BF)
            o_ref[group, head, :, first : first + step] = high
            r_ref[group, head, :, first : first + step] = (mixed - high.astype(F32)).astype(BF)
            l_ref[head, :, place : place + step] = jnp.log2(total)


def attend_back_kernel(
    masked, length_ref, q_ref, k_ref, v_ref, m_ref, r_ref, g_ref, l_ref, *outs
):
    groups, _, heads, dim, count = q_ref.shape
    step = step_of(count)
    scale = dim ** (-0.5)
    for head in range(heads):
        key = wide(k_ref, head)
        keys = key.shape[1]
        turned = key.T
        value = jnp.concatenate([wide(v_ref, head), jnp.ones((8, keys), BF)], 0).T
        g_key = g_value = None
        for place in range(0, groups * count, step):
            group, first = divmod(place, count)
            here = slice(first, first + step)
            query = q_ref[group, 0, head, :, here]
            grad = g_ref[group, head, :, here]
            mixed = m_ref[group, head, :, here].astype(F32)
            mixed = mixed + r_ref[group, head, :, here].astype(F32)
            delta = -jnp.sum(grad.astype(F32) * mixed, 0, keepdims=True)
            high = delta.astype(BF)
            rest = (delta - high.astype(F32)).astype(BF)
            more = jnp.concatenate([grad, high, rest, jnp.zeros((6, step), BF)], 0)
            probs = jnp.exp2(
                dot(turned, query, ((1,), (0,))) * (scale * LOG2E)
                - l_ref[head, :, place : place + step]
            )
            if masked:
                probs = jnp.where(valid_keys(length_ref, keys, step), probs, 0.0)
            product = (probs * dot(value, more, ((1,), (0,)))).astype(BF)
            g_query = dot(key, product, ((1,), (0,))) * scale
            part_value = dot(grad, probs.astype(BF), ((1,), (1,)))
            part_key = dot(query, product, ((1,), (1,)))
            g_value = part_value if g_value is None else g_value + part_value
            g_key = part_key if g_key is None else g_key + part_key
            outs[0][group, 0, head, :, here] = g_query.astype(outs[0].dtype)
        g_key = g_key * scale
        if len(outs) == 1:
            for group in range(groups):
                here = slice(group * count, (group + 1) * count)
                outs[0][group, 1, head] = g_key[:, here].astype(BF)
                outs[0][group, 2, head] = g_value[:, here].astype(BF)
        else:
            outs[1][0, 0, head] = g_key
            outs[2][0, 0, head] = g_value


def costs(heads, queries, keys, dim, products):
    return pl.CostEstimate(
        flops=2 * products * heads * queries * keys * 256,
        transcendentals=heads * queries * keys,
        bytes_accessed=2 * products * heads * dim * (queries + keys),
    )


def head_block(shape, count, kind=0):
    groups, _, _, dim, tokens = shape
    return pl.BlockSpec((groups, 1, count, dim, tokens), lambda h: (0, kind, h, 0, 0))


def mix_block(shape, count):
    groups, _, _, dim, tokens = shape
    return pl.BlockSpec((groups, count, dim, tokens), lambda h: (0, h, 0, 0))


def attend(length, query, key, value, kinds, masked, most):
    groups, _, heads, dim, count = query.shape
    many = math.gcd(heads, most)
    total = groups * count
    keys = key.shape[0] * key.shape[4]
    return pl.pallas_call(
        partial(attend_kernel, masked),
        grid=(heads // many,),
        in_specs=[pl.BlockSpec(memory_space=pltpu.SMEM)]
        + [head_block(a.shape, many, kind) for a, kind in zip((query, key, value), kinds)],
        out_specs=[
            mix_block(query.shape, many),
            mix_block(query.shape, many),
            pl.BlockSpec((many, 1, total), lambda h: (h, 0, 0)),
        ],
        out_shape=[
            jax.ShapeDtypeStruct((groups, heads, dim, count), BF),
            jax.ShapeDtypeStruct((groups, heads, dim, count), BF),
            jax.ShapeDtypeStruct((heads, 1, total), F32),
        ],
        cost_estimate=costs(heads, total, keys, dim, 2),
        compiler_params=params(),
        name="attend",
    )(length, query, key, value)


def attend_back(length, query, key, value, kinds, kept, grad, masked, most, stacked):
    mixed, rest, logs = kept
    groups, _, heads, dim, count = query.shape
    many = math.gcd(heads, most)
    total = groups * count
    keys = key.shape[0] * key.shape[4]
    if stacked:
        out_specs = pl.BlockSpec((groups, 3, many, dim, count), lambda h: (0, 0, h, 0, 0))
        out_shape = jax.ShapeDtypeStruct((groups, 3, heads, dim, count), BF)
    else:
        out_specs = [head_block(a.shape, many) for a in (query, key, value)]
        out_shape = [jax.ShapeDtypeStruct(a.shape, F32) for a in (query, key, value)]
    return pl.pallas_call(
        partial(attend_back_kernel, masked),
        grid=(heads // many,),
        in_specs=[pl.BlockSpec(memory_space=pltpu.SMEM)]
        + [head_block(a.shape, many, kind) for a, kind in zip((query, key, value), kinds)]
        + [mix_block(query.shape, many)] * 3
        + [pl.BlockSpec((many, 1, total), lambda h: (h, 0, 0))],
        out_specs=out_specs,
        out_shape=out_shape,
        cost_estimate=costs(heads, total, keys, dim, 5),
        compiler_params=params(),
        name="attend_back",
    )(length, query, key, value, mixed, rest, grad, logs)


def work(rows, depth, tokens, moved):
    return pl.CostEstimate(
        flops=2 * rows * depth * tokens,
        transcendentals=0,
        bytes_accessed=moved,
    )


def lanes(width):
    return -(-width // 128) * 128


def full(shape):
    return pl.BlockSpec(shape, lambda *_: (0,) * len(shape))


def project(weight, kinds, values, dtypes, joined=False):
    _, cols, depth, width = weight.shape
    tokens = values[0].shape[1]
    outs = 1 if joined else len(kinds)

    def kernel(*refs):
        blocks = refs[: len(kinds)]
        given = refs[len(kinds) : -outs]
        total = None
        for index, block in enumerate(blocks):
            part = dot(block[0, 0], given[index % len(given)][...], ((0,), (0,)))
            if not joined:
                refs[index - outs][...] = part.astype(dtypes[index])
            total = part if total is None else total + part
        if joined:
            refs[-1][...] = total.astype(dtypes[0])

    return pl.pallas_call(
        kernel,
        grid=(cols,),
        in_specs=[
            pl.BlockSpec((1, 1, depth, width), partial(lambda k, c: (k, c, 0, 0), kind))
            for kind in kinds
        ]
        + [full(v.shape) for v in values],
        out_specs=[pl.BlockSpec((width, tokens), lambda c: (c, 0))] * outs,
        out_shape=[jax.ShapeDtypeStruct((cols * width, tokens), dtypes[i]) for i in range(outs)],
        cost_estimate=work(len(kinds) * cols * width, depth, tokens, 8 * depth * tokens),
        compiler_params=params(),
        name="project",
    )(*([weight] * len(kinds)), *values)


def rebuild(weight, kinds, values, dtype):
    _, cols, depth, width = weight.shape
    tokens = values[0].shape[1]
    tile = depth // 4

    def kernel(*refs):
        total = None
        for block, given in zip(refs[: len(kinds)], refs[len(kinds) : -1]):
            for col in range(cols):
                part = dot(block[0, col], given[col * width : (col + 1) * width, :], ((1,), (0,)))
                total = part if total is None else total + part
        refs[-1][...] = total.astype(dtype)

    return pl.pallas_call(
        kernel,
        grid=(4,),
        in_specs=[
            pl.BlockSpec((1, cols, tile, width), partial(lambda k, j: (k, 0, j, 0), kind))
            for kind in kinds
        ]
        + [full(v.shape) for v in values],
        out_specs=pl.BlockSpec((tile, tokens), lambda j: (j, 0)),
        out_shape=jax.ShapeDtypeStruct((depth, tokens), dtype),
        cost_estimate=work(depth, len(kinds) * cols * width, tokens, 8 * depth * tokens),
        compiler_params=params(),
        name="rebuild",
    )(*([weight] * len(kinds)), *values)


def project_blocks(base, blocks, width, values):
    many = len(blocks)
    depth, broad = blocks[0].shape
    tokens = values.shape[1]
    tile = depth // 4

    def kernel(base_ref, *refs):
        values_ref, out_ref = refs[many:]

        @pl.when(pl.program_id(0) == 0)
        def _():
            out_ref[...] = jnp.zeros_like(out_ref)

        for index in range(many):
            here = pl.ds(pl.multiple_of((index ^ base_ref[0]) * width, width), width)
            out_ref[here, :] += dot(refs[index][...], values_ref[...], ((0,), (0,)))[:width]

    return pl.pallas_call(
        kernel,
        grid_spec=pltpu.PrefetchScalarGridSpec(
            num_scalar_prefetch=1,
            grid=(4,),
            in_specs=[pl.BlockSpec((tile, broad), lambda j, b: (j, 0))] * many
            + [pl.BlockSpec((tile, tokens), lambda j, b: (j, 0))],
            out_specs=pl.BlockSpec((many * width, tokens), lambda j, b: (0, 0)),
        ),
        out_shape=jax.ShapeDtypeStruct((many * width, tokens), F32),
        cost_estimate=work(many * width, depth, tokens, 4 * depth * tokens),
        compiler_params=params(),
        name="project_blocks",
    )(base, *blocks, values)


def rebuild_blocks(base, blocks, width, values):
    many = len(blocks)
    depth, broad = blocks[0].shape
    tokens = values.shape[1]
    tile = depth // 4

    def kernel(base_ref, *refs):
        values_ref, out_ref = refs[many:]
        total = None
        for index in range(many):
            here = pl.ds(pl.multiple_of((index ^ base_ref[0]) * width, width), width)
            part = dot(refs[index][:, :width], values_ref[here, :], ((1,), (0,)))
            total = part if total is None else total + part
        out_ref[...] = total.astype(BF)

    return pl.pallas_call(
        kernel,
        grid_spec=pltpu.PrefetchScalarGridSpec(
            num_scalar_prefetch=1,
            grid=(4,),
            in_specs=[pl.BlockSpec((tile, broad), lambda j, b: (j, 0))] * many
            + [pl.BlockSpec(values.shape, lambda j, b: (0, 0))],
            out_specs=pl.BlockSpec((tile, tokens), lambda j, b: (j, 0)),
        ),
        out_shape=jax.ShapeDtypeStruct((depth, tokens), BF),
        cost_estimate=work(many * width, depth, tokens, 4 * depth * tokens),
        compiler_params=params(),
        name="rebuild_blocks",
    )(base, *blocks, values)


def outer(place, pairs, across, got=None):
    cols = lax.axis_size("col")
    lefts = []
    for left, _ in pairs:
        if not any(left is other for other in lefts):
            lefts.append(left)
    which = [next(i for i, l in enumerate(lefts) if l is left) for left, _ in pairs]
    rights = [right for _, right in pairs]
    many = len(pairs)
    rows, tokens = lefts[0].shape
    width = rights[0].shape[0] // cols
    broad = lanes(width)
    chunk = rows // 8
    flip = 1 if got is None else 0

    def kernel(place_ref, *refs):
        left_refs = refs[: len(lefts)]
        right_refs = refs[len(lefts) : len(lefts) + many]
        rest = refs[len(lefts) + many :]
        for index in range(many):
            right = right_refs[index][...]
            if broad > width:
                right = jnp.concatenate([right, jnp.zeros((broad - width, tokens), BF)], 0)
            part = dot(left_refs[which[index]][...], right, ((1,), (1,)))
            if got is None:
                rest[0][index, 0] = part.astype(BF)
            elif not across:
                part = (part + rest[0][index, 0].astype(F32)).astype(BF)

                @pl.when(pl.program_id(0) == place_ref[2])
                def _():
                    rest[1][index] = part.reshape(4, 2, chunk, broad)

                @pl.when(pl.program_id(0) != place_ref[2])
                def _():
                    rest[2][index] = part.reshape(4, 2, chunk, broad)
            else:
                part = (part + rest[0][index, 0].astype(F32)).astype(BF)
                part = part.reshape(4, 2, chunk, broad)

                @pl.when(place_ref[1] == 0)
                def _():
                    rest[1][index, 0] = part[:, 0]
                    rest[2][index, 0] = part[:, 1]

                @pl.when(place_ref[1] != 0)
                def _():
                    rest[1][index, 0] = part[:, 1]
                    rest[2][index, 0] = part[:, 0]

    whole = pl.BlockSpec((many, 1, rows, broad), lambda y, place: (0, y, 0, 0))
    piece = pl.BlockSpec((many, 1, 4, chunk, broad), lambda y, place: (0, y, 0, 0, 0))
    all_rows = pl.BlockSpec((many, 4, 2, chunk, broad), lambda y, place: (0, 0, 0, 0, 0))
    if got is None:
        given, out_specs = [], whole
        out_shape = jax.ShapeDtypeStruct((many, cols // 2, rows, broad), BF)
    else:
        given, out_specs = [got], [piece, piece] if across else [all_rows, all_rows]
        shape = (many, cols // 2, 4, chunk, broad) if across else (many, 4, 2, chunk, broad)
        out_shape = [jax.ShapeDtypeStruct(shape, BF)] * 2
    return pl.pallas_call(
        kernel,
        grid_spec=pltpu.PrefetchScalarGridSpec(
            num_scalar_prefetch=1,
            grid=(cols // 2,),
            in_specs=[pl.BlockSpec((rows, tokens), lambda y, place: (0, 0)) for _ in lefts]
            + [
                pl.BlockSpec((width, tokens), lambda y, place: (2 * y + (place[0] ^ flip), 0))
                for _ in rights
            ]
            + [whole] * len(given),
            out_specs=out_specs,
        ),
        out_shape=out_shape,
        cost_estimate=work(
            rows, tokens, many * cols // 2 * broad, 2 * rows * cols * broad * many
        ),
        compiler_params=params(),
        name="outer",
    )(place, *lefts, *rights, *given)


def outer_all(pairs):
    cols = lax.axis_size("col")
    parts = lax.axis_size("row")
    if not custom_mesh():
        blocks = [einsum("kt,cnt->ckn", a, b.reshape(cols, -1, b.shape[1])) for a, b in pairs]
        blocks = [b.reshape(cols, parts, -1, b.shape[2]).astype(BF) for b in blocks]
        return jnp.concatenate(blocks, 2)
    lefts = []
    for left, _ in pairs:
        if not any(left is other for other in lefts):
            lefts.append(left)
    which = [next(i for i, l in enumerate(lefts) if l is left) for left, _ in pairs]
    rights = [right for _, right in pairs]
    sizes = [left.shape[0] // parts for left, _ in pairs]
    width = rights[0].shape[0] // cols

    def kernel(*refs):
        for index, size in enumerate(sizes):
            left = refs[which[index]][...]
            part = dot(left, refs[len(lefts) + index][...], ((1,), (1,))).astype(BF)
            start = sum(sizes[:index])
            refs[-1][0, :, start : start + size] = part.reshape(parts, size, width)

    return pl.pallas_call(
        kernel,
        grid=(cols,),
        in_specs=[full(left.shape) for left in lefts]
        + [pl.BlockSpec((width, right.shape[1]), lambda c: (c, 0)) for right in rights],
        out_specs=pl.BlockSpec((1, parts, sum(sizes), width), lambda c: (c, 0, 0, 0)),
        out_shape=jax.ShapeDtypeStruct((cols, parts, sum(sizes), width), BF),
        cost_estimate=work(
            parts * sum(sizes), lefts[0].shape[1], cols * width, 3 * parts * sum(sizes) * cols * width
        ),
        compiler_params=params(),
        name="outer_all",
    )(*lefts, *rights)


def expand(weight, kind, values):
    _, many, depth, hidden = weight.shape
    tokens = values.shape[1]
    tile = 384 if hidden % 384 == 0 else hidden
    slope = 0.79788456
    cubic = 0.044715

    def kernel(weight_ref, values_ref, act_ref, slope_ref):
        for index in range(many):
            inner = dot(weight_ref[0, index], values_ref[...], ((0,), (0,)))
            square = inner * inner
            bent = jnp.tanh(inner * (slope + slope * cubic * square))
            half = 0.5 + 0.5 * bent
            act_ref[index] = (inner * half).astype(BF)
            rise = slope + 3.0 * slope * cubic * square
            slope_ref[index] = (half + 0.5 * inner * (1.0 - bent * bent) * rise).astype(BF)

    return pl.pallas_call(
        kernel,
        grid=(hidden // tile,),
        in_specs=[
            pl.BlockSpec((1, many, depth, tile), lambda j: (kind, 0, 0, j)),
            full(values.shape),
        ],
        out_specs=[pl.BlockSpec((many, tile, tokens), lambda j: (0, j, 0))] * 2,
        out_shape=[jax.ShapeDtypeStruct((many, hidden, tokens), BF)] * 2,
        cost_estimate=work(many * hidden, depth, tokens, 3 * many * hidden * depth),
        compiler_params=params(),
        name="expand",
    )(weight, values)


def expand_back(weight, kind, values, slopes):
    _, many, depth, hidden = weight.shape
    tokens = values.shape[1]
    tile = 384 if hidden % 384 == 0 else hidden

    def kernel(weight_ref, values_ref, slope_ref, out_ref):
        for index in range(many):
            part = dot(weight_ref[0, index], values_ref[...], ((0,), (0,)))
            out_ref[index] = (part * slope_ref[index].astype(F32)).astype(BF)

    return pl.pallas_call(
        kernel,
        grid=(hidden // tile,),
        in_specs=[
            pl.BlockSpec((1, many, depth, tile), lambda j: (kind, 0, 0, j)),
            full(values.shape),
            pl.BlockSpec((many, tile, tokens), lambda j: (0, j, 0)),
        ],
        out_specs=pl.BlockSpec((many, tile, tokens), lambda j: (0, j, 0)),
        out_shape=jax.ShapeDtypeStruct((many, hidden, tokens), BF),
        cost_estimate=work(many * hidden, depth, tokens, 3 * many * hidden * depth),
        compiler_params=params(),
        name="expand_back",
    )(weight, values, slopes)


def contract(weight, kind, values, added, dtype):
    _, many, depth, hidden = weight.shape
    tokens = values.shape[2]
    tile = depth // 4
    extra = [] if added is None else [added]

    def kernel(weight_ref, values_ref, *refs):
        total = refs[0][...] if extra else None
        for index in range(many):
            part = dot(weight_ref[0, index], values_ref[index], ((1,), (0,)))
            total = part if total is None else total + part
        refs[-1][...] = total.astype(dtype)

    line = pl.BlockSpec((tile, tokens), lambda j: (j, 0))
    return pl.pallas_call(
        kernel,
        grid=(4,),
        in_specs=[
            pl.BlockSpec((1, many, tile, hidden), lambda j: (kind, 0, j, 0)),
            full(values.shape),
        ]
        + [line] * len(extra),
        out_specs=line,
        out_shape=jax.ShapeDtypeStruct((depth, tokens), dtype),
        cost_estimate=work(depth, many * hidden, tokens, 3 * many * hidden * depth),
        compiler_params=params(),
        name="contract",
    )(weight, values, *extra)


def hidden_outer(grad_out, act, normed, grad_inner):
    many, hidden, tokens = act.shape
    depth = grad_out.shape[0]
    parts = 2 if hidden % 256 == 0 else 1
    tile = hidden // parts

    def kernel(out_ref, act_ref, normed_ref, inner_ref, grad_ref):
        kind = pl.program_id(0)

        @pl.when(kind == 0)
        def _():
            grad_ref[0, 0] = dot(normed_ref[...], inner_ref[0], ((1,), (1,))).astype(BF)

        @pl.when(kind == 1)
        def _():
            grad_ref[0, 0] = dot(out_ref[...], act_ref[0], ((1,), (1,))).astype(BF)

    return pl.pallas_call(
        kernel,
        grid=(2, many, parts),
        in_specs=[
            pl.BlockSpec((depth, tokens), lambda s, p, j: (0, 0)),
            pl.BlockSpec((1, tile, tokens), lambda s, p, j: (s * p, s * j, 0)),
            pl.BlockSpec((depth, tokens), lambda s, p, j: (0, 0)),
            pl.BlockSpec(
                (1, tile, tokens),
                lambda s, p, j: (p + s * (many - 1 - p), j + s * (parts - 1 - j), 0),
            ),
        ],
        out_specs=pl.BlockSpec((1, 1, depth, tile), lambda s, p, j: (s, p, 0, j)),
        out_shape=jax.ShapeDtypeStruct((2, many, depth, hidden), BF),
        cost_estimate=work(2 * depth, tokens, many * hidden, 5 * many * depth * hidden),
        compiler_params=params(),
        name="hidden_outer",
    )(grad_out, act, normed, grad_inner)


def assemble(place, own, got, middle=None):
    rows, width = own.shape[-2:]

    def kernel(place_ref, own_ref, got_ref, out_ref):
        @pl.when(pl.program_id(0) == place_ref[1])
        def _():
            out_ref[0, 0] = own_ref[...].reshape(rows, width)

        @pl.when(pl.program_id(0) != place_ref[1])
        def _():
            out_ref[0, 0] = got_ref[...].reshape(rows, width)

    def spec(ours):
        def index(x, z, place):
            phase = place[1] if ours else 1 - place[1]
            inside = (x == phase).astype(jnp.int32)
            level = (inside * z + (1 - inside) * 3 * (1 - phase)) ^ place[0]
            return (level, 0, 0) if middle is None else (level, middle, 0, 0)

        shape = (1, rows, width) if middle is None else (1, 1, rows, width)
        return pl.BlockSpec(shape, index)

    return pl.pallas_call(
        kernel,
        grid_spec=pltpu.PrefetchScalarGridSpec(
            num_scalar_prefetch=1,
            grid=(2, 4),
            in_specs=[spec(True), spec(False)],
            out_specs=pl.BlockSpec((1, 1, rows, width), lambda x, z, place: (z, x, 0, 0)),
        ),
        out_shape=jax.ShapeDtypeStruct((4, 2, rows, width), BF),
        cost_estimate=work(1, 1, 1, 32 * rows * width),
        name="assemble",
    )(place, own, got).reshape(8 * rows, width)


def normalize(values):
    average = jnp.mean(values, 0, keepdims=True)
    centred = values - average
    inverse = lax.rsqrt(jnp.mean(centred * centred, 0, keepdims=True) + EPSILON)
    return centred * inverse, inverse


def norm_back(grad, normal, inverse):
    average = jnp.mean(grad, 0, keepdims=True)
    crossed = jnp.mean(grad * normal, 0, keepdims=True)
    return inverse * (grad - average - normal * crossed)


def head_norm(values, gain):
    average = jnp.mean(values, 1, keepdims=True)
    centred = values - average
    variance = jnp.mean(centred * centred, 1, keepdims=True)
    return centred * lax.rsqrt(variance + EPSILON) * gain[None, :, None]


def rope_tables(places, head_dim):
    quarter = head_dim // 4
    freqs = jnp.exp(jnp.arange(quarter, dtype=F32) * (-4.0 * math.log(10000.0) / head_dim))
    rows = freqs[:, None] * places[0].astype(F32)[None, :]
    cols = freqs[:, None] * places[1].astype(F32)[None, :]
    angles = jnp.concatenate([rows, rows, cols, cols], 0)
    return jnp.cos(angles), jnp.sin(angles)


def rotate(values):
    quarter = values.shape[1] // 4
    one, two, three, four = (values[:, i * quarter : (i + 1) * quarter] for i in range(4))
    return jnp.concatenate([-two, one, -four, three], 1)


class Piece:
    def __init__(self, start, count, group, sequence):
        self.start = start
        self.count = count
        self.group = group
        self.sequence = sequence


def pieces_of(cols, sequences):
    mine = lax.axis_index("col")
    if cols == 4 and sequences == 3:
        return [
            Piece(0, L // 2, 2, mine // 2),
            Piece(2 * L, L // 4, 4, jnp.int32(2)),
        ]
    return [Piece(s * L, L // cols, cols, jnp.int32(s)) for s in range(sequences)]


def groups_of(size, cols):
    return [list(range(i, i + size)) for i in range(0, cols, size)]


def exchange(values, size, cols):
    if size == cols:
        return lax.all_to_all(values, "col", 0, 0, tiled=True)
    return lax.all_to_all(
        values, "col", 0, 0, tiled=True, axis_index_groups=groups_of(size, cols)
    )


def cut_size(pieces):
    return math.gcd(*(p.count for p in pieces), *(p.start for p in pieces))


def locate(pieces, unit, block):
    device = inside = None
    at = 0
    for piece in pieces:
        each = piece.count // unit
        rest = block - piece.start // unit
        there = (rest // each, at + rest % each)
        if device is None:
            device, inside = there
        else:
            later = (rest >= 0).astype(jnp.int32)
            device = later * there[0] + (1 - later) * device
            inside = later * there[1] + (1 - later) * inside
        at += each
    return device, inside


def to_tokens(arrays, pieces, cols, rows):
    width, tokens = arrays[0].shape
    kinds = len(arrays)
    unit = cut_size(pieces)
    total = sum(p.count for p in pieces)
    if unit % 128:
        values = jnp.stack([a.reshape(-1, rows, tokens) for a in arrays], 1).astype(BF)
        values = values.reshape(kinds * width, tokens)
        parts = [
            jnp.concatenate(
                [values[:, p.start + j * p.count : p.start + (j + 1) * p.count] for p in pieces], 1
            )
            for j in range(cols)
        ]
        dealt = jnp.stack(parts, 0)
    else:

        def kernel(*refs):
            for kind in range(kinds):
                for at in range(0, width, rows):
                    to = at * kinds + kind * rows
                    refs[-1][0, to : to + rows] = refs[kind][at : at + rows].astype(BF)

        def index(block):
            device, inside = locate(pieces, unit, block)
            return (device, 0, inside)

        dealt = pl.pallas_call(
            kernel,
            grid=(tokens // unit,),
            in_specs=[pl.BlockSpec((width, unit), lambda b: (0, b))] * kinds,
            out_specs=pl.BlockSpec((1, kinds * width, unit), index),
            out_shape=jax.ShapeDtypeStruct((cols, kinds * width, total), BF),
            cost_estimate=pl.CostEstimate(
                flops=0, transcendentals=0, bytes_accessed=4 * kinds * width * tokens
            ),
            name="deal",
        )(*arrays)
    got = exchange(dealt, cols, cols)
    return got.reshape(-1, total)


def to_features(values, pieces, cols, kinds, rows):
    got = exchange(values.reshape(cols, -1, values.shape[1]), cols, cols)
    unit = cut_size(pieces)
    width = got.shape[1] // kinds
    tokens = cols * got.shape[2]
    if unit % 128:
        parts = []
        at = 0
        for piece in pieces:
            parts += [got[j, :, at : at + piece.count] for j in range(cols)]
            at += piece.count
        whole = jnp.concatenate(parts, 1).astype(F32).reshape(-1, kinds, rows, tokens)
        return [whole[:, kind].reshape(width, tokens) for kind in range(kinds)]

    def kernel(got_ref, *refs):
        for kind in range(kinds):
            for at in range(0, width, rows):
                start = at * kinds + kind * rows
                refs[kind][at : at + rows] = got_ref[0, start : start + rows].astype(F32)

    def index(block):
        device, inside = locate(pieces, unit, block)
        return (device, 0, inside)

    return pl.pallas_call(
        kernel,
        grid=(tokens // unit,),
        in_specs=[pl.BlockSpec((1, kinds * width, unit), index)],
        out_specs=[pl.BlockSpec((width, unit), lambda b: (0, b))] * kinds,
        out_shape=[jax.ShapeDtypeStruct((width, tokens), F32)] * kinds,
        cost_estimate=pl.CostEstimate(
            flops=0, transcendentals=0, bytes_accessed=6 * kinds * width * tokens
        ),
        name="undeal",
    )(got)


def shared(values, axis):
    size = lax.axis_size(axis)
    return lax.all_to_all(
        jnp.broadcast_to(values[None], (size, *values.shape)), axis, 0, 0, tiled=True
    )


def swap(values, axis, bit):
    size = lax.axis_size(axis)
    return lax.ppermute(values, axis, [(i, i ^ bit) for i in range(size)])


def custom_mesh():
    return (lax.axis_size("row"), lax.axis_size("col")) == (8, 4)


def gather_weights(blocks):
    cols = lax.axis_size("col")
    most = max(block.shape[0] for block in blocks)
    padded = [jnp.pad(b, ((0, most - b.shape[0]), (0, 0))) for b in blocks]
    whole = lax.all_gather(jnp.stack(padded, 0), DEVICES, axis=1, tiled=True)
    return whole.reshape(len(blocks), cols, -1, blocks[0].shape[1])


class Gathering:
    last = 4

    def __init__(self, block, up, place):
        self.up = up
        self.place = place
        self.stage = 0
        self.state = [block]
        if not custom_mesh():
            cols = lax.axis_size("col")
            whole = lax.all_gather(block, DEVICES, axis=0, tiled=True)
            self.state = list(whole.reshape(cols, -1, block.shape[1]))
            self.stage = self.last

    def levels(self, block):
        return [block] + [swap(block, "row", 2 * level) for level in (1, 2, 3)]

    def advance(self):
        state = self.state
        self.stage += 1
        if self.stage == 1:
            self.state = [state[0], swap(state[0], "col", 2)] if self.up else self.levels(state[0])
        elif self.stage == 2:
            stack = jnp.stack(state, 0)
            self.state = self.levels(stack) if self.up else [stack, swap(stack, "col", 2)]
        elif self.stage == 3 and self.up:
            stack = jnp.stack(state, 0)
            self.state = [stack, swap(stack, "row", 1)]
        elif self.stage == 3:
            self.state = state + [swap(a, "row", 1) for a in state]
        else:
            if self.up:
                mine, other = (assemble(self.place, *state, k) for k in (0, 1))
            else:
                mine = assemble(self.place, state[0], state[2])
                other = assemble(self.place, state[1], state[3])
            self.state = [mine, swap(mine, "col", 1), other, swap(other, "col", 1)]

    def result(self):
        while self.stage < self.last:
            self.advance()
        return self.state


def pick(values, axis, index):
    return lax.dynamic_index_in_dim(values, index, axis, False)


def add(left, right):
    return (left.astype(F32) + right.astype(F32)).astype(BF)


class Reduction:
    last = 4

    def __init__(self, place, pairs, across):
        self.place = place
        self.across = across
        self.pairs = pairs
        self.width = pairs[0][1].shape[0] // lax.axis_size("col")
        self.stage = 0
        if custom_mesh():
            self.state = [swap(outer(place, pairs, across), "col", 1)]
            return
        self.stage = self.last
        cols = lax.axis_size("col")
        whole = jnp.stack(
            [einsum("kt,cnt->ckn", a, b.reshape(cols, -1, b.shape[1])) for a, b in pairs], 0
        )
        flat = whole.reshape(len(pairs), -1, whole.shape[3]).astype(BF)
        self.state = [lax.psum_scatter(flat, DEVICES, scatter_dimension=1, tiled=True)]

    def advance(self):
        state = self.state
        self.stage += 1
        if self.stage == 1:
            here, away = outer(self.place, self.pairs, self.across, state[0])
            self.state = [here, swap(away, "row", 1) if self.across else swap(away, "col", 2)]
        elif self.stage == 2:
            axis, index = (1, self.place[2]) if self.across else (2, self.place[1])
            away = add(*(pick(a, axis, 1 - index) for a in state))
            here = add(*(pick(a, axis, index) for a in state))
            self.state = [here, swap(away, "col", 2) if self.across else swap(away, "row", 1)]
        elif self.stage == 3:
            level = lax.axis_index("row") // 2
            total = add(*state)
            self.state = [pick(total, 1, level)] + [
                swap(pick(total, 1, level ^ other), "row", 2 * other) for other in (1, 2, 3)
            ]
        else:
            total = state[0].astype(F32)
            for other in state[1:]:
                total = total + other.astype(F32)
            self.state = [total[..., : self.width]]

    def result(self):
        while self.stage < self.last:
            self.advance()
        return self.state[0].astype(F32)


def tick(values, running):
    active = [r for r in running if r.stage < r.last]
    if active:
        values, states = lax.optimization_barrier((values, [r.state for r in active]))
        for beside, state in zip(active, states):
            beside.state = state
            beside.advance()
    return values


def after(values, done):
    return lax.optimization_barrier((values, done))[0]


def shards(
    latents,
    skip_input,
    condition,
    text_states,
    text_lengths,
    positions,
    out_grad,
    skip_weight,
    modulation,
    self_inputs,
    self_output,
    cross_query,
    cross_keyvalue,
    cross_output,
    expand_weight,
    reduce_weight,
    skip_gain,
    skip_bias,
    cross_gain,
    cross_bias,
    hidden_gain,
    hidden_bias,
    query_gain,
    key_gain,
    cross_query_gain,
    text_key_gain,
):
    cols = lax.axis_size("col")
    rows = lax.axis_size("row")
    mine = lax.axis_index("col")
    my_row = lax.axis_index("row")
    width, row_tokens = latents.shape
    depth = width * cols
    dim = query_gain.shape[0]
    heads = depth // dim
    sequences = row_tokens // L
    tokens = row_tokens // cols
    texts = text_states.shape[1]
    keys = -(-texts // KEYPAD) * KEYPAD
    pieces = pieces_of(cols, sequences)
    starts = [sum(p.count for p in pieces[:i]) for i in range(len(pieces))]
    place = jnp.stack([my_row // 2, my_row % 2]).astype(jnp.int32)
    corner = jnp.stack([mine % 2, my_row % 2, mine // 2]).astype(jnp.int32)
    base = (mine if custom_mesh() else jnp.zeros_like(mine)).astype(jnp.int32)[None]

    def cut(values, index):
        return values[..., starts[index] : starts[index] + pieces[index].count]

    block_rows = depth // rows
    both = to_tokens([latents, skip_input], pieces, cols, block_rows)

    weights_one = gather_weights([*(self_inputs[:, i] for i in range(3)), self_output.T])
    weights_two = gather_weights(
        [cross_query, cross_output.T, *(cross_keyvalue[:, i] for i in range(2))]
    )
    skip_block = jnp.concatenate([skip_weight[0], skip_weight[1]], 0)
    skip_block = jnp.pad(skip_block, ((0, 0), (0, lanes(width) - width)))
    w_skip = Gathering(skip_block, False, place).result()
    weights_hidden = gather_weights([expand_weight, reduce_weight.T])

    places = jnp.concatenate(
        [
            lax.dynamic_slice_in_dim(positions, p.start + mine * p.count, p.count, 1)
            for p in pieces
        ],
        1,
    )

    embed = jax.nn.silu(after(condition, both).astype(F32)).astype(BF)
    embed = shared(embed, "row").reshape(-1, width)
    embed = shared(embed, "col").transpose(1, 0, 2).reshape(-1, depth)
    embed_rows = lax.dynamic_slice_in_dim(embed, my_row * block_rows, block_rows, 1)
    modul = einsum("sd,dke->ske", embed_rows, modulation).reshape(rows, sequences, 2, width)
    modul = jnp.sum(lax.all_to_all(modul, "row", 0, 0, tiled=True), 0)
    gains = jnp.stack(
        [skip_gain, skip_bias, cross_gain, cross_bias, hidden_gain, hidden_bias], 0
    )
    table = jnp.concatenate([gains, modul.reshape(-1, width)], 0)
    table = shared(table, "col").transpose(1, 0, 2).reshape(-1, depth)
    modul = table[6:].reshape(sequences, 2, depth)
    chosen = [lax.dynamic_index_in_dim(modul, p.sequence, 0, False) for p in pieces]
    columns = lax.optimization_barrier(jnp.concatenate([table[:6], *chosen], 0)).T
    gain_skip, bias_skip, gain_cross, bias_cross, gain_hidden, bias_hidden = (
        columns[:, i : i + 1] for i in range(6)
    )
    token_index = lax.broadcasted_iota(jnp.int32, (1, tokens), 1)

    def per_token(which):
        result = columns[:, 6 + which : 7 + which]
        for index in range(1, len(pieces)):
            column = columns[:, 6 + 2 * index + which : 7 + 2 * index + which]
            result = jnp.where(token_index >= starts[index], column, result)
        return jnp.broadcast_to(result, (depth, tokens))

    shifting = per_token(0)
    scaling = 1.0 + per_token(1)

    text = shared(jnp.pad(after(text_states, both), ((0, 0), (0, keys - texts), (0, 0))), "col")
    joined = project_blocks(base, w_skip, width, both)
    skip_normal, skip_inverse = normalize(joined)
    stream = skip_normal * gain_skip + bias_skip
    normal_one, inverse_one = normalize(stream)
    normed_one = (normal_one * scaling + shifting).astype(BF)
    raw = project(weights_one, [0, 1, 2], [normed_one], [F32, F32, BF])
    raw, text = lax.optimization_barrier((raw, text))
    raw = [r.reshape(heads, dim, tokens) for r in raw]
    cosine, sine = rope_tables(places, dim)

    def self_piece(value, gain):
        normal = head_norm(value, gain)
        return normal * cosine[None] + rotate(normal) * sine[None]

    rot_query, query_pull = jax.vjp(self_piece, raw[0], query_gain)
    rot_key, key_pull = jax.vjp(self_piece, raw[1], key_gain)
    triple = [rot_query.astype(BF), rot_key.astype(BF), raw[2]]

    def to_heads(parts, index):
        size = pieces[index].group
        split = [cut(p, index).reshape(size, heads // size, dim, -1) for p in parts]
        return exchange(jnp.stack(split, 1), size, cols)

    none = jnp.zeros((1,), jnp.int32)
    saved_self = []
    mixed_parts = []
    for index, piece in enumerate(pieces):
        whole = to_heads(triple, index)
        kept = attend(none, whole, whole, whole, (0, 1, 2), False, 2)
        saved_self.append((whole, kept))
        mixed_parts.append(exchange(kept[0], piece.group, cols).reshape(depth, -1))
    mixed_one = jnp.concatenate(mixed_parts, 1)
    text = after(text, mixed_one)
    stream = stream + rebuild(weights_one, [3], [mixed_one], F32)
    normal_two, inverse_two = normalize(stream)
    normed_two = (normal_two * gain_cross + bias_cross).astype(BF)
    raw_cross = project(weights_two, [0], [normed_two], [F32])[0].reshape(heads, dim, tokens)
    norm_query, cross_pull = jax.vjp(head_norm, raw_cross, cross_query_gain)
    text = jnp.concatenate(
        [lax.dynamic_index_in_dim(text, p.sequence, 1, False) for p in pieces], 1
    )
    text = text.transpose(0, 2, 1).reshape(-1, len(pieces) * keys)
    text_rows = text.shape[0] // rows
    text_wide = jnp.pad(
        text.reshape(rows, text_rows, -1), ((0, 0), (0, block_rows - text_rows), (0, 0))
    ).reshape(depth, -1)
    raw_text, value_two = project(weights_two, [2, 3], [text_wide], [F32, BF])
    norm_key, text_pull = jax.vjp(head_norm, raw_text.reshape(heads, dim, -1), text_key_gain)
    query_two = norm_query.astype(BF)
    key_two = norm_key.astype(BF)
    value_two = value_two.reshape(heads, dim, -1)
    saved_cross = []
    mixed_parts = []
    for index, piece in enumerate(pieces):
        length = lax.dynamic_index_in_dim(text_lengths, piece.sequence, 0, True)
        here = slice(index * keys, (index + 1) * keys)
        inputs = [cut(query_two, index), key_two[:, :, here], value_two[:, :, here]]
        inputs = [length] + [a[None, None] for a in inputs] + [(0, 0, 0)]
        kept = attend(*inputs, True, 4)
        saved_cross.append((inputs, kept))
        mixed_parts.append(kept[0].reshape(depth, -1))
    mixed_two = jnp.concatenate(mixed_parts, 1)
    stream = stream + rebuild(weights_two, [1], [mixed_two], F32)
    normal_three, inverse_three = normalize(stream)
    normed_three = (normal_three * gain_hidden + bias_hidden).astype(BF)
    grad_out = to_tokens([after(out_grad, joined)], pieces, cols, width)
    act, slopes = expand(weights_hidden, 0, normed_three)

    g_inner = expand_back(weights_hidden, 1, grad_out, slopes)
    g_hidden = hidden_outer(grad_out, act, normed_three, g_inner)
    g_inner, g_hidden = lax.optimization_barrier((g_inner, g_hidden))
    g_normed = contract(weights_hidden, 0, g_inner, None, F32)
    g_hidden = lax.psum_scatter(
        g_hidden.reshape(2, -1, g_hidden.shape[3]), DEVICES, scatter_dimension=1, tiled=True
    ).astype(F32)
    g_hidden_gain = jnp.sum(g_normed * normal_three, 1)
    g_hidden_bias = jnp.sum(g_normed, 1)
    g_stream = grad_out.astype(F32) + norm_back(g_normed * gain_hidden, normal_three, inverse_three)

    g_low = g_stream.astype(BF)
    g_mixed = project(weights_two, [1], [g_low], [BF])[0].reshape(heads, dim, tokens)
    pairs = [(g_low, mixed_two)]
    g_queries = []
    g_keys = []
    g_values = []
    for index, piece in enumerate(pieces):
        inputs, kept = saved_cross[index]
        grads = attend_back(*inputs, kept, cut(g_mixed, index)[None], True, 4, False)
        g_queries.append(grads[0][0, 0])
        g_keys.append(grads[1][0, 0])
        g_values.append(grads[2][0, 0])
    g_raw_cross, g_cq_gain = cross_pull(jnp.concatenate(g_queries, 2))
    g_raw_text, g_tk_gain = text_pull(jnp.concatenate(g_keys, 2))
    g_craw = g_raw_cross.astype(BF).reshape(depth, tokens)
    g_pair = [
        g_raw_text.astype(BF).reshape(depth, -1),
        jnp.concatenate(g_values, 2).astype(BF).reshape(depth, -1),
    ]
    g_normed = rebuild(weights_two, [0], [g_craw], F32)
    pairs.append((normed_two, g_craw))
    g_cross_gain = jnp.sum(g_normed * normal_two, 1)
    g_cross_bias = jnp.sum(g_normed, 1)
    g_stream = g_stream + norm_back(g_normed * gain_cross, normal_two, inverse_two)

    g_low = g_stream.astype(BF)
    g_mixed = project(weights_one, [3], [g_low], [BF])[0].reshape(heads, dim, tokens)
    pairs += [(g_low, mixed_one), *((text, g) for g in g_pair)]
    middle = outer_all(pairs)
    middle = lax.psum_scatter(
        middle.reshape(-1, width), DEVICES, scatter_dimension=0, tiled=True
    ).astype(F32)
    ends = [block_rows, 2 * block_rows, 3 * block_rows, 3 * block_rows + text_rows]
    middle = jnp.split(middle, ends, 0)
    g_parts = []
    for index, piece in enumerate(pieces):
        whole, kept = saved_self[index]
        grad = exchange(
            cut(g_mixed, index).reshape(piece.group, -1, dim, piece.count), piece.group, cols
        )
        part = attend_back(
            none, whole, whole, whole, (0, 1, 2), kept, grad, False, 2, True
        )
        g_parts.append(exchange(part, piece.group, cols))
    g_heads = [
        jnp.concatenate([p[:, i].reshape(heads, dim, -1) for p in g_parts], 2) for i in range(3)
    ]
    g_raw_q, g_q_gain = query_pull(g_heads[0].astype(F32))
    g_raw_k, g_k_gain = key_pull(g_heads[1].astype(F32))
    g_triple = [
        g.reshape(depth, tokens) for g in (g_raw_q.astype(BF), g_raw_k.astype(BF), g_heads[2])
    ]
    r_self = [
        Reduction(corner, [(normed_one, g) for g in g_triple[:2]], True),
        Reduction(corner, [(normed_one, g_triple[2])], False),
    ]
    g_normed = rebuild(weights_one, [0, 1, 2], g_triple, F32)
    g_normed = tick(g_normed, r_self)
    g_normed, kept = lax.optimization_barrier((g_normed, [r.state[0] for r in r_self]))
    for beside, part in zip(r_self, kept):
        beside.state[0] = part
    crossed = g_normed * normal_one
    sums = jnp.stack(
        [
            jnp.stack([jnp.sum(cut(g_normed, i), 1), jnp.sum(cut(crossed, i), 1)], 0)
            for i in range(len(pieces))
        ],
        0,
    )
    which = jnp.stack(
        [jnp.where(jnp.arange(sequences) == p.sequence, 1.0, 0.0) for p in pieces], 0
    )
    g_modul = jnp.sum(which[:, :, None, None] * sums[:, None], 0)
    g_modul = g_modul.reshape(sequences, 2, cols, width).transpose(2, 0, 1, 3)
    g_modul = jnp.sum(lax.all_to_all(g_modul, "col", 0, 0, tiled=True), 0).astype(BF)
    g_stream = g_stream + norm_back(g_normed * scaling, normal_one, inverse_one)

    g_skip_gain = jnp.sum(g_stream * skip_normal, 1)
    g_skip_bias = jnp.sum(g_stream, 1)
    g_joined = norm_back(g_stream * gain_skip, skip_normal, skip_inverse).astype(BF)
    g_joined, g_modul = lax.optimization_barrier((g_joined, g_modul))
    r_skip = Reduction(corner, [(both, g_joined)], True)
    g_both = rebuild_blocks(base, w_skip, width, g_joined)

    g_gains = jnp.stack(
        [g_skip_gain, g_skip_bias, g_cross_gain, g_cross_bias, g_hidden_gain, g_hidden_bias], 0
    )
    g_gains = g_gains.reshape(6, cols, width).transpose(1, 0, 2)
    g_head = jnp.stack([g_q_gain, g_k_gain, g_cq_gain, g_tk_gain], 0).reshape(1, -1, width)
    packed = jnp.concatenate([g_gains, jnp.broadcast_to(g_head, (cols, *g_head.shape[1:]))], 1)
    packed = jnp.sum(lax.all_to_all(packed, "col", 0, 0, tiled=True), 0)
    packed = jnp.concatenate([packed, g_modul.reshape(-1, width).astype(F32)], 0)
    packed = shared(packed, "row")
    many = packed.shape[1] - 2 * sequences
    packed, g_modul = jnp.sum(packed[:, :many], 0), packed[:, many:].astype(BF)
    g_modul = g_modul.reshape(-1, 2, width)

    g_both, packed, g_modul = lax.optimization_barrier((g_both, packed, g_modul))
    if custom_mesh():
        g_both, got = lax.optimization_barrier((g_both, r_skip.state[0]))
        here, away = outer(corner, r_skip.pairs, True, got)
        g_both, away, act = lax.optimization_barrier((g_both, away, act))
        r_skip.stage, r_skip.state = 1, [here, swap(away, "row", 1)]
    g_latents, g_skip = to_features(g_both, pieces, cols, 2, block_rows)
    output = contract(weights_hidden, 1, act, stream, BF)
    output = tick(output, r_self)
    output = tick(output, [r_skip])
    if custom_mesh():
        states = [r.state for r in r_self]
        states, r_skip.state = lax.optimization_barrier((states, r_skip.state))
        r_skip.advance()
        for beside, state in zip(r_self, states):
            beside.state = state
            beside.advance()
    output, g_hidden = lax.optimization_barrier((output, g_hidden))
    result = to_features(after(output, g_skip), pieces, cols, 1, width)[0]
    g_modulation = einsum("sd,ske->dke", embed_rows, g_modul)
    g_gains = packed[:6]
    g_head = packed[6:].reshape(4, dim)
    return (
        result,
        g_latents,
        g_skip,
        r_skip.result().reshape(2, block_rows, width),
        g_modulation,
        jnp.concatenate([r.result() for r in r_self], 0).transpose(1, 0, 2),
        middle[2].T,
        middle[1],
        jnp.stack(middle[3:], 1),
        middle[0].T,
        g_hidden[0],
        g_hidden[1].T,
        *[g_gains[i] for i in range(6)],
        *[g_head[i] for i in range(4)],
    )


def solution(mesh):
    return jax.shard_map(
        shards,
        mesh=mesh,
        in_specs=(
            P("col", "row"),
            P("col", "row"),
            P("row", "col"),
            P("row", None, "col"),
            P("row"),
            P(None, "row"),
            P("col", "row"),
            P(None, "row", "col"),
            P("row", None, "col"),
            P("row", None, "col"),
            P("col", "row"),
            P("row", "col"),
            P("row", None, "col"),
            P("col", "row"),
            P("row", "col"),
            P("col", "row"),
            P("col"),
            P("col"),
            P("col"),
            P("col"),
            P("col"),
            P("col"),
            P(),
            P(),
            P(),
            P(),
        ),
        out_specs=(
            P("col", "row"),
            P("col", "row"),
            P("col", "row"),
            P(None, "row", "col"),
            P("row", None, "col"),
            P("row", None, "col"),
            P("col", "row"),
            P("row", "col"),
            P("row", None, "col"),
            P("col", "row"),
            P("row", "col"),
            P("col", "row"),
            P("col"),
            P("col"),
            P("col"),
            P("col"),
            P("col"),
            P("col"),
            P(),
            P(),
            P(),
            P(),
        ),
        check_vma=False,
    )
```

```python
from functools import partial
import math

import jax
import jax.numpy as jnp
from jax import lax
from jax.experimental import pallas as pl
from jax.experimental.pallas import tpu as pltpu
from jax.sharding import PartitionSpec as P

L = 1024
EPSILON = 1e-06
BF = jnp.bfloat16
F32 = jnp.float32
KEYPAD = 128
DEVICES = ("col", "row")
LOG2E = math.log2(math.e)
VMEM = 60 << 20


def einsum(spec, left, right):
    return jnp.einsum(spec, left, right, preferred_element_type=F32)


def dot(left, right, dims):
    return lax.dot_general(left, right, (dims, ((), ())), preferred_element_type=F32)


def params():
    return pltpu.CompilerParams(vmem_limit_bytes=VMEM)


def step_of(count):
    return 256 if count % 256 == 0 else count


def wide(ref, head):
    parts = [ref[s, 0, head] for s in range(ref.shape[0])]
    return parts[0] if len(parts) == 1 else jnp.concatenate(parts, 1)


def valid_keys(length_ref, keys, step):
    return lax.broadcasted_iota(jnp.int32, (keys, step), 0) < length_ref[0]


def attend_kernel(masked, length_ref, q_ref, k_ref, v_ref, o_ref, r_ref, l_ref):
    groups, _, heads, dim, count = q_ref.shape
    step = step_of(count)
    factor = dim ** (-0.5) * LOG2E
    for head in range(heads):
        key = wide(k_ref, head).T
        value = wide(v_ref, head)
        keys = key.shape[0]
        value = jnp.concatenate([value, jnp.ones((8, keys), BF)], 0)
        for place in range(0, groups * count, step):
            group, first = divmod(place, count)
            query = q_ref[group, 0, head, :, first : first + step]
            expo = jnp.exp2(dot(key, query, ((1,), (0,))) * factor)
            if masked:
                expo = jnp.where(valid_keys(length_ref, keys, step), expo, 0.0)
            both = dot(value, expo.astype(BF), ((1,), (0,)))
            total = both[dim : dim + 1]
            mixed = both[:dim] * (1.0 / total)
            high = mixed.astype(BF)
            o_ref[group, head, :, first : first + step] = high
            r_ref[group, head, :, first : first + step] = (mixed - high.astype(F32)).astype(BF)
            l_ref[head, :, place : place + step] = jnp.log2(total)


def attend_back_kernel(
    masked, length_ref, q_ref, k_ref, v_ref, m_ref, r_ref, g_ref, l_ref, *outs
):
    groups, _, heads, dim, count = q_ref.shape
    step = step_of(count)
    scale = dim ** (-0.5)
    for head in range(heads):
        key = wide(k_ref, head)
        keys = key.shape[1]
        turned = key.T
        value = jnp.concatenate([wide(v_ref, head), jnp.ones((8, keys), BF)], 0).T
        g_key = g_value = None
        for place in range(0, groups * count, step):
            group, first = divmod(place, count)
            here = slice(first, first + step)
            query = q_ref[group, 0, head, :, here]
            grad = g_ref[group, head, :, here]
            mixed = m_ref[group, head, :, here].astype(F32)
            mixed = mixed + r_ref[group, head, :, here].astype(F32)
            delta = -jnp.sum(grad.astype(F32) * mixed, 0, keepdims=True)
            high = delta.astype(BF)
            rest = (delta - high.astype(F32)).astype(BF)
            more = jnp.concatenate([grad, high, rest, jnp.zeros((6, step), BF)], 0)
            probs = jnp.exp2(
                dot(turned, query, ((1,), (0,))) * (scale * LOG2E)
                - l_ref[head, :, place : place + step]
            )
            if masked:
                probs = jnp.where(valid_keys(length_ref, keys, step), probs, 0.0)
            product = (probs * dot(value, more, ((1,), (0,)))).astype(BF)
            g_query = dot(key, product, ((1,), (0,))) * scale
            part_value = dot(grad, probs.astype(BF), ((1,), (1,)))
            part_key = dot(query, product, ((1,), (1,)))
            g_value = part_value if g_value is None else g_value + part_value
            g_key = part_key if g_key is None else g_key + part_key
            outs[0][group, 0, head, :, here] = g_query.astype(outs[0].dtype)
        g_key = g_key * scale
        if len(outs) == 1:
            for group in range(groups):
                here = slice(group * count, (group + 1) * count)
                outs[0][group, 1, head] = g_key[:, here].astype(BF)
                outs[0][group, 2, head] = g_value[:, here].astype(BF)
        else:
            outs[1][0, 0, head] = g_key
            outs[2][0, 0, head] = g_value


def costs(heads, queries, keys, dim, products):
    return pl.CostEstimate(
        flops=2 * products * heads * queries * keys * 256,
        transcendentals=heads * queries * keys,
        bytes_accessed=2 * products * heads * dim * (queries + keys),
    )


def head_block(shape, count, kind=0):
    groups, _, _, dim, tokens = shape
    return pl.BlockSpec((groups, 1, count, dim, tokens), lambda h: (0, kind, h, 0, 0))


def mix_block(shape, count):
    groups, _, _, dim, tokens = shape
    return pl.BlockSpec((groups, count, dim, tokens), lambda h: (0, h, 0, 0))


def attend(length, query, key, value, kinds, masked, most):
    groups, _, heads, dim, count = query.shape
    many = math.gcd(heads, most)
    total = groups * count
    keys = key.shape[0] * key.shape[4]
    return pl.pallas_call(
        partial(attend_kernel, masked),
        grid=(heads // many,),
        in_specs=[pl.BlockSpec(memory_space=pltpu.SMEM)]
        + [head_block(a.shape, many, kind) for a, kind in zip((query, key, value), kinds)],
        out_specs=[
            mix_block(query.shape, many),
            mix_block(query.shape, many),
            pl.BlockSpec((many, 1, total), lambda h: (h, 0, 0)),
        ],
        out_shape=[
            jax.ShapeDtypeStruct((groups, heads, dim, count), BF),
            jax.ShapeDtypeStruct((groups, heads, dim, count), BF),
            jax.ShapeDtypeStruct((heads, 1, total), F32),
        ],
        cost_estimate=costs(heads, total, keys, dim, 2),
        compiler_params=params(),
        name="attend",
    )(length, query, key, value)


def attend_back(length, query, key, value, kinds, kept, grad, masked, most, stacked):
    mixed, rest, logs = kept
    groups, _, heads, dim, count = query.shape
    many = math.gcd(heads, most)
    total = groups * count
    keys = key.shape[0] * key.shape[4]
    if stacked:
        out_specs = pl.BlockSpec((groups, 3, many, dim, count), lambda h: (0, 0, h, 0, 0))
        out_shape = jax.ShapeDtypeStruct((groups, 3, heads, dim, count), BF)
    else:
        out_specs = [head_block(a.shape, many) for a in (query, key, value)]
        out_shape = [jax.ShapeDtypeStruct(a.shape, F32) for a in (query, key, value)]
    return pl.pallas_call(
        partial(attend_back_kernel, masked),
        grid=(heads // many,),
        in_specs=[pl.BlockSpec(memory_space=pltpu.SMEM)]
        + [head_block(a.shape, many, kind) for a, kind in zip((query, key, value), kinds)]
        + [mix_block(query.shape, many)] * 3
        + [pl.BlockSpec((many, 1, total), lambda h: (h, 0, 0))],
        out_specs=out_specs,
        out_shape=out_shape,
        cost_estimate=costs(heads, total, keys, dim, 5),
        compiler_params=params(),
        name="attend_back",
    )(length, query, key, value, mixed, rest, grad, logs)


def work(rows, depth, tokens, moved):
    return pl.CostEstimate(
        flops=2 * rows * depth * tokens,
        transcendentals=0,
        bytes_accessed=moved,
    )


def lanes(width):
    return -(-width // 128) * 128


def full(shape):
    return pl.BlockSpec(shape, lambda *_: (0,) * len(shape))


def project(weight, kinds, values, dtypes, joined=False):
    _, cols, depth, width = weight.shape
    tokens = values[0].shape[1]
    outs = 1 if joined else len(kinds)

    def kernel(*refs):
        blocks = refs[: len(kinds)]
        given = refs[len(kinds) : -outs]
        total = None
        for index, block in enumerate(blocks):
            part = dot(block[0, 0], given[index % len(given)][...], ((0,), (0,)))
            if not joined:
                refs[index - outs][...] = part.astype(dtypes[index])
            total = part if total is None else total + part
        if joined:
            refs[-1][...] = total.astype(dtypes[0])

    return pl.pallas_call(
        kernel,
        grid=(cols,),
        in_specs=[
            pl.BlockSpec((1, 1, depth, width), partial(lambda k, c: (k, c, 0, 0), kind))
            for kind in kinds
        ]
        + [full(v.shape) for v in values],
        out_specs=[pl.BlockSpec((width, tokens), lambda c: (c, 0))] * outs,
        out_shape=[jax.ShapeDtypeStruct((cols * width, tokens), dtypes[i]) for i in range(outs)],
        cost_estimate=work(len(kinds) * cols * width, depth, tokens, 8 * depth * tokens),
        compiler_params=params(),
        name="project",
    )(*([weight] * len(kinds)), *values)


def rebuild(weight, kinds, values, dtype):
    _, cols, depth, width = weight.shape
    tokens = values[0].shape[1]
    tile = depth // 4

    def kernel(*refs):
        total = None
        for block, given in zip(refs[: len(kinds)], refs[len(kinds) : -1]):
            for col in range(cols):
                part = dot(block[0, col], given[col * width : (col + 1) * width, :], ((1,), (0,)))
                total = part if total is None else total + part
        refs[-1][...] = total.astype(dtype)

    return pl.pallas_call(
        kernel,
        grid=(4,),
        in_specs=[
            pl.BlockSpec((1, cols, tile, width), partial(lambda k, j: (k, 0, j, 0), kind))
            for kind in kinds
        ]
        + [full(v.shape) for v in values],
        out_specs=pl.BlockSpec((tile, tokens), lambda j: (j, 0)),
        out_shape=jax.ShapeDtypeStruct((depth, tokens), dtype),
        cost_estimate=work(depth, len(kinds) * cols * width, tokens, 8 * depth * tokens),
        compiler_params=params(),
        name="rebuild",
    )(*([weight] * len(kinds)), *values)


def project_blocks(base, blocks, width, values):
    many = len(blocks)
    depth, broad = blocks[0].shape
    tokens = values.shape[1]
    tile = depth // 4

    def kernel(base_ref, *refs):
        values_ref, out_ref = refs[many:]

        @pl.when(pl.program_id(0) == 0)
        def _():
            out_ref[...] = jnp.zeros_like(out_ref)

        for index in range(many):
            here = pl.ds(pl.multiple_of((index ^ base_ref[0]) * width, width), width)
            out_ref[here, :] += dot(refs[index][...], values_ref[...], ((0,), (0,)))[:width]

    return pl.pallas_call(
        kernel,
        grid_spec=pltpu.PrefetchScalarGridSpec(
            num_scalar_prefetch=1,
            grid=(4,),
            in_specs=[pl.BlockSpec((tile, broad), lambda j, b: (j, 0))] * many
            + [pl.BlockSpec((tile, tokens), lambda j, b: (j, 0))],
            out_specs=pl.BlockSpec((many * width, tokens), lambda j, b: (0, 0)),
        ),
        out_shape=jax.ShapeDtypeStruct((many * width, tokens), F32),
        cost_estimate=work(many * width, depth, tokens, 4 * depth * tokens),
        compiler_params=params(),
        name="project_blocks",
    )(base, *blocks, values)


def rebuild_blocks(base, blocks, width, values):
    many = len(blocks)
    depth, broad = blocks[0].shape
    tokens = values.shape[1]
    tile = depth // 4

    def kernel(base_ref, *refs):
        values_ref, out_ref = refs[many:]
        total = None
        for index in range(many):
            here = pl.ds(pl.multiple_of((index ^ base_ref[0]) * width, width), width)
            part = dot(refs[index][:, :width], values_ref[here, :], ((1,), (0,)))
            total = part if total is None else total + part
        out_ref[...] = total.astype(BF)

    return pl.pallas_call(
        kernel,
        grid_spec=pltpu.PrefetchScalarGridSpec(
            num_scalar_prefetch=1,
            grid=(4,),
            in_specs=[pl.BlockSpec((tile, broad), lambda j, b: (j, 0))] * many
            + [pl.BlockSpec(values.shape, lambda j, b: (0, 0))],
            out_specs=pl.BlockSpec((tile, tokens), lambda j, b: (j, 0)),
        ),
        out_shape=jax.ShapeDtypeStruct((depth, tokens), BF),
        cost_estimate=work(many * width, depth, tokens, 4 * depth * tokens),
        compiler_params=params(),
        name="rebuild_blocks",
    )(base, *blocks, values)


def outer(place, pairs, across, got=None):
    cols = lax.axis_size("col")
    lefts = []
    for left, _ in pairs:
        if not any(left is other for other in lefts):
            lefts.append(left)
    which = [next(i for i, l in enumerate(lefts) if l is left) for left, _ in pairs]
    rights = [right for _, right in pairs]
    many = len(pairs)
    rows, tokens = lefts[0].shape
    width = rights[0].shape[0] // cols
    broad = lanes(width)
    chunk = rows // 8
    flip = 1 if got is None else 0

    def kernel(place_ref, *refs):
        left_refs = refs[: len(lefts)]
        right_refs = refs[len(lefts) : len(lefts) + many]
        rest = refs[len(lefts) + many :]
        for index in range(many):
            right = right_refs[index][...]
            if broad > width:
                right = jnp.concatenate([right, jnp.zeros((broad - width, tokens), BF)], 0)
            part = dot(left_refs[which[index]][...], right, ((1,), (1,)))
            if got is None:
                rest[0][index, 0] = part.astype(BF)
            elif not across:
                part = (part + rest[0][index, 0].astype(F32)).astype(BF)

                @pl.when(pl.program_id(0) == place_ref[2])
                def _():
                    rest[1][index] = part.reshape(4, 2, chunk, broad)

                @pl.when(pl.program_id(0) != place_ref[2])
                def _():
                    rest[2][index] = part.reshape(4, 2, chunk, broad)
            else:
                part = (part + rest[0][index, 0].astype(F32)).astype(BF)
                part = part.reshape(4, 2, chunk, broad)

                @pl.when(place_ref[1] == 0)
                def _():
                    rest[1][index, 0] = part[:, 0]
                    rest[2][index, 0] = part[:, 1]

                @pl.when(place_ref[1] != 0)
                def _():
                    rest[1][index, 0] = part[:, 1]
                    rest[2][index, 0] = part[:, 0]

    whole = pl.BlockSpec((many, 1, rows, broad), lambda y, place: (0, y, 0, 0))
    piece = pl.BlockSpec((many, 1, 4, chunk, broad), lambda y, place: (0, y, 0, 0, 0))
    all_rows = pl.BlockSpec((many, 4, 2, chunk, broad), lambda y, place: (0, 0, 0, 0, 0))
    if got is None:
        given, out_specs = [], whole
        out_shape = jax.ShapeDtypeStruct((many, cols // 2, rows, broad), BF)
    else:
        given, out_specs = [got], [piece, piece] if across else [all_rows, all_rows]
        shape = (many, cols // 2, 4, chunk, broad) if across else (many, 4, 2, chunk, broad)
        out_shape = [jax.ShapeDtypeStruct(shape, BF)] * 2
    return pl.pallas_call(
        kernel,
        grid_spec=pltpu.PrefetchScalarGridSpec(
            num_scalar_prefetch=1,
            grid=(cols // 2,),
            in_specs=[pl.BlockSpec((rows, tokens), lambda y, place: (0, 0)) for _ in lefts]
            + [
                pl.BlockSpec((width, tokens), lambda y, place: (2 * y + (place[0] ^ flip), 0))
                for _ in rights
            ]
            + [whole] * len(given),
            out_specs=out_specs,
        ),
        out_shape=out_shape,
        cost_estimate=work(
            rows, tokens, many * cols // 2 * broad, 2 * rows * cols * broad * many
        ),
        compiler_params=params(),
        name="outer",
    )(place, *lefts, *rights, *given)


def outer_all(pairs):
    cols = lax.axis_size("col")
    parts = lax.axis_size("row")
    if not custom_mesh():
        blocks = [einsum("kt,cnt->ckn", a, b.reshape(cols, -1, b.shape[1])) for a, b in pairs]
        blocks = [b.reshape(cols, parts, -1, b.shape[2]).astype(BF) for b in blocks]
        return jnp.concatenate(blocks, 2)
    lefts = []
    for left, _ in pairs:
        if not any(left is other for other in lefts):
            lefts.append(left)
    which = [next(i for i, l in enumerate(lefts) if l is left) for left, _ in pairs]
    rights = [right for _, right in pairs]
    sizes = [left.shape[0] // parts for left, _ in pairs]
    width = rights[0].shape[0] // cols

    def kernel(*refs):
        for index, size in enumerate(sizes):
            left = refs[which[index]][...]
            part = dot(left, refs[len(lefts) + index][...], ((1,), (1,))).astype(BF)
            start = sum(sizes[:index])
            refs[-1][0, :, start : start + size] = part.reshape(parts, size, width)

    return pl.pallas_call(
        kernel,
        grid=(cols,),
        in_specs=[full(left.shape) for left in lefts]
        + [pl.BlockSpec((width, right.shape[1]), lambda c: (c, 0)) for right in rights],
        out_specs=pl.BlockSpec((1, parts, sum(sizes), width), lambda c: (c, 0, 0, 0)),
        out_shape=jax.ShapeDtypeStruct((cols, parts, sum(sizes), width), BF),
        cost_estimate=work(
            parts * sum(sizes), lefts[0].shape[1], cols * width, 3 * parts * sum(sizes) * cols * width
        ),
        compiler_params=params(),
        name="outer_all",
    )(*lefts, *rights)


def expand(weight, kind, values):
    _, many, depth, hidden = weight.shape
    tokens = values.shape[1]
    tile = 384 if hidden % 384 == 0 else hidden
    slope = 0.79788456
    cubic = 0.044715

    def kernel(weight_ref, values_ref, act_ref, slope_ref):
        for index in range(many):
            inner = dot(weight_ref[0, index], values_ref[...], ((0,), (0,)))
            square = inner * inner
            bent = jnp.tanh(inner * (slope + slope * cubic * square))
            half = 0.5 + 0.5 * bent
            act_ref[index] = (inner * half).astype(BF)
            rise = slope + 3.0 * slope * cubic * square
            slope_ref[index] = (half + 0.5 * inner * (1.0 - bent * bent) * rise).astype(BF)

    return pl.pallas_call(
        kernel,
        grid=(hidden // tile,),
        in_specs=[
            pl.BlockSpec((1, many, depth, tile), lambda j: (kind, 0, 0, j)),
            full(values.shape),
        ],
        out_specs=[pl.BlockSpec((many, tile, tokens), lambda j: (0, j, 0))] * 2,
        out_shape=[jax.ShapeDtypeStruct((many, hidden, tokens), BF)] * 2,
        cost_estimate=work(many * hidden, depth, tokens, 3 * many * hidden * depth),
        compiler_params=params(),
        name="expand",
    )(weight, values)


def expand_back(weight, kind, values, slopes):
    _, many, depth, hidden = weight.shape
    tokens = values.shape[1]
    tile = 384 if hidden % 384 == 0 else hidden

    def kernel(weight_ref, values_ref, slope_ref, out_ref):
        for index in range(many):
            part = dot(weight_ref[0, index], values_ref[...], ((0,), (0,)))
            out_ref[index] = (part * slope_ref[index].astype(F32)).astype(BF)

    return pl.pallas_call(
        kernel,
        grid=(hidden // tile,),
        in_specs=[
            pl.BlockSpec((1, many, depth, tile), lambda j: (kind, 0, 0, j)),
            full(values.shape),
            pl.BlockSpec((many, tile, tokens), lambda j: (0, j, 0)),
        ],
        out_specs=pl.BlockSpec((many, tile, tokens), lambda j: (0, j, 0)),
        out_shape=jax.ShapeDtypeStruct((many, hidden, tokens), BF),
        cost_estimate=work(many * hidden, depth, tokens, 3 * many * hidden * depth),
        compiler_params=params(),
        name="expand_back",
    )(weight, values, slopes)


def contract(weight, kind, values, added, dtype):
    _, many, depth, hidden = weight.shape
    tokens = values.shape[2]
    tile = depth // 4
    extra = [] if added is None else [added]

    def kernel(weight_ref, values_ref, *refs):
        total = refs[0][...] if extra else None
        for index in range(many):
            part = dot(weight_ref[0, index], values_ref[index], ((1,), (0,)))
            total = part if total is None else total + part
        refs[-1][...] = total.astype(dtype)

    line = pl.BlockSpec((tile, tokens), lambda j: (j, 0))
    return pl.pallas_call(
        kernel,
        grid=(4,),
        in_specs=[
            pl.BlockSpec((1, many, tile, hidden), lambda j: (kind, 0, j, 0)),
            full(values.shape),
        ]
        + [line] * len(extra),
        out_specs=line,
        out_shape=jax.ShapeDtypeStruct((depth, tokens), dtype),
        cost_estimate=work(depth, many * hidden, tokens, 3 * many * hidden * depth),
        compiler_params=params(),
        name="contract",
    )(weight, values, *extra)


def hidden_outer(grad_out, act, normed, grad_inner):
    many, hidden, tokens = act.shape
    depth = grad_out.shape[0]
    parts = 2 if hidden % 256 == 0 else 1
    tile = hidden // parts

    def kernel(out_ref, act_ref, normed_ref, inner_ref, grad_ref):
        kind = pl.program_id(0)

        @pl.when(kind == 0)
        def _():
            grad_ref[0, 0] = dot(normed_ref[...], inner_ref[0], ((1,), (1,))).astype(BF)

        @pl.when(kind == 1)
        def _():
            grad_ref[0, 0] = dot(out_ref[...], act_ref[0], ((1,), (1,))).astype(BF)

    return pl.pallas_call(
        kernel,
        grid=(2, many, parts),
        in_specs=[
            pl.BlockSpec((depth, tokens), lambda s, p, j: (0, 0)),
            pl.BlockSpec((1, tile, tokens), lambda s, p, j: (s * p, s * j, 0)),
            pl.BlockSpec((depth, tokens), lambda s, p, j: (0, 0)),
            pl.BlockSpec(
                (1, tile, tokens),
                lambda s, p, j: (p + s * (many - 1 - p), j + s * (parts - 1 - j), 0),
            ),
        ],
        out_specs=pl.BlockSpec((1, 1, depth, tile), lambda s, p, j: (s, p, 0, j)),
        out_shape=jax.ShapeDtypeStruct((2, many, depth, hidden), BF),
        cost_estimate=work(2 * depth, tokens, many * hidden, 5 * many * depth * hidden),
        compiler_params=params(),
        name="hidden_outer",
    )(grad_out, act, normed, grad_inner)


def assemble(place, own, got, middle=None):
    rows, width = own.shape[-2:]

    def kernel(place_ref, own_ref, got_ref, out_ref):
        @pl.when(pl.program_id(0) == place_ref[1])
        def _():
            out_ref[0, 0] = own_ref[...].reshape(rows, width)

        @pl.when(pl.program_id(0) != place_ref[1])
        def _():
            out_ref[0, 0] = got_ref[...].reshape(rows, width)

    def spec(ours):
        def index(x, z, place):
            phase = place[1] if ours else 1 - place[1]
            inside = (x == phase).astype(jnp.int32)
            level = (inside * z + (1 - inside) * 3 * (1 - phase)) ^ place[0]
            return (level, 0, 0) if middle is None else (level, middle, 0, 0)

        shape = (1, rows, width) if middle is None else (1, 1, rows, width)
        return pl.BlockSpec(shape, index)

    return pl.pallas_call(
        kernel,
        grid_spec=pltpu.PrefetchScalarGridSpec(
            num_scalar_prefetch=1,
            grid=(2, 4),
            in_specs=[spec(True), spec(False)],
            out_specs=pl.BlockSpec((1, 1, rows, width), lambda x, z, place: (z, x, 0, 0)),
        ),
        out_shape=jax.ShapeDtypeStruct((4, 2, rows, width), BF),
        cost_estimate=work(1, 1, 1, 32 * rows * width),
        name="assemble",
    )(place, own, got).reshape(8 * rows, width)


def normalize(values):
    average = jnp.mean(values, 0, keepdims=True)
    centred = values - average
    inverse = lax.rsqrt(jnp.mean(centred * centred, 0, keepdims=True) + EPSILON)
    return centred * inverse, inverse


def norm_back(grad, normal, inverse):
    average = jnp.mean(grad, 0, keepdims=True)
    crossed = jnp.mean(grad * normal, 0, keepdims=True)
    return inverse * (grad - average - normal * crossed)


def head_norm(values, gain):
    average = jnp.mean(values, 1, keepdims=True)
    centred = values - average
    variance = jnp.mean(centred * centred, 1, keepdims=True)
    return centred * lax.rsqrt(variance + EPSILON) * gain[None, :, None]


def rope_tables(places, head_dim):
    quarter = head_dim // 4
    freqs = jnp.exp(jnp.arange(quarter, dtype=F32) * (-4.0 * math.log(10000.0) / head_dim))
    rows = freqs[:, None] * places[0].astype(F32)[None, :]
    cols = freqs[:, None] * places[1].astype(F32)[None, :]
    angles = jnp.concatenate([rows, rows, cols, cols], 0)
    return jnp.cos(angles), jnp.sin(angles)


def rotate(values):
    quarter = values.shape[1] // 4
    one, two, three, four = (values[:, i * quarter : (i + 1) * quarter] for i in range(4))
    return jnp.concatenate([-two, one, -four, three], 1)


class Piece:
    def __init__(self, start, count, group, sequence):
        self.start = start
        self.count = count
        self.group = group
        self.sequence = sequence


def pieces_of(cols, sequences):
    mine = lax.axis_index("col")
    if cols == 4 and sequences == 3:
        return [
            Piece(0, L // 2, 2, mine // 2),
            Piece(2 * L, L // 4, 4, jnp.int32(2)),
        ]
    return [Piece(s * L, L // cols, cols, jnp.int32(s)) for s in range(sequences)]


def groups_of(size, cols):
    return [list(range(i, i + size)) for i in range(0, cols, size)]


def exchange(values, size, cols):
    if size == cols:
        return lax.all_to_all(values, "col", 0, 0, tiled=True)
    return lax.all_to_all(
        values, "col", 0, 0, tiled=True, axis_index_groups=groups_of(size, cols)
    )


def cut_size(pieces):
    return math.gcd(*(p.count for p in pieces), *(p.start for p in pieces))


def locate(pieces, unit, block):
    device = inside = None
    at = 0
    for piece in pieces:
        each = piece.count // unit
        rest = block - piece.start // unit
        there = (rest // each, at + rest % each)
        if device is None:
            device, inside = there
        else:
            later = (rest >= 0).astype(jnp.int32)
            device = later * there[0] + (1 - later) * device
            inside = later * there[1] + (1 - later) * inside
        at += each
    return device, inside


def to_tokens(arrays, pieces, cols, rows):
    width, tokens = arrays[0].shape
    kinds = len(arrays)
    unit = cut_size(pieces)
    total = sum(p.count for p in pieces)
    if unit % 128:
        values = jnp.stack([a.reshape(-1, rows, tokens) for a in arrays], 1).astype(BF)
        values = values.reshape(kinds * width, tokens)
        parts = [
            jnp.concatenate(
                [values[:, p.start + j * p.count : p.start + (j + 1) * p.count] for p in pieces], 1
            )
            for j in range(cols)
        ]
        dealt = jnp.stack(parts, 0)
    else:

        def kernel(*refs):
            for kind in range(kinds):
                for at in range(0, width, rows):
                    to = at * kinds + kind * rows
                    refs[-1][0, to : to + rows] = refs[kind][at : at + rows].astype(BF)

        def index(block):
            device, inside = locate(pieces, unit, block)
            return (device, 0, inside)

        dealt = pl.pallas_call(
            kernel,
            grid=(tokens // unit,),
            in_specs=[pl.BlockSpec((width, unit), lambda b: (0, b))] * kinds,
            out_specs=pl.BlockSpec((1, kinds * width, unit), index),
            out_shape=jax.ShapeDtypeStruct((cols, kinds * width, total), BF),
            cost_estimate=pl.CostEstimate(
                flops=0, transcendentals=0, bytes_accessed=4 * kinds * width * tokens
            ),
            name="deal",
        )(*arrays)
    got = exchange(dealt, cols, cols)
    return got.reshape(-1, total)


def to_features(values, pieces, cols, kinds, rows):
    got = exchange(values.reshape(cols, -1, values.shape[1]), cols, cols)
    unit = cut_size(pieces)
    width = got.shape[1] // kinds
    tokens = cols * got.shape[2]
    if unit % 128:
        parts = []
        at = 0
        for piece in pieces:
            parts += [got[j, :, at : at + piece.count] for j in range(cols)]
            at += piece.count
        whole = jnp.concatenate(parts, 1).astype(F32).reshape(-1, kinds, rows, tokens)
        return [whole[:, kind].reshape(width, tokens) for kind in range(kinds)]

    def kernel(got_ref, *refs):
        for kind in range(kinds):
            for at in range(0, width, rows):
                start = at * kinds + kind * rows
                refs[kind][at : at + rows] = got_ref[0, start : start + rows].astype(F32)

    def index(block):
        device, inside = locate(pieces, unit, block)
        return (device, 0, inside)

    return pl.pallas_call(
        kernel,
        grid=(tokens // unit,),
        in_specs=[pl.BlockSpec((1, kinds * width, unit), index)],
        out_specs=[pl.BlockSpec((width, unit), lambda b: (0, b))] * kinds,
        out_shape=[jax.ShapeDtypeStruct((width, tokens), F32)] * kinds,
        cost_estimate=pl.CostEstimate(
            flops=0, transcendentals=0, bytes_accessed=6 * kinds * width * tokens
        ),
        name="undeal",
    )(got)


def shared(values, axis):
    size = lax.axis_size(axis)
    return lax.all_to_all(
        jnp.broadcast_to(values[None], (size, *values.shape)), axis, 0, 0, tiled=True
    )


def swap(values, axis, bit):
    size = lax.axis_size(axis)
    return lax.ppermute(values, axis, [(i, i ^ bit) for i in range(size)])


def custom_mesh():
    return (lax.axis_size("row"), lax.axis_size("col")) == (8, 4)


def gather_weights(blocks):
    cols = lax.axis_size("col")
    most = max(block.shape[0] for block in blocks)
    padded = [jnp.pad(b, ((0, most - b.shape[0]), (0, 0))) for b in blocks]
    whole = lax.all_gather(jnp.stack(padded, 0), DEVICES, axis=1, tiled=True)
    return whole.reshape(len(blocks), cols, -1, blocks[0].shape[1])


class Gathering:
    last = 4

    def __init__(self, block, up, place):
        self.up = up
        self.place = place
        self.stage = 0
        self.state = [block]
        if not custom_mesh():
            cols = lax.axis_size("col")
            whole = lax.all_gather(block, DEVICES, axis=0, tiled=True)
            self.state = list(whole.reshape(cols, -1, block.shape[1]))
            self.stage = self.last

    def levels(self, block):
        return [block] + [swap(block, "row", 2 * level) for level in (1, 2, 3)]

    def advance(self):
        state = self.state
        self.stage += 1
        if self.stage == 1:
            self.state = [state[0], swap(state[0], "col", 2)] if self.up else self.levels(state[0])
        elif self.stage == 2:
            stack = jnp.stack(state, 0)
            self.state = self.levels(stack) if self.up else [stack, swap(stack, "col", 2)]
        elif self.stage == 3 and self.up:
            stack = jnp.stack(state, 0)
            self.state = [stack, swap(stack, "row", 1)]
        elif self.stage == 3:
            self.state = state + [swap(a, "row", 1) for a in state]
        else:
            if self.up:
                mine, other = (assemble(self.place, *state, k) for k in (0, 1))
            else:
                mine = assemble(self.place, state[0], state[2])
                other = assemble(self.place, state[1], state[3])
            self.state = [mine, swap(mine, "col", 1), other, swap(other, "col", 1)]

    def result(self):
        while self.stage < self.last:
            self.advance()
        return self.state


def pick(values, axis, index):
    return lax.dynamic_index_in_dim(values, index, axis, False)


def add(left, right):
    return (left.astype(F32) + right.astype(F32)).astype(BF)


class Reduction:
    last = 4

    def __init__(self, place, pairs, across):
        self.place = place
        self.across = across
        self.pairs = pairs
        self.width = pairs[0][1].shape[0] // lax.axis_size("col")
        self.stage = 0
        if custom_mesh():
            self.state = [swap(outer(place, pairs, across), "col", 1)]
            return
        self.stage = self.last
        cols = lax.axis_size("col")
        whole = jnp.stack(
            [einsum("kt,cnt->ckn", a, b.reshape(cols, -1, b.shape[1])) for a, b in pairs], 0
        )
        flat = whole.reshape(len(pairs), -1, whole.shape[3]).astype(BF)
        self.state = [lax.psum_scatter(flat, DEVICES, scatter_dimension=1, tiled=True)]

    def advance(self):
        state = self.state
        self.stage += 1
        if self.stage == 1:
            here, away = outer(self.place, self.pairs, self.across, state[0])
            self.state = [here, swap(away, "row", 1) if self.across else swap(away, "col", 2)]
        elif self.stage == 2:
            axis, index = (1, self.place[2]) if self.across else (2, self.place[1])
            away = add(*(pick(a, axis, 1 - index) for a in state))
            here = add(*(pick(a, axis, index) for a in state))
            self.state = [here, swap(away, "col", 2) if self.across else swap(away, "row", 1)]
        elif self.stage == 3:
            level = lax.axis_index("row") // 2
            total = add(*state)
            self.state = [pick(total, 1, level)] + [
                swap(pick(total, 1, level ^ other), "row", 2 * other) for other in (1, 2, 3)
            ]
        else:
            total = state[0].astype(F32)
            for other in state[1:]:
                total = total + other.astype(F32)
            self.state = [total[..., : self.width]]

    def result(self):
        while self.stage < self.last:
            self.advance()
        return self.state[0].astype(F32)


def tick(values, running):
    active = [r for r in running if r.stage < r.last]
    if active:
        values, states = lax.optimization_barrier((values, [r.state for r in active]))
        for beside, state in zip(active, states):
            beside.state = state
            beside.advance()
    return values


def after(values, done):
    return lax.optimization_barrier((values, done))[0]


def shards(
    latents,
    skip_input,
    condition,
    text_states,
    text_lengths,
    positions,
    out_grad,
    skip_weight,
    modulation,
    self_inputs,
    self_output,
    cross_query,
    cross_keyvalue,
    cross_output,
    expand_weight,
    reduce_weight,
    skip_gain,
    skip_bias,
    cross_gain,
    cross_bias,
    hidden_gain,
    hidden_bias,
    query_gain,
    key_gain,
    cross_query_gain,
    text_key_gain,
):
    cols = lax.axis_size("col")
    rows = lax.axis_size("row")
    mine = lax.axis_index("col")
    my_row = lax.axis_index("row")
    width, row_tokens = latents.shape
    depth = width * cols
    dim = query_gain.shape[0]
    heads = depth // dim
    sequences = row_tokens // L
    tokens = row_tokens // cols
    texts = text_states.shape[1]
    keys = -(-texts // KEYPAD) * KEYPAD
    pieces = pieces_of(cols, sequences)
    starts = [sum(p.count for p in pieces[:i]) for i in range(len(pieces))]
    place = jnp.stack([my_row // 2, my_row % 2]).astype(jnp.int32)
    corner = jnp.stack([mine % 2, my_row % 2, mine // 2]).astype(jnp.int32)
    base = (mine if custom_mesh() else jnp.zeros_like(mine)).astype(jnp.int32)[None]

    def cut(values, index):
        return values[..., starts[index] : starts[index] + pieces[index].count]

    block_rows = depth // rows
    both = to_tokens([latents, skip_input], pieces, cols, block_rows)

    weights_one = gather_weights([*(self_inputs[:, i] for i in range(3)), self_output.T])
    weights_two = gather_weights(
        [cross_query, cross_output.T, *(cross_keyvalue[:, i] for i in range(2))]
    )
    skip_block = jnp.concatenate([skip_weight[0], skip_weight[1]], 0)
    skip_block = jnp.pad(skip_block, ((0, 0), (0, lanes(width) - width)))
    w_skip = Gathering(skip_block, False, place).result()
    weights_hidden = gather_weights([expand_weight, reduce_weight.T])

    places = jnp.concatenate(
        [
            lax.dynamic_slice_in_dim(positions, p.start + mine * p.count, p.count, 1)
            for p in pieces
        ],
        1,
    )

    embed = jax.nn.silu(after(condition, both).astype(F32)).astype(BF)
    embed = shared(embed, "row").reshape(-1, width)
    embed = shared(embed, "col").transpose(1, 0, 2).reshape(-1, depth)
    embed_rows = lax.dynamic_slice_in_dim(embed, my_row * block_rows, block_rows, 1)
    modul = einsum("sd,dke->ske", embed_rows, modulation).reshape(rows, sequences, 2, width)
    modul = jnp.sum(lax.all_to_all(modul, "row", 0, 0, tiled=True), 0)
    gains = jnp.stack(
        [skip_gain, skip_bias, cross_gain, cross_bias, hidden_gain, hidden_bias], 0
    )
    table = jnp.concatenate([gains, modul.reshape(-1, width)], 0)
    table = shared(table, "col").transpose(1, 0, 2).reshape(-1, depth)
    modul = table[6:].reshape(sequences, 2, depth)
    chosen = [lax.dynamic_index_in_dim(modul, p.sequence, 0, False) for p in pieces]
    columns = lax.optimization_barrier(jnp.concatenate([table[:6], *chosen], 0)).T
    gain_skip, bias_skip, gain_cross, bias_cross, gain_hidden, bias_hidden = (
        columns[:, i : i + 1] for i in range(6)
    )
    token_index = lax.broadcasted_iota(jnp.int32, (1, tokens), 1)

    def per_token(which):
        result = columns[:, 6 + which : 7 + which]
        for index in range(1, len(pieces)):
            column = columns[:, 6 + 2 * index + which : 7 + 2 * index + which]
            result = jnp.where(token_index >= starts[index], column, result)
        return jnp.broadcast_to(result, (depth, tokens))

    shifting = per_token(0)
    scaling = 1.0 + per_token(1)

    text = shared(jnp.pad(after(text_states, both), ((0, 0), (0, keys - texts), (0, 0))), "col")
    joined = project_blocks(base, w_skip, width, both)
    skip_normal, skip_inverse = normalize(joined)
    stream = skip_normal * gain_skip + bias_skip
    normal_one, inverse_one = normalize(stream)
    normed_one = (normal_one * scaling + shifting).astype(BF)
    raw = project(weights_one, [0, 1, 2], [normed_one], [F32, F32, BF])
    raw, text = lax.optimization_barrier((raw, text))
    raw = [r.reshape(heads, dim, tokens) for r in raw]
    cosine, sine = rope_tables(places, dim)

    def self_piece(value, gain):
        normal = head_norm(value, gain)
        return normal * cosine[None] + rotate(normal) * sine[None]

    rot_query, query_pull = jax.vjp(self_piece, raw[0], query_gain)
    rot_key, key_pull = jax.vjp(self_piece, raw[1], key_gain)
    triple = [rot_query.astype(BF), rot_key.astype(BF), raw[2]]

    def to_heads(parts, index):
        size = pieces[index].group
        split = [cut(p, index).reshape(size, heads // size, dim, -1) for p in parts]
        return exchange(jnp.stack(split, 1), size, cols)

    none = jnp.zeros((1,), jnp.int32)
    saved_self = []
    mixed_parts = []
    for index, piece in enumerate(pieces):
        whole = to_heads(triple, index)
        kept = attend(none, whole, whole, whole, (0, 1, 2), False, 2)
        saved_self.append((whole, kept))
        mixed_parts.append(exchange(kept[0], piece.group, cols).reshape(depth, -1))
    mixed_one = jnp.concatenate(mixed_parts, 1)
    text = after(text, mixed_one)
    stream = stream + rebuild(weights_one, [3], [mixed_one], F32)
    normal_two, inverse_two = normalize(stream)
    normed_two = (normal_two * gain_cross + bias_cross).astype(BF)
    raw_cross = project(weights_two, [0], [normed_two], [F32])[0].reshape(heads, dim, tokens)
    norm_query, cross_pull = jax.vjp(head_norm, raw_cross, cross_query_gain)
    text = jnp.concatenate(
        [lax.dynamic_index_in_dim(text, p.sequence, 1, False) for p in pieces], 1
    )
    text = text.transpose(0, 2, 1).reshape(-1, len(pieces) * keys)
    text_rows = text.shape[0] // rows
    text_wide = jnp.pad(
        text.reshape(rows, text_rows, -1), ((0, 0), (0, block_rows - text_rows), (0, 0))
    ).reshape(depth, -1)
    raw_text, value_two = project(weights_two, [2, 3], [text_wide], [F32, BF])
    norm_key, text_pull = jax.vjp(head_norm, raw_text.reshape(heads, dim, -1), text_key_gain)
    query_two = norm_query.astype(BF)
    key_two = norm_key.astype(BF)
    value_two = value_two.reshape(heads, dim, -1)
    saved_cross = []
    mixed_parts = []
    for index, piece in enumerate(pieces):
        length = lax.dynamic_index_in_dim(text_lengths, piece.sequence, 0, True)
        here = slice(index * keys, (index + 1) * keys)
        inputs = [cut(query_two, index), key_two[:, :, here], value_two[:, :, here]]
        inputs = [length] + [a[None, None] for a in inputs] + [(0, 0, 0)]
        kept = attend(*inputs, True, 4)
        saved_cross.append((inputs, kept))
        mixed_parts.append(kept[0].reshape(depth, -1))
    mixed_two = jnp.concatenate(mixed_parts, 1)
    stream = stream + rebuild(weights_two, [1], [mixed_two], F32)
    normal_three, inverse_three = normalize(stream)
    normed_three = (normal_three * gain_hidden + bias_hidden).astype(BF)
    grad_out = to_tokens([after(out_grad, joined)], pieces, cols, width)
    act, slopes = expand(weights_hidden, 0, normed_three)

    g_inner = expand_back(weights_hidden, 1, grad_out, slopes)
    g_hidden = hidden_outer(grad_out, act, normed_three, g_inner)
    g_inner, g_hidden = lax.optimization_barrier((g_inner, g_hidden))
    g_normed = contract(weights_hidden, 0, g_inner, None, F32)
    g_hidden = lax.psum_scatter(
        g_hidden.reshape(2, -1, g_hidden.shape[3]), DEVICES, scatter_dimension=1, tiled=True
    ).astype(F32)
    g_hidden_gain = jnp.sum(g_normed * normal_three, 1)
    g_hidden_bias = jnp.sum(g_normed, 1)
    g_stream = grad_out.astype(F32) + norm_back(g_normed * gain_hidden, normal_three, inverse_three)

    g_low = g_stream.astype(BF)
    g_mixed = project(weights_two, [1], [g_low], [BF])[0].reshape(heads, dim, tokens)
    pairs = [(g_low, mixed_two)]
    g_queries = []
    g_keys = []
    g_values = []
    for index, piece in enumerate(pieces):
        inputs, kept = saved_cross[index]
        grads = attend_back(*inputs, kept, cut(g_mixed, index)[None], True, 4, False)
        g_queries.append(grads[0][0, 0])
        g_keys.append(grads[1][0, 0])
        g_values.append(grads[2][0, 0])
    g_raw_cross, g_cq_gain = cross_pull(jnp.concatenate(g_queries, 2))
    g_raw_text, g_tk_gain = text_pull(jnp.concatenate(g_keys, 2))
    g_craw = g_raw_cross.astype(BF).reshape(depth, tokens)
    g_pair = [
        g_raw_text.astype(BF).reshape(depth, -1),
        jnp.concatenate(g_values, 2).astype(BF).reshape(depth, -1),
    ]
    g_normed = rebuild(weights_two, [0], [g_craw], F32)
    pairs.append((normed_two, g_craw))
    g_cross_gain = jnp.sum(g_normed * normal_two, 1)
    g_cross_bias = jnp.sum(g_normed, 1)
    g_stream = g_stream + norm_back(g_normed * gain_cross, normal_two, inverse_two)

    g_low = g_stream.astype(BF)
    g_mixed = project(weights_one, [3], [g_low], [BF])[0].reshape(heads, dim, tokens)
    pairs += [(g_low, mixed_one), *((text, g) for g in g_pair)]
    middle = outer_all(pairs)
    middle = lax.psum_scatter(
        middle.reshape(-1, width), DEVICES, scatter_dimension=0, tiled=True
    ).astype(F32)
    ends = [block_rows, 2 * block_rows, 3 * block_rows, 3 * block_rows + text_rows]
    middle = jnp.split(middle, ends, 0)
    g_parts = []
    for index, piece in enumerate(pieces):
        whole, kept = saved_self[index]
        grad = exchange(
            cut(g_mixed, index).reshape(piece.group, -1, dim, piece.count), piece.group, cols
        )
        part = attend_back(
            none, whole, whole, whole, (0, 1, 2), kept, grad, False, 2, True
        )
        g_parts.append(exchange(part, piece.group, cols))
    g_heads = [
        jnp.concatenate([p[:, i].reshape(heads, dim, -1) for p in g_parts], 2) for i in range(3)
    ]
    g_raw_q, g_q_gain = query_pull(g_heads[0].astype(F32))
    g_raw_k, g_k_gain = key_pull(g_heads[1].astype(F32))
    g_triple = [
        g.reshape(depth, tokens) for g in (g_raw_q.astype(BF), g_raw_k.astype(BF), g_heads[2])
    ]
    r_self = [
        Reduction(corner, [(normed_one, g) for g in g_triple[:2]], True),
        Reduction(corner, [(normed_one, g_triple[2])], False),
    ]
    g_normed = rebuild(weights_one, [0, 1, 2], g_triple, F32)
    g_normed = tick(g_normed, r_self)
    g_normed, kept = lax.optimization_barrier((g_normed, [r.state[0] for r in r_self]))
    for beside, part in zip(r_self, kept):
        beside.state[0] = part
    crossed = g_normed * normal_one
    sums = jnp.stack(
        [
            jnp.stack([jnp.sum(cut(g_normed, i), 1), jnp.sum(cut(crossed, i), 1)], 0)
            for i in range(len(pieces))
        ],
        0,
    )
    which = jnp.stack(
        [jnp.where(jnp.arange(sequences) == p.sequence, 1.0, 0.0) for p in pieces], 0
    )
    g_modul = jnp.sum(which[:, :, None, None] * sums[:, None], 0)
    g_modul = g_modul.reshape(sequences, 2, cols, width).transpose(2, 0, 1, 3)
    g_modul = jnp.sum(lax.all_to_all(g_modul, "col", 0, 0, tiled=True), 0).astype(BF)
    g_stream = g_stream + norm_back(g_normed * scaling, normal_one, inverse_one)

    g_skip_gain = jnp.sum(g_stream * skip_normal, 1)
    g_skip_bias = jnp.sum(g_stream, 1)
    g_joined = norm_back(g_stream * gain_skip, skip_normal, skip_inverse).astype(BF)
    g_joined, g_modul = lax.optimization_barrier((g_joined, g_modul))
    r_skip = Reduction(corner, [(both, g_joined)], True)
    g_both = rebuild_blocks(base, w_skip, width, g_joined)

    g_gains = jnp.stack(
        [g_skip_gain, g_skip_bias, g_cross_gain, g_cross_bias, g_hidden_gain, g_hidden_bias], 0
    )
    g_gains = g_gains.reshape(6, cols, width).transpose(1, 0, 2)
    g_head = jnp.stack([g_q_gain, g_k_gain, g_cq_gain, g_tk_gain], 0).reshape(1, -1, width)
    packed = jnp.concatenate([g_gains, jnp.broadcast_to(g_head, (cols, *g_head.shape[1:]))], 1)
    packed = jnp.sum(lax.all_to_all(packed, "col", 0, 0, tiled=True), 0)
    packed = jnp.concatenate([packed, g_modul.reshape(-1, width).astype(F32)], 0)
    packed = shared(packed, "row")
    many = packed.shape[1] - 2 * sequences
    packed, g_modul = jnp.sum(packed[:, :many], 0), packed[:, many:].astype(BF)
    g_modul = g_modul.reshape(-1, 2, width)

    g_both, packed, g_modul = lax.optimization_barrier((g_both, packed, g_modul))
    if custom_mesh():
        g_both, got = lax.optimization_barrier((g_both, r_skip.state[0]))
        here, away = outer(corner, r_skip.pairs, True, got)
        g_both, away, act = lax.optimization_barrier((g_both, away, act))
        r_skip.stage, r_skip.state = 1, [here, swap(away, "row", 1)]
    g_latents, g_skip = to_features(g_both, pieces, cols, 2, block_rows)
    output = contract(weights_hidden, 1, act, stream, BF)
    output = tick(output, r_self)
    output = tick(output, [r_skip])
    if custom_mesh():
        states = [r.state for r in r_self]
        states, r_skip.state, g_latents, g_skip = lax.optimization_barrier(
            (states, r_skip.state, g_latents, g_skip)
        )
        r_skip.advance()
        for beside, state in zip(r_self, states):
            beside.state = state
            beside.advance()
    output, g_hidden = lax.optimization_barrier((output, g_hidden))
    result = to_features(after(output, g_skip), pieces, cols, 1, width)[0]
    g_modulation = einsum("sd,ske->dke", embed_rows, g_modul)
    g_gains = packed[:6]
    g_head = packed[6:].reshape(4, dim)
    return (
        result,
        g_latents,
        g_skip,
        r_skip.result().reshape(2, block_rows, width),
        g_modulation,
        jnp.concatenate([r.result() for r in r_self], 0).transpose(1, 0, 2),
        middle[2].T,
        middle[1],
        jnp.stack(middle[3:], 1),
        middle[0].T,
        g_hidden[0],
        g_hidden[1].T,
        *[g_gains[i] for i in range(6)],
        *[g_head[i] for i in range(4)],
    )


def solution(mesh):
    return jax.shard_map(
        shards,
        mesh=mesh,
        in_specs=(
            P("col", "row"),
            P("col", "row"),
            P("row", "col"),
            P("row", None, "col"),
            P("row"),
            P(None, "row"),
            P("col", "row"),
            P(None, "row", "col"),
            P("row", None, "col"),
            P("row", None, "col"),
            P("col", "row"),
            P("row", "col"),
            P("row", None, "col"),
            P("col", "row"),
            P("row", "col"),
            P("col", "row"),
            P("col"),
            P("col"),
            P("col"),
            P("col"),
            P("col"),
            P("col"),
            P(),
            P(),
            P(),
            P(),
        ),
        out_specs=(
            P("col", "row"),
            P("col", "row"),
            P("col", "row"),
            P(None, "row", "col"),
            P("row", None, "col"),
            P("row", None, "col"),
            P("col", "row"),
            P("row", "col"),
            P("row", None, "col"),
            P("col", "row"),
            P("row", "col"),
            P("col", "row"),
            P("col"),
            P("col"),
            P("col"),
            P("col"),
            P("col"),
            P("col"),
            P(),
            P(),
            P(),
            P(),
        ),
        check_vma=False,
    )
```
